32 devices in a mesh: seq: 4 (over y, x), grp: 8 (over z, core).
Axes of the slice: x: 2, y: 2, z: 4, core: 2. Of those that a mesh axis runs over, the one named last changes fastest.
Arguments:
- tokens: bfloat16 [2, 8, 512, 512], P(None, 'grp', 'seq'), may hold values from -6 to 6
- layout: int32 [2, 8], P(None, 'grp'), may hold values from 0 to 1, as said below
- filters: float32 [512, 24], replicated, may hold values from -0.25 to 0.25
- gain_mix: bfloat16 [512], P(('seq', 'grp')), may hold values from 0.25 to 1.75
- spectral_proj: bfloat16 [24576, 512], P(('seq', 'grp')), may hold values from -0.0546875 to 0.0546875
- ar_proj: bfloat16 [1536, 512], P(('seq', 'grp')), may hold values from -0.15625 to 0.15625
- gain_mlp: bfloat16 [512], P(('seq', 'grp')), may hold values from 0.25 to 1.75
- w_gate: bfloat16 [512, 2048], P(('seq', 'grp')), may hold values from -0.25 to 0.25
- w_up: bfloat16 [512, 2048], P(('seq', 'grp')), may hold values from -0.25 to 0.25
- w_down: bfloat16 [2048, 512], P(('seq', 'grp')), may hold values from -0.1875 to 0.1875
- out_grad: bfloat16 [2, 8, 512, 512], P(None, 'grp', 'seq'), may hold values from -6 to 6
Outputs:
- out: float32 [2, 8, 512, 512], P(None, 'grp', 'seq')
- tokens_grad: float32 [2, 8, 512, 512], P(None, 'grp', 'seq')
- gain_mix_grad: float32 [512], P(('seq', 'grp'))
- spectral_proj_grad: float32 [24576, 512], P(('seq', 'grp'))
- ar_proj_grad: float32 [1536, 512], P(('seq', 'grp'))
- gain_mlp_grad: float32 [512], P(('seq', 'grp'))
- w_gate_grad: float32 [512, 2048], P(('seq', 'grp'))
- w_up_grad: float32 [512, 2048], P(('seq', 'grp'))
- w_down_grad: float32 [2048, 512], P(('seq', 'grp'))
The draws below stay inside these ranges and needn't reach their ends.
Inputs may be any that keep to these rules, and one draw needn't show every extreme that they name: In every group the layout alternates from one micro-batch to the next: 0 holds one sequence of 512 positions, 1 holds four of 128.
All inputs are finite; a program needn't handle non-finite values.
Results may differ from the reference program's by a relative error of at most 0.0069.
Values may be sent and summed in bfloat16 or wider, within the bound.
A program may use at most 208 MiB of HBM per device.

```python
import jax
import jax.numpy as jnp
from jax import lax

D = 512
K = 24
F = 2048
MICRO = 2
SEQLEN = 512
N_GRP = 8


def draw_layout(key, part):
    starting = jax.random.randint(key, (1, N_GRP), 0, 2)
    stepping = lax.broadcasted_iota(jnp.int32, (MICRO, N_GRP), 0)
    return ((starting + stepping) % 2).astype(jnp.int32)


def raised(values, stream_key, source, target, parts, factor):
    owner, partner = [(jnp.arange(values.shape[position]) // (values.shape[position] // parts)).reshape([-1 if axis == position else 1 for axis in range(values.ndim)]) for position in (source, target)]
    chosen = jax.random.permutation(stream_key, parts)[partner]
    strong = (owner == chosen) | (owner == (partner + parts // 2) % parts)
    return jnp.where(strong, factor * values, values)


def block_levels(stream_key, dims, cuts, low, largest):
    def one(dim, parts):
        steps = jax.random.uniform(jax.random.fold_in(jax.random.fold_in(stream_key, 6), dim), (parts,), jnp.float32, low / len(cuts), largest / len(cuts))
        return jnp.repeat(jnp.exp(steps), dims[dim] // parts).reshape((-1,) + (1,) * (len(dims) - dim - 1))

    level = one(*cuts[0])
    for cut in cuts[1:]:
        level = level * one(*cut)
    return level


def noise(own_key, shape, scale, bound, shards=(), dtype=jnp.bfloat16):
    entries = scale * jax.random.normal(own_key, shape, jnp.float32)
    if shards:
        entries = entries * block_levels(own_key, shape, shards, -0.22, 0.18)
    return jnp.clip(entries, -bound, bound).astype(dtype)


def heavy_noise(own_key, extent, spread, limit, cuts, heavy, dtype=jnp.bfloat16):
    array = spread * jax.random.normal(own_key, extent, jnp.float32)
    if cuts:
        array = array * block_levels(own_key, extent, cuts, -0.22, 0.18)
    return jnp.clip(raised(array, jax.random.fold_in(own_key, 3), *heavy), -limit, limit).astype(dtype)


def setup_inputs(seed: int = 0) -> dict:
    keys = jax.random.split(jax.random.key(seed), 12)
    return {
        "tokens": noise(keys[0], (MICRO, N_GRP, SEQLEN, D), 1.0, 6.0, ((1, 8), (2, 4))),
        "layout": draw_layout(jax.random.fold_in(keys[11], 71), 0),
        "filters": noise(keys[2], (SEQLEN, K), SEQLEN ** -0.5, 0.25, (), jnp.float32),
        "gain_mix": jnp.clip(1.0 + 0.15 * jax.random.normal(keys[3], (D,), jnp.float32), 0.25, 1.75).astype(jnp.bfloat16),
        "spectral_proj": noise(keys[4], (2 * K * D, D), (K * D) ** -0.5, 0.0546875, ((0, 32),)),
        "ar_proj": noise(keys[5], (3 * D, D), (3 * D) ** -0.5, 0.15625, ((0, 32),)),
        "gain_mlp": jnp.clip(1.0 + 0.15 * jax.random.normal(keys[6], (D,), jnp.float32), 0.25, 1.75).astype(jnp.bfloat16),
        "w_gate": noise(keys[7], (D, F), D ** -0.5, 0.25, ((0, 32),)),
        "w_up": noise(keys[8], (D, F), D ** -0.5, 0.25, ((0, 32),)),
        "w_down": noise(keys[9], (F, D), (F // 2) ** -0.5, 0.1875, ((0, 32),)),
        "out_grad": heavy_noise(keys[10], (MICRO, N_GRP, SEQLEN, D), 1.0, 6.0, ((1, 8), (2, 4)), (1, 3, 8, 2.0)),
    }


EPSILON = 1e-05
HIGHEST = lax.Precision.HIGHEST

@jax.custom_vjp
def low(v):
    return lax.optimization_barrier(v.astype(jnp.bfloat16)).astype(jnp.float32)

@jax.custom_vjp
def low_back(v):
    return v

def low_keep(v):
    return (low(v), None)

def low_pass(kept, grad):
    return (grad,)

def back_keep(v):
    return (v, None)

def back_low(kept, grad):
    return (low(grad),)
low.defvjp(low_keep, low_pass)
low_back.defvjp(back_keep, back_low)

def matmul(left, right):
    return jnp.dot(left, right, precision=HIGHEST, preferred_element_type=jnp.float32)

def filter_all(normed, table):
    seq_rows = normed.shape[0]
    signs = 1.0 - 2.0 * (jnp.arange(seq_rows) % 2).astype(jnp.float32)
    both = jnp.stack([normed, normed * signs[:, None]], axis=1)
    spectrum = jnp.fft.rfft(both, n=2 * seq_rows, axis=0)
    kernel = jnp.fft.rfft(table[:seq_rows], n=2 * seq_rows, axis=0)
    product = kernel[:, :, None, None] * spectrum[:, None, :, :]
    conv = jnp.fft.irfft(product, n=2 * seq_rows, axis=0)[:seq_rows]
    factor = jnp.stack([jnp.ones((seq_rows,), jnp.float32), signs], axis=1)
    return conv * factor[:, None, :, None]

def layer(params, inputs, layout_flag, filters):
    mix_gain, spec_proj, hist_proj, mlp_gain, gate_proj, up_proj, down_proj = params
    seq_rows, width = inputs.shape
    inv_one = lax.rsqrt(lax.optimization_barrier(jnp.mean(inputs * inputs, axis=-1, keepdims=True)) + EPSILON)
    normed = low(inputs * inv_one * mix_gain)
    whole = filter_all(normed, filters)
    quarter = seq_rows // 4
    pieces = jax.vmap(lambda part_rows: filter_all(part_rows, filters))(normed.reshape(4, quarter, width))
    pieces = pieces.reshape(whole.shape)
    spectral = low(jnp.where(layout_flag == 1, pieces, whole).reshape(seq_rows, -1))
    seg_len = jnp.where(layout_flag == 1, quarter, seq_rows)
    place = jnp.arange(seq_rows) % seg_len
    extended = jnp.concatenate([jnp.zeros((2, width), jnp.float32), normed], axis=0)
    lag_one = jnp.where((place >= 1)[:, None], extended[1:seq_rows + 1], 0.0)
    lag_two = jnp.where((place >= 2)[:, None], extended[:seq_rows], 0.0)
    history = jnp.concatenate([normed, lag_one, lag_two], axis=1)
    mixer = low_back(matmul(spectral, spec_proj) + matmul(history, hist_proj))
    hidden = inputs + mixer
    inv_two = lax.rsqrt(lax.optimization_barrier(jnp.mean(hidden * hidden, axis=-1, keepdims=True)) + EPSILON)
    mlp_in = low(hidden * inv_two * mlp_gain)
    gate = low_back(matmul(mlp_in, gate_proj))
    upval = low_back(matmul(mlp_in, up_proj))
    mixed = low(jax.nn.gelu(gate) * upval)
    return hidden + matmul(mixed, down_proj)

def reference(tokens, layout, filters, gain_mix, spectral_proj, ar_proj, gain_mlp, w_gate, w_up, w_down, out_grad):
    params = tuple((weight_arg.astype(jnp.float32) for weight_arg in (gain_mix, spectral_proj, ar_proj, gain_mlp, w_gate, w_up, w_down)))
    flat_in = tokens.astype(jnp.float32).reshape(MICRO * N_GRP, SEQLEN, D)
    flags = layout.reshape(MICRO * N_GRP)
    step_fn = jax.checkpoint(layer)

    def run(weights, sequences):

        def advance(carried, item):
            return (carried, step_fn(weights, item[0], item[1], filters))
        return lax.scan(advance, jnp.zeros((), jnp.float32), (sequences, flags))[1]
    outputs, pullback = jax.vjp(run, params, flat_in)
    weight_grads, input_grads = pullback(out_grad.astype(jnp.float32).reshape(MICRO * N_GRP, SEQLEN, D))
    full_shape = (MICRO, N_GRP, SEQLEN, D)
    return (outputs.reshape(full_shape), input_grads.reshape(full_shape), weight_grads[0], weight_grads[1], weight_grads[2], weight_grads[3], weight_grads[4], weight_grads[5], weight_grads[6])
```

```python
import functools

import jax
import jax.numpy as jnp
from jax import lax
from jax.experimental import pallas as pl
from jax.experimental.pallas import tpu as pltpu
from jax.sharding import PartitionSpec as P

EPSILON = 1e-05
BF16 = jnp.bfloat16
F32 = jnp.float32
MESH = pl.DeviceIdType.MESH
DMA = pltpu.SemaphoreType.DMA
ANY = pl.BlockSpec(memory_space=pl.ANY)
WHOLE = pl.BlockSpec(memory_space=pltpu.VMEM)
VMEM_LIMIT = 60 * 1024 * 1024
CORES = 2


def dot_nn(a, b):
    return lax.dot_general(a, b, (((1,), (0,)), ((), ())), preferred_element_type=F32)


def dot_tn(a, b):
    return lax.dot_general(a, b, (((0,), (0,)), ((), ())), preferred_element_type=F32)


def dot_nt(a, b):
    return lax.dot_general(a, b, (((1,), (1,)), ((), ())), preferred_element_type=F32)


def params(collective_id=None):
    return pltpu.CompilerParams(
        collective_id=collective_id,
        has_side_effects=collective_id is not None,
        vmem_limit_bytes=VMEM_LIMIT,
    )


def remote(src, dst, send, recv, where):
    return pltpu.make_async_remote_copy(
        src_ref=src, dst_ref=dst, send_sem=send, recv_sem=recv, device_id=where, device_id_type=MESH
    )


def place(seq_count, line):
    s = lax.axis_index("seq")
    g = lax.axis_index("grp")
    return s, lax.div(g, CORES), lax.rem(g, CORES), g


def greet(seq_count, line, s, z, c, g, chain=False, twin=False, side=False, whole_line=False):
    barrier = pltpu.get_barrier_semaphore()

    def call(where):
        pl.semaphore_signal(barrier, inc=1, device_id=where, device_id_type=MESH)

    expected = (1 if twin else 0) + (seq_count - 1 if side else 0) + (line - 1 if whole_line else 0)
    if twin:
        call({"grp": g + 1 - 2 * c})
    if side:
        for i in range(1, seq_count):
            call({"seq": lax.rem(s + i, seq_count)})
    if whole_line:
        for j in range(1, line):
            call({"grp": lax.rem(g + CORES * j, CORES * line)})
    if chain:
        expected = expected + (z > 0).astype(jnp.int32) + (z < line - 1).astype(jnp.int32)

        @pl.when(z > 0)
        def _():
            call({"grp": g - CORES})

        @pl.when(z < line - 1)
        def _():
            call({"grp": g + CORES})

    pl.semaphore_wait(barrier, expected)


def line_conditions(line, z, way, t):
    if way == 0:
        return (z < line - 1) & (z >= t), z >= t + 1, z - t, z - 1 - t
    return (z > 0) & (z + t <= line - 1), z + t + 1 <= line - 1, z + t, z + 1 + t


def gather_kernel(seq_count, line, n_deep, n_wide, *refs):
    n_in = 1 + n_deep + n_wide
    ins, outs = refs[:n_in], refs[n_in : 2 * n_in]
    rest = refs[2 * n_in :]
    stage = rest[:n_in]
    (local_sem, tok_send, tok_recv, zs, zr, ws, wr, ps, pr, dps, dpr) = rest[n_in:]
    s, z, c, g = place(seq_count, line)
    twin = {"grp": g + 1 - 2 * c}
    tok, tok_out = ins[0], outs[0]
    rows = tok.shape[1]
    items = list(range(n_deep + n_wide))

    def own(i, l):
        out = outs[1 + i]
        return out.at[l, c] if i < n_deep else out.at[s, l, c]

    loads = [pltpu.make_async_copy(ins[i], stage[i], local_sem.at[0, i]) for i in range(n_in)]
    for x in loads:
        x.start()
    greet(seq_count, line, s, z, c, g, chain=True, twin=True, side=True)

    toks = []
    for i in range(1, seq_count):
        toks.append(
            remote(
                tok,
                tok_out.at[:, pl.ds(pl.multiple_of(s * rows, rows), rows), :],
                tok_send.at[i - 1],
                tok_recv.at[i - 1],
                {"seq": lax.rem(s + i, seq_count)},
            )
        )
        toks[-1].start()

    def hop(i, way, t, origin):
        src = ins[1 + i] if t == 0 else own(i, origin)
        to = g + CORES if way == 0 else g - CORES
        return remote(src, own(i, origin), zs.at[i, way, t], zr.at[i, way, t], {"grp": to})

    def hops(which, t):
        for way in (0, 1):
            sends, _, origin, _ = line_conditions(line, z, way, t)

            @pl.when(sends)
            def _():
                for i in which:
                    hop(i, way, t, origin).start()

    def arrive(which, t, after=None):
        for way in (0, 1):
            _, receives, _, origin = line_conditions(line, z, way, t)

            @pl.when(receives)
            def _():
                for i in which:
                    hop(i, way, t, origin).wait_recv()
                if after is not None:
                    after(origin)

    deep, wide = items[:n_deep], items[n_deep:]
    for t in range(line - 1):
        hops(wide, t)
        if t == 0:
            stores = []
            for i in range(n_in):
                loads[i].wait()
                dst = (
                    tok_out.at[:, pl.ds(pl.multiple_of(s * rows, rows), rows), :]
                    if i == 0
                    else own(i - 1, z)
                )
                stores.append(pltpu.make_async_copy(stage[i], dst, local_sem.at[1, i]))
                stores[-1].start()
        arrive(wide, t)
    hops(deep, 0)
    for x in stores:
        x.wait()
    sides = []
    for i in wide:
        for j in range(1, seq_count):
            part = outs[1 + i].at[s, :, c]
            sides.append(
                remote(
                    part,
                    part,
                    ws.at[i - n_deep, j - 1],
                    wr.at[i - n_deep, j - 1],
                    {"seq": lax.rem(s + j, seq_count)},
                )
            )
            sides[-1].start()

    def twin_wide(i, k):
        part = outs[1 + i].at[k, :, c]
        return remote(part, part, ps.at[i - n_deep, k], pr.at[i - n_deep, k], twin)

    def twin_deep(i, l):
        part = outs[1 + i].at[l, c]
        return remote(part, part, dps.at[i, l], dpr.at[i, l], twin)

    for i in wide:
        twin_wide(i, s).start()
    for i in deep:
        twin_deep(i, z).start()

    def pass_on(origin):
        for i in deep:
            twin_deep(i, origin).start()

    for t in range(line - 1):
        if t > 0:
            hops(deep, t)
        arrive(deep, t, pass_on)
    for x in sides:
        x.wait_recv()
    for i in wide:
        for j in range(1, seq_count):
            twin_wide(i, lax.rem(s + seq_count - j, seq_count)).start()
    for x in toks:
        x.wait_recv()
    for i in deep:
        for l in range(line):
            twin_deep(i, l).wait()
    for i in wide:
        for k in range(seq_count):
            twin_wide(i, k).wait()
    for x in toks + sides:
        x.wait_send()
    for t in range(line - 1):
        for way in (0, 1):
            sends, _, origin, _ = line_conditions(line, z, way, t)

            @pl.when(sends)
            def _():
                for i in items:
                    hop(i, way, t, origin).wait_send()


def gather_all(seq_count, line, tok, deep, wide):
    n_deep, n_wide = len(deep), len(wide)
    shapes = [
        jax.ShapeDtypeStruct((tok.shape[0], tok.shape[1] * seq_count, tok.shape[2]), tok.dtype)
    ]
    shapes += [jax.ShapeDtypeStruct((line, CORES) + x.shape, x.dtype) for x in deep]
    shapes += [jax.ShapeDtypeStruct((seq_count, line, CORES) + x.shape, x.dtype) for x in wide]
    arrays = [tok] + list(deep) + list(wide)
    n = len(arrays)
    scratch = [pltpu.VMEM(x.shape, x.dtype) for x in arrays]
    scratch += [
        DMA((2, n)),
        DMA((seq_count - 1,)),
        DMA((seq_count - 1,)),
        DMA((n_deep + n_wide, 2, line - 1)),
        DMA((n_deep + n_wide, 2, line - 1)),
        DMA((n_wide, seq_count - 1)),
        DMA((n_wide, seq_count - 1)),
        DMA((n_wide, seq_count)),
        DMA((n_wide, seq_count)),
        DMA((n_deep, line)),
        DMA((n_deep, line)),
    ]
    return pl.pallas_call(
        functools.partial(gather_kernel, seq_count, line, n_deep, n_wide),
        out_shape=shapes,
        in_specs=[ANY] * n,
        out_specs=[ANY] * n,
        scratch_shapes=scratch,
        compiler_params=params(1),
        name="gather_all",
    )(*arrays)


def side_gather_kernel(seq_count, line, x_ref, out_ref, local_sem, send, recv):
    s, z, c, g = place(seq_count, line)
    rows = x_ref.shape[1]
    mine = out_ref.at[:, pl.ds(pl.multiple_of(s * rows, rows), rows), :]
    local = pltpu.make_async_copy(x_ref, mine, local_sem)
    local.start()
    greet(seq_count, line, s, z, c, g, side=True)
    copies = []
    for i in range(1, seq_count):
        copies.append(
            remote(
                x_ref, mine, send.at[i - 1], recv.at[i - 1], {"seq": lax.rem(s + i, seq_count)}
            )
        )
        copies[-1].start()
    local.wait()
    for x in copies:
        x.wait()


def side_gather(seq_count, line, x):
    return pl.pallas_call(
        functools.partial(side_gather_kernel, seq_count, line),
        out_shape=jax.ShapeDtypeStruct((x.shape[0], x.shape[1] * seq_count, x.shape[2]), x.dtype),
        in_specs=[WHOLE],
        out_specs=WHOLE,
        scratch_shapes=[DMA, DMA((seq_count - 1,)), DMA((seq_count - 1,))],
        compiler_params=params(2),
        name="side_gather",
    )(x)


def side_sum_kernel(seq_count, line, x_ref, out_ref, slots, send, recv):
    s, z, c, g = place(seq_count, line)
    rows = out_ref.shape[1]
    greet(seq_count, line, s, z, c, g, side=True)
    copies = []
    for i in range(1, seq_count):
        to = lax.rem(s + i, seq_count)
        copies.append(
            remote(
                x_ref.at[:, pl.ds(pl.multiple_of(to * rows, rows), rows), :],
                slots.at[i - 1],
                send.at[i - 1],
                recv.at[i - 1],
                {"seq": to},
            )
        )
        copies[-1].start()
    total = x_ref[:, pl.ds(pl.multiple_of(s * rows, rows), rows), :].astype(F32)
    for i, x in enumerate(copies):
        x.wait_recv()
        total = total + slots[i].astype(F32)
    out_ref[...] = total
    for x in copies:
        x.wait_send()


def side_sum(seq_count, line, x, collective_id):
    rows = x.shape[1] // seq_count
    return pl.pallas_call(
        functools.partial(side_sum_kernel, seq_count, line),
        out_shape=jax.ShapeDtypeStruct((x.shape[0], rows, x.shape[2]), F32),
        in_specs=[WHOLE],
        out_specs=WHOLE,
        scratch_shapes=[
            pltpu.VMEM((seq_count - 1, x.shape[0], rows, x.shape[2]), x.dtype),
            DMA((seq_count - 1,)),
            DMA((seq_count - 1,)),
        ],
        compiler_params=params(collective_id),
        name=f"side_sum_{collective_id}",
    )(x)


def sum_kernel(seq_count, line, n_deep, n_wide, *refs):
    n = n_deep + n_wide
    ins, outs = refs[: n + 1], refs[n + 1 : 2 * n + 2]
    rest = refs[2 * n + 2 :]
    pair, side, chain = rest[:n], rest[n : n + n_wide], rest[n + n_wide : 2 * n + n_wide]
    rest = rest[2 * n + n_wide :]
    g_pair, g_side, g_line, g_a, g_b = rest[:5]
    (ps, pr, ws, wr, zs, zr, gs, gr) = rest[5:]
    s, z, c, g = place(seq_count, line)
    twin = {"grp": g + 1 - 2 * c}
    deep, wide = list(range(n_deep)), list(range(n_deep, n))
    small = ins[n]
    greet(seq_count, line, s, z, c, g, twin=True, side=True, whole_line=True)

    def theirs(i):
        return ins[i].at[:, 1 - c] if i < n_deep else ins[i].at[:, :, 1 - c]

    pairs = [remote(theirs(i), pair[i], ps.at[i], pr.at[i], twin) for i in range(n)]
    small_pair = remote(small, g_pair, gs.at[0], gr.at[0], twin)
    small_pair.start()
    for x in pairs[n_deep:] + pairs[:n_deep]:
        x.start()

    small_pair.wait()
    g_a[...] = small[...] + g_pair[...]
    small_sides = []
    for j in range(1, seq_count):
        small_sides.append(
            remote(
                g_a,
                g_side.at[j - 1],
                gs.at[j],
                gr.at[j],
                {"seq": lax.rem(s + j, seq_count)},
            )
        )
        small_sides[-1].start()

    for i in wide:
        pairs[i].wait_recv()
        for k in range(seq_count):

            @pl.loop(0, line)
            def _(l):
                mixed = ins[i][k, l, c].astype(F32) + pair[i][k, l].astype(F32)
                pair[i][k, l] = mixed.astype(BF16)

    sides = {}
    for i in wide:
        for j in range(1, seq_count):
            to = lax.rem(s + j, seq_count)
            sides[i, j] = remote(
                pair[i].at[to],
                side[i - n_deep].at[j - 1],
                ws.at[i - n_deep, j - 1],
                wr.at[i - n_deep, j - 1],
                {"seq": to},
            )
            sides[i, j].start()
    for i in deep:
        pairs[i].wait_recv()
        for l in range(line):
            pair[i][l] = (ins[i][l, c].astype(F32) + pair[i][l].astype(F32)).astype(BF16)

    for x in small_sides:
        x.wait()
    total = g_a[...]
    for j in range(seq_count - 1):
        total = total + g_side[j]
    g_b[...] = total
    small_lines = []
    for j in range(1, line):
        small_lines.append(
            remote(
                g_b,
                g_line.at[j - 1],
                gs.at[seq_count - 1 + j],
                gr.at[seq_count - 1 + j],
                {"grp": lax.rem(g + CORES * j, CORES * line)},
            )
        )
        small_lines[-1].start()

    def piece(i, l):
        return pair[i].at[l] if i < n_deep else pair[i].at[s, l]

    def run_line(which):
        def hop(i, way, t, dest, first):
            src = piece(i, dest) if first else chain[i].at[way, t]
            to = g + CORES if way == 0 else g - CORES
            return remote(src, chain[i].at[way, t], zs.at[i, way, t], zr.at[i, way, t], {"grp": to})

        for t in range(line - 1):
            for way in (0, 1):
                dest = line - 1 - t if way == 0 else t
                starts = z == 0 if way == 0 else z == line - 1
                relays = (z > 0) & (z < dest) if way == 0 else (z < line - 1) & (z > dest)

                @pl.when(starts)
                def _():
                    for i in which:
                        hop(i, way, t, dest, True).start()

                @pl.when(relays)
                def _():
                    for i in which:
                        hop(i, way, t, dest, False).wait_recv()
                        mixed = chain[i][way, t].astype(F32) + piece(i, dest)[...].astype(F32)
                        chain[i][way, t] = mixed.astype(BF16)
                        hop(i, way, t, dest, False).start()

        for i in which:
            outs[i][...] = piece(i, z)[...].astype(F32)
        for t in range(line - 1):
            for way in (0, 1):
                dest = line - 1 - t if way == 0 else t

                @pl.when((z == dest))
                def _():
                    for i in which:
                        hop(i, way, t, dest, False).wait_recv()
                        outs[i][...] += chain[i][way, t].astype(F32)

                @pl.when(z == 0 if way == 0 else z == line - 1)
                def _():
                    for i in which:
                        hop(i, way, t, dest, True).wait_send()

                @pl.when((z > 0) & (z < dest) if way == 0 else (z < line - 1) & (z > dest))
                def _():
                    for i in which:
                        hop(i, way, t, dest, False).wait_send()

    run_line(deep)
    for i in wide:
        for j in range(1, seq_count):
            sides[i, j].wait()

        @pl.loop(0, line)
        def _(l):
            mixed = pair[i][s, l].astype(F32)
            for j in range(1, seq_count):
                mixed = mixed + side[i - n_deep][j - 1, l].astype(F32)
            pair[i][s, l] = mixed.astype(BF16)

    run_line(wide)
    for x in pairs:
        x.wait_send()
    for x in small_lines:
        x.wait()
    total = g_b[...]
    for j in range(line - 1):
        total = total + g_line[j]
    outs[n][...] = total


def sum_all(seq_count, line, deep, wide, small):
    n_deep, n_wide = len(deep), len(wide)
    n = n_deep + n_wide
    shapes = [jax.ShapeDtypeStruct(x.shape[2:], F32) for x in deep]
    shapes += [jax.ShapeDtypeStruct(x.shape[3:], F32) for x in wide]
    shapes += [jax.ShapeDtypeStruct(small.shape, F32)]
    scratch = [pltpu.VMEM((line,) + x.shape[2:], BF16) for x in deep]
    scratch += [pltpu.VMEM((seq_count, line) + x.shape[3:], BF16) for x in wide]
    scratch += [pltpu.VMEM((seq_count - 1, line) + x.shape[3:], BF16) for x in wide]
    scratch += [pltpu.VMEM((2, line - 1) + x.shape[2:], BF16) for x in deep]
    scratch += [pltpu.VMEM((2, line - 1) + x.shape[3:], BF16) for x in wide]
    scratch += [
        pltpu.VMEM(small.shape, F32),
        pltpu.VMEM((seq_count - 1,) + small.shape, F32),
        pltpu.VMEM((line - 1,) + small.shape, F32),
        pltpu.VMEM(small.shape, F32),
        pltpu.VMEM(small.shape, F32),
        DMA((n,)),
        DMA((n,)),
        DMA((n_wide, seq_count - 1)),
        DMA((n_wide, seq_count - 1)),
        DMA((n, 2, line - 1)),
        DMA((n, 2, line - 1)),
        DMA((seq_count + line,)),
        DMA((seq_count + line,)),
    ]
    return pl.pallas_call(
        functools.partial(sum_kernel, seq_count, line, n_deep, n_wide),
        out_shape=shapes,
        in_specs=[WHOLE] * (n + 1),
        out_specs=[WHOLE] * (n + 1),
        scratch_shapes=scratch,
        compiler_params=params(5),
        name="sum_all",
    )(*deep, *wide, small)


def signs_of(rows):
    pos = lax.broadcasted_iota(jnp.int32, (rows, 1), 0)
    return 1.0 - 2.0 * lax.rem(pos, 2).astype(F32)


def lagged(values, lag, span):
    pos = lax.broadcasted_iota(jnp.int32, (values.shape[0], 1), 0)
    return jnp.where(lax.rem(pos, span) >= lag, pltpu.roll(values, lag, 0), 0.0)


def led(values, lag, span):
    rows = values.shape[0]
    pos = lax.broadcasted_iota(jnp.int32, (rows, 1), 0)
    return jnp.where(lax.rem(pos, span) < span - lag, pltpu.roll(values, rows - lag, 0), 0.0)


def spread(row, rows):
    wide = jnp.broadcast_to(row, (rows, row.shape[1]))
    return pltpu.roll(wide, 0, 1, stride=1, stride_axis=0)[:, :rows].astype(BF16)


def forward_kernel(spans, x_ref, gain_ref, row_ref, w_ref, ar_ref, ul_ref, u_ref, y_ref, both, acc):
    k = pl.program_id(0)
    rows, width = x_ref.shape[1], x_ref.shape[2]
    signs = signs_of(rows)

    @pl.when(k == 0)
    def _():
        for m in range(2):
            x = x_ref[m].astype(F32)
            inv = lax.rsqrt(jnp.mean(x * x, axis=-1, keepdims=True) + EPSILON)
            u = (x * inv * gain_ref[...]).astype(BF16)
            wide = u.astype(F32)
            u_ref[m] = u
            both[m, :, :width] = u
            both[m, :, width:] = (wide * signs).astype(BF16)
            acc[m] = dot_nn(u, ar_ref[:width])
            for lag in (1, 2):
                acc[m] += dot_nn(
                    lagged(wide, lag, spans[m]).astype(BF16),
                    ar_ref[lag * width : (lag + 1) * width],
                )

    table = spread(row_ref[0], rows)
    for m in range(2):
        span = spans[m]
        for j in range(rows // span):
            part = slice(j * span, (j + 1) * span)
            conv = dot_nn(table[:span, :span], both[m, part, :])
            plus = conv[:, :width].astype(BF16)
            minus = (conv[:, width:] * signs[part]).astype(BF16)
            ul_ref[0, 0, m, part, :] = plus
            ul_ref[0, 1, m, part, :] = minus
        acc[m] += dot_nn(ul_ref[0, 0, m], w_ref[0, 0]) + dot_nn(ul_ref[0, 1, m], w_ref[0, 1])

    @pl.when(k == pl.num_programs(0) - 1)
    def _():
        y_ref[...] = acc[...].astype(BF16)


def forward_mix(spans, x, gain, table, w, ar):
    count = table.shape[0]
    _, rows, width = x.shape
    full = lambda *shape: pl.BlockSpec(shape, lambda k: (0,) * len(shape))
    return pl.pallas_call(
        functools.partial(forward_kernel, spans),
        grid=(count,),
        out_shape=[
            jax.ShapeDtypeStruct((count, 2, 2, rows, width), BF16),
            jax.ShapeDtypeStruct((2, rows, width), BF16),
            jax.ShapeDtypeStruct((2, rows, width), BF16),
        ],
        in_specs=[
            full(2, rows, width),
            full(1, width),
            pl.BlockSpec((1, 1, 2 * rows), lambda k: (k, 0, 0)),
            pl.BlockSpec((1, 2, width, width), lambda k: (k, 0, 0, 0)),
            full(3 * width, width),
        ],
        out_specs=[
            pl.BlockSpec((1, 2, 2, rows, width), lambda k: (k, 0, 0, 0, 0)),
            full(2, rows, width),
            full(2, rows, width),
        ],
        scratch_shapes=[pltpu.VMEM((2, rows, 2 * width), BF16), pltpu.VMEM((2, rows, width), F32)],
        compiler_params=params(),
        name="forward_mix",
    )(x, gain, table, w, ar)


def backward_kernel(
    spans, dy_ref, u_ref, row_ref, w_ref, ul_ref, ar_ref, dw_ref, dar_ref, du_ref, both, acc
):
    k = pl.program_id(0)
    rows, width = dy_ref.shape[1], dy_ref.shape[2]
    signs = signs_of(rows)

    @pl.when(k == 0)
    def _():
        for m in range(2):
            dy = dy_ref[m]
            both[m, :, :width] = dy
            both[m, :, width:] = (dy.astype(F32) * signs).astype(BF16)
            acc[m] = dot_nt(dy, ar_ref[:width])
            for lag in (1, 2):
                acc[m] += led(
                    dot_nt(dy, ar_ref[lag * width : (lag + 1) * width]), lag, spans[m]
                )
        for lag in (0, 1, 2):
            total = 0.0
            for m in range(2):
                u = u_ref[m]
                if lag:
                    u = lagged(u.astype(F32), lag, spans[m]).astype(BF16)
                total = total + dot_tn(u, dy_ref[m])
            dar_ref[lag * width : (lag + 1) * width, :] = total.astype(BF16)

    table = spread(row_ref[0], rows)
    for m in range(2):
        span = spans[m]
        for j in range(rows // span):
            part = slice(j * span, (j + 1) * span)
            conv = dot_nn(table[:span, :span], both[m, part, :])
            plus = conv[:, :width].astype(BF16)
            minus = (conv[:, width:] * signs[part]).astype(BF16)
            acc[m, part, :] += dot_nt(plus, w_ref[0, 0]) + dot_nt(minus, w_ref[0, 1])
    for p in range(2):
        total = dot_tn(ul_ref[0, p, 0], dy_ref[0]) + dot_tn(ul_ref[0, p, 1], dy_ref[1])
        dw_ref[0, p] = total.astype(BF16)

    @pl.when(k == pl.num_programs(0) - 1)
    def _():
        du_ref[...] = acc[...].astype(BF16)


def backward_mix(spans, dy, u, table, w, ul, ar):
    count = table.shape[0]
    _, rows, width = dy.shape
    full = lambda *shape: pl.BlockSpec(shape, lambda k: (0,) * len(shape))
    return pl.pallas_call(
        functools.partial(backward_kernel, spans),
        grid=(count,),
        out_shape=[
            jax.ShapeDtypeStruct((count, 2, width, width), BF16),
            jax.ShapeDtypeStruct((3 * width, width), BF16),
            jax.ShapeDtypeStruct((2, rows, width), BF16),
        ],
        in_specs=[
            full(2, rows, width),
            full(2, rows, width),
            pl.BlockSpec((1, 1, 2 * rows), lambda k: (k, 0, 0)),
            pl.BlockSpec((1, 2, width, width), lambda k: (k, 0, 0, 0)),
            pl.BlockSpec((1, 2, 2, rows, width), lambda k: (k, 0, 0, 0, 0)),
            full(3 * width, width),
        ],
        out_specs=[
            pl.BlockSpec((1, 2, width, width), lambda k: (k, 0, 0, 0)),
            full(3 * width, width),
            full(2, rows, width),
        ],
        scratch_shapes=[pltpu.VMEM((2, rows, 2 * width), BF16), pltpu.VMEM((2, rows, width), F32)],
        compiler_params=params(),
        name="backward_mix",
    )(dy, u, table, w, ul, ar)


def body(
    tokens,
    layout,
    filters,
    gain_mix,
    spectral_proj,
    ar_proj,
    gain_mlp,
    w_gate,
    w_up,
    w_down,
    out_grad,
):
    seq_count = lax.axis_size("seq")
    line = lax.axis_size("grp") // CORES
    s = lax.axis_index("seq")
    g = lax.axis_index("grp")
    block, width = tokens.shape[2], tokens.shape[3]
    rows = block * seq_count
    count = filters.shape[1] // seq_count
    hidden_units = w_gate.shape[1]
    spans = (rows, rows // 4)

    swap = layout[0, 0] == 1
    own = jnp.where(swap, tokens[::-1, 0], tokens[:, 0])
    cotangent = jnp.where(swap, out_grad[::-1, 0], out_grad[:, 0])
    share = gain_mix.shape[0]
    gains = jnp.zeros((16, 128), BF16)
    gains = gains.at[0, :share].set(gain_mix).at[1, :share].set(gain_mlp)

    x_all, spec, ar, gate_w, up_w, down_w, gains = gather_all(
        seq_count, line, own, (spectral_proj, ar_proj), (w_gate, w_up, w_down, gains)
    )
    spec = spec.reshape(count, 2, width, width)
    ar_rows = ar.shape[0] * ar.shape[1] * ar.shape[2]
    ar_full = lax.dynamic_update_slice(
        jnp.zeros((3 * width, width), BF16), ar.reshape(ar_rows, width), (s * ar_rows, 0)
    )
    gate_w = gate_w.reshape(width, hidden_units)
    up_w = up_w.reshape(width, hidden_units)
    down_w = down_w.reshape(hidden_units, width)
    gains = gains.reshape(-1, 16, 128).astype(F32)
    mix_scale = gains[:, 0, :share].reshape(1, width)
    mlp_scale = gains[:, 1, :share].reshape(1, width)

    mine = lax.dynamic_slice(filters.T, (s * count, 0), (count, rows))[:, None, :]
    nothing = jnp.zeros((count, 1, rows), F32)
    back_table = jnp.concatenate([mine, nothing], axis=2)
    fore_table = jnp.concatenate([mine[:, :, :1], nothing, mine[:, :, :0:-1]], axis=2)

    ul, u, y = forward_mix(spans, x_all, mix_scale, fore_table, spec, ar_full)
    mixer = side_sum(seq_count, line, y, 3).reshape(2 * block, width)

    inputs = own.reshape(2 * block, width).astype(F32)
    cot = cotangent.reshape(2 * block, width)
    hidden = inputs + mixer
    inv_two = lax.rsqrt(jnp.mean(hidden * hidden, axis=-1, keepdims=True) + EPSILON)
    mlp_in = (hidden * inv_two * mlp_scale).astype(BF16)
    gate = dot_nn(mlp_in, gate_w)
    upval = dot_nn(mlp_in, up_w)
    product_val, gelu_pull = jax.vjp(lambda a, b: jax.nn.gelu(a) * b, gate, upval)
    mixed = product_val.astype(BF16)
    out = hidden + dot_nn(mixed, down_w)
    down_grad = dot_tn(mixed, cot)
    mixed_grad = dot_nt(cot, down_w)
    gate_back, up_back = gelu_pull(mixed_grad)
    gate_back = gate_back.astype(BF16)
    up_back = up_back.astype(BF16)
    gate_grad = dot_tn(mlp_in, gate_back)
    up_grad = dot_tn(mlp_in, up_back)
    mlp_in_grad = dot_nt(gate_back, gate_w) + dot_nt(up_back, up_w)
    scaled_two = mlp_in_grad * mlp_scale
    mlp_grad = jnp.sum(mlp_in_grad * hidden * inv_two, axis=0, keepdims=True)
    hidden_grad = (
        cot.astype(F32)
        + inv_two * scaled_two
        - hidden * inv_two**3 * jnp.mean(scaled_two * hidden, axis=-1, keepdims=True)
    )
    mixer_grad = hidden_grad.astype(BF16)

    dy = side_gather(seq_count, line, mixer_grad.reshape(2, block, width))
    dw, dar, du = backward_mix(spans, dy, u, back_table, spec, ul, ar_full)
    normed_grad = side_sum(seq_count, line, du, 4).reshape(2 * block, width)

    inv_one = lax.rsqrt(jnp.mean(inputs * inputs, axis=-1, keepdims=True) + EPSILON)
    scaled_one = normed_grad * mix_scale
    mix_grad = jnp.sum(normed_grad * inputs * inv_one, axis=0, keepdims=True)
    input_grad = (
        hidden_grad
        + inv_one * scaled_one
        - inputs * inv_one**3 * jnp.mean(scaled_one * inputs, axis=-1, keepdims=True)
    )

    dar = lax.dynamic_slice(dar, (s * ar_rows, 0), (ar_rows, width))
    deep = (dw.reshape(line, CORES, -1, width), dar.reshape(line, CORES, -1, width))
    wide = tuple(
        x.astype(BF16).reshape(seq_count, line, CORES, -1, x.shape[1])
        for x in (gate_grad, up_grad, down_grad)
    )
    small = jnp.concatenate([mix_grad, mlp_grad, jnp.zeros((6, width), F32)], axis=0)
    dw, dar, gate_grad, up_grad, down_grad, small = sum_all(seq_count, line, deep, wide, small)
    small = lax.dynamic_slice(small, (0, (s * CORES * line + g) * share), (2, share))

    def settle(x):
        x = x.reshape(2, 1, block, width)
        return jnp.where(swap, x[::-1], x)

    return (
        settle(out),
        settle(input_grad),
        small[0],
        dw,
        dar,
        small[1],
        gate_grad,
        up_grad,
        down_grad,
    )


def solution(mesh):
    placed = (
        P(None, "grp", "seq", None),
        P(None, "grp"),
        P(),
        P(("seq", "grp")),
        P(("seq", "grp"), None),
        P(("seq", "grp"), None),
        P(("seq", "grp")),
        P(("seq", "grp"), None),
        P(("seq", "grp"), None),
        P(("seq", "grp"), None),
        P(None, "grp", "seq", None),
    )
    return jax.shard_map(
        body,
        mesh=mesh,
        in_specs=placed,
        out_specs=(
            P(None, "grp", "seq", None),
            P(None, "grp", "seq", None),
            P(("seq", "grp")),
            P(("seq", "grp"), None),
            P(("seq", "grp"), None),
            P(("seq", "grp")),
            P(("seq", "grp"), None),
            P(("seq", "grp"), None),
            P(("seq", "grp"), None),
        ),
        check_vma=False,
    )
```

```python
import functools

import jax
import jax.numpy as jnp
from jax import lax
from jax.experimental import pallas as pl
from jax.experimental.pallas import tpu as pltpu
from jax.sharding import PartitionSpec as P

EPSILON = 1e-05
BF16 = jnp.bfloat16
F32 = jnp.float32
MESH = pl.DeviceIdType.MESH
DMA = pltpu.SemaphoreType.DMA
ANY = pl.BlockSpec(memory_space=pl.ANY)
WHOLE = pl.BlockSpec(memory_space=pltpu.VMEM)
VMEM_LIMIT = 60 * 1024 * 1024
CORES = 2


def dot_nn(a, b):
    return lax.dot_general(a, b, (((1,), (0,)), ((), ())), preferred_element_type=F32)


def dot_tn(a, b):
    return lax.dot_general(a, b, (((0,), (0,)), ((), ())), preferred_element_type=F32)


def dot_nt(a, b):
    return lax.dot_general(a, b, (((1,), (1,)), ((), ())), preferred_element_type=F32)


def params(collective_id=None):
    return pltpu.CompilerParams(
        collective_id=collective_id,
        has_side_effects=collective_id is not None,
        vmem_limit_bytes=VMEM_LIMIT,
    )


def remote(src, dst, send, recv, where):
    return pltpu.make_async_remote_copy(
        src_ref=src, dst_ref=dst, send_sem=send, recv_sem=recv, device_id=where, device_id_type=MESH
    )


def place(seq_count, line):
    s = lax.axis_index("seq")
    g = lax.axis_index("grp")
    return s, lax.div(g, CORES), lax.rem(g, CORES), g


def greet(seq_count, line, s, z, c, g, chain=False, twin=False, side=False, whole_line=False):
    barrier = pltpu.get_barrier_semaphore()

    def call(where):
        pl.semaphore_signal(barrier, inc=1, device_id=where, device_id_type=MESH)

    expected = (1 if twin else 0) + (seq_count - 1 if side else 0) + (line - 1 if whole_line else 0)
    if twin:
        call({"grp": g + 1 - 2 * c})
    if side:
        for i in range(1, seq_count):
            call({"seq": lax.rem(s + i, seq_count)})
    if whole_line:
        for j in range(1, line):
            call({"grp": lax.rem(g + CORES * j, CORES * line)})
    if chain:
        expected = expected + (z > 0).astype(jnp.int32) + (z < line - 1).astype(jnp.int32)

        @pl.when(z > 0)
        def _():
            call({"grp": g - CORES})

        @pl.when(z < line - 1)
        def _():
            call({"grp": g + CORES})

    pl.semaphore_wait(barrier, expected)


def line_conditions(line, z, way, t):
    if way == 0:
        return (z < line - 1) & (z >= t), z >= t + 1, z - t, z - 1 - t
    return (z > 0) & (z + t <= line - 1), z + t + 1 <= line - 1, z + t, z + 1 + t


def gather_kernel(seq_count, line, n_deep, n_wide, *refs):
    n_in = 1 + n_deep + n_wide
    ins, outs = refs[:n_in], refs[n_in : 2 * n_in]
    rest = refs[2 * n_in :]
    stage = rest[:n_in]
    (local_sem, tok_send, tok_recv, zs, zr, ws, wr, ps, pr, dps, dpr) = rest[n_in:]
    s, z, c, g = place(seq_count, line)
    twin = {"grp": g + 1 - 2 * c}
    tok, tok_out = ins[0], outs[0]
    rows = tok.shape[1]
    items = list(range(n_deep + n_wide))

    def own(i, l):
        out = outs[1 + i]
        return out.at[l, c] if i < n_deep else out.at[s, l, c]

    loads = [pltpu.make_async_copy(ins[i], stage[i], local_sem.at[0, i]) for i in range(n_in)]
    for x in loads:
        x.start()
    greet(seq_count, line, s, z, c, g, chain=True, twin=True, side=True)

    toks = []
    for i in range(1, seq_count):
        toks.append(
            remote(
                tok,
                tok_out.at[:, pl.ds(pl.multiple_of(s * rows, rows), rows), :],
                tok_send.at[i - 1],
                tok_recv.at[i - 1],
                {"seq": lax.rem(s + i, seq_count)},
            )
        )
        toks[-1].start()

    def hop(i, way, t, origin):
        src = ins[1 + i] if t == 0 else own(i, origin)
        to = g + CORES if way == 0 else g - CORES
        return remote(src, own(i, origin), zs.at[i, way, t], zr.at[i, way, t], {"grp": to})

    def hops(which, t):
        for way in (0, 1):
            sends, _, origin, _ = line_conditions(line, z, way, t)

            @pl.when(sends)
            def _():
                for i in which:
                    hop(i, way, t, origin).start()

    def arrive(which, t, after=None):
        for way in (0, 1):
            _, receives, _, origin = line_conditions(line, z, way, t)

            @pl.when(receives)
            def _():
                for i in which:
                    hop(i, way, t, origin).wait_recv()
                if after is not None:
                    after(origin)

    deep, wide = items[:n_deep], items[n_deep:]
    for t in range(line - 1):
        hops(wide, t)
        if t == 0:
            stores = []
            for i in range(n_in):
                loads[i].wait()
                dst = (
                    tok_out.at[:, pl.ds(pl.multiple_of(s * rows, rows), rows), :]
                    if i == 0
                    else own(i - 1, z)
                )
                stores.append(pltpu.make_async_copy(stage[i], dst, local_sem.at[1, i]))
                stores[-1].start()
        arrive(wide, t)
    hops(deep, 0)
    for x in stores:
        x.wait()
    sides = []
    for i in wide:
        for j in range(1, seq_count):
            part = outs[1 + i].at[s, :, c]
            sides.append(
                remote(
                    part,
                    part,
                    ws.at[i - n_deep, j - 1],
                    wr.at[i - n_deep, j - 1],
                    {"seq": lax.rem(s + j, seq_count)},
                )
            )
            sides[-1].start()

    def twin_wide(i, k):
        part = outs[1 + i].at[k, :, c]
        return remote(part, part, ps.at[i - n_deep, k], pr.at[i - n_deep, k], twin)

    def twin_deep(i, l):
        part = outs[1 + i].at[l, c]
        return remote(part, part, dps.at[i, l], dpr.at[i, l], twin)

    for i in wide:
        twin_wide(i, s).start()
    for i in deep:
        twin_deep(i, z).start()

    def pass_on(origin):
        for i in deep:
            twin_deep(i, origin).start()

    for t in range(line - 1):
        if t > 0:
            hops(deep, t)
        arrive(deep, t, pass_on)
    for x in sides:
        x.wait_recv()
    for i in wide:
        for j in range(1, seq_count):
            twin_wide(i, lax.rem(s + seq_count - j, seq_count)).start()
    for x in toks:
        x.wait_recv()
    for i in deep:
        for l in range(line):
            twin_deep(i, l).wait()
    for i in wide:
        for k in range(seq_count):
            twin_wide(i, k).wait()
    for x in toks + sides:
        x.wait_send()
    for t in range(line - 1):
        for way in (0, 1):
            sends, _, origin, _ = line_conditions(line, z, way, t)

            @pl.when(sends)
            def _():
                for i in items:
                    hop(i, way, t, origin).wait_send()


def gather_all(seq_count, line, tok, deep, wide):
    n_deep, n_wide = len(deep), len(wide)
    shapes = [
        jax.ShapeDtypeStruct((tok.shape[0], tok.shape[1] * seq_count, tok.shape[2]), tok.dtype)
    ]
    shapes += [jax.ShapeDtypeStruct((line, CORES) + x.shape, x.dtype) for x in deep]
    shapes += [jax.ShapeDtypeStruct((seq_count, line, CORES) + x.shape, x.dtype) for x in wide]
    arrays = [tok] + list(deep) + list(wide)
    n = len(arrays)
    scratch = [pltpu.VMEM(x.shape, x.dtype) for x in arrays]
    scratch += [
        DMA((2, n)),
        DMA((seq_count - 1,)),
        DMA((seq_count - 1,)),
        DMA((n_deep + n_wide, 2, line - 1)),
        DMA((n_deep + n_wide, 2, line - 1)),
        DMA((n_wide, seq_count - 1)),
        DMA((n_wide, seq_count - 1)),
        DMA((n_wide, seq_count)),
        DMA((n_wide, seq_count)),
        DMA((n_deep, line)),
        DMA((n_deep, line)),
    ]
    return pl.pallas_call(
        functools.partial(gather_kernel, seq_count, line, n_deep, n_wide),
        out_shape=shapes,
        in_specs=[ANY] * n,
        out_specs=[ANY] * n,
        scratch_shapes=scratch,
        compiler_params=params(1),
        name="gather_all",
    )(*arrays)


def side_gather_kernel(seq_count, line, x_ref, out_ref, local_sem, send, recv):
    s, z, c, g = place(seq_count, line)
    rows = x_ref.shape[1]
    mine = out_ref.at[:, pl.ds(pl.multiple_of(s * rows, rows), rows), :]
    local = pltpu.make_async_copy(x_ref, mine, local_sem)
    local.start()
    greet(seq_count, line, s, z, c, g, side=True)
    copies = []
    for i in range(1, seq_count):
        copies.append(
            remote(
                x_ref, mine, send.at[i - 1], recv.at[i - 1], {"seq": lax.rem(s + i, seq_count)}
            )
        )
        copies[-1].start()
    local.wait()
    for x in copies:
        x.wait()


def side_gather(seq_count, line, x):
    return pl.pallas_call(
        functools.partial(side_gather_kernel, seq_count, line),
        out_shape=jax.ShapeDtypeStruct((x.shape[0], x.shape[1] * seq_count, x.shape[2]), x.dtype),
        in_specs=[WHOLE],
        out_specs=WHOLE,
        scratch_shapes=[DMA, DMA((seq_count - 1,)), DMA((seq_count - 1,))],
        compiler_params=params(2),
        name="side_gather",
    )(x)


def side_sum_kernel(seq_count, line, x_ref, out_ref, slots, send, recv):
    s, z, c, g = place(seq_count, line)
    rows = out_ref.shape[1]
    greet(seq_count, line, s, z, c, g, side=True)
    copies = []
    for i in range(1, seq_count):
        to = lax.rem(s + i, seq_count)
        copies.append(
            remote(
                x_ref.at[:, pl.ds(pl.multiple_of(to * rows, rows), rows), :],
                slots.at[i - 1],
                send.at[i - 1],
                recv.at[i - 1],
                {"seq": to},
            )
        )
        copies[-1].start()
    total = x_ref[:, pl.ds(pl.multiple_of(s * rows, rows), rows), :].astype(F32)
    for i, x in enumerate(copies):
        x.wait_recv()
        total = total + slots[i].astype(F32)
    out_ref[...] = total
    for x in copies:
        x.wait_send()


def side_sum(seq_count, line, x, collective_id):
    rows = x.shape[1] // seq_count
    return pl.pallas_call(
        functools.partial(side_sum_kernel, seq_count, line),
        out_shape=jax.ShapeDtypeStruct((x.shape[0], rows, x.shape[2]), F32),
        in_specs=[WHOLE],
        out_specs=WHOLE,
        scratch_shapes=[
            pltpu.VMEM((seq_count - 1, x.shape[0], rows, x.shape[2]), x.dtype),
            DMA((seq_count - 1,)),
            DMA((seq_count - 1,)),
        ],
        compiler_params=params(collective_id),
        name=f"side_sum_{collective_id}",
    )(x)


def sum_kernel(seq_count, line, n_deep, n_wide, *refs):
    n = n_deep + n_wide
    ins, outs = refs[: n + 1], refs[n + 1 : 2 * n + 2]
    rest = refs[2 * n + 2 :]
    pair, side, chain = rest[:n], rest[n : n + n_wide], rest[n + n_wide : 2 * n + n_wide]
    rest = rest[2 * n + n_wide :]
    g_pair, g_side, g_line, g_a, g_b = rest[:5]
    (ps, pr, ws, wr, zs, zr, gs, gr) = rest[5:]
    s, z, c, g = place(seq_count, line)
    twin = {"grp": g + 1 - 2 * c}
    deep, wide = list(range(n_deep)), list(range(n_deep, n))
    small = ins[n]
    greet(seq_count, line, s, z, c, g, twin=True, side=True, whole_line=True)

    def theirs(i):
        return ins[i].at[:, 1 - c] if i < n_deep else ins[i].at[:, :, 1 - c]

    pairs = [remote(theirs(i), pair[i], ps.at[i], pr.at[i], twin) for i in range(n)]
    small_pair = remote(small, g_pair, gs.at[0], gr.at[0], twin)
    small_pair.start()
    for x in pairs[n_deep:] + pairs[:n_deep]:
        x.start()

    small_pair.wait()
    g_a[...] = small[...] + g_pair[...]
    small_sides = []
    for j in range(1, seq_count):
        small_sides.append(
            remote(
                g_a,
                g_side.at[j - 1],
                gs.at[j],
                gr.at[j],
                {"seq": lax.rem(s + j, seq_count)},
            )
        )
        small_sides[-1].start()

    for i in wide:
        pairs[i].wait_recv()
        for k in range(seq_count):

            @pl.loop(0, line)
            def _(l):
                mixed = ins[i][k, l, c].astype(F32) + pair[i][k, l].astype(F32)
                pair[i][k, l] = mixed.astype(BF16)

    sides = {}
    for i in wide:
        for j in range(1, seq_count):
            to = lax.rem(s + j, seq_count)
            sides[i, j] = remote(
                pair[i].at[to],
                side[i - n_deep].at[j - 1],
                ws.at[i - n_deep, j - 1],
                wr.at[i - n_deep, j - 1],
                {"seq": to},
            )
            sides[i, j].start()
    for i in deep:
        pairs[i].wait_recv()
        for l in range(line):
            pair[i][l] = (ins[i][l, c].astype(F32) + pair[i][l].astype(F32)).astype(BF16)

    for x in small_sides:
        x.wait()
    total = g_a[...]
    for j in range(seq_count - 1):
        total = total + g_side[j]
    g_b[...] = total
    small_lines = []
    for j in range(1, line):
        small_lines.append(
            remote(
                g_b,
                g_line.at[j - 1],
                gs.at[seq_count - 1 + j],
                gr.at[seq_count - 1 + j],
                {"grp": lax.rem(g + CORES * j, CORES * line)},
            )
        )
        small_lines[-1].start()

    def piece(i, l):
        return pair[i].at[l] if i < n_deep else pair[i].at[s, l]

    def run_line(which):
        def hop(i, way, t, dest, first):
            src = piece(i, dest) if first else chain[i].at[way, t]
            to = g + CORES if way == 0 else g - CORES
            return remote(src, chain[i].at[way, t], zs.at[i, way, t], zr.at[i, way, t], {"grp": to})

        for t in range(line - 1):
            for way in (0, 1):
                dest = line - 1 - t if way == 0 else t
                starts = z == 0 if way == 0 else z == line - 1
                relays = (z > 0) & (z < dest) if way == 0 else (z < line - 1) & (z > dest)

                @pl.when(starts)
                def _():
                    for i in which:
                        hop(i, way, t, dest, True).start()

                @pl.when(relays)
                def _():
                    for i in which:
                        hop(i, way, t, dest, False).wait_recv()
                        mixed = chain[i][way, t].astype(F32) + piece(i, dest)[...].astype(F32)
                        chain[i][way, t] = mixed.astype(BF16)
                        hop(i, way, t, dest, False).start()

        for i in which:
            outs[i][...] = piece(i, z)[...].astype(F32)
        for t in range(line - 1):
            for way in (0, 1):
                dest = line - 1 - t if way == 0 else t

                @pl.when((z == dest))
                def _():
                    for i in which:
                        hop(i, way, t, dest, False).wait_recv()
                        outs[i][...] += chain[i][way, t].astype(F32)

                @pl.when(z == 0 if way == 0 else z == line - 1)
                def _():
                    for i in which:
                        hop(i, way, t, dest, True).wait_send()

                @pl.when((z > 0) & (z < dest) if way == 0 else (z < line - 1) & (z > dest))
                def _():
                    for i in which:
                        hop(i, way, t, dest, False).wait_send()

    run_line(deep)
    for i in wide:
        for j in range(1, seq_count):
            sides[i, j].wait()

        @pl.loop(0, line)
        def _(l):
            mixed = pair[i][s, l].astype(F32)
            for j in range(1, seq_count):
                mixed = mixed + side[i - n_deep][j - 1, l].astype(F32)
            pair[i][s, l] = mixed.astype(BF16)

    run_line(wide)
    for x in pairs:
        x.wait_send()
    for x in small_lines:
        x.wait()
    total = g_b[...]
    for j in range(line - 1):
        total = total + g_line[j]
    outs[n][...] = total


def sum_all(seq_count, line, deep, wide, small):
    n_deep, n_wide = len(deep), len(wide)
    n = n_deep + n_wide
    shapes = [jax.ShapeDtypeStruct(x.shape[2:], F32) for x in deep]
    shapes += [jax.ShapeDtypeStruct(x.shape[3:], F32) for x in wide]
    shapes += [jax.ShapeDtypeStruct(small.shape, F32)]
    scratch = [pltpu.VMEM((line,) + x.shape[2:], BF16) for x in deep]
    scratch += [pltpu.VMEM((seq_count, line) + x.shape[3:], BF16) for x in wide]
    scratch += [pltpu.VMEM((seq_count - 1, line) + x.shape[3:], BF16) for x in wide]
    scratch += [pltpu.VMEM((2, line - 1) + x.shape[2:], BF16) for x in deep]
    scratch += [pltpu.VMEM((2, line - 1) + x.shape[3:], BF16) for x in wide]
    scratch += [
        pltpu.VMEM(small.shape, F32),
        pltpu.VMEM((seq_count - 1,) + small.shape, F32),
        pltpu.VMEM((line - 1,) + small.shape, F32),
        pltpu.VMEM(small.shape, F32),
        pltpu.VMEM(small.shape, F32),
        DMA((n,)),
        DMA((n,)),
        DMA((n_wide, seq_count - 1)),
        DMA((n_wide, seq_count - 1)),
        DMA((n, 2, line - 1)),
        DMA((n, 2, line - 1)),
        DMA((seq_count + line,)),
        DMA((seq_count + line,)),
    ]
    return pl.pallas_call(
        functools.partial(sum_kernel, seq_count, line, n_deep, n_wide),
        out_shape=shapes,
        in_specs=[WHOLE] * (n + 1),
        out_specs=[WHOLE] * (n + 1),
        scratch_shapes=scratch,
        compiler_params=params(5),
        name="sum_all",
    )(*deep, *wide, small)


def signs_of(rows):
    pos = lax.broadcasted_iota(jnp.int32, (rows, 1), 0)
    return 1.0 - 2.0 * lax.rem(pos, 2).astype(F32)


def lagged(values, lag, span):
    pos = lax.broadcasted_iota(jnp.int32, (values.shape[0], 1), 0)
    return jnp.where(lax.rem(pos, span) >= lag, pltpu.roll(values, lag, 0), 0.0)


def led(values, lag, span):
    rows = values.shape[0]
    pos = lax.broadcasted_iota(jnp.int32, (rows, 1), 0)
    return jnp.where(lax.rem(pos, span) < span - lag, pltpu.roll(values, rows - lag, 0), 0.0)


def spread(row, rows):
    wide = jnp.broadcast_to(row, (rows, row.shape[1]))
    return pltpu.roll(wide, 0, 1, stride=1, stride_axis=0)[:, :rows].astype(BF16)


def forward_kernel(spans, x_ref, gain_ref, row_ref, w_ref, ar_ref, ul_ref, u_ref, y_ref, both, acc):
    k = pl.program_id(0)
    rows, width = x_ref.shape[1], x_ref.shape[2]
    signs = signs_of(rows)

    @pl.when(k == 0)
    def _():
        for m in range(2):
            x = x_ref[m].astype(F32)
            inv = lax.rsqrt(jnp.mean(x * x, axis=-1, keepdims=True) + EPSILON)
            u = (x * inv * gain_ref[...]).astype(BF16)
            wide = u.astype(F32)
            u_ref[m] = u
            both[m, :, :width] = u
            both[m, :, width:] = (wide * signs).astype(BF16)
            acc[m] = dot_nn(u, ar_ref[:width])
            for lag in (1, 2):
                acc[m] += dot_nn(
                    lagged(wide, lag, spans[m]).astype(BF16),
                    ar_ref[lag * width : (lag + 1) * width],
                )

    table = spread(row_ref[0], rows)
    for m in range(2):
        span = spans[m]
        for j in range(rows // span):
            part = slice(j * span, (j + 1) * span)
            conv = dot_nn(table[:span, :span], both[m, part, :])
            plus = conv[:, :width].astype(BF16)
            minus = (conv[:, width:] * signs[part]).astype(BF16)
            ul_ref[0, 0, m, part, :] = plus
            ul_ref[0, 1, m, part, :] = minus
        acc[m] += dot_nn(ul_ref[0, 0, m], w_ref[0, 0]) + dot_nn(ul_ref[0, 1, m], w_ref[0, 1])

    @pl.when(k == pl.num_programs(0) - 1)
    def _():
        y_ref[...] = acc[...].astype(BF16)


def forward_mix(spans, x, gain, table, w, ar):
    count = table.shape[0]
    _, rows, width = x.shape
    full = lambda *shape: pl.BlockSpec(shape, lambda k: (0,) * len(shape))
    return pl.pallas_call(
        functools.partial(forward_kernel, spans),
        grid=(count,),
        out_shape=[
            jax.ShapeDtypeStruct((count, 2, 2, rows, width), BF16),
            jax.ShapeDtypeStruct((2, rows, width), BF16),
            jax.ShapeDtypeStruct((2, rows, width), BF16),
        ],
        in_specs=[
            full(2, rows, width),
            full(1, width),
            pl.BlockSpec((1, 1, 2 * rows), lambda k: (k, 0, 0)),
            pl.BlockSpec((1, 2, width, width), lambda k: (k, 0, 0, 0)),
            full(3 * width, width),
        ],
        out_specs=[
            pl.BlockSpec((1, 2, 2, rows, width), lambda k: (k, 0, 0, 0, 0)),
            full(2, rows, width),
            full(2, rows, width),
        ],
        scratch_shapes=[pltpu.VMEM((2, rows, 2 * width), BF16), pltpu.VMEM((2, rows, width), F32)],
        compiler_params=params(),
        name="forward_mix",
    )(x, gain, table, w, ar)


def backward_kernel(
    spans, dy_ref, u_ref, row_ref, w_ref, ul_ref, ar_ref, dw_ref, dar_ref, du_ref, both, acc
):
    k = pl.program_id(0)
    rows, width = dy_ref.shape[1], dy_ref.shape[2]
    signs = signs_of(rows)

    @pl.when(k == 0)
    def _():
        for m in range(2):
            dy = dy_ref[m]
            both[m, :, :width] = dy
            both[m, :, width:] = (dy.astype(F32) * signs).astype(BF16)
            acc[m] = dot_nt(dy, ar_ref[:width])
            for lag in (1, 2):
                acc[m] += led(
                    dot_nt(dy, ar_ref[lag * width : (lag + 1) * width]), lag, spans[m]
                )
        for lag in (0, 1, 2):
            total = 0.0
            for m in range(2):
                u = u_ref[m]
                if lag:
                    u = lagged(u.astype(F32), lag, spans[m]).astype(BF16)
                total = total + dot_tn(u, dy_ref[m])
            dar_ref[lag * width : (lag + 1) * width, :] = total.astype(BF16)

    table = spread(row_ref[0], rows)
    for m in range(2):
        span = spans[m]
        for j in range(rows // span):
            part = slice(j * span, (j + 1) * span)
            conv = dot_nn(table[:span, :span], both[m, part, :])
            plus = conv[:, :width].astype(BF16)
            minus = (conv[:, width:] * signs[part]).astype(BF16)
            acc[m, part, :] += dot_nt(plus, w_ref[0, 0]) + dot_nt(minus, w_ref[0, 1])
    for p in range(2):
        total = dot_tn(ul_ref[0, p, 0], dy_ref[0]) + dot_tn(ul_ref[0, p, 1], dy_ref[1])
        dw_ref[0, p] = total.astype(BF16)

    @pl.when(k == pl.num_programs(0) - 1)
    def _():
        du_ref[...] = acc[...].astype(BF16)


def backward_mix(spans, dy, u, table, w, ul, ar):
    count = table.shape[0]
    _, rows, width = dy.shape
    full = lambda *shape: pl.BlockSpec(shape, lambda k: (0,) * len(shape))
    return pl.pallas_call(
        functools.partial(backward_kernel, spans),
        grid=(count,),
        out_shape=[
            jax.ShapeDtypeStruct((count, 2, width, width), BF16),
            jax.ShapeDtypeStruct((3 * width, width), BF16),
            jax.ShapeDtypeStruct((2, rows, width), BF16),
        ],
        in_specs=[
            full(2, rows, width),
            full(2, rows, width),
            pl.BlockSpec((1, 1, 2 * rows), lambda k: (k, 0, 0)),
            pl.BlockSpec((1, 2, width, width), lambda k: (k, 0, 0, 0)),
            pl.BlockSpec((1, 2, 2, rows, width), lambda k: (k, 0, 0, 0, 0)),
            full(3 * width, width),
        ],
        out_specs=[
            pl.BlockSpec((1, 2, width, width), lambda k: (k, 0, 0, 0)),
            full(3 * width, width),
            full(2, rows, width),
        ],
        scratch_shapes=[pltpu.VMEM((2, rows, 2 * width), BF16), pltpu.VMEM((2, rows, width), F32)],
        compiler_params=params(),
        name="backward_mix",
    )(dy, u, table, w, ul, ar)


def lag_by(values, lag, span, move):
    return jnp.where(
        lag == 0, values, jnp.where(lag == 1, move(values, 1, span), move(values, 2, span))
    )


def mix_back_kernel(seq_count, line, spans, *refs):
    (dy_ref, u_ref, row_ref, w_hbm, ul_hbm, ar_ref, x_ref, hg_ref, scale_ref) = refs[:9]
    (z_ref, gb_ref, ub_ref, mixed_ref, cot_ref, mlp_ref) = refs[9:15]
    (tg_ref, dw_ref, dar_ref, gg_ref, ug_ref, dg_ref, small_ref) = refs[15:22]
    (dy, dsig, acc, conv, du_in, ul_buf, w_buf, dar) = refs[22:30]
    (deep, deep_in, deep_run, wide, wide_in, wide_side, wide_run) = refs[30:37]
    (g_own, g_pair, g_side, g_sum, g_line) = refs[37:42]
    (load_sem, dys, dyr, dus, dur, ps, pr, zs, zr, wps, wpr, ws, wr, wzs, wzr, gs, gr) = refs[42:]
    s, z, c, g = place(seq_count, line)
    twin = {"grp": g + 1 - 2 * c}
    rows, width = dy.shape[1], dy.shape[2]
    block = dy_ref.shape[1]
    count = w_hbm.shape[0]
    per_chip = 2 * count // line
    n = per_chip * width // CORES
    ar_rows = ar_ref.shape[0]
    ar_share = ar_rows // (line * CORES)
    lanes = 128
    ar_chunks = ar_rows // lanes
    share = gg_ref.shape[0]
    mine = pl.ds(pl.multiple_of(s * block, block), block)
    low = (z < line // 2).astype(jnp.int32)

    def dest(i):
        return low * (line - 1 - 2 * i) + i

    def load(i):
        return pltpu.make_async_copy(
            ul_hbm.at[pl.ds(dest(i) * per_chip, per_chip)], ul_buf.at[i % 2], load_sem.at[i % 2]
        )

    load_w = pltpu.make_async_copy(w_hbm, w_buf, load_sem.at[2])
    load(0).start()
    if line > 1:
        load(1).start()
    load_w.start()
    greet(seq_count, line, s, z, c, g, twin=True, side=True, whole_line=True)

    dy_copies = []
    for i in range(1, seq_count):
        dy_copies.append(
            remote(
                dy_ref,
                dy.at[:, mine, :],
                dys.at[i - 1],
                dyr.at[i - 1],
                {"seq": lax.rem(s + i, seq_count)},
            )
        )
        dy_copies[-1].start()
    dy[:, mine, :] = dy_ref[...]

    span_f = gb_ref.shape[1] // seq_count
    down_share = dg_ref.shape[0]
    for j in range(seq_count):
        part = slice(j * span_f, (j + 1) * span_f)
        for which, back in ((0, gb_ref), (1, ub_ref)):
            val = dot_tn(z_ref[...], back[:, part]).astype(BF16)
            for k in range(seq_count):
                for l in range(line):
                    for cc in range(CORES):
                        r = ((k * line + l) * CORES + cc) * share
                        wide[cc, k, l, which * share : (which + 1) * share, part] = val[
                            r : r + share
                        ]
        val = dot_tn(mixed_ref[:, part], cot_ref[...]).astype(BF16)
        for l in range(line):
            for cc in range(CORES):
                r = (l * CORES + cc) * down_share
                for q in range(down_share // share):
                    wide[cc, j, l, 2 * share :, q * width : (q + 1) * width] = val[
                        r + q * share : r + (q + 1) * share
                    ]
    wide_twin = remote(wide.at[1 - c], wide_in, wps, wpr, twin)
    wide_twin.start()

    for x in dy_copies:
        x.wait_recv()

    def ar_place(i):
        at = s * ar_chunks + i
        lag = lax.div(at, width // lanes)
        col = lax.rem(at, width // lanes)
        return lag, pl.ds(pl.multiple_of(col * lanes, lanes), lanes)

    for i in range(ar_chunks):
        lag, cols = ar_place(i)
        total = 0.0
        for m in range(2):
            v = lag_by(u_ref[m, :, cols].astype(F32), lag, spans[m], lagged).astype(BF16)
            total = total + dot_tn(v, dy[m])
        dar[i * lanes : (i + 1) * lanes, :] = total.astype(BF16)
    for l in range(line):
        for cc in range(CORES):
            r = (l * CORES + cc) * ar_share
            deep[cc, l, n:, :] = dar[r : r + ar_share, :]

    def twin_deep(i):
        l = dest(i)
        return remote(deep.at[1 - c, l], deep_in.at[l], ps.at[i], pr.at[i], twin)

    def hop(run, own, send, recv, way, t, first):
        target = line - 1 - t if way == 0 else t
        src = own(target) if first else run.at[way, t]
        to = g + CORES if way == 0 else g - CORES
        return remote(src, run.at[way, t], send.at[way, t], recv.at[way, t], {"grp": to})

    def deep_own(l):
        return deep_in.at[l]

    def wide_own(l):
        return wide_in.at[s, l]

    deep_line = (deep_run, deep_own, zs, zr)
    wide_line = (wide_run, wide_own, wzs, wzr)

    def begin(kind, t):
        for way in (0, 1):

            @pl.when(z == 0 if way == 0 else z == line - 1)
            def _():
                hop(*kind, way, t, True).start()

    def relay(kind, phase):
        run, own = kind[0], kind[1]
        for way in (0, 1):
            for t in range(phase):
                at = phase - t if way == 0 else line - 1 - (phase - t)
                target = line - 1 - t if way == 0 else t

                @pl.when(z == at)
                def _():
                    hop(*kind, way, t, False).wait_recv()
                    mixed = run[way, t].astype(F32) + own(target)[...].astype(F32)
                    run[way, t] = mixed.astype(BF16)
                    hop(*kind, way, t, False).start()

    def compute(i):
        l = dest(i)
        load(i).wait()
        for j in range(per_chip):
            val = dot_tn(ul_buf[i % 2, j, 0], dy[0]) + dot_tn(ul_buf[i % 2, j, 1], dy[1])
            val = val.astype(BF16)
            for cc in range(CORES):
                lo, hi = max(j * width, cc * n), min((j + 1) * width, (cc + 1) * n)
                if lo < hi:
                    deep[cc, l, lo - cc * n : hi - cc * n, :] = val[lo - j * width : hi - j * width]
        twin_deep(i).start()
        if i + 2 < line:
            load(i + 2).start()

    def combine(i):
        l = dest(i)
        twin_deep(i).wait_recv()
        deep_in[l] = (deep[c, l].astype(F32) + deep_in[l].astype(F32)).astype(BF16)
        if i < line - 1:
            begin(deep_line, i)

    for i in range(line):
        compute(i)
        if i > 0:
            combine(i - 1)
    combine(line - 1)

    wide_twin.wait_recv()
    for k in range(seq_count):

        @pl.loop(0, line)
        def _(l):
            mixed = wide[c, k, l].astype(F32) + wide_in[k, l].astype(F32)
            wide_in[k, l] = mixed.astype(BF16)

    sides = []
    for j in range(1, seq_count):
        to = lax.rem(s + j, seq_count)
        sides.append(
            remote(wide_in.at[to], wide_side.at[j - 1], ws.at[j - 1], wr.at[j - 1], {"seq": to})
        )
        sides[-1].start()

    signs = signs_of(rows)
    for m in range(2):
        dsig[m] = (dy[m].astype(F32) * signs).astype(BF16)
    acc[...] = jnp.zeros_like(acc)
    for i in range(ar_chunks):
        lag, cols = ar_place(i)
        for m in range(2):
            val = dot_nt(dy[m], ar_ref[i * lanes : (i + 1) * lanes, :])
            acc[m, :, cols] += lag_by(val, lag, spans[m], led)
    load_w.wait()

    def filter_step(k):
        table = spread(row_ref[k], rows)
        for m in range(2):
            span = spans[m]
            for j in range(rows // span):
                part = slice(j * span, (j + 1) * span)
                conv[0, part, :] = dot_nn(table[:span, :span], dy[m, part, :]).astype(BF16)
                minus = dot_nn(table[:span, :span], dsig[m, part, :])
                conv[1, part, :] = (minus * signs[part]).astype(BF16)
            acc[m] += dot_nt(conv[0], w_buf[k, 0]) + dot_nt(conv[1], w_buf[k, 1])

    half = count // 2
    pl.loop(0, half)(filter_step)
    for phase in range(1, line - 2):
        relay(deep_line, phase)
    pl.loop(half, count)(filter_step)
    conv[...] = acc[...].astype(BF16)
    du_copies = []
    for i in range(1, seq_count):
        to = lax.rem(s + i, seq_count)
        du_copies.append(
            remote(
                conv.at[:, pl.ds(pl.multiple_of(to * block, block), block), :],
                du_in.at[i - 1],
                dus.at[i - 1],
                dur.at[i - 1],
                {"seq": to},
            )
        )
        du_copies[-1].start()
    if line > 2:
        relay(deep_line, line - 2)

    for x in du_copies:
        x.wait_recv()
    gain = jnp.zeros((1, width), F32)
    for m in range(2):
        grad = conv[m, mine, :].astype(F32)
        for i in range(seq_count - 1):
            grad = grad + du_in[i, m].astype(F32)
        x = x_ref[m].astype(F32)
        inv = lax.rsqrt(jnp.mean(x * x, axis=-1, keepdims=True) + EPSILON)
        scaled = grad * scale_ref[...]
        gain = gain + jnp.sum(grad * x * inv, axis=0, keepdims=True)
        centre = jnp.mean(scaled * x, axis=-1, keepdims=True)
        tg_ref[m] = hg_ref[m] + inv * scaled - x * (inv * inv * inv) * centre
    g_own[...] = jnp.zeros_like(g_own)
    g_own[0:1, :] = gain
    g_own[1:2, :] = mlp_ref[...]
    small_pair = remote(g_own, g_pair, gs.at[0], gr.at[0], twin)
    small_pair.start()

    for x in sides:
        x.wait_recv()

    @pl.loop(0, line)
    def _(l):
        mixed = wide_in[s, l].astype(F32)
        for j in range(seq_count - 1):
            mixed = mixed + wide_side[j, l].astype(F32)
        wide_in[s, l] = mixed.astype(BF16)

    for t in range(line - 1):
        begin(wide_line, t)

    small_pair.wait()
    g_own[...] = g_own[...] + g_pair[...]
    small_sides = []
    for j in range(1, seq_count):
        small_sides.append(
            remote(
                g_own, g_side.at[j - 1], gs.at[j], gr.at[j], {"seq": lax.rem(s + j, seq_count)}
            )
        )
        small_sides[-1].start()

    dw_ref[...] = deep_in[z, :n, :].astype(F32)
    dar_ref[...] = deep_in[z, n:, :].astype(F32)
    for x in small_sides:
        x.wait()
    total = g_own[...]
    for j in range(seq_count - 1):
        total = total + g_side[j]
    g_sum[...] = total
    small_lines = []
    for j in range(1, line):
        small_lines.append(
            remote(
                g_sum,
                g_line.at[j - 1],
                gs.at[seq_count - 1 + j],
                gr.at[seq_count - 1 + j],
                {"grp": lax.rem(g + CORES * j, CORES * line)},
            )
        )
        small_lines[-1].start()

    def last(kind, add):
        for t in range(line - 1):
            for way in (0, 1):
                target = line - 1 - t if way == 0 else t

                @pl.when(z == target)
                def _():
                    hop(*kind, way, t, False).wait_recv()
                    add(kind[0][way, t].astype(F32))

    def add_deep(val):
        dw_ref[...] += val[:n]
        dar_ref[...] += val[n:]

    def add_wide(val):
        gg_ref[...] += val[:share]
        ug_ref[...] += val[share : 2 * share]
        for q in range(down_share // share):
            dg_ref[q * share : (q + 1) * share, :] += val[2 * share :, q * width : (q + 1) * width]

    last(deep_line, add_deep)
    for phase in range(1, line - 1):
        relay(wide_line, phase)
    own = wide_in[s, z].astype(F32)
    gg_ref[...] = own[:share]
    ug_ref[...] = own[share : 2 * share]
    for q in range(down_share // share):
        dg_ref[q * share : (q + 1) * share, :] = own[2 * share :, q * width : (q + 1) * width]
    last(wide_line, add_wide)

    for x in small_lines:
        x.wait()
    total = g_sum[...]
    for j in range(line - 1):
        total = total + g_line[j]
    small_ref[...] = total

    for x in dy_copies + sides + du_copies:
        x.wait_send()
    wide_twin.wait_send()
    for i in range(line):
        twin_deep(i).wait_send()
    for kind in (deep_line, wide_line):
        for t in range(line - 1):
            for way in (0, 1):
                target = line - 1 - t if way == 0 else t

                @pl.when(z < target if way == 0 else z > target)
                def _():
                    hop(*kind, way, t, False).wait_send()


def mix_back(seq_count, line, spans, dy, u, table, w, ul, ar, x, hg, scale, mlp, mlp_grad, shares):
    z, gate_back, up_back, mixed, cot = mlp
    share, down_share, deep_share, ar_share = shares
    _, block, width = dy.shape
    rows = block * seq_count
    count = w.shape[0]
    per_chip = 2 * count // line
    small = (8, width)
    hidden_units = gate_back.shape[1]
    part = (2 * share + down_share * width // hidden_units, hidden_units)
    out_shape = [
        jax.ShapeDtypeStruct((2, block, width), F32),
        jax.ShapeDtypeStruct((deep_share, width), F32),
        jax.ShapeDtypeStruct((ar_share, width), F32),
        jax.ShapeDtypeStruct((share, hidden_units), F32),
        jax.ShapeDtypeStruct((share, hidden_units), F32),
        jax.ShapeDtypeStruct((down_share, width), F32),
        jax.ShapeDtypeStruct(small, F32),
    ]
    deep = (deep_share + ar_share, width)
    scratch = [
        pltpu.VMEM((2, rows, width), BF16),
        pltpu.VMEM((2, rows, width), BF16),
        pltpu.VMEM((2, rows, width), F32),
        pltpu.VMEM((2, rows, width), BF16),
        pltpu.VMEM((seq_count - 1, 2, block, width), BF16),
        pltpu.VMEM((2, per_chip, 2, rows, width), BF16),
        pltpu.VMEM(w.shape, BF16),
        pltpu.VMEM(ar.shape, BF16),
        pltpu.VMEM((CORES, line) + deep, BF16),
        pltpu.VMEM((line,) + deep, BF16),
        pltpu.VMEM((2, line - 1) + deep, BF16),
        pltpu.VMEM((CORES, seq_count, line) + part, BF16),
        pltpu.VMEM((seq_count, line) + part, BF16),
        pltpu.VMEM((seq_count - 1, line) + part, BF16),
        pltpu.VMEM((2, line - 1) + part, BF16),
        pltpu.VMEM(small, F32),
        pltpu.VMEM(small, F32),
        pltpu.VMEM((seq_count - 1,) + small, F32),
        pltpu.VMEM(small, F32),
        pltpu.VMEM((line - 1,) + small, F32),
        DMA((3,)),
        DMA((seq_count - 1,)),
        DMA((seq_count - 1,)),
        DMA((seq_count - 1,)),
        DMA((seq_count - 1,)),
        DMA((line,)),
        DMA((line,)),
        DMA((2, line - 1)),
        DMA((2, line - 1)),
        DMA,
        DMA,
        DMA((seq_count - 1,)),
        DMA((seq_count - 1,)),
        DMA((2, line - 1)),
        DMA((2, line - 1)),
        DMA((seq_count + line,)),
        DMA((seq_count + line,)),
    ]
    return pl.pallas_call(
        functools.partial(mix_back_kernel, seq_count, line, spans),
        out_shape=out_shape,
        in_specs=[WHOLE] * 3 + [ANY] * 2 + [WHOLE] * 10,
        out_specs=[WHOLE] * 7,
        scratch_shapes=scratch,
        compiler_params=params(6),
        name="mix_back",
    )(dy, u, table, w, ul.reshape(2 * count, 2, rows, width), ar, x, hg, scale, z, gate_back, up_back, mixed, cot, mlp_grad)


def body(
    tokens,
    layout,
    filters,
    gain_mix,
    spectral_proj,
    ar_proj,
    gain_mlp,
    w_gate,
    w_up,
    w_down,
    out_grad,
):
    seq_count = lax.axis_size("seq")
    line = lax.axis_size("grp") // CORES
    s = lax.axis_index("seq")
    g = lax.axis_index("grp")
    block, width = tokens.shape[2], tokens.shape[3]
    rows = block * seq_count
    count = filters.shape[1] // seq_count
    hidden_units = w_gate.shape[1]
    spans = (rows, rows // 4)

    swap = layout[0, 0] == 1
    own = jnp.where(swap, tokens[::-1, 0], tokens[:, 0])
    cotangent = jnp.where(swap, out_grad[::-1, 0], out_grad[:, 0])
    share = gain_mix.shape[0]
    gains = jnp.zeros((16, 128), BF16)
    gains = gains.at[0, :share].set(gain_mix).at[1, :share].set(gain_mlp)

    x_all, spec, ar, gate_w, up_w, down_w, gains = gather_all(
        seq_count, line, own, (spectral_proj, ar_proj), (w_gate, w_up, w_down, gains)
    )
    spec = spec.reshape(count, 2, width, width)
    ar_rows = ar.shape[0] * ar.shape[1] * ar.shape[2]
    ar_full = lax.dynamic_update_slice(
        jnp.zeros((3 * width, width), BF16), ar.reshape(ar_rows, width), (s * ar_rows, 0)
    )
    gate_w = gate_w.reshape(width, hidden_units)
    up_w = up_w.reshape(width, hidden_units)
    down_w = down_w.reshape(hidden_units, width)
    gains = gains.reshape(-1, 16, 128).astype(F32)
    mix_scale = gains[:, 0, :share].reshape(1, width)
    mlp_scale = gains[:, 1, :share].reshape(1, width)

    mine = lax.dynamic_slice(filters.T, (s * count, 0), (count, rows))[:, None, :]
    nothing = jnp.zeros((count, 1, rows), F32)
    back_table = jnp.concatenate([mine, nothing], axis=2)
    fore_table = jnp.concatenate([mine[:, :, :1], nothing, mine[:, :, :0:-1]], axis=2)

    ul, u, y = forward_mix(spans, x_all, mix_scale, fore_table, spec, ar_full)
    mixer = side_sum(seq_count, line, y, 3).reshape(2 * block, width)

    inputs = own.reshape(2 * block, width).astype(F32)
    cot = cotangent.reshape(2 * block, width)
    hidden = inputs + mixer
    inv_two = lax.rsqrt(jnp.mean(hidden * hidden, axis=-1, keepdims=True) + EPSILON)
    mlp_in = (hidden * inv_two * mlp_scale).astype(BF16)
    gate = dot_nn(mlp_in, gate_w)
    upval = dot_nn(mlp_in, up_w)
    product_val, gelu_pull = jax.vjp(lambda a, b: jax.nn.gelu(a) * b, gate, upval)
    mixed = product_val.astype(BF16)
    out = hidden + dot_nn(mixed, down_w)
    mixed_grad = dot_nt(cot, down_w)
    gate_back, up_back = gelu_pull(mixed_grad)
    gate_back = gate_back.astype(BF16)
    up_back = up_back.astype(BF16)
    mlp_in_grad = dot_nt(gate_back, gate_w) + dot_nt(up_back, up_w)
    scaled_two = mlp_in_grad * mlp_scale
    mlp_grad = jnp.sum(mlp_in_grad * hidden * inv_two, axis=0, keepdims=True)
    hidden_grad = (
        cot.astype(F32)
        + inv_two * scaled_two
        - hidden * inv_two**3 * jnp.mean(scaled_two * hidden, axis=-1, keepdims=True)
    )
    mixer_grad = hidden_grad.astype(BF16)

    ar_share = ar_rows // (line * CORES)
    if w_gate.shape[0] % 16 == 0 and ar_share % 16 == 0 and 2 * count % line == 0:
        input_grad, dw, dar, gate_grad, up_grad, down_grad, small = mix_back(
            seq_count,
            line,
            spans,
            mixer_grad.reshape(2, block, width),
            u,
            back_table,
            spec,
            ul,
            ar.reshape(ar_rows, width),
            own,
            hidden_grad.reshape(2, block, width),
            mix_scale,
            (mlp_in, gate_back, up_back, mixed, cot),
            mlp_grad,
            (w_gate.shape[0], w_down.shape[0], spectral_proj.shape[0], ar_share),
        )
    else:
        down_grad = dot_tn(mixed, cot)
        gate_grad = dot_tn(mlp_in, gate_back)
        up_grad = dot_tn(mlp_in, up_back)
        dy = side_gather(seq_count, line, mixer_grad.reshape(2, block, width))
        dw, dar, du = backward_mix(spans, dy, u, back_table, spec, ul, ar_full)
        normed_grad = side_sum(seq_count, line, du, 4).reshape(2 * block, width)

        inv_one = lax.rsqrt(jnp.mean(inputs * inputs, axis=-1, keepdims=True) + EPSILON)
        scaled_one = normed_grad * mix_scale
        mix_grad = jnp.sum(normed_grad * inputs * inv_one, axis=0, keepdims=True)
        input_grad = (
            hidden_grad
            + inv_one * scaled_one
            - inputs * inv_one**3 * jnp.mean(scaled_one * inputs, axis=-1, keepdims=True)
        )

        dar = lax.dynamic_slice(dar, (s * ar_rows, 0), (ar_rows, width))
        deep = (dw.reshape(line, CORES, -1, width), dar.reshape(line, CORES, -1, width))
        wide = tuple(
            x.astype(BF16).reshape(seq_count, line, CORES, -1, x.shape[1])
            for x in (gate_grad, up_grad, down_grad)
        )
        small = jnp.concatenate([mix_grad, mlp_grad, jnp.zeros((6, width), F32)], axis=0)
        dw, dar, gate_grad, up_grad, down_grad, small = sum_all(seq_count, line, deep, wide, small)
    small = lax.dynamic_slice(small, (0, (s * CORES * line + g) * share), (2, share))

    def settle(x):
        x = x.reshape(2, 1, block, width)
        return jnp.where(swap, x[::-1], x)

    return (
        settle(out),
        settle(input_grad),
        small[0],
        dw,
        dar,
        small[1],
        gate_grad,
        up_grad,
        down_grad,
    )


def solution(mesh):
    placed = (
        P(None, "grp", "seq", None),
        P(None, "grp"),
        P(),
        P(("seq", "grp")),
        P(("seq", "grp"), None),
        P(("seq", "grp"), None),
        P(("seq", "grp")),
        P(("seq", "grp"), None),
        P(("seq", "grp"), None),
        P(("seq", "grp"), None),
        P(None, "grp", "seq", None),
    )
    return jax.shard_map(
        body,
        mesh=mesh,
        in_specs=placed,
        out_specs=(
            P(None, "grp", "seq", None),
            P(None, "grp", "seq", None),
            P(("seq", "grp")),
            P(("seq", "grp"), None),
            P(("seq", "grp"), None),
            P(("seq", "grp")),
            P(("seq", "grp"), None),
            P(("seq", "grp"), None),
            P(("seq", "grp"), None),
        ),
        check_vma=False,
    )
```

```python
import functools

import jax
import jax.numpy as jnp
from jax import lax
from jax.experimental import pallas as pl
from jax.experimental.pallas import tpu as pltpu
from jax.sharding import PartitionSpec as P

EPSILON = 1e-05
BF16 = jnp.bfloat16
F32 = jnp.float32
MESH = pl.DeviceIdType.MESH
DMA = pltpu.SemaphoreType.DMA
ANY = pl.BlockSpec(memory_space=pl.ANY)
WHOLE = pl.BlockSpec(memory_space=pltpu.VMEM)
VMEM_LIMIT = 60 * 1024 * 1024
CORES = 2


def dot_nn(a, b):
    return lax.dot_general(a, b, (((1,), (0,)), ((), ())), preferred_element_type=F32)


def dot_tn(a, b):
    return lax.dot_general(a, b, (((0,), (0,)), ((), ())), preferred_element_type=F32)


def dot_nt(a, b):
    return lax.dot_general(a, b, (((1,), (1,)), ((), ())), preferred_element_type=F32)


def params(collective_id=None):
    return pltpu.CompilerParams(
        collective_id=collective_id,
        has_side_effects=collective_id is not None,
        vmem_limit_bytes=VMEM_LIMIT,
    )


def remote(src, dst, send, recv, where):
    return pltpu.make_async_remote_copy(
        src_ref=src, dst_ref=dst, send_sem=send, recv_sem=recv, device_id=where, device_id_type=MESH
    )


def place(seq_count, line):
    s = lax.axis_index("seq")
    g = lax.axis_index("grp")
    return s, lax.div(g, CORES), lax.rem(g, CORES), g


def greet(seq_count, line, s, z, c, g, chain=False, twin=False, side=False, whole_line=False):
    barrier = pltpu.get_barrier_semaphore()

    def call(where):
        pl.semaphore_signal(barrier, inc=1, device_id=where, device_id_type=MESH)

    expected = (1 if twin else 0) + (seq_count - 1 if side else 0) + (line - 1 if whole_line else 0)
    if twin:
        call({"grp": g + 1 - 2 * c})
    if side:
        for i in range(1, seq_count):
            call({"seq": lax.rem(s + i, seq_count)})
    if whole_line:
        for j in range(1, line):
            call({"grp": lax.rem(g + CORES * j, CORES * line)})
    if chain:
        expected = expected + (z > 0).astype(jnp.int32) + (z < line - 1).astype(jnp.int32)

        @pl.when(z > 0)
        def _():
            call({"grp": g - CORES})

        @pl.when(z < line - 1)
        def _():
            call({"grp": g + CORES})

    pl.semaphore_wait(barrier, expected)


def line_conditions(line, z, way, t):
    if way == 0:
        return (z < line - 1) & (z >= t), z >= t + 1, z - t, z - 1 - t
    return (z > 0) & (z + t <= line - 1), z + t + 1 <= line - 1, z + t, z + 1 + t


def gather_kernel(seq_count, line, n_deep, n_wide, *refs):
    n_in = 1 + n_deep + n_wide
    ins, outs = refs[:n_in], refs[n_in : 2 * n_in]
    rest = refs[2 * n_in :]
    stage = rest[:n_in]
    (local_sem, tok_send, tok_recv, zs, zr, ws, wr, ps, pr, dps, dpr) = rest[n_in:]
    s, z, c, g = place(seq_count, line)
    twin = {"grp": g + 1 - 2 * c}
    tok, tok_out = ins[0], outs[0]
    rows = tok.shape[1]
    items = list(range(n_deep + n_wide))

    def own(i, l):
        out = outs[1 + i]
        return out.at[l, c] if i < n_deep else out.at[s, l, c]

    loads = [pltpu.make_async_copy(ins[i], stage[i], local_sem.at[0, i]) for i in range(n_in)]
    for x in loads:
        x.start()
    greet(seq_count, line, s, z, c, g, chain=True, twin=True, side=True)

    toks = []
    for i in range(1, seq_count):
        toks.append(
            remote(
                tok,
                tok_out.at[:, pl.ds(pl.multiple_of(s * rows, rows), rows), :],
                tok_send.at[i - 1],
                tok_recv.at[i - 1],
                {"seq": lax.rem(s + i, seq_count)},
            )
        )
        toks[-1].start()

    def hop(i, way, t, origin):
        src = ins[1 + i] if t == 0 else own(i, origin)
        to = g + CORES if way == 0 else g - CORES
        return remote(src, own(i, origin), zs.at[i, way, t], zr.at[i, way, t], {"grp": to})

    def hops(which, t):
        for way in (0, 1):
            sends, _, origin, _ = line_conditions(line, z, way, t)

            @pl.when(sends)
            def _():
                for i in which:
                    hop(i, way, t, origin).start()

    def arrive(which, t, after=None):
        for way in (0, 1):
            _, receives, _, origin = line_conditions(line, z, way, t)

            @pl.when(receives)
            def _():
                for i in which:
                    hop(i, way, t, origin).wait_recv()
                if after is not None:
                    after(origin)

    deep, wide = items[:n_deep], items[n_deep:]
    for t in range(line - 1):
        hops(wide, t)
        if t == 0:
            stores = []
            for i in range(n_in):
                loads[i].wait()
                dst = (
                    tok_out.at[:, pl.ds(pl.multiple_of(s * rows, rows), rows), :]
                    if i == 0
                    else own(i - 1, z)
                )
                stores.append(pltpu.make_async_copy(stage[i], dst, local_sem.at[1, i]))
                stores[-1].start()
        arrive(wide, t)
    hops(deep, 0)
    for x in stores:
        x.wait()
    sides = []
    for i in wide:
        for j in range(1, seq_count):
            part = outs[1 + i].at[s, :, c]
            sides.append(
                remote(
                    part,
                    part,
                    ws.at[i - n_deep, j - 1],
                    wr.at[i - n_deep, j - 1],
                    {"seq": lax.rem(s + j, seq_count)},
                )
            )
            sides[-1].start()

    def twin_wide(i, k):
        part = outs[1 + i].at[k, :, c]
        return remote(part, part, ps.at[i - n_deep, k], pr.at[i - n_deep, k], twin)

    def twin_deep(i, l):
        part = outs[1 + i].at[l, c]
        return remote(part, part, dps.at[i, l], dpr.at[i, l], twin)

    for i in wide:
        twin_wide(i, s).start()
    for i in deep:
        twin_deep(i, z).start()

    def pass_on(origin):
        for i in deep:
            twin_deep(i, origin).start()

    for t in range(line - 1):
        if t > 0:
            hops(deep, t)
        arrive(deep, t, pass_on)
    for x in sides:
        x.wait_recv()
    for i in wide:
        for j in range(1, seq_count):
            twin_wide(i, lax.rem(s + seq_count - j, seq_count)).start()
    for x in toks:
        x.wait_recv()
    for i in deep:
        for l in range(line):
            twin_deep(i, l).wait()
    for i in wide:
        for k in range(seq_count):
            twin_wide(i, k).wait()
    for x in toks + sides:
        x.wait_send()
    for t in range(line - 1):
        for way in (0, 1):
            sends, _, origin, _ = line_conditions(line, z, way, t)

            @pl.when(sends)
            def _():
                for i in items:
                    hop(i, way, t, origin).wait_send()


def gather_all(seq_count, line, tok, deep, wide):
    n_deep, n_wide = len(deep), len(wide)
    shapes = [
        jax.ShapeDtypeStruct((tok.shape[0], tok.shape[1] * seq_count, tok.shape[2]), tok.dtype)
    ]
    shapes += [jax.ShapeDtypeStruct((line, CORES) + x.shape, x.dtype) for x in deep]
    shapes += [jax.ShapeDtypeStruct((seq_count, line, CORES) + x.shape, x.dtype) for x in wide]
    arrays = [tok] + list(deep) + list(wide)
    n = len(arrays)
    scratch = [pltpu.VMEM(x.shape, x.dtype) for x in arrays]
    scratch += [
        DMA((2, n)),
        DMA((seq_count - 1,)),
        DMA((seq_count - 1,)),
        DMA((n_deep + n_wide, 2, line - 1)),
        DMA((n_deep + n_wide, 2, line - 1)),
        DMA((n_wide, seq_count - 1)),
        DMA((n_wide, seq_count - 1)),
        DMA((n_wide, seq_count)),
        DMA((n_wide, seq_count)),
        DMA((n_deep, line)),
        DMA((n_deep, line)),
    ]
    return pl.pallas_call(
        functools.partial(gather_kernel, seq_count, line, n_deep, n_wide),
        out_shape=shapes,
        in_specs=[ANY] * n,
        out_specs=[ANY] * n,
        scratch_shapes=scratch,
        compiler_params=params(1),
        name="gather_all",
    )(*arrays)


def side_gather_kernel(seq_count, line, x_ref, out_ref, local_sem, send, recv):
    s, z, c, g = place(seq_count, line)
    rows = x_ref.shape[1]
    mine = out_ref.at[:, pl.ds(pl.multiple_of(s * rows, rows), rows), :]
    local = pltpu.make_async_copy(x_ref, mine, local_sem)
    local.start()
    greet(seq_count, line, s, z, c, g, side=True)
    copies = []
    for i in range(1, seq_count):
        copies.append(
            remote(
                x_ref, mine, send.at[i - 1], recv.at[i - 1], {"seq": lax.rem(s + i, seq_count)}
            )
        )
        copies[-1].start()
    local.wait()
    for x in copies:
        x.wait()


def side_gather(seq_count, line, x):
    return pl.pallas_call(
        functools.partial(side_gather_kernel, seq_count, line),
        out_shape=jax.ShapeDtypeStruct((x.shape[0], x.shape[1] * seq_count, x.shape[2]), x.dtype),
        in_specs=[WHOLE],
        out_specs=WHOLE,
        scratch_shapes=[DMA, DMA((seq_count - 1,)), DMA((seq_count - 1,))],
        compiler_params=params(2),
        name="side_gather",
    )(x)


def side_sum_kernel(seq_count, line, x_ref, out_ref, slots, send, recv):
    s, z, c, g = place(seq_count, line)
    rows = out_ref.shape[1]
    greet(seq_count, line, s, z, c, g, side=True)
    copies = []
    for i in range(1, seq_count):
        to = lax.rem(s + i, seq_count)
        copies.append(
            remote(
                x_ref.at[:, pl.ds(pl.multiple_of(to * rows, rows), rows), :],
                slots.at[i - 1],
                send.at[i - 1],
                recv.at[i - 1],
                {"seq": to},
            )
        )
        copies[-1].start()
    total = x_ref[:, pl.ds(pl.multiple_of(s * rows, rows), rows), :].astype(F32)
    for i, x in enumerate(copies):
        x.wait_recv()
        total = total + slots[i].astype(F32)
    out_ref[...] = total
    for x in copies:
        x.wait_send()


def side_sum(seq_count, line, x, collective_id):
    rows = x.shape[1] // seq_count
    return pl.pallas_call(
        functools.partial(side_sum_kernel, seq_count, line),
        out_shape=jax.ShapeDtypeStruct((x.shape[0], rows, x.shape[2]), F32),
        in_specs=[WHOLE],
        out_specs=WHOLE,
        scratch_shapes=[
            pltpu.VMEM((seq_count - 1, x.shape[0], rows, x.shape[2]), x.dtype),
            DMA((seq_count - 1,)),
            DMA((seq_count - 1,)),
        ],
        compiler_params=params(collective_id),
        name=f"side_sum_{collective_id}",
    )(x)


def sum_kernel(seq_count, line, n_deep, n_wide, *refs):
    n = n_deep + n_wide
    ins, outs = refs[: n + 1], refs[n + 1 : 2 * n + 2]
    rest = refs[2 * n + 2 :]
    pair, side, chain = rest[:n], rest[n : n + n_wide], rest[n + n_wide : 2 * n + n_wide]
    rest = rest[2 * n + n_wide :]
    g_pair, g_side, g_line, g_a, g_b = rest[:5]
    (ps, pr, ws, wr, zs, zr, gs, gr) = rest[5:]
    s, z, c, g = place(seq_count, line)
    twin = {"grp": g + 1 - 2 * c}
    deep, wide = list(range(n_deep)), list(range(n_deep, n))
    small = ins[n]
    greet(seq_count, line, s, z, c, g, twin=True, side=True, whole_line=True)

    def theirs(i):
        return ins[i].at[:, 1 - c] if i < n_deep else ins[i].at[:, :, 1 - c]

    pairs = [remote(theirs(i), pair[i], ps.at[i], pr.at[i], twin) for i in range(n)]
    small_pair = remote(small, g_pair, gs.at[0], gr.at[0], twin)
    small_pair.start()
    for x in pairs[n_deep:] + pairs[:n_deep]:
        x.start()

    small_pair.wait()
    g_a[...] = small[...] + g_pair[...]
    small_sides = []
    for j in range(1, seq_count):
        small_sides.append(
            remote(
                g_a,
                g_side.at[j - 1],
                gs.at[j],
                gr.at[j],
                {"seq": lax.rem(s + j, seq_count)},
            )
        )
        small_sides[-1].start()

    for i in wide:
        pairs[i].wait_recv()
        for k in range(seq_count):

            @pl.loop(0, line)
            def _(l):
                mixed = ins[i][k, l, c].astype(F32) + pair[i][k, l].astype(F32)
                pair[i][k, l] = mixed.astype(BF16)

    sides = {}
    for i in wide:
        for j in range(1, seq_count):
            to = lax.rem(s + j, seq_count)
            sides[i, j] = remote(
                pair[i].at[to],
                side[i - n_deep].at[j - 1],
                ws.at[i - n_deep, j - 1],
                wr.at[i - n_deep, j - 1],
                {"seq": to},
            )
            sides[i, j].start()
    for i in deep:
        pairs[i].wait_recv()
        for l in range(line):
            pair[i][l] = (ins[i][l, c].astype(F32) + pair[i][l].astype(F32)).astype(BF16)

    for x in small_sides:
        x.wait()
    total = g_a[...]
    for j in range(seq_count - 1):
        total = total + g_side[j]
    g_b[...] = total
    small_lines = []
    for j in range(1, line):
        small_lines.append(
            remote(
                g_b,
                g_line.at[j - 1],
                gs.at[seq_count - 1 + j],
                gr.at[seq_count - 1 + j],
                {"grp": lax.rem(g + CORES * j, CORES * line)},
            )
        )
        small_lines[-1].start()

    def piece(i, l):
        return pair[i].at[l] if i < n_deep else pair[i].at[s, l]

    def run_line(which):
        def hop(i, way, t, dest, first):
            src = piece(i, dest) if first else chain[i].at[way, t]
            to = g + CORES if way == 0 else g - CORES
            return remote(src, chain[i].at[way, t], zs.at[i, way, t], zr.at[i, way, t], {"grp": to})

        for t in range(line - 1):
            for way in (0, 1):
                dest = line - 1 - t if way == 0 else t
                starts = z == 0 if way == 0 else z == line - 1
                relays = (z > 0) & (z < dest) if way == 0 else (z < line - 1) & (z > dest)

                @pl.when(starts)
                def _():
                    for i in which:
                        hop(i, way, t, dest, True).start()

                @pl.when(relays)
                def _():
                    for i in which:
                        hop(i, way, t, dest, False).wait_recv()
                        mixed = chain[i][way, t].astype(F32) + piece(i, dest)[...].astype(F32)
                        chain[i][way, t] = mixed.astype(BF16)
                        hop(i, way, t, dest, False).start()

        for i in which:
            outs[i][...] = piece(i, z)[...].astype(F32)
        for t in range(line - 1):
            for way in (0, 1):
                dest = line - 1 - t if way == 0 else t

                @pl.when((z == dest))
                def _():
                    for i in which:
                        hop(i, way, t, dest, False).wait_recv()
                        outs[i][...] += chain[i][way, t].astype(F32)

                @pl.when(z == 0 if way == 0 else z == line - 1)
                def _():
                    for i in which:
                        hop(i, way, t, dest, True).wait_send()

                @pl.when((z > 0) & (z < dest) if way == 0 else (z < line - 1) & (z > dest))
                def _():
                    for i in which:
                        hop(i, way, t, dest, False).wait_send()

    run_line(deep)
    for i in wide:
        for j in range(1, seq_count):
            sides[i, j].wait()

        @pl.loop(0, line)
        def _(l):
            mixed = pair[i][s, l].astype(F32)
            for j in range(1, seq_count):
                mixed = mixed + side[i - n_deep][j - 1, l].astype(F32)
            pair[i][s, l] = mixed.astype(BF16)

    run_line(wide)
    for x in pairs:
        x.wait_send()
    for x in small_lines:
        x.wait()
    total = g_b[...]
    for j in range(line - 1):
        total = total + g_line[j]
    outs[n][...] = total


def sum_all(seq_count, line, deep, wide, small):
    n_deep, n_wide = len(deep), len(wide)
    n = n_deep + n_wide
    shapes = [jax.ShapeDtypeStruct(x.shape[2:], F32) for x in deep]
    shapes += [jax.ShapeDtypeStruct(x.shape[3:], F32) for x in wide]
    shapes += [jax.ShapeDtypeStruct(small.shape, F32)]
    scratch = [pltpu.VMEM((line,) + x.shape[2:], BF16) for x in deep]
    scratch += [pltpu.VMEM((seq_count, line) + x.shape[3:], BF16) for x in wide]
    scratch += [pltpu.VMEM((seq_count - 1, line) + x.shape[3:], BF16) for x in wide]
    scratch += [pltpu.VMEM((2, line - 1) + x.shape[2:], BF16) for x in deep]
    scratch += [pltpu.VMEM((2, line - 1) + x.shape[3:], BF16) for x in wide]
    scratch += [
        pltpu.VMEM(small.shape, F32),
        pltpu.VMEM((seq_count - 1,) + small.shape, F32),
        pltpu.VMEM((line - 1,) + small.shape, F32),
        pltpu.VMEM(small.shape, F32),
        pltpu.VMEM(small.shape, F32),
        DMA((n,)),
        DMA((n,)),
        DMA((n_wide, seq_count - 1)),
        DMA((n_wide, seq_count - 1)),
        DMA((n, 2, line - 1)),
        DMA((n, 2, line - 1)),
        DMA((seq_count + line,)),
        DMA((seq_count + line,)),
    ]
    return pl.pallas_call(
        functools.partial(sum_kernel, seq_count, line, n_deep, n_wide),
        out_shape=shapes,
        in_specs=[WHOLE] * (n + 1),
        out_specs=[WHOLE] * (n + 1),
        scratch_shapes=scratch,
        compiler_params=params(5),
        name="sum_all",
    )(*deep, *wide, small)


def signs_of(rows):
    pos = lax.broadcasted_iota(jnp.int32, (rows, 1), 0)
    return 1.0 - 2.0 * lax.rem(pos, 2).astype(F32)


def lagged(values, lag, span):
    pos = lax.broadcasted_iota(jnp.int32, (values.shape[0], 1), 0)
    return jnp.where(lax.rem(pos, span) >= lag, pltpu.roll(values, lag, 0), 0.0)


def led(values, lag, span):
    rows = values.shape[0]
    pos = lax.broadcasted_iota(jnp.int32, (rows, 1), 0)
    return jnp.where(lax.rem(pos, span) < span - lag, pltpu.roll(values, rows - lag, 0), 0.0)


def spread(row, rows):
    wide = jnp.broadcast_to(row, (rows, row.shape[1]))
    return pltpu.roll(wide, 0, 1, stride=1, stride_axis=0)[:, :rows].astype(BF16)


def forward_kernel(spans, x_ref, gain_ref, row_ref, w_ref, ar_ref, ul_ref, u_ref, y_ref, both, acc):
    k = pl.program_id(0)
    rows, width = x_ref.shape[1], x_ref.shape[2]
    signs = signs_of(rows)

    @pl.when(k == 0)
    def _():
        for m in range(2):
            x = x_ref[m].astype(F32)
            inv = lax.rsqrt(jnp.mean(x * x, axis=-1, keepdims=True) + EPSILON)
            u = (x * inv * gain_ref[...]).astype(BF16)
            wide = u.astype(F32)
            u_ref[m] = u
            both[m, :, :width] = u
            both[m, :, width:] = (wide * signs).astype(BF16)
            acc[m] = dot_nn(u, ar_ref[:width])
            for lag in (1, 2):
                acc[m] += dot_nn(
                    lagged(wide, lag, spans[m]).astype(BF16),
                    ar_ref[lag * width : (lag + 1) * width],
                )

    table = spread(row_ref[0], rows)
    for m in range(2):
        span = spans[m]
        for j in range(rows // span):
            part = slice(j * span, (j + 1) * span)
            conv = dot_nn(table[:span, :span], both[m, part, :])
            plus = conv[:, :width].astype(BF16)
            minus = (conv[:, width:] * signs[part]).astype(BF16)
            ul_ref[0, 0, m, part, :] = plus
            ul_ref[0, 1, m, part, :] = minus
        acc[m] += dot_nn(ul_ref[0, 0, m], w_ref[0, 0]) + dot_nn(ul_ref[0, 1, m], w_ref[0, 1])

    @pl.when(k == pl.num_programs(0) - 1)
    def _():
        y_ref[...] = acc[...].astype(BF16)


def forward_mix(spans, x, gain, table, w, ar):
    count = table.shape[0]
    _, rows, width = x.shape
    full = lambda *shape: pl.BlockSpec(shape, lambda k: (0,) * len(shape))
    return pl.pallas_call(
        functools.partial(forward_kernel, spans),
        grid=(count,),
        out_shape=[
            jax.ShapeDtypeStruct((count, 2, 2, rows, width), BF16),
            jax.ShapeDtypeStruct((2, rows, width), BF16),
            jax.ShapeDtypeStruct((2, rows, width), BF16),
        ],
        in_specs=[
            full(2, rows, width),
            full(1, width),
            pl.BlockSpec((1, 1, 2 * rows), lambda k: (k, 0, 0)),
            pl.BlockSpec((1, 2, width, width), lambda k: (k, 0, 0, 0)),
            full(3 * width, width),
        ],
        out_specs=[
            pl.BlockSpec((1, 2, 2, rows, width), lambda k: (k, 0, 0, 0, 0)),
            full(2, rows, width),
            full(2, rows, width),
        ],
        scratch_shapes=[pltpu.VMEM((2, rows, 2 * width), BF16), pltpu.VMEM((2, rows, width), F32)],
        compiler_params=params(),
        name="forward_mix",
    )(x, gain, table, w, ar)


def backward_kernel(
    spans, dy_ref, u_ref, row_ref, w_ref, ul_ref, ar_ref, dw_ref, dar_ref, du_ref, both, acc
):
    k = pl.program_id(0)
    rows, width = dy_ref.shape[1], dy_ref.shape[2]
    signs = signs_of(rows)

    @pl.when(k == 0)
    def _():
        for m in range(2):
            dy = dy_ref[m]
            both[m, :, :width] = dy
            both[m, :, width:] = (dy.astype(F32) * signs).astype(BF16)
            acc[m] = dot_nt(dy, ar_ref[:width])
            for lag in (1, 2):
                acc[m] += led(
                    dot_nt(dy, ar_ref[lag * width : (lag + 1) * width]), lag, spans[m]
                )
        for lag in (0, 1, 2):
            total = 0.0
            for m in range(2):
                u = u_ref[m]
                if lag:
                    u = lagged(u.astype(F32), lag, spans[m]).astype(BF16)
                total = total + dot_tn(u, dy_ref[m])
            dar_ref[lag * width : (lag + 1) * width, :] = total.astype(BF16)

    table = spread(row_ref[0], rows)
    for m in range(2):
        span = spans[m]
        for j in range(rows // span):
            part = slice(j * span, (j + 1) * span)
            conv = dot_nn(table[:span, :span], both[m, part, :])
            plus = conv[:, :width].astype(BF16)
            minus = (conv[:, width:] * signs[part]).astype(BF16)
            acc[m, part, :] += dot_nt(plus, w_ref[0, 0]) + dot_nt(minus, w_ref[0, 1])
    for p in range(2):
        total = dot_tn(ul_ref[0, p, 0], dy_ref[0]) + dot_tn(ul_ref[0, p, 1], dy_ref[1])
        dw_ref[0, p] = total.astype(BF16)

    @pl.when(k == pl.num_programs(0) - 1)
    def _():
        du_ref[...] = acc[...].astype(BF16)


def backward_mix(spans, dy, u, table, w, ul, ar):
    count = table.shape[0]
    _, rows, width = dy.shape
    full = lambda *shape: pl.BlockSpec(shape, lambda k: (0,) * len(shape))
    return pl.pallas_call(
        functools.partial(backward_kernel, spans),
        grid=(count,),
        out_shape=[
            jax.ShapeDtypeStruct((count, 2, width, width), BF16),
            jax.ShapeDtypeStruct((3 * width, width), BF16),
            jax.ShapeDtypeStruct((2, rows, width), BF16),
        ],
        in_specs=[
            full(2, rows, width),
            full(2, rows, width),
            pl.BlockSpec((1, 1, 2 * rows), lambda k: (k, 0, 0)),
            pl.BlockSpec((1, 2, width, width), lambda k: (k, 0, 0, 0)),
            pl.BlockSpec((1, 2, 2, rows, width), lambda k: (k, 0, 0, 0, 0)),
            full(3 * width, width),
        ],
        out_specs=[
            pl.BlockSpec((1, 2, width, width), lambda k: (k, 0, 0, 0)),
            full(3 * width, width),
            full(2, rows, width),
        ],
        scratch_shapes=[pltpu.VMEM((2, rows, 2 * width), BF16), pltpu.VMEM((2, rows, width), F32)],
        compiler_params=params(),
        name="backward_mix",
    )(dy, u, table, w, ul, ar)


def lag_by(values, lag, span, move):
    return jnp.where(
        lag == 0, values, jnp.where(lag == 1, move(values, 1, span), move(values, 2, span))
    )


def mix_back_kernel(seq_count, line, spans, *refs):
    (dy_ref, u_ref, row_ref, w_hbm, ul_hbm, ar_ref, x_ref, hg_ref, scale_ref) = refs[:9]
    (z_ref, gb_ref, ub_ref, mixed_ref, cot_ref, mlp_ref) = refs[9:15]
    (tg_ref, dw_ref, dar_ref, gg_ref, ug_ref, dg_ref, small_ref) = refs[15:22]
    (dy, dsig, acc, conv, du_in, ul_buf, w_buf, dar) = refs[22:30]
    (deep, deep_in, deep_run, wide, wide_in, wide_side, wide_run) = refs[30:37]
    (g_own, g_pair, g_side, g_sum, g_line) = refs[37:42]
    (load_sem, dys, dyr, dus, dur, ps, pr, zs, zr, wps, wpr, ws, wr, wzs, wzr, gs, gr) = refs[42:]
    s, z, c, g = place(seq_count, line)
    twin = {"grp": g + 1 - 2 * c}
    rows, width = dy.shape[1], dy.shape[2]
    block = dy_ref.shape[1]
    count = w_hbm.shape[0]
    per_chip = 2 * count // line
    n = per_chip * width // CORES
    ar_rows = ar_ref.shape[0]
    ar_share = ar_rows // (line * CORES)
    lanes = 128
    ar_chunks = ar_rows // lanes
    share = gg_ref.shape[0]
    mine = pl.ds(pl.multiple_of(s * block, block), block)
    low = (z < line // 2).astype(jnp.int32)

    def dest(i):
        return low * (line - 1 - 2 * i) + i

    def load(i):
        return pltpu.make_async_copy(
            ul_hbm.at[pl.ds(dest(i) * per_chip, per_chip)], ul_buf.at[i % 2], load_sem.at[i % 2]
        )

    load_w = pltpu.make_async_copy(w_hbm, w_buf, load_sem.at[2])
    load(0).start()
    if line > 1:
        load(1).start()
    load_w.start()
    greet(seq_count, line, s, z, c, g, twin=True, side=True, whole_line=True)

    dy_copies = []
    for i in range(1, seq_count):
        dy_copies.append(
            remote(
                dy_ref,
                dy.at[:, mine, :],
                dys.at[i - 1],
                dyr.at[i - 1],
                {"seq": lax.rem(s + i, seq_count)},
            )
        )
        dy_copies[-1].start()
    dy[:, mine, :] = dy_ref[...]

    span_f = gb_ref.shape[1] // seq_count
    down_share = dg_ref.shape[0]
    for j in range(seq_count):
        part = slice(j * span_f, (j + 1) * span_f)
        for which, back in ((0, gb_ref), (1, ub_ref)):
            val = dot_tn(z_ref[...], back[:, part]).astype(BF16)
            for k in range(seq_count):
                for l in range(line):
                    for cc in range(CORES):
                        r = ((k * line + l) * CORES + cc) * share
                        wide[cc, k, l, which * share : (which + 1) * share, part] = val[
                            r : r + share
                        ]
        val = dot_tn(mixed_ref[:, part], cot_ref[...]).astype(BF16)
        for l in range(line):
            for cc in range(CORES):
                r = (l * CORES + cc) * down_share
                for q in range(down_share // share):
                    wide[cc, j, l, 2 * share :, q * width : (q + 1) * width] = val[
                        r + q * share : r + (q + 1) * share
                    ]
    wide_twin = remote(wide.at[1 - c], wide_in, wps, wpr, twin)
    wide_twin.start()

    for x in dy_copies:
        x.wait_recv()

    def ar_place(i):
        at = s * ar_chunks + i
        lag = lax.div(at, width // lanes)
        col = lax.rem(at, width // lanes)
        return lag, pl.ds(pl.multiple_of(col * lanes, lanes), lanes)

    for i in range(ar_chunks):
        lag, cols = ar_place(i)
        total = 0.0
        for m in range(2):
            v = lag_by(u_ref[m, :, cols].astype(F32), lag, spans[m], lagged).astype(BF16)
            total = total + dot_tn(v, dy[m])
        dar[i * lanes : (i + 1) * lanes, :] = total.astype(BF16)
    for l in range(line):
        for cc in range(CORES):
            r = (l * CORES + cc) * ar_share
            deep[cc, l, n:, :] = dar[r : r + ar_share, :]

    def twin_deep(i):
        l = dest(i)
        return remote(deep.at[1 - c, l], deep_in.at[l], ps.at[i], pr.at[i], twin)

    def hop(run, own, send, recv, way, t, first):
        target = line - 1 - t if way == 0 else t
        src = own(target) if first else run.at[way, t]
        to = g + CORES if way == 0 else g - CORES
        return remote(src, run.at[way, t], send.at[way, t], recv.at[way, t], {"grp": to})

    def deep_own(l):
        return deep_in.at[l]

    def wide_own(l):
        return wide_in.at[s, l]

    deep_line = (deep_run, deep_own, zs, zr)
    wide_line = (wide_run, wide_own, wzs, wzr)

    def begin(kind, t):
        for way in (0, 1):

            @pl.when(z == 0 if way == 0 else z == line - 1)
            def _():
                hop(*kind, way, t, True).start()

    def relay(kind, phase):
        run, own = kind[0], kind[1]
        for way in (0, 1):
            for t in range(phase):
                at = phase - t if way == 0 else line - 1 - (phase - t)
                target = line - 1 - t if way == 0 else t

                @pl.when(z == at)
                def _():
                    hop(*kind, way, t, False).wait_recv()
                    mixed = run[way, t].astype(F32) + own(target)[...].astype(F32)
                    run[way, t] = mixed.astype(BF16)
                    hop(*kind, way, t, False).start()

    def compute(i):
        l = dest(i)
        load(i).wait()
        for j in range(per_chip):
            val = dot_tn(ul_buf[i % 2, j, 0], dy[0]) + dot_tn(ul_buf[i % 2, j, 1], dy[1])
            val = val.astype(BF16)
            for cc in range(CORES):
                lo, hi = max(j * width, cc * n), min((j + 1) * width, (cc + 1) * n)
                if lo < hi:
                    deep[cc, l, lo - cc * n : hi - cc * n, :] = val[lo - j * width : hi - j * width]
        twin_deep(i).start()
        if i + 2 < line:
            load(i + 2).start()

    def combine(i):
        l = dest(i)
        twin_deep(i).wait_recv()
        deep_in[l] = (deep[c, l].astype(F32) + deep_in[l].astype(F32)).astype(BF16)
        if i < line - 1:
            begin(deep_line, i)

    for i in range(line):
        compute(i)
        if i > 0:
            combine(i - 1)
    combine(line - 1)

    wide_twin.wait_recv()
    for k in range(seq_count):

        @pl.loop(0, line)
        def _(l):
            mixed = wide[c, k, l].astype(F32) + wide_in[k, l].astype(F32)
            wide_in[k, l] = mixed.astype(BF16)

    sides = []
    for j in range(1, seq_count):
        to = lax.rem(s + j, seq_count)
        sides.append(
            remote(wide_in.at[to], wide_side.at[j - 1], ws.at[j - 1], wr.at[j - 1], {"seq": to})
        )
        sides[-1].start()

    signs = signs_of(rows)
    for m in range(2):
        dsig[m] = (dy[m].astype(F32) * signs).astype(BF16)
    acc[...] = jnp.zeros_like(acc)
    for i in range(ar_chunks):
        lag, cols = ar_place(i)
        for m in range(2):
            val = dot_nt(dy[m], ar_ref[i * lanes : (i + 1) * lanes, :])
            acc[m, :, cols] += lag_by(val, lag, spans[m], led)
    load_w.wait()

    def filter_step(k):
        table = spread(row_ref[k], rows)
        for m in range(2):
            span = spans[m]
            for j in range(rows // span):
                part = slice(j * span, (j + 1) * span)
                conv[0, part, :] = dot_nn(table[:span, :span], dy[m, part, :]).astype(BF16)
                minus = dot_nn(table[:span, :span], dsig[m, part, :])
                conv[1, part, :] = (minus * signs[part]).astype(BF16)
            acc[m] += dot_nt(conv[0], w_buf[k, 0]) + dot_nt(conv[1], w_buf[k, 1])

    half = count // 2
    pl.loop(0, half)(filter_step)
    for phase in range(1, line - 2):
        relay(deep_line, phase)
    pl.loop(half, count)(filter_step)
    conv[...] = acc[...].astype(BF16)
    du_copies = []
    for i in range(1, seq_count):
        to = lax.rem(s + i, seq_count)
        du_copies.append(
            remote(
                conv.at[:, pl.ds(pl.multiple_of(to * block, block), block), :],
                du_in.at[i - 1],
                dus.at[i - 1],
                dur.at[i - 1],
                {"seq": to},
            )
        )
        du_copies[-1].start()
    if line > 2:
        relay(deep_line, line - 2)

    for x in du_copies:
        x.wait_recv()
    gain = jnp.zeros((1, width), F32)
    for m in range(2):
        grad = conv[m, mine, :].astype(F32)
        for i in range(seq_count - 1):
            grad = grad + du_in[i, m].astype(F32)
        x = x_ref[m].astype(F32)
        inv = lax.rsqrt(jnp.mean(x * x, axis=-1, keepdims=True) + EPSILON)
        scaled = grad * scale_ref[...]
        gain = gain + jnp.sum(grad * x * inv, axis=0, keepdims=True)
        centre = jnp.mean(scaled * x, axis=-1, keepdims=True)
        tg_ref[m] = hg_ref[m] + inv * scaled - x * (inv * inv * inv) * centre
    g_own[...] = jnp.zeros_like(g_own)
    g_own[0:1, :] = gain
    g_own[1:2, :] = mlp_ref[...]
    small_pair = remote(g_own, g_pair, gs.at[0], gr.at[0], twin)
    small_pair.start()

    for x in sides:
        x.wait_recv()

    @pl.loop(0, line)
    def _(l):
        mixed = wide_in[s, l].astype(F32)
        for j in range(seq_count - 1):
            mixed = mixed + wide_side[j, l].astype(F32)
        wide_in[s, l] = mixed.astype(BF16)

    for t in range(line - 1):
        begin(wide_line, t)

    small_pair.wait()
    g_own[...] = g_own[...] + g_pair[...]
    small_sides = []
    for j in range(1, seq_count):
        small_sides.append(
            remote(
                g_own, g_side.at[j - 1], gs.at[j], gr.at[j], {"seq": lax.rem(s + j, seq_count)}
            )
        )
        small_sides[-1].start()

    dw_ref[...] = deep_in[z, :n, :].astype(F32)
    dar_ref[...] = deep_in[z, n:, :].astype(F32)
    for x in small_sides:
        x.wait()
    total = g_own[...]
    for j in range(seq_count - 1):
        total = total + g_side[j]
    g_sum[...] = total
    small_lines = []
    for j in range(1, line):
        small_lines.append(
            remote(
                g_sum,
                g_line.at[j - 1],
                gs.at[seq_count - 1 + j],
                gr.at[seq_count - 1 + j],
                {"grp": lax.rem(g + CORES * j, CORES * line)},
            )
        )
        small_lines[-1].start()

    def last(kind, add):
        for t in range(line - 1):
            for way in (0, 1):
                target = line - 1 - t if way == 0 else t

                @pl.when(z == target)
                def _():
                    hop(*kind, way, t, False).wait_recv()
                    add(kind[0][way, t].astype(F32))

    def add_deep(val):
        dw_ref[...] += val[:n]
        dar_ref[...] += val[n:]

    def add_wide(val):
        gg_ref[...] += val[:share]
        ug_ref[...] += val[share : 2 * share]
        for q in range(down_share // share):
            dg_ref[q * share : (q + 1) * share, :] += val[2 * share :, q * width : (q + 1) * width]

    last(deep_line, add_deep)
    for phase in range(1, line - 1):
        relay(wide_line, phase)
    own = wide_in[s, z].astype(F32)
    gg_ref[...] = own[:share]
    ug_ref[...] = own[share : 2 * share]
    for q in range(down_share // share):
        dg_ref[q * share : (q + 1) * share, :] = own[2 * share :, q * width : (q + 1) * width]
    last(wide_line, add_wide)

    for x in small_lines:
        x.wait()
    total = g_sum[...]
    for j in range(line - 1):
        total = total + g_line[j]
    small_ref[...] = total

    for x in dy_copies + sides + du_copies:
        x.wait_send()
    wide_twin.wait_send()
    for i in range(line):
        twin_deep(i).wait_send()
    for kind in (deep_line, wide_line):
        for t in range(line - 1):
            for way in (0, 1):
                target = line - 1 - t if way == 0 else t

                @pl.when(z < target if way == 0 else z > target)
                def _():
                    hop(*kind, way, t, False).wait_send()


def mix_back(seq_count, line, spans, dy, u, table, w, ul, ar, x, hg, scale, mlp, mlp_grad, shares):
    z, gate_back, up_back, mixed, cot = mlp
    share, down_share, deep_share, ar_share = shares
    _, block, width = dy.shape
    rows = block * seq_count
    count = w.shape[0]
    per_chip = 2 * count // line
    small = (8, width)
    hidden_units = gate_back.shape[1]
    part = (2 * share + down_share * width // hidden_units, hidden_units)
    out_shape = [
        jax.ShapeDtypeStruct((2, block, width), F32),
        jax.ShapeDtypeStruct((deep_share, width), F32),
        jax.ShapeDtypeStruct((ar_share, width), F32),
        jax.ShapeDtypeStruct((share, hidden_units), F32),
        jax.ShapeDtypeStruct((share, hidden_units), F32),
        jax.ShapeDtypeStruct((down_share, width), F32),
        jax.ShapeDtypeStruct(small, F32),
    ]
    deep = (deep_share + ar_share, width)
    scratch = [
        pltpu.VMEM((2, rows, width), BF16),
        pltpu.VMEM((2, rows, width), BF16),
        pltpu.VMEM((2, rows, width), F32),
        pltpu.VMEM((2, rows, width), BF16),
        pltpu.VMEM((seq_count - 1, 2, block, width), BF16),
        pltpu.VMEM((2, per_chip, 2, rows, width), BF16),
        pltpu.VMEM(w.shape, BF16),
        pltpu.VMEM(ar.shape, BF16),
        pltpu.VMEM((CORES, line) + deep, BF16),
        pltpu.VMEM((line,) + deep, BF16),
        pltpu.VMEM((2, line - 1) + deep, BF16),
        pltpu.VMEM((CORES, seq_count, line) + part, BF16),
        pltpu.VMEM((seq_count, line) + part, BF16),
        pltpu.VMEM((seq_count - 1, line) + part, BF16),
        pltpu.VMEM((2, line - 1) + part, BF16),
        pltpu.VMEM(small, F32),
        pltpu.VMEM(small, F32),
        pltpu.VMEM((seq_count - 1,) + small, F32),
        pltpu.VMEM(small, F32),
        pltpu.VMEM((line - 1,) + small, F32),
        DMA((3,)),
        DMA((seq_count - 1,)),
        DMA((seq_count - 1,)),
        DMA((seq_count - 1,)),
        DMA((seq_count - 1,)),
        DMA((line,)),
        DMA((line,)),
        DMA((2, line - 1)),
        DMA((2, line - 1)),
        DMA,
        DMA,
        DMA((seq_count - 1,)),
        DMA((seq_count - 1,)),
        DMA((2, line - 1)),
        DMA((2, line - 1)),
        DMA((seq_count + line,)),
        DMA((seq_count + line,)),
    ]
    return pl.pallas_call(
        functools.partial(mix_back_kernel, seq_count, line, spans),
        out_shape=out_shape,
        in_specs=[WHOLE] * 3 + [ANY] * 2 + [WHOLE] * 10,
        out_specs=[WHOLE] * 7,
        scratch_shapes=scratch,
        compiler_params=params(6),
        name="mix_back",
    )(dy, u, table, w, ul.reshape(2 * count, 2, rows, width), ar, x, hg, scale, z, gate_back, up_back, mixed, cot, mlp_grad)


def mix_front_kernel(seq_count, line, spans, *refs):
    (tok_ref, row_ref, gain_ref, spec_hbm, ar_hbm) = refs[:5]
    wide_in = refs[5:8]
    (w_hbm, ul_hbm, u_ref, y_ref, ar_ref, gain_out) = refs[8:14]
    wide_out = refs[14:17]
    (x_all, both, acc, y_bf, y_in, w_buf, ul_buf) = refs[17:24]
    stage = refs[24:27]
    (g_own, g_side, g_sum, g_line, g_all, g_twin) = refs[27:33]
    (load_sem, store_sem, ul_sem, w_sem, ts, tr, ys, yr, zs, zr, hs, hr) = refs[33:45]
    (ps, pr, ws, wr, wps, wpr, gs, gr) = refs[45:]
    s, z, c, g = place(seq_count, line)
    twin = {"grp": g + 1 - 2 * c}
    rows, width = x_all.shape[1], x_all.shape[2]
    block = tok_ref.shape[1]
    n = spec_hbm.shape[0]
    blocks = ul_buf.shape[0]
    count = blocks // 2
    per_chip = blocks // line
    lanes = 128
    wide = range(3)
    mine = pl.ds(pl.multiple_of(s * block, block), block)

    def piece(l):
        return w_buf.at[l, pl.ds(pl.multiple_of(c * n, n), n), :]

    load_w = pltpu.make_async_copy(spec_hbm, piece(z), load_sem.at[0])
    load_ar = pltpu.make_async_copy(ar_hbm, ar_ref.at[z, c], load_sem.at[1])
    loads = [pltpu.make_async_copy(wide_in[i], stage[i], load_sem.at[2 + i]) for i in wide]
    for x in loads + [load_ar, load_w]:
        x.start()
    at = (s * (CORES * line) + g) * (width // (seq_count * CORES * line))
    g_own[...] = pltpu.roll(gain_ref[...], at, 1).astype(BF16)
    greet(seq_count, line, s, z, c, g, twin=True, side=True, whole_line=True)

    gain_sides = []
    toks = []
    for i in range(1, seq_count):
        to = {"seq": lax.rem(s + i, seq_count)}
        gain_sides.append(remote(g_own, g_side.at[i - 1], gs.at[i - 1], gr.at[i - 1], to))
        gain_sides[-1].start()
    for i in range(1, seq_count):
        to = {"seq": lax.rem(s + i, seq_count)}
        toks.append(remote(tok_ref, x_all.at[:, mine, :], ts.at[i - 1], tr.at[i - 1], to))
        toks[-1].start()

    def early_own(i, l):
        return ar_ref.at[l, c] if i == 3 else wide_out[i].at[s, l, c]

    def early_hop(i, way, t, origin):
        if t > 0:
            src = early_own(i, origin)
        else:
            src = ar_hbm if i == 3 else wide_in[i]
        to = g + CORES if way == 0 else g - CORES
        return remote(src, early_own(i, origin), hs.at[i, way, t], hr.at[i, way, t], {"grp": to})

    def deep_hop(way, t, origin):
        to = g + CORES if way == 0 else g - CORES
        return remote(
            piece(origin), piece(origin), zs.at[way, t], zr.at[way, t], {"grp": to}
        )

    def each_hop(way, t, which, origin, act):
        if which == "early":
            for i in range(4):
                act(early_hop(i, way, t, origin))
        else:
            act(deep_hop(way, t, origin))

    def first(which):
        for way in (0, 1):
            sends, _, origin, _ = line_conditions(line, z, way, 0)

            @pl.when(sends)
            def _():
                each_hop(way, 0, which, origin, lambda x: x.start())

    def arrive(which, t, after=None):
        for way in (0, 1):
            _, receives, _, origin = line_conditions(line, z, way, t)

            @pl.when(receives)
            def _():
                each_hop(way, t, which, origin, lambda x: x.wait_recv())
                if t + 1 < line - 1:
                    sends = line_conditions(line, z, way, t + 1)[0]

                    @pl.when(sends)
                    def _():
                        each_hop(way, t + 1, which, origin, lambda x: x.start())

                if after is not None:
                    after(origin)

    def sent(which):
        for t in range(line - 1):
            for way in (0, 1):
                sends, _, origin, _ = line_conditions(line, z, way, t)

                @pl.when(sends)
                def _():
                    each_hop(way, t, which, origin, lambda x: x.wait_send())

    first("early")
    x_all[:, mine, :] = tok_ref[...]
    stores = []
    for i in wide:
        loads[i].wait()
        stores.append(pltpu.make_async_copy(stage[i], wide_out[i].at[s, z, c], store_sem.at[i]))
        stores[-1].start()
    load_ar.wait()
    load_w.wait()

    def twin_deep(l):
        return remote(piece(l), piece(l), ps.at[l], pr.at[l], twin)

    twin_deep(z).start()

    total = g_own[...]
    for i, x in enumerate(gain_sides):
        x.wait_recv()
        total = total + g_side[i]
    g_sum[...] = total
    gain_lines = []
    for j in range(1, line):
        k = seq_count - 2 + j
        to = {"grp": lax.rem(g + CORES * j, CORES * line)}
        gain_lines.append(remote(g_sum, g_line.at[j - 1], gs.at[k], gr.at[k], to))
        gain_lines[-1].start()
    arrive("early", 0)
    first("deep")
    total = g_sum[...]
    for j, x in enumerate(gain_lines):
        x.wait_recv()
        total = total + g_line[j]
    g_all[...] = total
    k = seq_count + line - 2
    gain_twin = remote(g_all, g_twin, gs.at[k], gr.at[k], twin)
    gain_twin.start()
    for x in toks:
        x.wait_recv()
    gain_twin.wait_recv()
    gain = g_all[...].astype(F32) + g_twin[...].astype(F32)
    gain_out[...] = gain[:8]

    signs = signs_of(rows)
    for m in range(2):
        x = x_all[m].astype(F32)
        inv = lax.rsqrt(jnp.mean(x * x, axis=-1, keepdims=True) + EPSILON)
        u = (x * inv * gain[0:1, :]).astype(BF16)
        u_ref[m] = u
        both[m, :, :width] = u
        both[m, :, width:] = (u.astype(F32) * signs).astype(BF16)

    def ul_store(k):
        part = pl.ds(2 * k, 2)
        return pltpu.make_async_copy(ul_buf.at[part], ul_hbm.at[part], ul_sem.at[k])

    def filter_step(k):
        table = spread(row_ref[k], rows)
        for m in range(2):
            span = spans[m]
            for j in range(rows // span):
                part = slice(j * span, (j + 1) * span)
                val = dot_tn(table[:span, :span], both[m, part, :])
                ul_buf[2 * k, m, part, :] = val[:, :width].astype(BF16)
                ul_buf[2 * k + 1, m, part, :] = (val[:, width:] * signs[part]).astype(BF16)
        ul_store(k).start()

    half = count // 2
    pl.loop(0, half)(filter_step)
    if line > 2:
        arrive("early", 1)
    pl.loop(half, count)(filter_step)
    for x in stores:
        x.wait()

    acc[...] = jnp.zeros_like(acc)

    def add_chip(l):
        for m in range(2):
            total = 0.0
            for j in range(per_chip):
                total = total + dot_nn(
                    ul_buf[l * per_chip + j, m], w_buf[l, j * width : (j + 1) * width, :]
                )
            acc[m] += total

    def w_store(l):
        return pltpu.make_async_copy(w_buf.at[l], w_hbm.at[l], w_sem.at[l])

    twin_deep(z).wait_recv()
    w_store(z).start()
    add_chip(z)
    for t in range(2, line - 1):
        arrive("early", t)

    ar_twin = remote(ar_ref.at[:, c], ar_ref.at[:, c], wps.at[3, 0], wpr.at[3, 0], twin)
    ar_twin.start()
    sides = []
    for i in wide:
        for j in range(1, seq_count):
            part = wide_out[i].at[s, :, c]
            to = {"seq": lax.rem(s + j, seq_count)}
            sides.append(remote(part, part, ws.at[i, j - 1], wr.at[i, j - 1], to))
            sides[-1].start()

    def twin_wide(i, k):
        part = wide_out[i].at[k, :, c]
        return remote(part, part, wps.at[i, k], wpr.at[i, k], twin)

    for i in wide:
        twin_wide(i, s).start()

    ar_twin.wait_recv()
    ar_rows = ar_ref.shape[0] * ar_ref.shape[1] * ar_ref.shape[2]
    ar_all = ar_ref[...].reshape(ar_rows, width)
    chunks = ar_rows // lanes
    for i in range(chunks):
        place_at = s * chunks + i
        lag = lax.div(place_at, width // lanes)
        col = lax.rem(place_at, width // lanes)
        cols = pl.ds(pl.multiple_of(col * lanes, lanes), lanes)
        for m in range(2):
            v = lag_by(u_ref[m, :, cols].astype(F32), lag, spans[m], lagged).astype(BF16)
            acc[m] += dot_nn(v, ar_all[i * lanes : (i + 1) * lanes])

    for t in range(line - 1):
        if t == line - 2:
            for x in sides:
                x.wait_recv()
            for i in wide:
                for j in range(1, seq_count):
                    twin_wide(i, lax.rem(s + seq_count - j, seq_count)).start()
        arrive("deep", t, lambda origin: twin_deep(origin).start())
        for way in (0, 1):
            _, receives, _, origin = line_conditions(line, z, way, t)

            @pl.when(receives)
            def _():
                twin_deep(origin).wait_recv()
                w_store(origin).start()
                add_chip(origin)

    y_bf[...] = acc[...].astype(BF16)
    y_copies = []
    for i in range(1, seq_count):
        to = lax.rem(s + i, seq_count)
        y_copies.append(
            remote(
                y_bf.at[:, pl.ds(pl.multiple_of(to * block, block), block), :],
                y_in.at[i - 1],
                ys.at[i - 1],
                yr.at[i - 1],
                {"seq": to},
            )
        )
        y_copies[-1].start()

    sent("early")
    sent("deep")
    for l in range(line):
        twin_deep(l).wait_send()
        w_store(l).wait()
    for i in wide:
        for k in range(seq_count):
            twin_wide(i, k).wait()
    for x in toks + sides + gain_sides + gain_lines + [ar_twin, gain_twin]:
        x.wait_send()
    for k in range(count):
        ul_store(k).wait()
    for m in range(2):
        y_ref[m] = acc[m, mine, :]
    for i, x in enumerate(y_copies):
        x.wait_recv()
        y_ref[...] += y_in[i].astype(F32)
    for x in y_copies:
        x.wait_send()


def mix_front(seq_count, line, spans, tok, table, gain, spec, ar, wide):
    _, block, width = tok.shape
    rows = block * seq_count
    count = table.shape[0]
    small = (16, width)
    out_shape = [
        jax.ShapeDtypeStruct((line, CORES * spec.shape[0], width), BF16),
        jax.ShapeDtypeStruct((2 * count, 2, rows, width), BF16),
        jax.ShapeDtypeStruct((2, rows, width), BF16),
        jax.ShapeDtypeStruct((2, block, width), F32),
        jax.ShapeDtypeStruct((line, CORES) + ar.shape, BF16),
        jax.ShapeDtypeStruct((8, width), F32),
    ] + [jax.ShapeDtypeStruct((seq_count, line, CORES) + x.shape, BF16) for x in wide]
    scratch = [
        pltpu.VMEM((2, rows, width), BF16),
        pltpu.VMEM((2, rows, 2 * width), BF16),
        pltpu.VMEM((2, rows, width), F32),
        pltpu.VMEM((2, rows, width), BF16),
        pltpu.VMEM((seq_count - 1, 2, block, width), BF16),
        pltpu.VMEM((line, CORES * spec.shape[0], width), BF16),
        pltpu.VMEM((2 * count, 2, rows, width), BF16),
    ]
    scratch += [pltpu.VMEM(x.shape, BF16) for x in wide]
    scratch += [
        pltpu.VMEM(small, BF16),
        pltpu.VMEM((seq_count - 1,) + small, BF16),
        pltpu.VMEM(small, BF16),
        pltpu.VMEM((line - 1,) + small, BF16),
        pltpu.VMEM(small, BF16),
        pltpu.VMEM(small, BF16),
        DMA((5,)),
        DMA((3,)),
        DMA((count,)),
        DMA((line,)),
        DMA((seq_count - 1,)),
        DMA((seq_count - 1,)),
        DMA((seq_count - 1,)),
        DMA((seq_count - 1,)),
        DMA((2, line - 1)),
        DMA((2, line - 1)),
        DMA((4, 2, line - 1)),
        DMA((4, 2, line - 1)),
        DMA((line,)),
        DMA((line,)),
        DMA((3, seq_count - 1)),
        DMA((3, seq_count - 1)),
        DMA((4, seq_count)),
        DMA((4, seq_count)),
        DMA((seq_count + line,)),
        DMA((seq_count + line,)),
    ]
    return pl.pallas_call(
        functools.partial(mix_front_kernel, seq_count, line, spans),
        out_shape=out_shape,
        in_specs=[WHOLE] * 3 + [ANY] * 5,
        out_specs=[ANY] * 2 + [WHOLE] * 4 + [ANY] * 3,
        scratch_shapes=scratch,
        compiler_params=params(7),
        name="mix_front",
    )(tok, table, gain, spec, ar, *wide)


def body(
    tokens,
    layout,
    filters,
    gain_mix,
    spectral_proj,
    ar_proj,
    gain_mlp,
    w_gate,
    w_up,
    w_down,
    out_grad,
):
    seq_count = lax.axis_size("seq")
    line = lax.axis_size("grp") // CORES
    s = lax.axis_index("seq")
    g = lax.axis_index("grp")
    block, width = tokens.shape[2], tokens.shape[3]
    rows = block * seq_count
    count = filters.shape[1] // seq_count
    hidden_units = w_gate.shape[1]
    spans = (rows, rows // 4)

    swap = layout[0, 0] == 1
    own = jnp.where(swap, tokens[::-1, 0], tokens[:, 0])
    cotangent = jnp.where(swap, out_grad[::-1, 0], out_grad[:, 0])
    share = gain_mix.shape[0]
    ar_rows = ar_proj.shape[0] * CORES * line
    mine = lax.dynamic_slice(filters.T, (s * count, 0), (count, rows))[:, None, :]
    nothing = jnp.zeros((count, 1, rows), F32)
    back_table = jnp.concatenate([mine, nothing], axis=2)
    aligned = share % 16 == 0 and ar_proj.shape[0] % 16 == 0 and 2 * count % line == 0
    aligned = aligned and ar_rows % 128 == 0

    if aligned:
        gains = jnp.pad(jnp.stack([gain_mix, gain_mlp]), ((0, 14), (0, width - share)))
        spec, ul, u, mixer, ar, gains, gate_w, up_w, down_w = mix_front(
            seq_count,
            line,
            spans,
            own,
            back_table,
            gains.astype(F32),
            spectral_proj,
            ar_proj,
            (w_gate, w_up, w_down),
        )
        mix_scale, mlp_scale = gains[0:1], gains[1:2]
        mixer = mixer.reshape(2 * block, width)
    else:
        gains = jnp.zeros((16, 128), BF16)
        gains = gains.at[0, :share].set(gain_mix).at[1, :share].set(gain_mlp)
        x_all, spec, ar, gate_w, up_w, down_w, gains = gather_all(
            seq_count, line, own, (spectral_proj, ar_proj), (w_gate, w_up, w_down, gains)
        )
        ar_full = lax.dynamic_update_slice(
            jnp.zeros((3 * width, width), BF16), ar.reshape(ar_rows, width), (s * ar_rows, 0)
        )
        gains = gains.reshape(-1, 16, 128).astype(F32)
        mix_scale = gains[:, 0, :share].reshape(1, width)
        mlp_scale = gains[:, 1, :share].reshape(1, width)
        fore_table = jnp.concatenate([mine[:, :, :1], nothing, mine[:, :, :0:-1]], axis=2)
        split = spec.reshape(count, 2, width, width)
        ul, u, y = forward_mix(spans, x_all, mix_scale, fore_table, split, ar_full)
        mixer = side_sum(seq_count, line, y, 3).reshape(2 * block, width)
    spec = spec.reshape(count, 2, width, width)
    gate_w = gate_w.reshape(width, hidden_units)
    up_w = up_w.reshape(width, hidden_units)
    down_w = down_w.reshape(hidden_units, width)

    inputs = own.reshape(2 * block, width).astype(F32)
    cot = cotangent.reshape(2 * block, width)
    hidden = inputs + mixer
    inv_two = lax.rsqrt(jnp.mean(hidden * hidden, axis=-1, keepdims=True) + EPSILON)
    mlp_in = (hidden * inv_two * mlp_scale).astype(BF16)
    gate = dot_nn(mlp_in, gate_w)
    upval = dot_nn(mlp_in, up_w)
    product_val, gelu_pull = jax.vjp(lambda a, b: jax.nn.gelu(a) * b, gate, upval)
    mixed = product_val.astype(BF16)
    out = hidden + dot_nn(mixed, down_w)
    mixed_grad = dot_nt(cot, down_w)
    gate_back, up_back = gelu_pull(mixed_grad)
    gate_back = gate_back.astype(BF16)
    up_back = up_back.astype(BF16)
    mlp_in_grad = dot_nt(gate_back, gate_w) + dot_nt(up_back, up_w)
    scaled_two = mlp_in_grad * mlp_scale
    mlp_grad = jnp.sum(mlp_in_grad * hidden * inv_two, axis=0, keepdims=True)
    hidden_grad = (
        cot.astype(F32)
        + inv_two * scaled_two
        - hidden * inv_two**3 * jnp.mean(scaled_two * hidden, axis=-1, keepdims=True)
    )
    mixer_grad = hidden_grad.astype(BF16)

    if aligned:
        input_grad, dw, dar, gate_grad, up_grad, down_grad, small = mix_back(
            seq_count,
            line,
            spans,
            mixer_grad.reshape(2, block, width),
            u,
            back_table,
            spec,
            ul,
            ar.reshape(ar_rows, width),
            own,
            hidden_grad.reshape(2, block, width),
            mix_scale,
            (mlp_in, gate_back, up_back, mixed, cot),
            mlp_grad,
            (share, w_down.shape[0], spectral_proj.shape[0], ar_proj.shape[0]),
        )
    else:
        down_grad = dot_tn(mixed, cot)
        gate_grad = dot_tn(mlp_in, gate_back)
        up_grad = dot_tn(mlp_in, up_back)
        dy = side_gather(seq_count, line, mixer_grad.reshape(2, block, width))
        dw, dar, du = backward_mix(spans, dy, u, back_table, spec, ul, ar_full)
        normed_grad = side_sum(seq_count, line, du, 4).reshape(2 * block, width)

        inv_one = lax.rsqrt(jnp.mean(inputs * inputs, axis=-1, keepdims=True) + EPSILON)
        scaled_one = normed_grad * mix_scale
        mix_grad = jnp.sum(normed_grad * inputs * inv_one, axis=0, keepdims=True)
        input_grad = (
            hidden_grad
            + inv_one * scaled_one
            - inputs * inv_one**3 * jnp.mean(scaled_one * inputs, axis=-1, keepdims=True)
        )

        dar = lax.dynamic_slice(dar, (s * ar_rows, 0), (ar_rows, width))
        deep = (dw.reshape(line, CORES, -1, width), dar.reshape(line, CORES, -1, width))
        wide = tuple(
            x.astype(BF16).reshape(seq_count, line, CORES, -1, x.shape[1])
            for x in (gate_grad, up_grad, down_grad)
        )
        small = jnp.concatenate([mix_grad, mlp_grad, jnp.zeros((6, width), F32)], axis=0)
        dw, dar, gate_grad, up_grad, down_grad, small = sum_all(seq_count, line, deep, wide, small)
    small = lax.dynamic_slice(small, (0, (s * CORES * line + g) * share), (2, share))

    def settle(x):
        x = x.reshape(2, 1, block, width)
        return jnp.where(swap, x[::-1], x)

    return (
        settle(out),
        settle(input_grad),
        small[0],
        dw,
        dar,
        small[1],
        gate_grad,
        up_grad,
        down_grad,
    )


def solution(mesh):
    placed = (
        P(None, "grp", "seq", None),
        P(None, "grp"),
        P(),
        P(("seq", "grp")),
        P(("seq", "grp"), None),
        P(("seq", "grp"), None),
        P(("seq", "grp")),
        P(("seq", "grp"), None),
        P(("seq", "grp"), None),
        P(("seq", "grp"), None),
        P(None, "grp", "seq", None),
    )
    return jax.shard_map(
        body,
        mesh=mesh,
        in_specs=placed,
        out_specs=(
            P(None, "grp", "seq", None),
            P(None, "grp", "seq", None),
            P(("seq", "grp")),
            P(("seq", "grp"), None),
            P(("seq", "grp"), None),
            P(("seq", "grp")),
            P(("seq", "grp"), None),
            P(("seq", "grp"), None),
            P(("seq", "grp"), None),
        ),
        check_vma=False,
    )
```

```python
import functools

import jax
import jax.numpy as jnp
from jax import lax
from jax.experimental import pallas as pl
from jax.experimental.pallas import tpu as pltpu
from jax.sharding import PartitionSpec as P

EPSILON = 1e-05
BF16 = jnp.bfloat16
F32 = jnp.float32
MESH = pl.DeviceIdType.MESH
DMA = pltpu.SemaphoreType.DMA
ANY = pl.BlockSpec(memory_space=pl.ANY)
WHOLE = pl.BlockSpec(memory_space=pltpu.VMEM)
VMEM_LIMIT = 60 * 1024 * 1024
CORES = 2


def dot_nn(a, b):
    return lax.dot_general(a, b, (((1,), (0,)), ((), ())), preferred_element_type=F32)


def dot_tn(a, b):
    return lax.dot_general(a, b, (((0,), (0,)), ((), ())), preferred_element_type=F32)


def dot_nt(a, b):
    return lax.dot_general(a, b, (((1,), (1,)), ((), ())), preferred_element_type=F32)


def params(collective_id=None):
    return pltpu.CompilerParams(
        collective_id=collective_id,
        has_side_effects=collective_id is not None,
        vmem_limit_bytes=VMEM_LIMIT,
    )


def remote(src, dst, send, recv, where):
    return pltpu.make_async_remote_copy(
        src_ref=src, dst_ref=dst, send_sem=send, recv_sem=recv, device_id=where, device_id_type=MESH
    )


def place(seq_count, line):
    s = lax.axis_index("seq")
    g = lax.axis_index("grp")
    return s, lax.div(g, CORES), lax.rem(g, CORES), g


def greet(seq_count, line, s, z, c, g, chain=False, twin=False, side=False, whole_line=False):
    barrier = pltpu.get_barrier_semaphore()

    def call(where):
        pl.semaphore_signal(barrier, inc=1, device_id=where, device_id_type=MESH)

    expected = (1 if twin else 0) + (seq_count - 1 if side else 0) + (line - 1 if whole_line else 0)
    if twin:
        call({"grp": g + 1 - 2 * c})
    if side:
        for i in range(1, seq_count):
            call({"seq": lax.rem(s + i, seq_count)})
    if whole_line:
        for j in range(1, line):
            call({"grp": lax.rem(g + CORES * j, CORES * line)})
    if chain:
        expected = expected + (z > 0).astype(jnp.int32) + (z < line - 1).astype(jnp.int32)

        @pl.when(z > 0)
        def _():
            call({"grp": g - CORES})

        @pl.when(z < line - 1)
        def _():
            call({"grp": g + CORES})

    pl.semaphore_wait(barrier, expected)


def line_conditions(line, z, way, t):
    if way == 0:
        return (z < line - 1) & (z >= t), z >= t + 1, z - t, z - 1 - t
    return (z > 0) & (z + t <= line - 1), z + t + 1 <= line - 1, z + t, z + 1 + t


def gather_kernel(seq_count, line, n_deep, n_wide, *refs):
    n_in = 1 + n_deep + n_wide
    ins, outs = refs[:n_in], refs[n_in : 2 * n_in]
    rest = refs[2 * n_in :]
    stage = rest[:n_in]
    (local_sem, tok_send, tok_recv, zs, zr, ws, wr, ps, pr, dps, dpr) = rest[n_in:]
    s, z, c, g = place(seq_count, line)
    twin = {"grp": g + 1 - 2 * c}
    tok, tok_out = ins[0], outs[0]
    rows = tok.shape[1]
    items = list(range(n_deep + n_wide))

    def own(i, l):
        out = outs[1 + i]
        return out.at[l, c] if i < n_deep else out.at[s, l, c]

    loads = [pltpu.make_async_copy(ins[i], stage[i], local_sem.at[0, i]) for i in range(n_in)]
    for x in loads:
        x.start()
    greet(seq_count, line, s, z, c, g, chain=True, twin=True, side=True)

    toks = []
    for i in range(1, seq_count):
        toks.append(
            remote(
                tok,
                tok_out.at[:, pl.ds(pl.multiple_of(s * rows, rows), rows), :],
                tok_send.at[i - 1],
                tok_recv.at[i - 1],
                {"seq": lax.rem(s + i, seq_count)},
            )
        )
        toks[-1].start()

    def hop(i, way, t, origin):
        src = ins[1 + i] if t == 0 else own(i, origin)
        to = g + CORES if way == 0 else g - CORES
        return remote(src, own(i, origin), zs.at[i, way, t], zr.at[i, way, t], {"grp": to})

    def hops(which, t):
        for way in (0, 1):
            sends, _, origin, _ = line_conditions(line, z, way, t)

            @pl.when(sends)
            def _():
                for i in which:
                    hop(i, way, t, origin).start()

    def arrive(which, t, after=None):
        for way in (0, 1):
            _, receives, _, origin = line_conditions(line, z, way, t)

            @pl.when(receives)
            def _():
                for i in which:
                    hop(i, way, t, origin).wait_recv()
                if after is not None:
                    after(origin)

    deep, wide = items[:n_deep], items[n_deep:]
    for t in range(line - 1):
        hops(wide, t)
        if t == 0:
            stores = []
            for i in range(n_in):
                loads[i].wait()
                dst = (
                    tok_out.at[:, pl.ds(pl.multiple_of(s * rows, rows), rows), :]
                    if i == 0
                    else own(i - 1, z)
                )
                stores.append(pltpu.make_async_copy(stage[i], dst, local_sem.at[1, i]))
                stores[-1].start()
        arrive(wide, t)
    hops(deep, 0)
    for x in stores:
        x.wait()
    sides = []
    for i in wide:
        for j in range(1, seq_count):
            part = outs[1 + i].at[s, :, c]
            sides.append(
                remote(
                    part,
                    part,
                    ws.at[i - n_deep, j - 1],
                    wr.at[i - n_deep, j - 1],
                    {"seq": lax.rem(s + j, seq_count)},
                )
            )
            sides[-1].start()

    def twin_wide(i, k):
        part = outs[1 + i].at[k, :, c]
        return remote(part, part, ps.at[i - n_deep, k], pr.at[i - n_deep, k], twin)

    def twin_deep(i, l):
        part = outs[1 + i].at[l, c]
        return remote(part, part, dps.at[i, l], dpr.at[i, l], twin)

    for i in wide:
        twin_wide(i, s).start()
    for i in deep:
        twin_deep(i, z).start()

    def pass_on(origin):
        for i in deep:
            twin_deep(i, origin).start()

    for t in range(line - 1):
        if t > 0:
            hops(deep, t)
        arrive(deep, t, pass_on)
    for x in sides:
        x.wait_recv()
    for i in wide:
        for j in range(1, seq_count):
            twin_wide(i, lax.rem(s + seq_count - j, seq_count)).start()
    for x in toks:
        x.wait_recv()
    for i in deep:
        for l in range(line):
            twin_deep(i, l).wait()
    for i in wide:
        for k in range(seq_count):
            twin_wide(i, k).wait()
    for x in toks + sides:
        x.wait_send()
    for t in range(line - 1):
        for way in (0, 1):
            sends, _, origin, _ = line_conditions(line, z, way, t)

            @pl.when(sends)
            def _():
                for i in items:
                    hop(i, way, t, origin).wait_send()


def gather_all(seq_count, line, tok, deep, wide):
    n_deep, n_wide = len(deep), len(wide)
    shapes = [
        jax.ShapeDtypeStruct((tok.shape[0], tok.shape[1] * seq_count, tok.shape[2]), tok.dtype)
    ]
    shapes += [jax.ShapeDtypeStruct((line, CORES) + x.shape, x.dtype) for x in deep]
    shapes += [jax.ShapeDtypeStruct((seq_count, line, CORES) + x.shape, x.dtype) for x in wide]
    arrays = [tok] + list(deep) + list(wide)
    n = len(arrays)
    scratch = [pltpu.VMEM(x.shape, x.dtype) for x in arrays]
    scratch += [
        DMA((2, n)),
        DMA((seq_count - 1,)),
        DMA((seq_count - 1,)),
        DMA((n_deep + n_wide, 2, line - 1)),
        DMA((n_deep + n_wide, 2, line - 1)),
        DMA((n_wide, seq_count - 1)),
        DMA((n_wide, seq_count - 1)),
        DMA((n_wide, seq_count)),
        DMA((n_wide, seq_count)),
        DMA((n_deep, line)),
        DMA((n_deep, line)),
    ]
    return pl.pallas_call(
        functools.partial(gather_kernel, seq_count, line, n_deep, n_wide),
        out_shape=shapes,
        in_specs=[ANY] * n,
        out_specs=[ANY] * n,
        scratch_shapes=scratch,
        compiler_params=params(1),
        name="gather_all",
    )(*arrays)


def side_gather_kernel(seq_count, line, x_ref, out_ref, local_sem, send, recv):
    s, z, c, g = place(seq_count, line)
    rows = x_ref.shape[1]
    mine = out_ref.at[:, pl.ds(pl.multiple_of(s * rows, rows), rows), :]
    local = pltpu.make_async_copy(x_ref, mine, local_sem)
    local.start()
    greet(seq_count, line, s, z, c, g, side=True)
    copies = []
    for i in range(1, seq_count):
        copies.append(
            remote(
                x_ref, mine, send.at[i - 1], recv.at[i - 1], {"seq": lax.rem(s + i, seq_count)}
            )
        )
        copies[-1].start()
    local.wait()
    for x in copies:
        x.wait()


def side_gather(seq_count, line, x):
    return pl.pallas_call(
        functools.partial(side_gather_kernel, seq_count, line),
        out_shape=jax.ShapeDtypeStruct((x.shape[0], x.shape[1] * seq_count, x.shape[2]), x.dtype),
        in_specs=[WHOLE],
        out_specs=WHOLE,
        scratch_shapes=[DMA, DMA((seq_count - 1,)), DMA((seq_count - 1,))],
        compiler_params=params(2),
        name="side_gather",
    )(x)


def side_sum_kernel(seq_count, line, x_ref, out_ref, slots, send, recv):
    s, z, c, g = place(seq_count, line)
    rows = out_ref.shape[1]
    greet(seq_count, line, s, z, c, g, side=True)
    copies = []
    for i in range(1, seq_count):
        to = lax.rem(s + i, seq_count)
        copies.append(
            remote(
                x_ref.at[:, pl.ds(pl.multiple_of(to * rows, rows), rows), :],
                slots.at[i - 1],
                send.at[i - 1],
                recv.at[i - 1],
                {"seq": to},
            )
        )
        copies[-1].start()
    total = x_ref[:, pl.ds(pl.multiple_of(s * rows, rows), rows), :].astype(F32)
    for i, x in enumerate(copies):
        x.wait_recv()
        total = total + slots[i].astype(F32)
    out_ref[...] = total
    for x in copies:
        x.wait_send()


def side_sum(seq_count, line, x, collective_id):
    rows = x.shape[1] // seq_count
    return pl.pallas_call(
        functools.partial(side_sum_kernel, seq_count, line),
        out_shape=jax.ShapeDtypeStruct((x.shape[0], rows, x.shape[2]), F32),
        in_specs=[WHOLE],
        out_specs=WHOLE,
        scratch_shapes=[
            pltpu.VMEM((seq_count - 1, x.shape[0], rows, x.shape[2]), x.dtype),
            DMA((seq_count - 1,)),
            DMA((seq_count - 1,)),
        ],
        compiler_params=params(collective_id),
        name=f"side_sum_{collective_id}",
    )(x)


def sum_kernel(seq_count, line, n_deep, n_wide, *refs):
    n = n_deep + n_wide
    ins, outs = refs[: n + 1], refs[n + 1 : 2 * n + 2]
    rest = refs[2 * n + 2 :]
    pair, side, chain = rest[:n], rest[n : n + n_wide], rest[n + n_wide : 2 * n + n_wide]
    rest = rest[2 * n + n_wide :]
    g_pair, g_side, g_line, g_a, g_b = rest[:5]
    (ps, pr, ws, wr, zs, zr, gs, gr) = rest[5:]
    s, z, c, g = place(seq_count, line)
    twin = {"grp": g + 1 - 2 * c}
    deep, wide = list(range(n_deep)), list(range(n_deep, n))
    small = ins[n]
    greet(seq_count, line, s, z, c, g, twin=True, side=True, whole_line=True)

    def theirs(i):
        return ins[i].at[:, 1 - c] if i < n_deep else ins[i].at[:, :, 1 - c]

    pairs = [remote(theirs(i), pair[i], ps.at[i], pr.at[i], twin) for i in range(n)]
    small_pair = remote(small, g_pair, gs.at[0], gr.at[0], twin)
    small_pair.start()
    for x in pairs[n_deep:] + pairs[:n_deep]:
        x.start()

    small_pair.wait()
    g_a[...] = small[...] + g_pair[...]
    small_sides = []
    for j in range(1, seq_count):
        small_sides.append(
            remote(
                g_a,
                g_side.at[j - 1],
                gs.at[j],
                gr.at[j],
                {"seq": lax.rem(s + j, seq_count)},
            )
        )
        small_sides[-1].start()

    for i in wide:
        pairs[i].wait_recv()
        for k in range(seq_count):

            @pl.loop(0, line)
            def _(l):
                mixed = ins[i][k, l, c].astype(F32) + pair[i][k, l].astype(F32)
                pair[i][k, l] = mixed.astype(BF16)

    sides = {}
    for i in wide:
        for j in range(1, seq_count):
            to = lax.rem(s + j, seq_count)
            sides[i, j] = remote(
                pair[i].at[to],
                side[i - n_deep].at[j - 1],
                ws.at[i - n_deep, j - 1],
                wr.at[i - n_deep, j - 1],
                {"seq": to},
            )
            sides[i, j].start()
    for i in deep:
        pairs[i].wait_recv()
        for l in range(line):
            pair[i][l] = (ins[i][l, c].astype(F32) + pair[i][l].astype(F32)).astype(BF16)

    for x in small_sides:
        x.wait()
    total = g_a[...]
    for j in range(seq_count - 1):
        total = total + g_side[j]
    g_b[...] = total
    small_lines = []
    for j in range(1, line):
        small_lines.append(
            remote(
                g_b,
                g_line.at[j - 1],
                gs.at[seq_count - 1 + j],
                gr.at[seq_count - 1 + j],
                {"grp": lax.rem(g + CORES * j, CORES * line)},
            )
        )
        small_lines[-1].start()

    def piece(i, l):
        return pair[i].at[l] if i < n_deep else pair[i].at[s, l]

    def run_line(which):
        def hop(i, way, t, dest, first):
            src = piece(i, dest) if first else chain[i].at[way, t]
            to = g + CORES if way == 0 else g - CORES
            return remote(src, chain[i].at[way, t], zs.at[i, way, t], zr.at[i, way, t], {"grp": to})

        for t in range(line - 1):
            for way in (0, 1):
                dest = line - 1 - t if way == 0 else t
                starts = z == 0 if way == 0 else z == line - 1
                relays = (z > 0) & (z < dest) if way == 0 else (z < line - 1) & (z > dest)

                @pl.when(starts)
                def _():
                    for i in which:
                        hop(i, way, t, dest, True).start()

                @pl.when(relays)
                def _():
                    for i in which:
                        hop(i, way, t, dest, False).wait_recv()
                        mixed = chain[i][way, t].astype(F32) + piece(i, dest)[...].astype(F32)
                        chain[i][way, t] = mixed.astype(BF16)
                        hop(i, way, t, dest, False).start()

        for i in which:
            outs[i][...] = piece(i, z)[...].astype(F32)
        for t in range(line - 1):
            for way in (0, 1):
                dest = line - 1 - t if way == 0 else t

                @pl.when((z == dest))
                def _():
                    for i in which:
                        hop(i, way, t, dest, False).wait_recv()
                        outs[i][...] += chain[i][way, t].astype(F32)

                @pl.when(z == 0 if way == 0 else z == line - 1)
                def _():
                    for i in which:
                        hop(i, way, t, dest, True).wait_send()

                @pl.when((z > 0) & (z < dest) if way == 0 else (z < line - 1) & (z > dest))
                def _():
                    for i in which:
                        hop(i, way, t, dest, False).wait_send()

    run_line(deep)
    for i in wide:
        for j in range(1, seq_count):
            sides[i, j].wait()

        @pl.loop(0, line)
        def _(l):
            mixed = pair[i][s, l].astype(F32)
            for j in range(1, seq_count):
                mixed = mixed + side[i - n_deep][j - 1, l].astype(F32)
            pair[i][s, l] = mixed.astype(BF16)

    run_line(wide)
    for x in pairs:
        x.wait_send()
    for x in small_lines:
        x.wait()
    total = g_b[...]
    for j in range(line - 1):
        total = total + g_line[j]
    outs[n][...] = total


def sum_all(seq_count, line, deep, wide, small):
    n_deep, n_wide = len(deep), len(wide)
    n = n_deep + n_wide
    shapes = [jax.ShapeDtypeStruct(x.shape[2:], F32) for x in deep]
    shapes += [jax.ShapeDtypeStruct(x.shape[3:], F32) for x in wide]
    shapes += [jax.ShapeDtypeStruct(small.shape, F32)]
    scratch = [pltpu.VMEM((line,) + x.shape[2:], BF16) for x in deep]
    scratch += [pltpu.VMEM((seq_count, line) + x.shape[3:], BF16) for x in wide]
    scratch += [pltpu.VMEM((seq_count - 1, line) + x.shape[3:], BF16) for x in wide]
    scratch += [pltpu.VMEM((2, line - 1) + x.shape[2:], BF16) for x in deep]
    scratch += [pltpu.VMEM((2, line - 1) + x.shape[3:], BF16) for x in wide]
    scratch += [
        pltpu.VMEM(small.shape, F32),
        pltpu.VMEM((seq_count - 1,) + small.shape, F32),
        pltpu.VMEM((line - 1,) + small.shape, F32),
        pltpu.VMEM(small.shape, F32),
        pltpu.VMEM(small.shape, F32),
        DMA((n,)),
        DMA((n,)),
        DMA((n_wide, seq_count - 1)),
        DMA((n_wide, seq_count - 1)),
        DMA((n, 2, line - 1)),
        DMA((n, 2, line - 1)),
        DMA((seq_count + line,)),
        DMA((seq_count + line,)),
    ]
    return pl.pallas_call(
        functools.partial(sum_kernel, seq_count, line, n_deep, n_wide),
        out_shape=shapes,
        in_specs=[WHOLE] * (n + 1),
        out_specs=[WHOLE] * (n + 1),
        scratch_shapes=scratch,
        compiler_params=params(5),
        name="sum_all",
    )(*deep, *wide, small)


def signs_of(rows):
    pos = lax.broadcasted_iota(jnp.int32, (rows, 1), 0)
    return 1.0 - 2.0 * lax.rem(pos, 2).astype(F32)


def lagged(values, lag, span):
    pos = lax.broadcasted_iota(jnp.int32, (values.shape[0], 1), 0)
    return jnp.where(lax.rem(pos, span) >= lag, pltpu.roll(values, lag, 0), 0.0)


def led(values, lag, span):
    rows = values.shape[0]
    pos = lax.broadcasted_iota(jnp.int32, (rows, 1), 0)
    return jnp.where(lax.rem(pos, span) < span - lag, pltpu.roll(values, rows - lag, 0), 0.0)


def spread(row, rows):
    wide = jnp.broadcast_to(row, (rows, row.shape[1]))
    return pltpu.roll(wide, 0, 1, stride=1, stride_axis=0)[:, :rows].astype(BF16)


def forward_kernel(spans, x_ref, gain_ref, row_ref, w_ref, ar_ref, ul_ref, u_ref, y_ref, both, acc):
    k = pl.program_id(0)
    rows, width = x_ref.shape[1], x_ref.shape[2]
    signs = signs_of(rows)

    @pl.when(k == 0)
    def _():
        for m in range(2):
            x = x_ref[m].astype(F32)
            inv = lax.rsqrt(jnp.mean(x * x, axis=-1, keepdims=True) + EPSILON)
            u = (x * inv * gain_ref[...]).astype(BF16)
            wide = u.astype(F32)
            u_ref[m] = u
            both[m, :, :width] = u
            both[m, :, width:] = (wide * signs).astype(BF16)
            acc[m] = dot_nn(u, ar_ref[:width])
            for lag in (1, 2):
                acc[m] += dot_nn(
                    lagged(wide, lag, spans[m]).astype(BF16),
                    ar_ref[lag * width : (lag + 1) * width],
                )

    table = spread(row_ref[0], rows)
    for m in range(2):
        span = spans[m]
        for j in range(rows // span):
            part = slice(j * span, (j + 1) * span)
            conv = dot_nn(table[:span, :span], both[m, part, :])
            plus = conv[:, :width].astype(BF16)
            minus = (conv[:, width:] * signs[part]).astype(BF16)
            ul_ref[0, 0, m, part, :] = plus
            ul_ref[0, 1, m, part, :] = minus
        acc[m] += dot_nn(ul_ref[0, 0, m], w_ref[0, 0]) + dot_nn(ul_ref[0, 1, m], w_ref[0, 1])

    @pl.when(k == pl.num_programs(0) - 1)
    def _():
        y_ref[...] = acc[...].astype(BF16)


def forward_mix(spans, x, gain, table, w, ar):
    count = table.shape[0]
    _, rows, width = x.shape
    full = lambda *shape: pl.BlockSpec(shape, lambda k: (0,) * len(shape))
    return pl.pallas_call(
        functools.partial(forward_kernel, spans),
        grid=(count,),
        out_shape=[
            jax.ShapeDtypeStruct((count, 2, 2, rows, width), BF16),
            jax.ShapeDtypeStruct((2, rows, width), BF16),
            jax.ShapeDtypeStruct((2, rows, width), BF16),
        ],
        in_specs=[
            full(2, rows, width),
            full(1, width),
            pl.BlockSpec((1, 1, 2 * rows), lambda k: (k, 0, 0)),
            pl.BlockSpec((1, 2, width, width), lambda k: (k, 0, 0, 0)),
            full(3 * width, width),
        ],
        out_specs=[
            pl.BlockSpec((1, 2, 2, rows, width), lambda k: (k, 0, 0, 0, 0)),
            full(2, rows, width),
            full(2, rows, width),
        ],
        scratch_shapes=[pltpu.VMEM((2, rows, 2 * width), BF16), pltpu.VMEM((2, rows, width), F32)],
        compiler_params=params(),
        name="forward_mix",
    )(x, gain, table, w, ar)


def backward_kernel(
    spans, dy_ref, u_ref, row_ref, w_ref, ul_ref, ar_ref, dw_ref, dar_ref, du_ref, both, acc
):
    k = pl.program_id(0)
    rows, width = dy_ref.shape[1], dy_ref.shape[2]
    signs = signs_of(rows)

    @pl.when(k == 0)
    def _():
        for m in range(2):
            dy = dy_ref[m]
            both[m, :, :width] = dy
            both[m, :, width:] = (dy.astype(F32) * signs).astype(BF16)
            acc[m] = dot_nt(dy, ar_ref[:width])
            for lag in (1, 2):
                acc[m] += led(
                    dot_nt(dy, ar_ref[lag * width : (lag + 1) * width]), lag, spans[m]
                )
        for lag in (0, 1, 2):
            total = 0.0
            for m in range(2):
                u = u_ref[m]
                if lag:
                    u = lagged(u.astype(F32), lag, spans[m]).astype(BF16)
                total = total + dot_tn(u, dy_ref[m])
            dar_ref[lag * width : (lag + 1) * width, :] = total.astype(BF16)

    table = spread(row_ref[0], rows)
    for m in range(2):
        span = spans[m]
        for j in range(rows // span):
            part = slice(j * span, (j + 1) * span)
            conv = dot_nn(table[:span, :span], both[m, part, :])
            plus = conv[:, :width].astype(BF16)
            minus = (conv[:, width:] * signs[part]).astype(BF16)
            acc[m, part, :] += dot_nt(plus, w_ref[0, 0]) + dot_nt(minus, w_ref[0, 1])
    for p in range(2):
        total = dot_tn(ul_ref[0, p, 0], dy_ref[0]) + dot_tn(ul_ref[0, p, 1], dy_ref[1])
        dw_ref[0, p] = total.astype(BF16)

    @pl.when(k == pl.num_programs(0) - 1)
    def _():
        du_ref[...] = acc[...].astype(BF16)


def backward_mix(spans, dy, u, table, w, ul, ar):
    count = table.shape[0]
    _, rows, width = dy.shape
    full = lambda *shape: pl.BlockSpec(shape, lambda k: (0,) * len(shape))
    return pl.pallas_call(
        functools.partial(backward_kernel, spans),
        grid=(count,),
        out_shape=[
            jax.ShapeDtypeStruct((count, 2, width, width), BF16),
            jax.ShapeDtypeStruct((3 * width, width), BF16),
            jax.ShapeDtypeStruct((2, rows, width), BF16),
        ],
        in_specs=[
            full(2, rows, width),
            full(2, rows, width),
            pl.BlockSpec((1, 1, 2 * rows), lambda k: (k, 0, 0)),
            pl.BlockSpec((1, 2, width, width), lambda k: (k, 0, 0, 0)),
            pl.BlockSpec((1, 2, 2, rows, width), lambda k: (k, 0, 0, 0, 0)),
            full(3 * width, width),
        ],
        out_specs=[
            pl.BlockSpec((1, 2, width, width), lambda k: (k, 0, 0, 0)),
            full(3 * width, width),
            full(2, rows, width),
        ],
        scratch_shapes=[pltpu.VMEM((2, rows, 2 * width), BF16), pltpu.VMEM((2, rows, width), F32)],
        compiler_params=params(),
        name="backward_mix",
    )(dy, u, table, w, ul, ar)


def mix_back_kernel(seq_count, line, *refs):
    (layout_ref, dy, u_ref, row_ref, w_hbm, ul_hbm, ar_ref, x_ref, hg_ref, scale_ref) = refs[:10]
    (z_ref, gb_ref, ub_ref, mixed_ref, cot_ref, mlp_ref) = refs[10:16]
    (tg_ref, dw_ref, dar_ref, gg_ref, ug_ref, dg_ref, small_ref) = refs[16:23]
    (keep, dsig, acc, conv, du_in, ul_buf, w_buf, dar) = refs[23:31]
    (deep, deep_in, deep_run, wide, wide_in, wide_side, wide_run) = refs[31:38]
    (g_own, g_pair, g_side, g_sum, g_line) = refs[38:43]
    (load_sem, dus, dur, ps, pr, zs, zr, wps, wpr, ws, wr, wzs, wzr, gs, gr) = refs[43:]
    s, z, c, g = place(seq_count, line)
    twin = {"grp": g + 1 - 2 * c}
    rows, width = dy.shape[1], dy.shape[2]
    block = x_ref.shape[1]
    short = [layout_ref[m, 0].astype(F32) for m in range(2)]
    count = w_hbm.shape[0]
    per_chip = 2 * count // line
    n = per_chip * width // CORES
    ar_rows = ar_ref.shape[0]
    ar_share = ar_rows // (line * CORES)
    lanes = 128
    ar_chunks = ar_rows // lanes
    share = gg_ref.shape[0]
    mine = pl.ds(pl.multiple_of(s * block, block), block)
    low = (z < line // 2).astype(jnp.int32)

    def dest(i):
        return low * (line - 1 - 2 * i) + i

    def load(i):
        return pltpu.make_async_copy(
            ul_hbm.at[pl.ds(dest(i) * per_chip, per_chip)], ul_buf.at[i % 2], load_sem.at[i % 2]
        )

    load_w = pltpu.make_async_copy(w_hbm, w_buf, load_sem.at[2])
    load(0).start()
    if line > 1:
        load(1).start()
    load_w.start()
    greet(seq_count, line, s, z, c, g, twin=True, side=True, whole_line=True)

    def ar_place(i):
        at = s * ar_chunks + i
        lag = lax.div(at, width // lanes)
        col = lax.rem(at, width // lanes)
        return lag, pl.ds(pl.multiple_of(col * lanes, lanes), lanes)

    for i in range(ar_chunks):
        lag, cols = ar_place(i)
        total = 0.0
        for m in range(2):
            v = lagged_by(u_ref[m, :, cols].astype(F32), lag, short[m]).astype(BF16)
            total = total + dot_tn(v, dy[m])
        dar[i * lanes : (i + 1) * lanes, :] = total.astype(BF16)
    for l in range(line):
        for cc in range(CORES):
            r = (l * CORES + cc) * ar_share
            deep[cc, l, n:, :] = dar[r : r + ar_share, :]

    def twin_deep(i):
        l = dest(i)
        return remote(deep.at[1 - c, l], deep_in.at[l], ps.at[i], pr.at[i], twin)

    def hop(run, own, send, recv, way, t, first):
        target = line - 1 - t if way == 0 else t
        src = own(target) if first else run.at[way, t]
        to = g + CORES if way == 0 else g - CORES
        return remote(src, run.at[way, t], send.at[way, t], recv.at[way, t], {"grp": to})

    def deep_own(l):
        return deep_in.at[l]

    def wide_own(l):
        return wide_in.at[s, l]

    deep_line = (deep_run, deep_own, zs, zr)
    wide_line = (wide_run, wide_own, wzs, wzr)

    def begin(kind, t):
        for way in (0, 1):

            @pl.when(z == 0 if way == 0 else z == line - 1)
            def _():
                hop(*kind, way, t, True).start()

    def relay(kind, phase):
        run, own = kind[0], kind[1]
        for way in (0, 1):
            for t in range(phase):
                at = phase - t if way == 0 else line - 1 - (phase - t)
                target = line - 1 - t if way == 0 else t

                @pl.when(z == at)
                def _():
                    hop(*kind, way, t, False).wait_recv()
                    mixed = run[way, t].astype(F32) + own(target)[...].astype(F32)
                    run[way, t] = mixed.astype(BF16)
                    hop(*kind, way, t, False).start()

    def compute(i):
        l = dest(i)
        load(i).wait()
        for j in range(per_chip):
            val = dot_tn(ul_buf[i % 2, j, 0], dy[0]) + dot_tn(ul_buf[i % 2, j, 1], dy[1])
            val = val.astype(BF16)
            for cc in range(CORES):
                lo, hi = max(j * width, cc * n), min((j + 1) * width, (cc + 1) * n)
                if lo < hi:
                    deep[cc, l, lo - cc * n : hi - cc * n, :] = val[lo - j * width : hi - j * width]
        twin_deep(i).start()
        if i + 2 < line:
            load(i + 2).start()

    def combine(i):
        l = dest(i)
        twin_deep(i).wait_recv()
        deep_in[l] = (deep[c, l].astype(F32) + deep_in[l].astype(F32)).astype(BF16)
        if i < line - 1:
            begin(deep_line, i)

    compute(0)
    compute(1)
    combine(0)

    span_f = gb_ref.shape[1] // seq_count
    down_share = dg_ref.shape[0]

    @pl.loop(0, seq_count)
    def _(j):
        part = pl.ds(pl.multiple_of(j * span_f, span_f), span_f)
        for which, back in ((0, gb_ref), (1, ub_ref)):
            val = dot_tn(z_ref[...], back[:, part]).astype(BF16)
            for k in range(seq_count):
                for l in range(line):
                    for cc in range(CORES):
                        r = ((k * line + l) * CORES + cc) * share
                        wide[cc, k, l, which * share : (which + 1) * share, part] = val[
                            r : r + share
                        ]
        val = dot_tn(mixed_ref[:, part], cot_ref[...]).astype(BF16)
        for l in range(line):
            for cc in range(CORES):
                r = (l * CORES + cc) * down_share
                for q in range(down_share // share):
                    wide[cc, j, l, 2 * share :, q * width : (q + 1) * width] = val[
                        r + q * share : r + (q + 1) * share
                    ]
    wide_twin = remote(wide.at[1 - c], wide_in, wps, wpr, twin)
    wide_twin.start()

    for i in range(2, line):
        compute(i)
        combine(i - 1)
    combine(line - 1)

    wide_twin.wait_recv()
    for k in range(seq_count):

        @pl.loop(0, line)
        def _(l):
            mixed = wide[c, k, l].astype(F32) + wide_in[k, l].astype(F32)
            wide_in[k, l] = mixed.astype(BF16)

    sides = []
    for j in range(1, seq_count):
        to = lax.rem(s + j, seq_count)
        sides.append(
            remote(wide_in.at[to], wide_side.at[j - 1], ws.at[j - 1], wr.at[j - 1], {"seq": to})
        )
        sides[-1].start()

    signs = signs_of(rows)
    for m in range(2):
        dsig[m] = (dy[m].astype(F32) * signs).astype(BF16)
        keep[m] = same_quarter(rows, short[m])
    acc[...] = jnp.zeros_like(acc)
    for i in range(ar_chunks):
        lag, cols = ar_place(i)
        for m in range(2):
            val = dot_nt(dy[m], ar_ref[i * lanes : (i + 1) * lanes, :])
            acc[m, :, cols] += led_by(val, lag, short[m])
    load_w.wait()

    def filter_step(k):
        table = spread(row_ref[k], rows)
        for m in range(2):
            kept_table = table * keep[m]
            conv[0] = dot_nn(kept_table, dy[m]).astype(BF16)
            conv[1] = (dot_nn(kept_table, dsig[m]) * signs).astype(BF16)
            acc[m] += dot_nt(conv[0], w_buf[k, 0]) + dot_nt(conv[1], w_buf[k, 1])

    half = count // 2
    pl.loop(0, half)(filter_step)
    for phase in range(1, line - 2):
        relay(deep_line, phase)
    pl.loop(half, count)(filter_step)
    conv[...] = acc[...].astype(BF16)
    du_copies = []
    for i in range(1, seq_count):
        to = lax.rem(s + i, seq_count)
        du_copies.append(
            remote(
                conv.at[:, pl.ds(pl.multiple_of(to * block, block), block), :],
                du_in.at[i - 1],
                dus.at[i - 1],
                dur.at[i - 1],
                {"seq": to},
            )
        )
        du_copies[-1].start()
    if line > 2:
        relay(deep_line, line - 2)

    for x in du_copies:
        x.wait_recv()
    gain = jnp.zeros((1, width), F32)
    for m in range(2):
        grad = conv[m, mine, :].astype(F32)
        for i in range(seq_count - 1):
            grad = grad + du_in[i, m].astype(F32)
        x = x_ref[m].astype(F32)
        inv = lax.rsqrt(jnp.mean(x * x, axis=-1, keepdims=True) + EPSILON)
        scaled = grad * scale_ref[...]
        gain = gain + jnp.sum(grad * x * inv, axis=0, keepdims=True)
        centre = jnp.mean(scaled * x, axis=-1, keepdims=True)
        tg_ref[m] = hg_ref[m] + inv * scaled - x * (inv * inv * inv) * centre
    g_own[...] = jnp.zeros_like(g_own)
    g_own[0:1, :] = gain
    g_own[1:2, :] = mlp_ref[0:1, :]
    small_pair = remote(g_own, g_pair, gs.at[0], gr.at[0], twin)
    small_pair.start()

    for x in sides:
        x.wait_recv()

    @pl.loop(0, line)
    def _(l):
        mixed = wide_in[s, l].astype(F32)
        for j in range(seq_count - 1):
            mixed = mixed + wide_side[j, l].astype(F32)
        wide_in[s, l] = mixed.astype(BF16)

    for t in range(line - 1):
        begin(wide_line, t)

    small_pair.wait()
    g_own[...] = g_own[...] + g_pair[...]
    small_sides = []
    for j in range(1, seq_count):
        small_sides.append(
            remote(
                g_own, g_side.at[j - 1], gs.at[j], gr.at[j], {"seq": lax.rem(s + j, seq_count)}
            )
        )
        small_sides[-1].start()

    dw_ref[...] = deep_in[z, :n, :].astype(F32)
    dar_ref[...] = deep_in[z, n:, :].astype(F32)
    for x in small_sides:
        x.wait()
    total = g_own[...]
    for j in range(seq_count - 1):
        total = total + g_side[j]
    g_sum[...] = total
    small_lines = []
    for j in range(1, line):
        small_lines.append(
            remote(
                g_sum,
                g_line.at[j - 1],
                gs.at[seq_count - 1 + j],
                gr.at[seq_count - 1 + j],
                {"grp": lax.rem(g + CORES * j, CORES * line)},
            )
        )
        small_lines[-1].start()

    def last(kind, add):
        for t in range(line - 1):
            for way in (0, 1):
                target = line - 1 - t if way == 0 else t

                @pl.when(z == target)
                def _():
                    hop(*kind, way, t, False).wait_recv()
                    add(kind[0][way, t].astype(F32))

    def add_deep(val):
        dw_ref[...] += val[:n]
        dar_ref[...] += val[n:]

    def add_wide(val):
        gg_ref[...] += val[:share]
        ug_ref[...] += val[share : 2 * share]
        for q in range(down_share // share):
            dg_ref[q * share : (q + 1) * share, :] += val[2 * share :, q * width : (q + 1) * width]

    last(deep_line, add_deep)
    for phase in range(1, line - 1):
        relay(wide_line, phase)
    own = wide_in[s, z].astype(F32)
    gg_ref[...] = own[:share]
    ug_ref[...] = own[share : 2 * share]
    for q in range(down_share // share):
        dg_ref[q * share : (q + 1) * share, :] = own[2 * share :, q * width : (q + 1) * width]
    last(wide_line, add_wide)

    for x in small_lines:
        x.wait()
    total = g_sum[...]
    for j in range(line - 1):
        total = total + g_line[j]
    at = (s * (CORES * line) + g) * (width // (seq_count * CORES * line))
    small_ref[...] = pltpu.roll(total, lax.rem(width - at, width), 1)

    for x in sides + du_copies:
        x.wait_send()
    wide_twin.wait_send()
    for i in range(line):
        twin_deep(i).wait_send()
    for kind in (deep_line, wide_line):
        for t in range(line - 1):
            for way in (0, 1):
                target = line - 1 - t if way == 0 else t

                @pl.when(z < target if way == 0 else z > target)
                def _():
                    hop(*kind, way, t, False).wait_send()


def mix_back(seq_count, line, layout, dy, u, table, w, ul, ar, x, hg, scale, mlp, mlp_grad, shares):
    z, gate_back, up_back, mixed, cot = mlp
    share, down_share, deep_share, ar_share = shares
    _, block, width = x.shape
    rows = block * seq_count
    count = w.shape[0]
    per_chip = 2 * count // line
    small = (8, width)
    hidden_units = gate_back.shape[1]
    part = (2 * share + down_share * width // hidden_units, hidden_units)
    out_shape = [
        jax.ShapeDtypeStruct((2, block, width), F32),
        jax.ShapeDtypeStruct((deep_share, width), F32),
        jax.ShapeDtypeStruct((ar_share, width), F32),
        jax.ShapeDtypeStruct((share, hidden_units), F32),
        jax.ShapeDtypeStruct((share, hidden_units), F32),
        jax.ShapeDtypeStruct((down_share, width), F32),
        jax.ShapeDtypeStruct(small, F32),
    ]
    deep = (deep_share + ar_share, width)
    scratch = [
        pltpu.VMEM((2, rows, rows), BF16),
        pltpu.VMEM((2, rows, width), BF16),
        pltpu.VMEM((2, rows, width), F32),
        pltpu.VMEM((2, rows, width), BF16),
        pltpu.VMEM((seq_count - 1, 2, block, width), BF16),
        pltpu.VMEM((2, per_chip, 2, rows, width), BF16),
        pltpu.VMEM(w.shape, BF16),
        pltpu.VMEM(ar.shape, BF16),
        pltpu.VMEM((CORES, line) + deep, BF16),
        pltpu.VMEM((line,) + deep, BF16),
        pltpu.VMEM((2, line - 1) + deep, BF16),
        pltpu.VMEM((CORES, seq_count, line) + part, BF16),
        pltpu.VMEM((seq_count, line) + part, BF16),
        pltpu.VMEM((seq_count - 1, line) + part, BF16),
        pltpu.VMEM((2, line - 1) + part, BF16),
        pltpu.VMEM(small, F32),
        pltpu.VMEM(small, F32),
        pltpu.VMEM((seq_count - 1,) + small, F32),
        pltpu.VMEM(small, F32),
        pltpu.VMEM((line - 1,) + small, F32),
        DMA((3,)),
        DMA((seq_count - 1,)),
        DMA((seq_count - 1,)),
        DMA((line,)),
        DMA((line,)),
        DMA((2, line - 1)),
        DMA((2, line - 1)),
        DMA,
        DMA,
        DMA((seq_count - 1,)),
        DMA((seq_count - 1,)),
        DMA((2, line - 1)),
        DMA((2, line - 1)),
        DMA((seq_count + line,)),
        DMA((seq_count + line,)),
    ]
    return pl.pallas_call(
        functools.partial(mix_back_kernel, seq_count, line),
        out_shape=out_shape,
        in_specs=[pl.BlockSpec(memory_space=pltpu.SMEM)] + [WHOLE] * 3 + [ANY] * 2 + [WHOLE] * 10,
        out_specs=[WHOLE] * 7,
        scratch_shapes=scratch,
        compiler_params=params(6),
        name="mix_back",
    )(layout, dy, u, table, w, ul, ar, x, hg, scale, z, gate_back, up_back, mixed, cot, mlp_grad)


def kept(rows, short, lag):
    pos = lax.broadcasted_iota(jnp.int32, (rows, 1), 0)
    whole = (pos >= lag).astype(F32)
    return whole * (1.0 - short * (1.0 - (lax.rem(pos, rows // 4) >= lag).astype(F32)))


def lagged_by(values, lag, short):
    rows = values.shape[0]
    one = pltpu.roll(values, 1, 0) * kept(rows, short, 1)
    two = pltpu.roll(values, 2, 0) * kept(rows, short, 2)
    return jnp.where(lag == 0, values, jnp.where(lag == 1, one, two))


def led_by(values, lag, short):
    rows = values.shape[0]
    one = pltpu.roll(values * kept(rows, short, 1), rows - 1, 0)
    two = pltpu.roll(values * kept(rows, short, 2), rows - 2, 0)
    return jnp.where(lag == 0, values, jnp.where(lag == 1, one, two))


def same_quarter(rows, short):
    down = lax.div(lax.broadcasted_iota(jnp.int32, (rows, rows), 0), rows // 4)
    over = lax.div(lax.broadcasted_iota(jnp.int32, (rows, rows), 1), rows // 4)
    return (1.0 - short * (1.0 - (down == over).astype(F32))).astype(BF16)


def mix_front_kernel(seq_count, line, *refs):
    (layout_ref, tok_ref, row_ref, gain_ref, cot_ref, spec_hbm, ar_hbm) = refs[:7]
    wide_in = refs[7:10]
    (w_hbm, ul_hbm, u_ref, ar_ref, gain_out) = refs[10:15]
    (z_ref, gb_ref, ub_ref, mixed_ref, hg_ref, dy_ref, mlp_ref, out_ref) = refs[15:23]
    (x_all, both, acc, y_bf, y_in, w_buf, ul_buf, keep, hid, dz, dy_own) = refs[23:34]
    wide_buf = refs[34:37]
    (g_own, g_side, g_sum, g_line, g_all, g_twin) = refs[37:43]
    (load_sem, ul_sem, w_sem, ts, tr, ys, yr, zs, zr, hs, hr) = refs[43:54]
    (ps, pr, ws, wr, wps, wpr, gs, gr, ds_, dr_) = refs[54:]
    s, z, c, g = place(seq_count, line)
    twin = {"grp": g + 1 - 2 * c}
    rows, width = x_all.shape[1], x_all.shape[2]
    block = tok_ref.shape[1]
    n = spec_hbm.shape[0]
    hn = n // 2
    blocks = ul_buf.shape[0]
    count = blocks // 2
    per_chip = blocks // line
    lanes = 128
    wide = range(3)
    mine = pl.ds(pl.multiple_of(s * block, block), block)
    short = [layout_ref[m, 0].astype(F32) for m in range(2)]

    def piece(l, h):
        return w_buf.at[l, pl.ds(pl.multiple_of(c * n + h * hn, hn), hn), :]

    def wide_own(i, l):
        return wide_buf[i].at[s, l, c]

    load_w = [
        pltpu.make_async_copy(spec_hbm.at[pl.ds(h * hn, hn)], piece(z, h), load_sem.at[h])
        for h in range(2)
    ]
    load_ar = pltpu.make_async_copy(ar_hbm, ar_ref.at[z, c], load_sem.at[2])
    loads = [pltpu.make_async_copy(wide_in[i], wide_own(i, z), load_sem.at[3 + i]) for i in wide]
    for x in load_w + [load_ar] + loads:
        x.start()
    at = (s * (CORES * line) + g) * (width // (seq_count * CORES * line))
    g_own[...] = pltpu.roll(gain_ref[...], at, 1).astype(BF16)
    greet(seq_count, line, s, z, c, g, twin=True, side=True, whole_line=True)

    gain_sides = []
    toks = []
    for i in range(1, seq_count):
        to = {"seq": lax.rem(s + i, seq_count)}
        gain_sides.append(remote(g_own, g_side.at[i - 1], gs.at[i - 1], gr.at[i - 1], to))
        gain_sides[-1].start()
    for i in range(1, seq_count):
        to = {"seq": lax.rem(s + i, seq_count)}
        toks.append(remote(tok_ref, x_all.at[:, mine, :], ts.at[i - 1], tr.at[i - 1], to))
        toks[-1].start()

    def onward(way):
        return {"grp": g + CORES if way == 0 else g - CORES}

    def early_own(i, l):
        return ar_ref.at[l, c] if i == 3 else wide_own(i, l)

    def early_hops(way, t, origin):
        hops = []
        for i in range(4):
            if t > 0:
                src = early_own(i, origin)
            else:
                src = ar_hbm if i == 3 else wide_in[i]
            hops.append(
                remote(src, early_own(i, origin), hs.at[i, way, t], hr.at[i, way, t], onward(way))
            )
        return hops

    def deep_hops(h):
        def build(way, t, origin):
            src = spec_hbm.at[pl.ds(h * hn, hn)] if t == 0 else piece(origin, h)
            dst = piece(origin, h)
            return [remote(src, dst, zs.at[h, way, t], zr.at[h, way, t], onward(way))]

        return build

    def first(build):
        for way in (0, 1):
            sends, _, origin, _ = line_conditions(line, z, way, 0)

            @pl.when(sends)
            def _():
                for x in build(way, 0, origin):
                    x.start()

    def arrive(build, t, after):
        for way in (0, 1):
            _, receives, _, origin = line_conditions(line, z, way, t)

            @pl.when(receives)
            def _():
                for x in build(way, t, origin):
                    x.wait_recv()
                if t + 1 < line - 1:
                    sends = line_conditions(line, z, way, t + 1)[0]

                    @pl.when(sends)
                    def _():
                        for x in build(way, t + 1, origin):
                            x.start()

                after(origin)

    def sent(build):
        for t in range(line - 1):
            for way in (0, 1):
                sends, _, origin, _ = line_conditions(line, z, way, t)

                @pl.when(sends)
                def _():
                    for x in build(way, t, origin):
                        x.wait_send()

    def sides(l, own=False):
        copies = []
        for i in wide:
            for j in range(1, seq_count):
                src = wide_in[i] if own else wide_own(i, l)
                to = {"seq": lax.rem(s + j, seq_count)}
                copies.append(
                    remote(src, wide_own(i, l), ws.at[i, l, j - 1], wr.at[i, l, j - 1], to)
                )
        return copies

    def begin_sides(l):
        for x in sides(l):
            x.start()

    def twin_deep(l, h):
        return remote(piece(l, h), piece(l, h), ps.at[h, l], pr.at[h, l], twin)

    first(early_hops)
    total = g_own[...]
    for i, x in enumerate(gain_sides):
        x.wait_recv()
        total = total + g_side[i]
    g_sum[...] = total
    gain_lines = []
    for j in range(1, line):
        k = seq_count - 2 + j
        to = {"grp": lax.rem(g + CORES * j, CORES * line)}
        gain_lines.append(remote(g_sum, g_line.at[j - 1], gs.at[k], gr.at[k], to))
        gain_lines[-1].start()
    first(deep_hops(0))
    for x in sides(z, True):
        x.start()
    x_all[:, mine, :] = tok_ref[...]
    for h in range(2):
        load_w[h].wait()
        twin_deep(z, h).start()
    for x in loads + [load_ar]:
        x.wait()
    for m in range(2):
        keep[m] = same_quarter(rows, short[m])
    arrive(early_hops, 0, begin_sides)
    first(deep_hops(1))
    total = g_sum[...]
    for j, x in enumerate(gain_lines):
        x.wait_recv()
        total = total + g_line[j]
    g_all[...] = total
    k = seq_count + line - 2
    gain_twin = remote(g_all, g_twin, gs.at[k], gr.at[k], twin)
    gain_twin.start()
    for x in toks:
        x.wait_recv()
    gain_twin.wait_recv()
    gain = g_all[...].astype(F32) + g_twin[...].astype(F32)
    gain_out[...] = gain[:8]

    signs = signs_of(rows)
    for m in range(2):
        x = x_all[m].astype(F32)
        inv = lax.rsqrt(jnp.mean(x * x, axis=-1, keepdims=True) + EPSILON)
        u = (x * inv * gain[0:1, :]).astype(BF16)
        u_ref[m] = u
        both[m, :, :width] = u
        both[m, :, width:] = (u.astype(F32) * signs).astype(BF16)

    def ul_store(k):
        part = pl.ds(2 * k, 2)
        return pltpu.make_async_copy(ul_buf.at[part], ul_hbm.at[part], ul_sem.at[k])

    def filter_step(k):
        table = spread(row_ref[k], rows)
        for m in range(2):
            val = dot_tn(table * keep[m], both[m])
            ul_buf[2 * k, m] = val[:, :width].astype(BF16)
            ul_buf[2 * k + 1, m] = (val[:, width:] * signs).astype(BF16)
        ul_store(k).start()

    def add_part(l, h):
        @pl.loop(0, 2)
        def _(m):
            total = 0.0
            for cc in range(CORES):
                lo, end = cc * n + h * hn, cc * n + (h + 1) * hn
                while lo < end:
                    j = lo // width
                    hi = min(end, (j + 1) * width)
                    left = ul_buf[l * per_chip + j, m, :, lo - j * width : hi - j * width]
                    total = total + dot_nn(left, w_buf[l, lo:hi, :])
                    lo = hi
            acc[m] += total

    def w_store(l):
        return pltpu.make_async_copy(w_buf.at[l], w_hbm.at[l], w_sem.at[l])

    def nothing(origin):
        pass

    def deep_arrive(t, h):
        arrive(deep_hops(h), t, lambda origin: twin_deep(origin, h).start())

    def deep_add(t, h):
        for way in (0, 1):
            _, receives, _, origin = line_conditions(line, z, way, t)

            @pl.when(receives)
            def _():
                twin_deep(origin, h).wait_recv()
                if h == 1:
                    w_store(origin).start()
                add_part(origin, h)

    half = count // 2
    acc[...] = jnp.zeros_like(acc)
    pl.loop(0, half)(filter_step)
    if line > 2:
        arrive(early_hops, 1, begin_sides)
    deep_arrive(0, 0)
    pl.loop(half, count)(filter_step)
    for h in range(2):
        twin_deep(z, h).wait_recv()
        add_part(z, h)
    w_store(z).start()
    deep_arrive(0, 1)
    for t in range(2, line - 1):
        arrive(early_hops, t, begin_sides)
    ar_twin = remote(ar_ref.at[:, c], ar_ref.at[:, c], wps.at[3, 0], wpr.at[3, 0], twin)
    ar_twin.start()
    for h in range(2):
        deep_add(0, h)

    ar_twin.wait_recv()
    ar_rows = ar_ref.shape[0] * ar_ref.shape[1] * ar_ref.shape[2]
    ar_all = ar_ref[...].reshape(ar_rows, width)
    chunks = ar_rows // lanes
    for i in range(chunks):
        place_at = s * chunks + i
        lag = lax.div(place_at, width // lanes)
        col = lax.rem(place_at, width // lanes)
        cols = pl.ds(pl.multiple_of(col * lanes, lanes), lanes)
        for m in range(2):
            v = lagged_by(u_ref[m, :, cols].astype(F32), lag, short[m]).astype(BF16)
            acc[m] += dot_nn(v, ar_all[i * lanes : (i + 1) * lanes])

    def twin_wide(i, k):
        part = wide_buf[i].at[k, :, c]
        return remote(part, part, wps.at[i, k], wpr.at[i, k], twin)

    for t in range(1, line - 1):
        deep_arrive(t, 0)
        if t == line - 2:
            for l in range(line):
                for x in sides(l):
                    x.wait_recv()
            for i in wide:
                for k in range(seq_count):
                    twin_wide(i, k).start()
        deep_add(t, 0)
        deep_arrive(t, 1)
        deep_add(t, 1)

    y_bf[...] = acc[...].astype(BF16)
    y_copies = []
    for i in range(1, seq_count):
        to = lax.rem(s + i, seq_count)
        y_copies.append(
            remote(
                y_bf.at[:, pl.ds(pl.multiple_of(to * block, block), block), :],
                y_in.at[i - 1],
                ys.at[i - 1],
                yr.at[i - 1],
                {"seq": to},
            )
        )
        y_copies[-1].start()

    for i in wide:
        for k in range(seq_count):
            twin_wide(i, k).wait()
    sent(early_hops)
    for h in range(2):
        sent(deep_hops(h))
        for l in range(line):
            twin_deep(l, h).wait_send()
    for l in range(line):
        w_store(l).wait()
        for x in sides(l):
            x.wait_send()
    for x in toks + gain_sides + gain_lines + [ar_twin, gain_twin]:
        x.wait_send()
    for k in range(count):
        ul_store(k).wait()

    for m in range(2):
        part = slice(m * block, (m + 1) * block)
        hid[part, :] = tok_ref[m].astype(F32) + acc[m, mine, :]
    for i, x in enumerate(y_copies):
        x.wait_recv()
        for m in range(2):
            hid[m * block : (m + 1) * block, :] += y_in[i, m].astype(F32)
    h = hid[...]
    inv_two = lax.rsqrt(jnp.mean(h * h, axis=-1, keepdims=True) + EPSILON)
    mlp_scale = gain[1:2, :]
    z_ref[...] = (h * inv_two * mlp_scale).astype(BF16)
    dz[...] = jnp.zeros_like(dz)
    hidden_units = gb_ref.shape[1]
    step = hidden_units // seq_count
    root = 0.7978845608028654

    @pl.loop(0, seq_count)
    def _(j):
        part = pl.ds(pl.multiple_of(j * step, step), step)
        gate_w = wide_buf[0][:, :, :, :, part].reshape(width, step)
        up_w = wide_buf[1][:, :, :, :, part].reshape(width, step)
        down_w = wide_buf[2][j].reshape(step, width)
        gate = dot_nn(z_ref[...], gate_w)
        up = dot_nn(z_ref[...], up_w)
        back = dot_nt(cot_ref[...], down_w)
        square = gate * gate
        tan = jnp.tanh(root * (gate + 0.044715 * (square * gate)))
        share = 0.5 * (1.0 + tan)
        gelu = gate * share
        slope = share + 0.5 * gate * (1.0 - tan * tan) * (
            root * (1.0 + (3.0 * 0.044715) * square)
        )
        mixed_ref[:, part] = (gelu * up).astype(BF16)
        gate_back = (back * up * slope).astype(BF16)
        up_back = (back * gelu).astype(BF16)
        gb_ref[:, part] = gate_back
        ub_ref[:, part] = up_back
        dz[...] += dot_nt(gate_back, gate_w) + dot_nt(up_back, up_w)
    grad = dz[...]
    h = hid[...]
    scaled = grad * mlp_scale
    centre = jnp.mean(scaled * h, axis=-1, keepdims=True)
    dh = cot_ref[...].astype(F32) + inv_two * scaled - h * (inv_two * inv_two * inv_two) * centre
    mlp_ref[...] = jnp.zeros_like(mlp_ref)
    mlp_ref[0:1, :] = jnp.sum(grad * h * inv_two, axis=0, keepdims=True)
    for m in range(2):
        part = slice(m * block, (m + 1) * block)
        hg_ref[m] = dh[part]
        dy_own[m] = dh[part].astype(BF16)
    dy_copies = []
    for i in range(1, seq_count):
        to = {"seq": lax.rem(s + i, seq_count)}
        dy_copies.append(remote(dy_own, dy_ref.at[:, mine, :], ds_.at[i - 1], dr_.at[i - 1], to))
        dy_copies[-1].start()
    dy_ref[:, mine, :] = dy_own[...]
    total = hid[...]
    for j in range(seq_count):
        down_w = wide_buf[2][j].reshape(step, width)
        total = total + dot_nn(mixed_ref[:, j * step : (j + 1) * step], down_w)
    for m in range(2):
        out_ref[m] = total[m * block : (m + 1) * block]
    for x in y_copies:
        x.wait_send()
    for x in dy_copies:
        x.wait()


def mix_front(seq_count, line, layout, tok, table, gain, cot, spec, ar, wide):
    _, block, width = tok.shape
    rows = block * seq_count
    count = table.shape[0]
    hidden_units = wide[0].shape[1]
    small = (16, width)
    vmem = pltpu.VMEM
    out_shape = [
        jax.ShapeDtypeStruct((line, CORES * spec.shape[0], width), BF16),
        jax.ShapeDtypeStruct((2 * count, 2, rows, width), BF16),
        jax.ShapeDtypeStruct((2, rows, width), BF16),
        jax.ShapeDtypeStruct((line, CORES) + ar.shape, BF16),
        jax.ShapeDtypeStruct((8, width), F32),
        jax.ShapeDtypeStruct((2 * block, width), BF16),
        jax.ShapeDtypeStruct((2 * block, hidden_units), BF16),
        jax.ShapeDtypeStruct((2 * block, hidden_units), BF16),
        jax.ShapeDtypeStruct((2 * block, hidden_units), BF16),
        jax.ShapeDtypeStruct((2, block, width), F32),
        jax.ShapeDtypeStruct((2, rows, width), BF16),
        jax.ShapeDtypeStruct((8, width), F32),
        jax.ShapeDtypeStruct((2, block, width), F32),
    ]
    scratch = [
        vmem((2, rows, width), BF16),
        vmem((2, rows, 2 * width), BF16),
        vmem((2, rows, width), F32),
        vmem((2, rows, width), BF16),
        vmem((seq_count - 1, 2, block, width), BF16),
        vmem((line, CORES * spec.shape[0], width), BF16),
        vmem((2 * count, 2, rows, width), BF16),
        vmem((2, rows, rows), BF16),
        vmem((2 * block, width), F32),
        vmem((2 * block, width), F32),
        vmem((2, block, width), BF16),
    ]
    scratch += [vmem((seq_count, line, CORES) + x.shape, BF16) for x in wide]
    scratch += [
        vmem(small, BF16),
        vmem((seq_count - 1,) + small, BF16),
        vmem(small, BF16),
        vmem((line - 1,) + small, BF16),
        vmem(small, BF16),
        vmem(small, BF16),
        DMA((6,)),
        DMA((count,)),
        DMA((line,)),
        DMA((seq_count - 1,)),
        DMA((seq_count - 1,)),
        DMA((seq_count - 1,)),
        DMA((seq_count - 1,)),
        DMA((2, 2, line - 1)),
        DMA((2, 2, line - 1)),
        DMA((4, 2, line - 1)),
        DMA((4, 2, line - 1)),
        DMA((2, line)),
        DMA((2, line)),
        DMA((3, line, seq_count - 1)),
        DMA((3, line, seq_count - 1)),
        DMA((4, seq_count)),
        DMA((4, seq_count)),
        DMA((seq_count + line,)),
        DMA((seq_count + line,)),
        DMA((seq_count - 1,)),
        DMA((seq_count - 1,)),
    ]
    return pl.pallas_call(
        functools.partial(mix_front_kernel, seq_count, line),
        out_shape=out_shape,
        in_specs=[pl.BlockSpec(memory_space=pltpu.SMEM)] + [WHOLE] * 4 + [ANY] * 5,
        out_specs=[ANY] * 2 + [WHOLE] * 11,
        scratch_shapes=scratch,
        compiler_params=params(7),
        name="mix_front",
    )(layout, tok, table, gain, cot, spec, ar, *wide)


def body(
    tokens,
    layout,
    filters,
    gain_mix,
    spectral_proj,
    ar_proj,
    gain_mlp,
    w_gate,
    w_up,
    w_down,
    out_grad,
):
    seq_count = lax.axis_size("seq")
    line = lax.axis_size("grp") // CORES
    s = lax.axis_index("seq")
    g = lax.axis_index("grp")
    block, width = tokens.shape[2], tokens.shape[3]
    rows = block * seq_count
    count = filters.shape[1] // seq_count
    hidden_units = w_gate.shape[1]
    spans = (rows, rows // 4)

    share = gain_mix.shape[0]
    ar_rows = ar_proj.shape[0] * CORES * line
    mine = lax.dynamic_slice(filters.T, (s * count, 0), (count, rows))[:, None, :]
    nothing = jnp.zeros((count, 1, rows), F32)
    back_table = jnp.concatenate([mine, nothing], axis=2)
    aligned = share % 16 == 0 and ar_proj.shape[0] % 16 == 0 and 2 * count % line == 0
    aligned = aligned and ar_rows % 128 == 0 and line > 2

    if aligned:
        gains = jnp.pad(jnp.stack([gain_mix, gain_mlp]), ((0, 14), (0, width - share)))
        own = tokens[:, 0]
        cot = out_grad.reshape(2 * block, width)
        spec, ul, u, ar, gains, mlp_in, gate_back, up_back, mixed, dh, dy, mlp_grad, out = mix_front(
            seq_count,
            line,
            layout,
            own,
            back_table,
            gains.astype(F32),
            cot,
            spectral_proj,
            ar_proj,
            (w_gate, w_up, w_down),
        )
        input_grad, dw, dar, gate_grad, up_grad, down_grad, small = mix_back(
            seq_count,
            line,
            layout,
            dy,
            u,
            back_table,
            spec.reshape(count, 2, width, width),
            ul,
            ar.reshape(ar_rows, width),
            own,
            dh,
            gains[0:1],
            (mlp_in, gate_back, up_back, mixed, cot),
            mlp_grad,
            (share, w_down.shape[0], spectral_proj.shape[0], ar_proj.shape[0]),
        )
        return (
            out.reshape(tokens.shape),
            input_grad.reshape(tokens.shape),
            small[0, :share],
            dw,
            dar,
            small[1, :share],
            gate_grad,
            up_grad,
            down_grad,
        )

    swap = layout[0, 0] == 1
    own = jnp.where(swap, tokens[::-1, 0], tokens[:, 0])
    cotangent = jnp.where(swap, out_grad[::-1, 0], out_grad[:, 0])
    gains = jnp.zeros((16, 128), BF16)
    gains = gains.at[0, :share].set(gain_mix).at[1, :share].set(gain_mlp)
    x_all, spec, ar, gate_w, up_w, down_w, gains = gather_all(
        seq_count, line, own, (spectral_proj, ar_proj), (w_gate, w_up, w_down, gains)
    )
    ar_full = lax.dynamic_update_slice(
        jnp.zeros((3 * width, width), BF16), ar.reshape(ar_rows, width), (s * ar_rows, 0)
    )
    gains = gains.reshape(-1, 16, 128).astype(F32)
    mix_scale = gains[:, 0, :share].reshape(1, width)
    mlp_scale = gains[:, 1, :share].reshape(1, width)
    fore_table = jnp.concatenate([mine[:, :, :1], nothing, mine[:, :, :0:-1]], axis=2)
    split = spec.reshape(count, 2, width, width)
    ul, u, y = forward_mix(spans, x_all, mix_scale, fore_table, split, ar_full)
    mixer = side_sum(seq_count, line, y, 3).reshape(2 * block, width)
    spec = spec.reshape(count, 2, width, width)
    gate_w = gate_w.reshape(width, hidden_units)
    up_w = up_w.reshape(width, hidden_units)
    down_w = down_w.reshape(hidden_units, width)

    inputs = own.reshape(2 * block, width).astype(F32)
    cot = cotangent.reshape(2 * block, width)
    hidden = inputs + mixer
    inv_two = lax.rsqrt(jnp.mean(hidden * hidden, axis=-1, keepdims=True) + EPSILON)
    mlp_in = (hidden * inv_two * mlp_scale).astype(BF16)
    gate = dot_nn(mlp_in, gate_w)
    upval = dot_nn(mlp_in, up_w)
    product_val, gelu_pull = jax.vjp(lambda a, b: jax.nn.gelu(a) * b, gate, upval)
    mixed = product_val.astype(BF16)
    out = hidden + dot_nn(mixed, down_w)
    mixed_grad = dot_nt(cot, down_w)
    gate_back, up_back = gelu_pull(mixed_grad)
    gate_back = gate_back.astype(BF16)
    up_back = up_back.astype(BF16)
    mlp_in_grad = dot_nt(gate_back, gate_w) + dot_nt(up_back, up_w)
    scaled_two = mlp_in_grad * mlp_scale
    mlp_grad = jnp.sum(mlp_in_grad * hidden * inv_two, axis=0, keepdims=True)
    hidden_grad = (
        cot.astype(F32)
        + inv_two * scaled_two
        - hidden * inv_two**3 * jnp.mean(scaled_two * hidden, axis=-1, keepdims=True)
    )
    mixer_grad = hidden_grad.astype(BF16)

    down_grad = dot_tn(mixed, cot)
    gate_grad = dot_tn(mlp_in, gate_back)
    up_grad = dot_tn(mlp_in, up_back)
    dy = side_gather(seq_count, line, mixer_grad.reshape(2, block, width))
    dw, dar, du = backward_mix(spans, dy, u, back_table, spec, ul, ar_full)
    normed_grad = side_sum(seq_count, line, du, 4).reshape(2 * block, width)

    inv_one = lax.rsqrt(jnp.mean(inputs * inputs, axis=-1, keepdims=True) + EPSILON)
    scaled_one = normed_grad * mix_scale
    mix_grad = jnp.sum(normed_grad * inputs * inv_one, axis=0, keepdims=True)
    input_grad = (
        hidden_grad
        + inv_one * scaled_one
        - inputs * inv_one**3 * jnp.mean(scaled_one * inputs, axis=-1, keepdims=True)
    )

    dar = lax.dynamic_slice(dar, (s * ar_rows, 0), (ar_rows, width))
    deep = (dw.reshape(line, CORES, -1, width), dar.reshape(line, CORES, -1, width))
    wide = tuple(
        x.astype(BF16).reshape(seq_count, line, CORES, -1, x.shape[1])
        for x in (gate_grad, up_grad, down_grad)
    )
    small = jnp.concatenate([mix_grad, mlp_grad, jnp.zeros((6, width), F32)], axis=0)
    dw, dar, gate_grad, up_grad, down_grad, small = sum_all(seq_count, line, deep, wide, small)
    small = lax.dynamic_slice(small, (0, (s * CORES * line + g) * share), (2, share))

    def settle(x):
        x = x.reshape(2, 1, block, width)
        return jnp.where(swap, x[::-1], x)

    return (
        settle(out),
        settle(input_grad),
        small[0],
        dw,
        dar,
        small[1],
        gate_grad,
        up_grad,
        down_grad,
    )


def solution(mesh):
    placed = (
        P(None, "grp", "seq", None),
        P(None, "grp"),
        P(),
        P(("seq", "grp")),
        P(("seq", "grp"), None),
        P(("seq", "grp"), None),
        P(("seq", "grp")),
        P(("seq", "grp"), None),
        P(("seq", "grp"), None),
        P(("seq", "grp"), None),
        P(None, "grp", "seq", None),
    )
    return jax.shard_map(
        body,
        mesh=mesh,
        in_specs=placed,
        out_specs=(
            P(None, "grp", "seq", None),
            P(None, "grp", "seq", None),
            P(("seq", "grp")),
            P(("seq", "grp"), None),
            P(("seq", "grp"), None),
            P(("seq", "grp")),
            P(("seq", "grp"), None),
            P(("seq", "grp"), None),
            P(("seq", "grp"), None),
        ),
        check_vma=False,
    )
```

```python
import functools

import jax
import jax.numpy as jnp
from jax import lax
from jax.experimental import pallas as pl
from jax.experimental.pallas import tpu as pltpu
from jax.sharding import PartitionSpec as P

EPSILON = 1e-05
BF16 = jnp.bfloat16
F32 = jnp.float32
MESH = pl.DeviceIdType.MESH
DMA = pltpu.SemaphoreType.DMA
ANY = pl.BlockSpec(memory_space=pl.ANY)
WHOLE = pl.BlockSpec(memory_space=pltpu.VMEM)
VMEM_LIMIT = 60 * 1024 * 1024
CORES = 2


def dot_nn(a, b):
    return lax.dot_general(a, b, (((1,), (0,)), ((), ())), preferred_element_type=F32)


def dot_tn(a, b):
    return lax.dot_general(a, b, (((0,), (0,)), ((), ())), preferred_element_type=F32)


def dot_nt(a, b):
    return lax.dot_general(a, b, (((1,), (1,)), ((), ())), preferred_element_type=F32)


def params(collective_id=None):
    return pltpu.CompilerParams(
        collective_id=collective_id,
        has_side_effects=collective_id is not None,
        vmem_limit_bytes=VMEM_LIMIT,
    )


def remote(src, dst, send, recv, where):
    return pltpu.make_async_remote_copy(
        src_ref=src, dst_ref=dst, send_sem=send, recv_sem=recv, device_id=where, device_id_type=MESH
    )


def place(seq_count, line):
    s = lax.axis_index("seq")
    g = lax.axis_index("grp")
    return s, lax.div(g, CORES), lax.rem(g, CORES), g


def greet(seq_count, line, s, z, c, g, chain=False, twin=False, side=False, whole_line=False):
    barrier = pltpu.get_barrier_semaphore()

    def call(where):
        pl.semaphore_signal(barrier, inc=1, device_id=where, device_id_type=MESH)

    expected = (1 if twin else 0) + (seq_count - 1 if side else 0) + (line - 1 if whole_line else 0)
    if twin:
        call({"grp": g + 1 - 2 * c})
    if side:
        for i in range(1, seq_count):
            call({"seq": lax.rem(s + i, seq_count)})
    if whole_line:
        for j in range(1, line):
            call({"grp": lax.rem(g + CORES * j, CORES * line)})
    if chain:
        expected = expected + (z > 0).astype(jnp.int32) + (z < line - 1).astype(jnp.int32)

        @pl.when(z > 0)
        def _():
            call({"grp": g - CORES})

        @pl.when(z < line - 1)
        def _():
            call({"grp": g + CORES})

    pl.semaphore_wait(barrier, expected)


def line_conditions(line, z, way, t):
    if way == 0:
        return (z < line - 1) & (z >= t), z >= t + 1, z - t, z - 1 - t
    return (z > 0) & (z + t <= line - 1), z + t + 1 <= line - 1, z + t, z + 1 + t


def gather_kernel(seq_count, line, n_deep, n_wide, *refs):
    n_in = 1 + n_deep + n_wide
    ins, outs = refs[:n_in], refs[n_in : 2 * n_in]
    rest = refs[2 * n_in :]
    stage = rest[:n_in]
    (local_sem, tok_send, tok_recv, zs, zr, ws, wr, ps, pr, dps, dpr) = rest[n_in:]
    s, z, c, g = place(seq_count, line)
    twin = {"grp": g + 1 - 2 * c}
    tok, tok_out = ins[0], outs[0]
    rows = tok.shape[1]
    items = list(range(n_deep + n_wide))

    def own(i, l):
        out = outs[1 + i]
        return out.at[l, c] if i < n_deep else out.at[s, l, c]

    loads = [pltpu.make_async_copy(ins[i], stage[i], local_sem.at[0, i]) for i in range(n_in)]
    for x in loads:
        x.start()
    greet(seq_count, line, s, z, c, g, chain=True, twin=True, side=True)

    toks = []
    for i in range(1, seq_count):
        toks.append(
            remote(
                tok,
                tok_out.at[:, pl.ds(pl.multiple_of(s * rows, rows), rows), :],
                tok_send.at[i - 1],
                tok_recv.at[i - 1],
                {"seq": lax.rem(s + i, seq_count)},
            )
        )
        toks[-1].start()

    def hop(i, way, t, origin):
        src = ins[1 + i] if t == 0 else own(i, origin)
        to = g + CORES if way == 0 else g - CORES
        return remote(src, own(i, origin), zs.at[i, way, t], zr.at[i, way, t], {"grp": to})

    def hops(which, t):
        for way in (0, 1):
            sends, _, origin, _ = line_conditions(line, z, way, t)

            @pl.when(sends)
            def _():
                for i in which:
                    hop(i, way, t, origin).start()

    def arrive(which, t, after=None):
        for way in (0, 1):
            _, receives, _, origin = line_conditions(line, z, way, t)

            @pl.when(receives)
            def _():
                for i in which:
                    hop(i, way, t, origin).wait_recv()
                if after is not None:
                    after(origin)

    deep, wide = items[:n_deep], items[n_deep:]
    for t in range(line - 1):
        hops(wide, t)
        if t == 0:
            stores = []
            for i in range(n_in):
                loads[i].wait()
                dst = (
                    tok_out.at[:, pl.ds(pl.multiple_of(s * rows, rows), rows), :]
                    if i == 0
                    else own(i - 1, z)
                )
                stores.append(pltpu.make_async_copy(stage[i], dst, local_sem.at[1, i]))
                stores[-1].start()
        arrive(wide, t)
    hops(deep, 0)
    for x in stores:
        x.wait()
    sides = []
    for i in wide:
        for j in range(1, seq_count):
            part = outs[1 + i].at[s, :, c]
            sides.append(
                remote(
                    part,
                    part,
                    ws.at[i - n_deep, j - 1],
                    wr.at[i - n_deep, j - 1],
                    {"seq": lax.rem(s + j, seq_count)},
                )
            )
            sides[-1].start()

    def twin_wide(i, k):
        part = outs[1 + i].at[k, :, c]
        return remote(part, part, ps.at[i - n_deep, k], pr.at[i - n_deep, k], twin)

    def twin_deep(i, l):
        part = outs[1 + i].at[l, c]
        return remote(part, part, dps.at[i, l], dpr.at[i, l], twin)

    for i in wide:
        twin_wide(i, s).start()
    for i in deep:
        twin_deep(i, z).start()

    def pass_on(origin):
        for i in deep:
            twin_deep(i, origin).start()

    for t in range(line - 1):
        if t > 0:
            hops(deep, t)
        arrive(deep, t, pass_on)
    for x in sides:
        x.wait_recv()
    for i in wide:
        for j in range(1, seq_count):
            twin_wide(i, lax.rem(s + seq_count - j, seq_count)).start()
    for x in toks:
        x.wait_recv()
    for i in deep:
        for l in range(line):
            twin_deep(i, l).wait()
    for i in wide:
        for k in range(seq_count):
            twin_wide(i, k).wait()
    for x in toks + sides:
        x.wait_send()
    for t in range(line - 1):
        for way in (0, 1):
            sends, _, origin, _ = line_conditions(line, z, way, t)

            @pl.when(sends)
            def _():
                for i in items:
                    hop(i, way, t, origin).wait_send()


def gather_all(seq_count, line, tok, deep, wide):
    n_deep, n_wide = len(deep), len(wide)
    shapes = [
        jax.ShapeDtypeStruct((tok.shape[0], tok.shape[1] * seq_count, tok.shape[2]), tok.dtype)
    ]
    shapes += [jax.ShapeDtypeStruct((line, CORES) + x.shape, x.dtype) for x in deep]
    shapes += [jax.ShapeDtypeStruct((seq_count, line, CORES) + x.shape, x.dtype) for x in wide]
    arrays = [tok] + list(deep) + list(wide)
    n = len(arrays)
    scratch = [pltpu.VMEM(x.shape, x.dtype) for x in arrays]
    scratch += [
        DMA((2, n)),
        DMA((seq_count - 1,)),
        DMA((seq_count - 1,)),
        DMA((n_deep + n_wide, 2, line - 1)),
        DMA((n_deep + n_wide, 2, line - 1)),
        DMA((n_wide, seq_count - 1)),
        DMA((n_wide, seq_count - 1)),
        DMA((n_wide, seq_count)),
        DMA((n_wide, seq_count)),
        DMA((n_deep, line)),
        DMA((n_deep, line)),
    ]
    return pl.pallas_call(
        functools.partial(gather_kernel, seq_count, line, n_deep, n_wide),
        out_shape=shapes,
        in_specs=[ANY] * n,
        out_specs=[ANY] * n,
        scratch_shapes=scratch,
        compiler_params=params(1),
        name="gather_all",
    )(*arrays)


def side_gather_kernel(seq_count, line, x_ref, out_ref, local_sem, send, recv):
    s, z, c, g = place(seq_count, line)
    rows = x_ref.shape[1]
    mine = out_ref.at[:, pl.ds(pl.multiple_of(s * rows, rows), rows), :]
    local = pltpu.make_async_copy(x_ref, mine, local_sem)
    local.start()
    greet(seq_count, line, s, z, c, g, side=True)
    copies = []
    for i in range(1, seq_count):
        copies.append(
            remote(
                x_ref, mine, send.at[i - 1], recv.at[i - 1], {"seq": lax.rem(s + i, seq_count)}
            )
        )
        copies[-1].start()
    local.wait()
    for x in copies:
        x.wait()


def side_gather(seq_count, line, x):
    return pl.pallas_call(
        functools.partial(side_gather_kernel, seq_count, line),
        out_shape=jax.ShapeDtypeStruct((x.shape[0], x.shape[1] * seq_count, x.shape[2]), x.dtype),
        in_specs=[WHOLE],
        out_specs=WHOLE,
        scratch_shapes=[DMA, DMA((seq_count - 1,)), DMA((seq_count - 1,))],
        compiler_params=params(2),
        name="side_gather",
    )(x)


def side_sum_kernel(seq_count, line, x_ref, out_ref, slots, send, recv):
    s, z, c, g = place(seq_count, line)
    rows = out_ref.shape[1]
    greet(seq_count, line, s, z, c, g, side=True)
    copies = []
    for i in range(1, seq_count):
        to = lax.rem(s + i, seq_count)
        copies.append(
            remote(
                x_ref.at[:, pl.ds(pl.multiple_of(to * rows, rows), rows), :],
                slots.at[i - 1],
                send.at[i - 1],
                recv.at[i - 1],
                {"seq": to},
            )
        )
        copies[-1].start()
    total = x_ref[:, pl.ds(pl.multiple_of(s * rows, rows), rows), :].astype(F32)
    for i, x in enumerate(copies):
        x.wait_recv()
        total = total + slots[i].astype(F32)
    out_ref[...] = total
    for x in copies:
        x.wait_send()


def side_sum(seq_count, line, x, collective_id):
    rows = x.shape[1] // seq_count
    return pl.pallas_call(
        functools.partial(side_sum_kernel, seq_count, line),
        out_shape=jax.ShapeDtypeStruct((x.shape[0], rows, x.shape[2]), F32),
        in_specs=[WHOLE],
        out_specs=WHOLE,
        scratch_shapes=[
            pltpu.VMEM((seq_count - 1, x.shape[0], rows, x.shape[2]), x.dtype),
            DMA((seq_count - 1,)),
            DMA((seq_count - 1,)),
        ],
        compiler_params=params(collective_id),
        name=f"side_sum_{collective_id}",
    )(x)


def sum_kernel(seq_count, line, n_deep, n_wide, *refs):
    n = n_deep + n_wide
    ins, outs = refs[: n + 1], refs[n + 1 : 2 * n + 2]
    rest = refs[2 * n + 2 :]
    pair, side, chain = rest[:n], rest[n : n + n_wide], rest[n + n_wide : 2 * n + n_wide]
    rest = rest[2 * n + n_wide :]
    g_pair, g_side, g_line, g_a, g_b = rest[:5]
    (ps, pr, ws, wr, zs, zr, gs, gr) = rest[5:]
    s, z, c, g = place(seq_count, line)
    twin = {"grp": g + 1 - 2 * c}
    deep, wide = list(range(n_deep)), list(range(n_deep, n))
    small = ins[n]
    greet(seq_count, line, s, z, c, g, twin=True, side=True, whole_line=True)

    def theirs(i):
        return ins[i].at[:, 1 - c] if i < n_deep else ins[i].at[:, :, 1 - c]

    pairs = [remote(theirs(i), pair[i], ps.at[i], pr.at[i], twin) for i in range(n)]
    small_pair = remote(small, g_pair, gs.at[0], gr.at[0], twin)
    small_pair.start()
    for x in pairs[n_deep:] + pairs[:n_deep]:
        x.start()

    small_pair.wait()
    g_a[...] = small[...] + g_pair[...]
    small_sides = []
    for j in range(1, seq_count):
        small_sides.append(
            remote(
                g_a,
                g_side.at[j - 1],
                gs.at[j],
                gr.at[j],
                {"seq": lax.rem(s + j, seq_count)},
            )
        )
        small_sides[-1].start()

    for i in wide:
        pairs[i].wait_recv()
        for k in range(seq_count):

            @pl.loop(0, line)
            def _(l):
                mixed = ins[i][k, l, c].astype(F32) + pair[i][k, l].astype(F32)
                pair[i][k, l] = mixed.astype(BF16)

    sides = {}
    for i in wide:
        for j in range(1, seq_count):
            to = lax.rem(s + j, seq_count)
            sides[i, j] = remote(
                pair[i].at[to],
                side[i - n_deep].at[j - 1],
                ws.at[i - n_deep, j - 1],
                wr.at[i - n_deep, j - 1],
                {"seq": to},
            )
            sides[i, j].start()
    for i in deep:
        pairs[i].wait_recv()
        for l in range(line):
            pair[i][l] = (ins[i][l, c].astype(F32) + pair[i][l].astype(F32)).astype(BF16)

    for x in small_sides:
        x.wait()
    total = g_a[...]
    for j in range(seq_count - 1):
        total = total + g_side[j]
    g_b[...] = total
    small_lines = []
    for j in range(1, line):
        small_lines.append(
            remote(
                g_b,
                g_line.at[j - 1],
                gs.at[seq_count - 1 + j],
                gr.at[seq_count - 1 + j],
                {"grp": lax.rem(g + CORES * j, CORES * line)},
            )
        )
        small_lines[-1].start()

    def piece(i, l):
        return pair[i].at[l] if i < n_deep else pair[i].at[s, l]

    def run_line(which):
        def hop(i, way, t, dest, first):
            src = piece(i, dest) if first else chain[i].at[way, t]
            to = g + CORES if way == 0 else g - CORES
            return remote(src, chain[i].at[way, t], zs.at[i, way, t], zr.at[i, way, t], {"grp": to})

        for t in range(line - 1):
            for way in (0, 1):
                dest = line - 1 - t if way == 0 else t
                starts = z == 0 if way == 0 else z == line - 1
                relays = (z > 0) & (z < dest) if way == 0 else (z < line - 1) & (z > dest)

                @pl.when(starts)
                def _():
                    for i in which:
                        hop(i, way, t, dest, True).start()

                @pl.when(relays)
                def _():
                    for i in which:
                        hop(i, way, t, dest, False).wait_recv()
                        mixed = chain[i][way, t].astype(F32) + piece(i, dest)[...].astype(F32)
                        chain[i][way, t] = mixed.astype(BF16)
                        hop(i, way, t, dest, False).start()

        for i in which:
            outs[i][...] = piece(i, z)[...].astype(F32)
        for t in range(line - 1):
            for way in (0, 1):
                dest = line - 1 - t if way == 0 else t

                @pl.when((z == dest))
                def _():
                    for i in which:
                        hop(i, way, t, dest, False).wait_recv()
                        outs[i][...] += chain[i][way, t].astype(F32)

                @pl.when(z == 0 if way == 0 else z == line - 1)
                def _():
                    for i in which:
                        hop(i, way, t, dest, True).wait_send()

                @pl.when((z > 0) & (z < dest) if way == 0 else (z < line - 1) & (z > dest))
                def _():
                    for i in which:
                        hop(i, way, t, dest, False).wait_send()

    run_line(deep)
    for i in wide:
        for j in range(1, seq_count):
            sides[i, j].wait()

        @pl.loop(0, line)
        def _(l):
            mixed = pair[i][s, l].astype(F32)
            for j in range(1, seq_count):
                mixed = mixed + side[i - n_deep][j - 1, l].astype(F32)
            pair[i][s, l] = mixed.astype(BF16)

    run_line(wide)
    for x in pairs:
        x.wait_send()
    for x in small_lines:
        x.wait()
    total = g_b[...]
    for j in range(line - 1):
        total = total + g_line[j]
    outs[n][...] = total


def sum_all(seq_count, line, deep, wide, small):
    n_deep, n_wide = len(deep), len(wide)
    n = n_deep + n_wide
    shapes = [jax.ShapeDtypeStruct(x.shape[2:], F32) for x in deep]
    shapes += [jax.ShapeDtypeStruct(x.shape[3:], F32) for x in wide]
    shapes += [jax.ShapeDtypeStruct(small.shape, F32)]
    scratch = [pltpu.VMEM((line,) + x.shape[2:], BF16) for x in deep]
    scratch += [pltpu.VMEM((seq_count, line) + x.shape[3:], BF16) for x in wide]
    scratch += [pltpu.VMEM((seq_count - 1, line) + x.shape[3:], BF16) for x in wide]
    scratch += [pltpu.VMEM((2, line - 1) + x.shape[2:], BF16) for x in deep]
    scratch += [pltpu.VMEM((2, line - 1) + x.shape[3:], BF16) for x in wide]
    scratch += [
        pltpu.VMEM(small.shape, F32),
        pltpu.VMEM((seq_count - 1,) + small.shape, F32),
        pltpu.VMEM((line - 1,) + small.shape, F32),
        pltpu.VMEM(small.shape, F32),
        pltpu.VMEM(small.shape, F32),
        DMA((n,)),
        DMA((n,)),
        DMA((n_wide, seq_count - 1)),
        DMA((n_wide, seq_count - 1)),
        DMA((n, 2, line - 1)),
        DMA((n, 2, line - 1)),
        DMA((seq_count + line,)),
        DMA((seq_count + line,)),
    ]
    return pl.pallas_call(
        functools.partial(sum_kernel, seq_count, line, n_deep, n_wide),
        out_shape=shapes,
        in_specs=[WHOLE] * (n + 1),
        out_specs=[WHOLE] * (n + 1),
        scratch_shapes=scratch,
        compiler_params=params(5),
        name="sum_all",
    )(*deep, *wide, small)


def signs_of(rows):
    pos = lax.broadcasted_iota(jnp.int32, (rows, 1), 0)
    return 1.0 - 2.0 * lax.rem(pos, 2).astype(F32)


def lagged(values, lag, span):
    pos = lax.broadcasted_iota(jnp.int32, (values.shape[0], 1), 0)
    return jnp.where(lax.rem(pos, span) >= lag, pltpu.roll(values, lag, 0), 0.0)


def led(values, lag, span):
    rows = values.shape[0]
    pos = lax.broadcasted_iota(jnp.int32, (rows, 1), 0)
    return jnp.where(lax.rem(pos, span) < span - lag, pltpu.roll(values, rows - lag, 0), 0.0)


def spread(row, rows):
    wide = jnp.broadcast_to(row, (rows, row.shape[1]))
    return pltpu.roll(wide, 0, 1, stride=1, stride_axis=0)[:, :rows].astype(BF16)


def forward_kernel(spans, x_ref, gain_ref, row_ref, w_ref, ar_ref, ul_ref, u_ref, y_ref, both, acc):
    k = pl.program_id(0)
    rows, width = x_ref.shape[1], x_ref.shape[2]
    signs = signs_of(rows)

    @pl.when(k == 0)
    def _():
        for m in range(2):
            x = x_ref[m].astype(F32)
            inv = lax.rsqrt(jnp.mean(x * x, axis=-1, keepdims=True) + EPSILON)
            u = (x * inv * gain_ref[...]).astype(BF16)
            wide = u.astype(F32)
            u_ref[m] = u
            both[m, :, :width] = u
            both[m, :, width:] = (wide * signs).astype(BF16)
            acc[m] = dot_nn(u, ar_ref[:width])
            for lag in (1, 2):
                acc[m] += dot_nn(
                    lagged(wide, lag, spans[m]).astype(BF16),
                    ar_ref[lag * width : (lag + 1) * width],
                )

    table = spread(row_ref[0], rows)
    for m in range(2):
        span = spans[m]
        for j in range(rows // span):
            part = slice(j * span, (j + 1) * span)
            conv = dot_nn(table[:span, :span], both[m, part, :])
            plus = conv[:, :width].astype(BF16)
            minus = (conv[:, width:] * signs[part]).astype(BF16)
            ul_ref[0, 0, m, part, :] = plus
            ul_ref[0, 1, m, part, :] = minus
        acc[m] += dot_nn(ul_ref[0, 0, m], w_ref[0, 0]) + dot_nn(ul_ref[0, 1, m], w_ref[0, 1])

    @pl.when(k == pl.num_programs(0) - 1)
    def _():
        y_ref[...] = acc[...].astype(BF16)


def forward_mix(spans, x, gain, table, w, ar):
    count = table.shape[0]
    _, rows, width = x.shape
    full = lambda *shape: pl.BlockSpec(shape, lambda k: (0,) * len(shape))
    return pl.pallas_call(
        functools.partial(forward_kernel, spans),
        grid=(count,),
        out_shape=[
            jax.ShapeDtypeStruct((count, 2, 2, rows, width), BF16),
            jax.ShapeDtypeStruct((2, rows, width), BF16),
            jax.ShapeDtypeStruct((2, rows, width), BF16),
        ],
        in_specs=[
            full(2, rows, width),
            full(1, width),
            pl.BlockSpec((1, 1, 2 * rows), lambda k: (k, 0, 0)),
            pl.BlockSpec((1, 2, width, width), lambda k: (k, 0, 0, 0)),
            full(3 * width, width),
        ],
        out_specs=[
            pl.BlockSpec((1, 2, 2, rows, width), lambda k: (k, 0, 0, 0, 0)),
            full(2, rows, width),
            full(2, rows, width),
        ],
        scratch_shapes=[pltpu.VMEM((2, rows, 2 * width), BF16), pltpu.VMEM((2, rows, width), F32)],
        compiler_params=params(),
        name="forward_mix",
    )(x, gain, table, w, ar)


def backward_kernel(
    spans, dy_ref, u_ref, row_ref, w_ref, ul_ref, ar_ref, dw_ref, dar_ref, du_ref, both, acc
):
    k = pl.program_id(0)
    rows, width = dy_ref.shape[1], dy_ref.shape[2]
    signs = signs_of(rows)

    @pl.when(k == 0)
    def _():
        for m in range(2):
            dy = dy_ref[m]
            both[m, :, :width] = dy
            both[m, :, width:] = (dy.astype(F32) * signs).astype(BF16)
            acc[m] = dot_nt(dy, ar_ref[:width])
            for lag in (1, 2):
                acc[m] += led(
                    dot_nt(dy, ar_ref[lag * width : (lag + 1) * width]), lag, spans[m]
                )
        for lag in (0, 1, 2):
            total = 0.0
            for m in range(2):
                u = u_ref[m]
                if lag:
                    u = lagged(u.astype(F32), lag, spans[m]).astype(BF16)
                total = total + dot_tn(u, dy_ref[m])
            dar_ref[lag * width : (lag + 1) * width, :] = total.astype(BF16)

    table = spread(row_ref[0], rows)
    for m in range(2):
        span = spans[m]
        for j in range(rows // span):
            part = slice(j * span, (j + 1) * span)
            conv = dot_nn(table[:span, :span], both[m, part, :])
            plus = conv[:, :width].astype(BF16)
            minus = (conv[:, width:] * signs[part]).astype(BF16)
            acc[m, part, :] += dot_nt(plus, w_ref[0, 0]) + dot_nt(minus, w_ref[0, 1])
    for p in range(2):
        total = dot_tn(ul_ref[0, p, 0], dy_ref[0]) + dot_tn(ul_ref[0, p, 1], dy_ref[1])
        dw_ref[0, p] = total.astype(BF16)

    @pl.when(k == pl.num_programs(0) - 1)
    def _():
        du_ref[...] = acc[...].astype(BF16)


def backward_mix(spans, dy, u, table, w, ul, ar):
    count = table.shape[0]
    _, rows, width = dy.shape
    full = lambda *shape: pl.BlockSpec(shape, lambda k: (0,) * len(shape))
    return pl.pallas_call(
        functools.partial(backward_kernel, spans),
        grid=(count,),
        out_shape=[
            jax.ShapeDtypeStruct((count, 2, width, width), BF16),
            jax.ShapeDtypeStruct((3 * width, width), BF16),
            jax.ShapeDtypeStruct((2, rows, width), BF16),
        ],
        in_specs=[
            full(2, rows, width),
            full(2, rows, width),
            pl.BlockSpec((1, 1, 2 * rows), lambda k: (k, 0, 0)),
            pl.BlockSpec((1, 2, width, width), lambda k: (k, 0, 0, 0)),
            pl.BlockSpec((1, 2, 2, rows, width), lambda k: (k, 0, 0, 0, 0)),
            full(3 * width, width),
        ],
        out_specs=[
            pl.BlockSpec((1, 2, width, width), lambda k: (k, 0, 0, 0)),
            full(3 * width, width),
            full(2, rows, width),
        ],
        scratch_shapes=[pltpu.VMEM((2, rows, 2 * width), BF16), pltpu.VMEM((2, rows, width), F32)],
        compiler_params=params(),
        name="backward_mix",
    )(dy, u, table, w, ul, ar)


def mix_back_kernel(seq_count, line, *refs):
    (layout_ref, row_ref, ar_ref, x_ref, scale_ref, cot_ref, mlp_ref, w_hbm, ul_hbm) = refs[:9]
    large = refs[9:16]
    (tg_ref, dw_ref, dar_ref, gg_ref, ug_ref, dg_ref, small_ref) = refs[16:23]
    (keep, dsig, acc, conv, du_in, ul_buf, w_buf, dar) = refs[23:31]
    (deep, deep_in, deep_run, wide, wide_in, wide_side, wide_run) = refs[31:38]
    (g_own, g_pair, g_side, g_sum, g_line) = refs[38:43]
    (dy, u_ref, z_ref, gb_ref, ub_ref, mixed_ref, hg_ref) = held = refs[43:50]
    (load_sem, dus, dur, ps, pr, zs, zr, wps, wpr, ws, wr, wzs, wzr, gs, gr) = refs[50:]
    s, z, c, g = place(seq_count, line)
    twin = {"grp": g + 1 - 2 * c}
    rows, width = dy.shape[1], dy.shape[2]
    block = x_ref.shape[1]
    short = [layout_ref[0, m].astype(F32) for m in range(2)]
    count = w_hbm.shape[0]
    per_chip = 2 * count // line
    n = per_chip * width // CORES
    ar_rows = ar_ref.shape[0]
    ar_share = ar_rows // (line * CORES)
    lanes = 128
    ar_chunks = ar_rows // lanes
    share = gg_ref.shape[0]
    mine = pl.ds(pl.multiple_of(s * block, block), block)
    low = (z < line // 2).astype(jnp.int32)

    def dest(i):
        return low * (line - 1 - 2 * i) + i

    def load(i):
        return pltpu.make_async_copy(
            ul_hbm.at[pl.ds(dest(i) * per_chip, per_chip)], ul_buf.at[i % 2], load_sem.at[i % 2]
        )

    load_w = pltpu.make_async_copy(w_hbm, w_buf, load_sem.at[2])
    fetch = [pltpu.make_async_copy(large[i], held[i], load_sem.at[3 + i]) for i in range(7)]
    for x in fetch[:2] + [load(0), load(1)] + fetch[2:] + [load_w]:
        x.start()
    greet(seq_count, line, s, z, c, g, twin=True, side=True, whole_line=True)

    def ar_place(i):
        at = s * ar_chunks + i
        lag = lax.div(at, width // lanes)
        col = lax.rem(at, width // lanes)
        return lag, pl.ds(pl.multiple_of(col * lanes, lanes), lanes)

    for x in fetch[:2]:
        x.wait()
    for i in range(ar_chunks):
        lag, cols = ar_place(i)
        total = 0.0
        for m in range(2):
            v = lagged_by(u_ref[m, :, cols].astype(F32), lag, short[m]).astype(BF16)
            total = total + dot_tn(v, dy[m])
        dar[i * lanes : (i + 1) * lanes, :] = total.astype(BF16)
    for l in range(line):
        for cc in range(CORES):
            r = (l * CORES + cc) * ar_share
            deep[cc, l, n:, :] = dar[r : r + ar_share, :]

    def twin_deep(i):
        l = dest(i)
        return remote(deep.at[1 - c, l], deep_in.at[l], ps.at[i], pr.at[i], twin)

    def hop(run, own, send, recv, way, t, first):
        target = line - 1 - t if way == 0 else t
        src = own(target) if first else run.at[way, t]
        to = g + CORES if way == 0 else g - CORES
        return remote(src, run.at[way, t], send.at[way, t], recv.at[way, t], {"grp": to})

    def deep_own(l):
        return deep_in.at[l]

    def wide_own(l):
        return wide_in.at[s, l]

    deep_line = (deep_run, deep_own, zs, zr)
    wide_line = (wide_run, wide_own, wzs, wzr)

    def begin(kind, t):
        for way in (0, 1):

            @pl.when(z == 0 if way == 0 else z == line - 1)
            def _():
                hop(*kind, way, t, True).start()

    def relay(kind, phase):
        run, own = kind[0], kind[1]
        for way in (0, 1):
            for t in range(phase):
                at = phase - t if way == 0 else line - 1 - (phase - t)
                target = line - 1 - t if way == 0 else t

                @pl.when(z == at)
                def _():
                    hop(*kind, way, t, False).wait_recv()
                    mixed = run[way, t].astype(F32) + own(target)[...].astype(F32)
                    run[way, t] = mixed.astype(BF16)
                    hop(*kind, way, t, False).start()

    def compute(i):
        l = dest(i)
        load(i).wait()
        for j in range(per_chip):
            val = dot_tn(ul_buf[i % 2, j, 0], dy[0]) + dot_tn(ul_buf[i % 2, j, 1], dy[1])
            val = val.astype(BF16)
            for cc in range(CORES):
                lo, hi = max(j * width, cc * n), min((j + 1) * width, (cc + 1) * n)
                if lo < hi:
                    deep[cc, l, lo - cc * n : hi - cc * n, :] = val[lo - j * width : hi - j * width]
        twin_deep(i).start()
        if i + 2 < line:
            load(i + 2).start()

    def combine(i):
        l = dest(i)
        twin_deep(i).wait_recv()
        deep_in[l] = (deep[c, l].astype(F32) + deep_in[l].astype(F32)).astype(BF16)
        if i < line - 1:
            begin(deep_line, i)

    compute(0)
    compute(1)
    combine(0)

    span_f = gb_ref.shape[1] // seq_count
    down_share = dg_ref.shape[0]
    for x in fetch[2:]:
        x.wait()

    @pl.loop(0, seq_count)
    def _(j):
        part = pl.ds(pl.multiple_of(j * span_f, span_f), span_f)
        for which, back in ((0, gb_ref), (1, ub_ref)):
            val = dot_tn(z_ref[...], back[:, part]).astype(BF16)
            for k in range(seq_count):
                for l in range(line):
                    for cc in range(CORES):
                        r = ((k * line + l) * CORES + cc) * share
                        wide[cc, k, l, which * share : (which + 1) * share, part] = val[
                            r : r + share
                        ]
        val = dot_tn(mixed_ref[:, part], cot_ref[...]).astype(BF16)
        for l in range(line):
            for cc in range(CORES):
                r = (l * CORES + cc) * down_share
                for q in range(down_share // share):
                    wide[cc, j, l, 2 * share :, q * width : (q + 1) * width] = val[
                        r + q * share : r + (q + 1) * share
                    ]
    wide_twin = remote(wide.at[1 - c], wide_in, wps, wpr, twin)
    wide_twin.start()

    for i in range(2, line):
        compute(i)
        combine(i - 1)
    combine(line - 1)

    wide_twin.wait_recv()
    for k in range(seq_count):

        @pl.loop(0, line)
        def _(l):
            mixed = wide[c, k, l].astype(F32) + wide_in[k, l].astype(F32)
            wide_in[k, l] = mixed.astype(BF16)

    sides = []
    for j in range(1, seq_count):
        to = lax.rem(s + j, seq_count)
        sides.append(
            remote(wide_in.at[to], wide_side.at[j - 1], ws.at[j - 1], wr.at[j - 1], {"seq": to})
        )
        sides[-1].start()

    signs = signs_of(rows)
    for m in range(2):
        dsig[m] = (dy[m].astype(F32) * signs).astype(BF16)
        keep[m] = reach(rows, short[m])
    acc[...] = jnp.zeros_like(acc)
    for i in range(ar_chunks):
        lag, cols = ar_place(i)
        for m in range(2):
            val = dot_nt(dy[m], ar_ref[i * lanes : (i + 1) * lanes, :])
            acc[m, :, cols] += led_by(val, lag, short[m])
    load_w.wait()

    def filter_step(k):
        table = shifted(row_ref[pl.ds(s * count + k, 1), :], rows)
        for m in range(2):
            kept_table = table * keep[m]
            conv[0] = dot_nn(kept_table, dy[m]).astype(BF16)
            conv[1] = (dot_nn(kept_table, dsig[m]) * signs).astype(BF16)
            acc[m] += dot_nt(conv[0], w_buf[k, 0]) + dot_nt(conv[1], w_buf[k, 1])

    half = count // 2
    pl.loop(0, half)(filter_step)
    for phase in range(1, line - 2):
        relay(deep_line, phase)
    pl.loop(half, count)(filter_step)
    conv[...] = acc[...].astype(BF16)
    du_copies = []
    for i in range(1, seq_count):
        to = lax.rem(s + i, seq_count)
        du_copies.append(
            remote(
                conv.at[:, pl.ds(pl.multiple_of(to * block, block), block), :],
                du_in.at[i - 1],
                dus.at[i - 1],
                dur.at[i - 1],
                {"seq": to},
            )
        )
        du_copies[-1].start()
    if line > 2:
        relay(deep_line, line - 2)

    for x in du_copies:
        x.wait_recv()
    gain = jnp.zeros((1, width), F32)
    for m in range(2):
        grad = conv[m, mine, :].astype(F32)
        for i in range(seq_count - 1):
            grad = grad + du_in[i, m].astype(F32)
        x = x_ref[m].astype(F32)
        inv = lax.rsqrt(jnp.mean(x * x, axis=-1, keepdims=True) + EPSILON)
        scaled = grad * scale_ref[0:1, :]
        gain = gain + jnp.sum(grad * x * inv, axis=0, keepdims=True)
        centre = jnp.mean(scaled * x, axis=-1, keepdims=True)
        tg_ref[m] = hg_ref[m] + inv * scaled - x * (inv * inv * inv) * centre
    g_own[...] = jnp.zeros_like(g_own)
    g_own[0:1, :] = gain
    g_own[1:2, :] = mlp_ref[0:1, :]
    small_pair = remote(g_own, g_pair, gs.at[0], gr.at[0], twin)
    small_pair.start()

    for x in sides:
        x.wait_recv()

    @pl.loop(0, line)
    def _(l):
        mixed = wide_in[s, l].astype(F32)
        for j in range(seq_count - 1):
            mixed = mixed + wide_side[j, l].astype(F32)
        wide_in[s, l] = mixed.astype(BF16)

    for t in range(line - 1):
        begin(wide_line, t)

    small_pair.wait()
    g_own[...] = g_own[...] + g_pair[...]
    small_sides = []
    for j in range(1, seq_count):
        small_sides.append(
            remote(
                g_own, g_side.at[j - 1], gs.at[j], gr.at[j], {"seq": lax.rem(s + j, seq_count)}
            )
        )
        small_sides[-1].start()

    dw_ref[...] = deep_in[z, :n, :].astype(F32)
    dar_ref[...] = deep_in[z, n:, :].astype(F32)
    for x in small_sides:
        x.wait()
    total = g_own[...]
    for j in range(seq_count - 1):
        total = total + g_side[j]
    g_sum[...] = total
    small_lines = []
    for j in range(1, line):
        small_lines.append(
            remote(
                g_sum,
                g_line.at[j - 1],
                gs.at[seq_count - 1 + j],
                gr.at[seq_count - 1 + j],
                {"grp": lax.rem(g + CORES * j, CORES * line)},
            )
        )
        small_lines[-1].start()

    def last(kind, add):
        for t in range(line - 1):
            for way in (0, 1):
                target = line - 1 - t if way == 0 else t

                @pl.when(z == target)
                def _():
                    hop(*kind, way, t, False).wait_recv()
                    add(kind[0][way, t].astype(F32))

    def add_deep(val):
        dw_ref[...] += val[:n]
        dar_ref[...] += val[n:]

    def add_wide(val):
        gg_ref[...] += val[:share]
        ug_ref[...] += val[share : 2 * share]
        for q in range(down_share // share):
            dg_ref[q * share : (q + 1) * share, :] += val[2 * share :, q * width : (q + 1) * width]

    last(deep_line, add_deep)
    for phase in range(1, line - 1):
        relay(wide_line, phase)
    own = wide_in[s, z].astype(F32)
    gg_ref[...] = own[:share]
    ug_ref[...] = own[share : 2 * share]
    for q in range(down_share // share):
        dg_ref[q * share : (q + 1) * share, :] = own[2 * share :, q * width : (q + 1) * width]
    last(wide_line, add_wide)

    for x in small_lines:
        x.wait()
    total = g_sum[...]
    for j in range(line - 1):
        total = total + g_line[j]
    at = (s * (CORES * line) + g) * (width // (seq_count * CORES * line))
    small_ref[...] = pltpu.roll(total, lax.rem(width - at, width), 1)

    for x in sides + du_copies:
        x.wait_send()
    wide_twin.wait_send()
    for i in range(line):
        twin_deep(i).wait_send()
    for kind in (deep_line, wide_line):
        for t in range(line - 1):
            for way in (0, 1):
                target = line - 1 - t if way == 0 else t

                @pl.when(z < target if way == 0 else z > target)
                def _():
                    hop(*kind, way, t, False).wait_send()


def mix_back(
    seq_count, line, layout, dy, u, filters, w, ul, ar, x, hg, scale, mlp, mlp_grad, shares
):
    z, gate_back, up_back, mixed, cot = mlp
    share, down_share, deep_share, ar_share = shares
    _, block, width = x.shape
    rows = block * seq_count
    count = w.shape[0]
    per_chip = 2 * count // line
    small = (8, width)
    hidden_units = gate_back.shape[1]
    part = (2 * share + down_share * width // hidden_units, hidden_units)
    out_shape = [
        jax.ShapeDtypeStruct((2, block, width), F32),
        jax.ShapeDtypeStruct((deep_share, width), F32),
        jax.ShapeDtypeStruct((ar_share, width), F32),
        jax.ShapeDtypeStruct((share, hidden_units), F32),
        jax.ShapeDtypeStruct((share, hidden_units), F32),
        jax.ShapeDtypeStruct((down_share, width), F32),
        jax.ShapeDtypeStruct(small, F32),
    ]
    deep = (deep_share + ar_share, width)
    scratch = [
        pltpu.VMEM((2, rows, rows), BF16),
        pltpu.VMEM((2, rows, width), BF16),
        pltpu.VMEM((2, rows, width), F32),
        pltpu.VMEM((2, rows, width), BF16),
        pltpu.VMEM((seq_count - 1, 2, block, width), BF16),
        pltpu.VMEM((2, per_chip, 2, rows, width), BF16),
        pltpu.VMEM(w.shape, BF16),
        pltpu.VMEM(ar.shape, BF16),
        pltpu.VMEM((CORES, line) + deep, BF16),
        pltpu.VMEM((line,) + deep, BF16),
        pltpu.VMEM((2, line - 1) + deep, BF16),
        pltpu.VMEM((CORES, seq_count, line) + part, BF16),
        pltpu.VMEM((seq_count, line) + part, BF16),
        pltpu.VMEM((seq_count - 1, line) + part, BF16),
        pltpu.VMEM((2, line - 1) + part, BF16),
        pltpu.VMEM(small, F32),
        pltpu.VMEM(small, F32),
        pltpu.VMEM((seq_count - 1,) + small, F32),
        pltpu.VMEM(small, F32),
        pltpu.VMEM((line - 1,) + small, F32),
    ]
    large = [dy, u, z, gate_back, up_back, mixed, hg]
    scratch += [pltpu.VMEM(v.shape, v.dtype) for v in large]
    scratch += [
        DMA((10,)),
        DMA((seq_count - 1,)),
        DMA((seq_count - 1,)),
        DMA((line,)),
        DMA((line,)),
        DMA((2, line - 1)),
        DMA((2, line - 1)),
        DMA,
        DMA,
        DMA((seq_count - 1,)),
        DMA((seq_count - 1,)),
        DMA((2, line - 1)),
        DMA((2, line - 1)),
        DMA((seq_count + line,)),
        DMA((seq_count + line,)),
    ]
    return pl.pallas_call(
        functools.partial(mix_back_kernel, seq_count, line),
        out_shape=out_shape,
        in_specs=[pl.BlockSpec(memory_space=pltpu.SMEM)] + [WHOLE] * 6 + [ANY] * 9,
        out_specs=[WHOLE] * 7,
        scratch_shapes=scratch,
        compiler_params=params(6),
        name="mix_back",
    )(layout, filters, ar, x, scale, cot, mlp_grad, w, ul, *large)


def kept(rows, short, lag):
    pos = lax.broadcasted_iota(jnp.int32, (rows, 1), 0)
    whole = (pos >= lag).astype(F32)
    return whole * (1.0 - short * (1.0 - (lax.rem(pos, rows // 4) >= lag).astype(F32)))


def lagged_by(values, lag, short):
    rows = values.shape[0]
    one = pltpu.roll(values, 1, 0) * kept(rows, short, 1)
    two = pltpu.roll(values, 2, 0) * kept(rows, short, 2)
    return jnp.where(lag == 0, values, jnp.where(lag == 1, one, two))


def led_by(values, lag, short):
    rows = values.shape[0]
    one = pltpu.roll(values * kept(rows, short, 1), rows - 1, 0)
    two = pltpu.roll(values * kept(rows, short, 2), rows - 2, 0)
    return jnp.where(lag == 0, values, jnp.where(lag == 1, one, two))


def reach(rows, short):
    down = lax.broadcasted_iota(jnp.int32, (rows, rows), 0)
    over = lax.broadcasted_iota(jnp.int32, (rows, rows), 1)
    same = (lax.div(down, rows // 4) == lax.div(over, rows // 4)).astype(F32)
    return ((over >= down).astype(F32) * (1.0 - short * (1.0 - same))).astype(BF16)


def shifted(row, rows):
    wide = jnp.broadcast_to(row, (rows, rows))
    return pltpu.roll(wide, 0, 1, stride=1, stride_axis=0).astype(BF16)


def mix_front_kernel(seq_count, line, *refs):
    (layout_ref, tok_ref, row_ref, mix_gain, mlp_gain, cot_ref, spec_hbm, ar_hbm) = refs[:8]
    wide_in = refs[8:11]
    (w_hbm, ul_hbm, u_hbm) = refs[11:14]
    results = refs[14:20]
    dy_hbm = refs[20]
    (ar_ref, gain_out, mlp_ref) = refs[21:24]
    (x_all, both, acc, y_bf, y_in, w_buf, ul_buf, keep, hid, dz, dy_own) = refs[24:35]
    (z_ref, gb_ref, ub_ref, mixed_ref, hg_ref, out_ref) = local = refs[35:41]
    wide_buf = refs[41:44]
    (g_pad, g_own, g_side, g_sum, g_line, g_all, g_twin) = refs[44:51]
    (load_sem, ul_sem, w_sem, ts, tr, ys, yr, zs, zr, hs, hr) = refs[51:62]
    (ps, pr, ws, wr, wps, wpr, gs, gr, ds_, dr_, end_sem) = refs[62:]
    s, z, c, g = place(seq_count, line)
    twin = {"grp": g + 1 - 2 * c}
    rows, width = x_all.shape[1], x_all.shape[2]
    block = tok_ref.shape[1]
    n = spec_hbm.shape[0]
    hn = n // 2
    blocks = ul_buf.shape[0]
    count = blocks // 2
    per_chip = blocks // line
    lanes = 128
    wide = range(3)
    mine = pl.ds(pl.multiple_of(s * block, block), block)
    short = [layout_ref[0, m].astype(F32) for m in range(2)]

    def piece(l, h):
        return w_buf.at[l, pl.ds(pl.multiple_of(c * n + h * hn, hn), hn), :]

    def wide_own(i, l):
        return wide_buf[i].at[s, l, c]

    load_w = [
        pltpu.make_async_copy(spec_hbm.at[pl.ds(h * hn, hn)], piece(z, h), load_sem.at[h])
        for h in range(2)
    ]
    load_ar = pltpu.make_async_copy(ar_hbm, ar_ref.at[z, c], load_sem.at[2])
    loads = [pltpu.make_async_copy(wide_in[i], wide_own(i, z), load_sem.at[3 + i]) for i in wide]
    for x in load_w + [load_ar] + loads:
        x.start()
    at = (s * (CORES * line) + g) * (width // (seq_count * CORES * line))
    g_pad[...] = jnp.zeros_like(g_pad)
    g_pad[0:1, : mix_gain.shape[1]] = mix_gain[...].astype(F32)
    g_pad[1:2, : mlp_gain.shape[1]] = mlp_gain[...].astype(F32)
    g_own[...] = pltpu.roll(g_pad[...], at, 1).astype(BF16)
    greet(seq_count, line, s, z, c, g, twin=True, side=True, whole_line=True)

    gain_sides = []
    toks = []
    for i in range(1, seq_count):
        to = {"seq": lax.rem(s + i, seq_count)}
        gain_sides.append(remote(g_own, g_side.at[i - 1], gs.at[i - 1], gr.at[i - 1], to))
        gain_sides[-1].start()
    for i in range(1, seq_count):
        to = {"seq": lax.rem(s + i, seq_count)}
        toks.append(remote(tok_ref, x_all.at[:, mine, :], ts.at[i - 1], tr.at[i - 1], to))
        toks[-1].start()

    def onward(way):
        return {"grp": g + CORES if way == 0 else g - CORES}

    def early_own(i, l):
        return ar_ref.at[l, c] if i == 3 else wide_own(i, l)

    def early_hops(way, t, origin):
        hops = []
        for i in range(4):
            if t > 0:
                src = early_own(i, origin)
            else:
                src = ar_hbm if i == 3 else wide_in[i]
            hops.append(
                remote(src, early_own(i, origin), hs.at[i, way, t], hr.at[i, way, t], onward(way))
            )
        return hops

    def deep_hops(h):
        def build(way, t, origin):
            src = spec_hbm.at[pl.ds(h * hn, hn)] if t == 0 else piece(origin, h)
            dst = piece(origin, h)
            return [remote(src, dst, zs.at[h, way, t], zr.at[h, way, t], onward(way))]

        return build

    def first(build):
        for way in (0, 1):
            sends, _, origin, _ = line_conditions(line, z, way, 0)

            @pl.when(sends)
            def _():
                for x in build(way, 0, origin):
                    x.start()

    def arrive(build, t, after):
        for way in (0, 1):
            _, receives, _, origin = line_conditions(line, z, way, t)

            @pl.when(receives)
            def _():
                for x in build(way, t, origin):
                    x.wait_recv()
                if t + 1 < line - 1:
                    sends = line_conditions(line, z, way, t + 1)[0]

                    @pl.when(sends)
                    def _():
                        for x in build(way, t + 1, origin):
                            x.start()

                after(origin)

    def sent(build):
        for t in range(line - 1):
            for way in (0, 1):
                sends, _, origin, _ = line_conditions(line, z, way, t)

                @pl.when(sends)
                def _():
                    for x in build(way, t, origin):
                        x.wait_send()

    def sides(l, own=False):
        copies = []
        for i in wide:
            for j in range(1, seq_count):
                src = wide_in[i] if own else wide_own(i, l)
                to = {"seq": lax.rem(s + j, seq_count)}
                copies.append(
                    remote(src, wide_own(i, l), ws.at[i, l, j - 1], wr.at[i, l, j - 1], to)
                )
        return copies

    def begin_sides(l):
        for x in sides(l):
            x.start()

    def twin_deep(l, h):
        return remote(piece(l, h), piece(l, h), ps.at[h, l], pr.at[h, l], twin)

    first(early_hops)
    total = g_own[...]
    for i, x in enumerate(gain_sides):
        x.wait_recv()
        total = total + g_side[i]
    g_sum[...] = total
    gain_lines = []
    for j in range(1, line):
        k = seq_count - 2 + j
        to = {"grp": lax.rem(g + CORES * j, CORES * line)}
        gain_lines.append(remote(g_sum, g_line.at[j - 1], gs.at[k], gr.at[k], to))
        gain_lines[-1].start()
    first(deep_hops(0))
    for x in sides(z, True):
        x.start()
    x_all[:, mine, :] = tok_ref[...]
    for h in range(2):
        load_w[h].wait()
        twin_deep(z, h).start()
    for x in loads + [load_ar]:
        x.wait()
    for m in range(2):
        keep[m] = reach(rows, short[m])
    arrive(early_hops, 0, begin_sides)
    first(deep_hops(1))
    total = g_sum[...]
    for j, x in enumerate(gain_lines):
        x.wait_recv()
        total = total + g_line[j]
    g_all[...] = total
    k = seq_count + line - 2
    gain_twin = remote(g_all, g_twin, gs.at[k], gr.at[k], twin)
    gain_twin.start()
    for x in toks:
        x.wait_recv()
    gain_twin.wait_recv()
    gain = g_all[...].astype(F32) + g_twin[...].astype(F32)
    gain_out[...] = gain[:8]

    signs = signs_of(rows)
    for m in range(2):
        x = x_all[m].astype(F32)
        inv = lax.rsqrt(jnp.mean(x * x, axis=-1, keepdims=True) + EPSILON)
        u = (x * inv * gain[0:1, :]).astype(BF16)
        both[m, :, :width] = u
        both[m, :, width:] = (u.astype(F32) * signs).astype(BF16)
    u_store = pltpu.make_async_copy(both.at[:, :, pl.ds(0, width)], u_hbm, end_sem.at[0])
    u_store.start()

    def ul_store(k):
        part = pl.ds(2 * k, 2)
        return pltpu.make_async_copy(ul_buf.at[part], ul_hbm.at[part], ul_sem.at[k])

    def filter_step(k):
        table = shifted(row_ref[pl.ds(s * count + k, 1), :], rows)
        for m in range(2):
            val = dot_tn(table * keep[m], both[m])
            ul_buf[2 * k, m] = val[:, :width].astype(BF16)
            ul_buf[2 * k + 1, m] = (val[:, width:] * signs).astype(BF16)
        ul_store(k).start()

    def add_part(l, h):
        @pl.loop(0, 2)
        def _(m):
            total = 0.0
            for cc in range(CORES):
                lo, end = cc * n + h * hn, cc * n + (h + 1) * hn
                while lo < end:
                    j = lo // width
                    hi = min(end, (j + 1) * width)
                    left = ul_buf[l * per_chip + j, m, :, lo - j * width : hi - j * width]
                    total = total + dot_nn(left, w_buf[l, lo:hi, :])
                    lo = hi
            acc[m] += total

    def w_store(l):
        return pltpu.make_async_copy(w_buf.at[l], w_hbm.at[l], w_sem.at[l])

    def nothing(origin):
        pass

    def deep_arrive(t, h):
        arrive(deep_hops(h), t, lambda origin: twin_deep(origin, h).start())

    def deep_add(t, h):
        for way in (0, 1):
            _, receives, _, origin = line_conditions(line, z, way, t)

            @pl.when(receives)
            def _():
                twin_deep(origin, h).wait_recv()
                if h == 1:
                    w_store(origin).start()
                add_part(origin, h)

    half = count // 2
    acc[...] = jnp.zeros_like(acc)
    pl.loop(0, half)(filter_step)
    if line > 2:
        arrive(early_hops, 1, begin_sides)
    deep_arrive(0, 0)
    pl.loop(half, count)(filter_step)
    for h in range(2):
        twin_deep(z, h).wait_recv()
        add_part(z, h)
    w_store(z).start()
    deep_arrive(0, 1)
    for t in range(2, line - 1):
        arrive(early_hops, t, begin_sides)
    ar_twin = remote(ar_ref.at[:, c], ar_ref.at[:, c], wps.at[3, 0], wpr.at[3, 0], twin)
    ar_twin.start()
    for h in range(2):
        deep_add(0, h)

    ar_twin.wait_recv()
    ar_rows = ar_ref.shape[0] * ar_ref.shape[1] * ar_ref.shape[2]
    ar_all = ar_ref[...].reshape(ar_rows, width)
    chunks = ar_rows // lanes
    for i in range(chunks):
        place_at = s * chunks + i
        lag = lax.div(place_at, width // lanes)
        col = lax.rem(place_at, width // lanes)
        cols = pl.ds(pl.multiple_of(col * lanes, lanes), lanes)
        for m in range(2):
            v = lagged_by(both[m, :, cols].astype(F32), lag, short[m]).astype(BF16)
            acc[m] += dot_nn(v, ar_all[i * lanes : (i + 1) * lanes])

    def twin_wide(i, k):
        part = wide_buf[i].at[k, :, c]
        return remote(part, part, wps.at[i, k], wpr.at[i, k], twin)

    for t in range(1, line - 1):
        deep_arrive(t, 0)
        if t == line - 2:
            for l in range(line):
                for x in sides(l):
                    x.wait_recv()
            for i in wide:
                for k in range(seq_count):
                    twin_wide(i, k).start()
        deep_add(t, 0)
        deep_arrive(t, 1)
        deep_add(t, 1)

    y_bf[...] = acc[...].astype(BF16)
    y_copies = []
    for i in range(1, seq_count):
        to = lax.rem(s + i, seq_count)
        y_copies.append(
            remote(
                y_bf.at[:, pl.ds(pl.multiple_of(to * block, block), block), :],
                y_in.at[i - 1],
                ys.at[i - 1],
                yr.at[i - 1],
                {"seq": to},
            )
        )
        y_copies[-1].start()

    for i in wide:
        for k in range(seq_count):
            twin_wide(i, k).wait()
    sent(early_hops)
    for h in range(2):
        sent(deep_hops(h))
        for l in range(line):
            twin_deep(l, h).wait_send()
    for l in range(line):
        w_store(l).wait()
        for x in sides(l):
            x.wait_send()
    for x in toks + gain_sides + gain_lines + [ar_twin, gain_twin]:
        x.wait_send()
    for k in range(count):
        ul_store(k).wait()

    for m in range(2):
        part = slice(m * block, (m + 1) * block)
        hid[part, :] = tok_ref[m].astype(F32) + acc[m, mine, :]
    for i, x in enumerate(y_copies):
        x.wait_recv()
        for m in range(2):
            hid[m * block : (m + 1) * block, :] += y_in[i, m].astype(F32)
    h = hid[...]
    inv_two = lax.rsqrt(jnp.mean(h * h, axis=-1, keepdims=True) + EPSILON)
    mlp_scale = gain[1:2, :]
    z_ref[...] = (h * inv_two * mlp_scale).astype(BF16)
    dz[...] = jnp.zeros_like(dz)
    hidden_units = gb_ref.shape[1]
    step = hidden_units // seq_count
    root = 0.7978845608028654

    @pl.loop(0, seq_count)
    def _(j):
        part = pl.ds(pl.multiple_of(j * step, step), step)
        gate_w = wide_buf[0][:, :, :, :, part].reshape(width, step)
        up_w = wide_buf[1][:, :, :, :, part].reshape(width, step)
        down_w = wide_buf[2][j].reshape(step, width)
        gate = dot_nn(z_ref[...], gate_w)
        up = dot_nn(z_ref[...], up_w)
        back = dot_nt(cot_ref[...], down_w)
        square = gate * gate
        tan = jnp.tanh(root * (gate + 0.044715 * (square * gate)))
        share = 0.5 * (1.0 + tan)
        gelu = gate * share
        slope = share + 0.5 * gate * (1.0 - tan * tan) * (
            root * (1.0 + (3.0 * 0.044715) * square)
        )
        mixed_ref[:, part] = (gelu * up).astype(BF16)
        gate_back = (back * up * slope).astype(BF16)
        up_back = (back * gelu).astype(BF16)
        gb_ref[:, part] = gate_back
        ub_ref[:, part] = up_back
        dz[...] += dot_nt(gate_back, gate_w) + dot_nt(up_back, up_w)
    grad = dz[...]
    h = hid[...]
    scaled = grad * mlp_scale
    centre = jnp.mean(scaled * h, axis=-1, keepdims=True)
    dh = cot_ref[...].astype(F32) + inv_two * scaled - h * (inv_two * inv_two * inv_two) * centre
    mlp_ref[...] = jnp.zeros_like(mlp_ref)
    mlp_ref[0:1, :] = jnp.sum(grad * h * inv_two, axis=0, keepdims=True)
    for m in range(2):
        part = slice(m * block, (m + 1) * block)
        hg_ref[m] = dh[part]
        dy_own[m] = dh[part].astype(BF16)
    dy_copies = []
    for i in range(1, seq_count):
        to = {"seq": lax.rem(s + i, seq_count)}
        dy_copies.append(remote(dy_own, dy_hbm.at[:, mine, :], ds_.at[i - 1], dr_.at[i - 1], to))
        dy_copies[-1].start()
    ends = [pltpu.make_async_copy(dy_own, dy_hbm.at[:, mine, :], end_sem.at[1])]
    ends += [
        pltpu.make_async_copy(local[i], results[i], end_sem.at[2 + i]) for i in range(6)
    ]
    for x in ends[:6]:
        x.start()
    total = hid[...]
    for j in range(seq_count):
        down_w = wide_buf[2][j].reshape(step, width)
        total = total + dot_nn(mixed_ref[:, j * step : (j + 1) * step], down_w)
    for m in range(2):
        out_ref[m] = total[m * block : (m + 1) * block]
    ends[6].start()
    for x in y_copies:
        x.wait_send()
    for x in ends + [u_store]:
        x.wait()
    for x in dy_copies:
        x.wait()


def mix_front(seq_count, line, layout, tok, filters, gains, cot, spec, ar, wide):
    _, block, width = tok.shape
    rows = block * seq_count
    count = filters.shape[0] // seq_count
    hidden_units = wide[0].shape[1]
    small = (16, width)
    vmem = pltpu.VMEM
    out_shape = [
        jax.ShapeDtypeStruct((line, CORES * spec.shape[0], width), BF16),
        jax.ShapeDtypeStruct((2 * count, 2, rows, width), BF16),
        jax.ShapeDtypeStruct((2, rows, width), BF16),
    ]
    local = [
        ((2 * block, width), BF16),
        ((2 * block, hidden_units), BF16),
        ((2 * block, hidden_units), BF16),
        ((2 * block, hidden_units), BF16),
        ((2, block, width), F32),
        ((2, block, width), F32),
    ]
    out_shape += [jax.ShapeDtypeStruct(*x) for x in local]
    out_shape += [
        jax.ShapeDtypeStruct((2, rows, width), BF16),
        jax.ShapeDtypeStruct((line, CORES) + ar.shape, BF16),
        jax.ShapeDtypeStruct((8, width), F32),
        jax.ShapeDtypeStruct((8, width), F32),
    ]
    scratch = [
        vmem((2, rows, width), BF16),
        vmem((2, rows, 2 * width), BF16),
        vmem((2, rows, width), F32),
        vmem((2, rows, width), BF16),
        vmem((seq_count - 1, 2, block, width), BF16),
        vmem((line, CORES * spec.shape[0], width), BF16),
        vmem((2 * count, 2, rows, width), BF16),
        vmem((2, rows, rows), BF16),
        vmem((2 * block, width), F32),
        vmem((2 * block, width), F32),
        vmem((2, block, width), BF16),
    ]
    scratch += [vmem(*x) for x in local]
    scratch += [vmem((seq_count, line, CORES) + x.shape, BF16) for x in wide]
    scratch += [
        vmem(small, F32),
        vmem(small, BF16),
        vmem((seq_count - 1,) + small, BF16),
        vmem(small, BF16),
        vmem((line - 1,) + small, BF16),
        vmem(small, BF16),
        vmem(small, BF16),
        DMA((6,)),
        DMA((count,)),
        DMA((line,)),
        DMA((seq_count - 1,)),
        DMA((seq_count - 1,)),
        DMA((seq_count - 1,)),
        DMA((seq_count - 1,)),
        DMA((2, 2, line - 1)),
        DMA((2, 2, line - 1)),
        DMA((4, 2, line - 1)),
        DMA((4, 2, line - 1)),
        DMA((2, line)),
        DMA((2, line)),
        DMA((3, line, seq_count - 1)),
        DMA((3, line, seq_count - 1)),
        DMA((4, seq_count)),
        DMA((4, seq_count)),
        DMA((seq_count + line,)),
        DMA((seq_count + line,)),
        DMA((seq_count - 1,)),
        DMA((seq_count - 1,)),
        DMA((8,)),
    ]
    return pl.pallas_call(
        functools.partial(mix_front_kernel, seq_count, line),
        out_shape=out_shape,
        in_specs=[pl.BlockSpec(memory_space=pltpu.SMEM)] + [WHOLE] * 5 + [ANY] * 5,
        out_specs=[ANY] * 10 + [WHOLE] * 3,
        scratch_shapes=scratch,
        compiler_params=params(7),
        name="mix_front",
    )(layout, tok, filters, *gains, cot, spec, ar, *wide)


def finish_kernel(count, share, *refs):
    ins, small = refs[:count], refs[count]
    outs, first, second = refs[count + 1 : 2 * count + 1], refs[2 * count + 1], refs[2 * count + 2]
    held, sem = refs[2 * count + 3 : 3 * count + 3], refs[3 * count + 3]
    loads = [pltpu.make_async_copy(ins[i], held[i], sem.at[0, i]) for i in range(count)]
    stores = [pltpu.make_async_copy(held[i], outs[i], sem.at[1, i]) for i in range(count)]
    for x in loads:
        x.start()
    first[...] = small[0:1, :share]
    second[...] = small[1:2, :share]
    for x, y in zip(loads, stores):
        x.wait()
        y.start()
    for x in stores:
        x.wait()


def finish(share, arrays, small):
    count = len(arrays)
    row = jax.ShapeDtypeStruct((1, share), F32)
    return pl.pallas_call(
        functools.partial(finish_kernel, count, share),
        out_shape=[jax.ShapeDtypeStruct(x.shape, x.dtype) for x in arrays] + [row, row],
        in_specs=[ANY] * count + [WHOLE],
        out_specs=[ANY] * count + [WHOLE] * 2,
        scratch_shapes=[pltpu.VMEM(x.shape, x.dtype) for x in arrays] + [DMA((2, count))],
        compiler_params=params(),
        name="finish",
    )(*arrays, small)


def body(
    tokens,
    layout,
    filters,
    gain_mix,
    spectral_proj,
    ar_proj,
    gain_mlp,
    w_gate,
    w_up,
    w_down,
    out_grad,
):
    seq_count = lax.axis_size("seq")
    line = lax.axis_size("grp") // CORES
    s = lax.axis_index("seq")
    g = lax.axis_index("grp")
    block, width = tokens.shape[2], tokens.shape[3]
    rows = block * seq_count
    count = filters.shape[1] // seq_count
    hidden_units = w_gate.shape[1]
    spans = (rows, rows // 4)

    share = gain_mix.shape[0]
    ar_rows = ar_proj.shape[0] * CORES * line
    mine = lax.dynamic_slice(filters.T, (s * count, 0), (count, rows))[:, None, :]
    nothing = jnp.zeros((count, 1, rows), F32)
    back_table = jnp.concatenate([mine, nothing], axis=2)
    aligned = share % 16 == 0 and ar_proj.shape[0] % 16 == 0 and 2 * count % line == 0
    aligned = aligned and ar_rows % 128 == 0 and line > 2

    if aligned:
        own = tokens[:, 0]
        cot = out_grad.reshape(2 * block, width)
        flags = layout.reshape(1, 2)
        spec, ul, u, mlp_in, gate_back, up_back, mixed, dh, out, dy, ar, gains, mlp_grad = mix_front(
            seq_count,
            line,
            flags,
            own,
            filters.T,
            (gain_mix.reshape(1, share), gain_mlp.reshape(1, share)),
            cot,
            spectral_proj,
            ar_proj,
            (w_gate, w_up, w_down),
        )
        input_grad, dw, dar, gate_grad, up_grad, down_grad, small = mix_back(
            seq_count,
            line,
            flags,
            dy,
            u,
            filters.T,
            spec.reshape(count, 2, width, width),
            ul,
            ar.reshape(ar_rows, width),
            own,
            dh,
            gains,
            (mlp_in, gate_back, up_back, mixed, cot),
            mlp_grad,
            (share, w_down.shape[0], spectral_proj.shape[0], ar_proj.shape[0]),
        )
        dw, out, input_grad, down_grad, gate_grad, up_grad, dar, mix_grad, mlp_grad = finish(
            share, (dw, out, input_grad, down_grad, gate_grad, up_grad, dar), small
        )
        return (
            out.reshape(tokens.shape),
            input_grad.reshape(tokens.shape),
            mix_grad.reshape(share),
            dw,
            dar,
            mlp_grad.reshape(share),
            gate_grad,
            up_grad,
            down_grad,
        )

    swap = layout[0, 0] == 1
    own = jnp.where(swap, tokens[::-1, 0], tokens[:, 0])
    cotangent = jnp.where(swap, out_grad[::-1, 0], out_grad[:, 0])
    gains = jnp.zeros((16, 128), BF16)
    gains = gains.at[0, :share].set(gain_mix).at[1, :share].set(gain_mlp)
    x_all, spec, ar, gate_w, up_w, down_w, gains = gather_all(
        seq_count, line, own, (spectral_proj, ar_proj), (w_gate, w_up, w_down, gains)
    )
    ar_full = lax.dynamic_update_slice(
        jnp.zeros((3 * width, width), BF16), ar.reshape(ar_rows, width), (s * ar_rows, 0)
    )
    gains = gains.reshape(-1, 16, 128).astype(F32)
    mix_scale = gains[:, 0, :share].reshape(1, width)
    mlp_scale = gains[:, 1, :share].reshape(1, width)
    fore_table = jnp.concatenate([mine[:, :, :1], nothing, mine[:, :, :0:-1]], axis=2)
    split = spec.reshape(count, 2, width, width)
    ul, u, y = forward_mix(spans, x_all, mix_scale, fore_table, split, ar_full)
    mixer = side_sum(seq_count, line, y, 3).reshape(2 * block, width)
    spec = spec.reshape(count, 2, width, width)
    gate_w = gate_w.reshape(width, hidden_units)
    up_w = up_w.reshape(width, hidden_units)
    down_w = down_w.reshape(hidden_units, width)

    inputs = own.reshape(2 * block, width).astype(F32)
    cot = cotangent.reshape(2 * block, width)
    hidden = inputs + mixer
    inv_two = lax.rsqrt(jnp.mean(hidden * hidden, axis=-1, keepdims=True) + EPSILON)
    mlp_in = (hidden * inv_two * mlp_scale).astype(BF16)
    gate = dot_nn(mlp_in, gate_w)
    upval = dot_nn(mlp_in, up_w)
    product_val, gelu_pull = jax.vjp(lambda a, b: jax.nn.gelu(a) * b, gate, upval)
    mixed = product_val.astype(BF16)
    out = hidden + dot_nn(mixed, down_w)
    mixed_grad = dot_nt(cot, down_w)
    gate_back, up_back = gelu_pull(mixed_grad)
    gate_back = gate_back.astype(BF16)
    up_back = up_back.astype(BF16)
    mlp_in_grad = dot_nt(gate_back, gate_w) + dot_nt(up_back, up_w)
    scaled_two = mlp_in_grad * mlp_scale
    mlp_grad = jnp.sum(mlp_in_grad * hidden * inv_two, axis=0, keepdims=True)
    hidden_grad = (
        cot.astype(F32)
        + inv_two * scaled_two
        - hidden * inv_two**3 * jnp.mean(scaled_two * hidden, axis=-1, keepdims=True)
    )
    mixer_grad = hidden_grad.astype(BF16)

    down_grad = dot_tn(mixed, cot)
    gate_grad = dot_tn(mlp_in, gate_back)
    up_grad = dot_tn(mlp_in, up_back)
    dy = side_gather(seq_count, line, mixer_grad.reshape(2, block, width))
    dw, dar, du = backward_mix(spans, dy, u, back_table, spec, ul, ar_full)
    normed_grad = side_sum(seq_count, line, du, 4).reshape(2 * block, width)

    inv_one = lax.rsqrt(jnp.mean(inputs * inputs, axis=-1, keepdims=True) + EPSILON)
    scaled_one = normed_grad * mix_scale
    mix_grad = jnp.sum(normed_grad * inputs * inv_one, axis=0, keepdims=True)
    input_grad = (
        hidden_grad
        + inv_one * scaled_one
        - inputs * inv_one**3 * jnp.mean(scaled_one * inputs, axis=-1, keepdims=True)
    )

    dar = lax.dynamic_slice(dar, (s * ar_rows, 0), (ar_rows, width))
    deep = (dw.reshape(line, CORES, -1, width), dar.reshape(line, CORES, -1, width))
    wide = tuple(
        x.astype(BF16).reshape(seq_count, line, CORES, -1, x.shape[1])
        for x in (gate_grad, up_grad, down_grad)
    )
    small = jnp.concatenate([mix_grad, mlp_grad, jnp.zeros((6, width), F32)], axis=0)
    dw, dar, gate_grad, up_grad, down_grad, small = sum_all(seq_count, line, deep, wide, small)
    small = lax.dynamic_slice(small, (0, (s * CORES * line + g) * share), (2, share))

    def settle(x):
        x = x.reshape(2, 1, block, width)
        return jnp.where(swap, x[::-1], x)

    return (
        settle(out),
        settle(input_grad),
        small[0],
        dw,
        dar,
        small[1],
        gate_grad,
        up_grad,
        down_grad,
    )


def solution(mesh):
    placed = (
        P(None, "grp", "seq", None),
        P(None, "grp"),
        P(),
        P(("seq", "grp")),
        P(("seq", "grp"), None),
        P(("seq", "grp"), None),
        P(("seq", "grp")),
        P(("seq", "grp"), None),
        P(("seq", "grp"), None),
        P(("seq", "grp"), None),
        P(None, "grp", "seq", None),
    )
    return jax.shard_map(
        body,
        mesh=mesh,
        in_specs=placed,
        out_specs=(
            P(None, "grp", "seq", None),
            P(None, "grp", "seq", None),
            P(("seq", "grp")),
            P(("seq", "grp"), None),
            P(("seq", "grp"), None),
            P(("seq", "grp")),
            P(("seq", "grp"), None),
            P(("seq", "grp"), None),
            P(("seq", "grp"), None),
        ),
        check_vma=False,
    )
```

```python
import functools

import jax
import jax.numpy as jnp
from jax import lax
from jax.experimental import pallas as pl
from jax.experimental.pallas import tpu as pltpu
from jax.sharding import PartitionSpec as P

EPSILON = 1e-05
BF16 = jnp.bfloat16
F32 = jnp.float32
MESH = pl.DeviceIdType.MESH
DMA = pltpu.SemaphoreType.DMA
ANY = pl.BlockSpec(memory_space=pl.ANY)
WHOLE = pl.BlockSpec(memory_space=pltpu.VMEM)
VMEM_LIMIT = 60 * 1024 * 1024
CORES = 2


def dot_nn(a, b):
    return lax.dot_general(a, b, (((1,), (0,)), ((), ())), preferred_element_type=F32)


def dot_tn(a, b):
    return lax.dot_general(a, b, (((0,), (0,)), ((), ())), preferred_element_type=F32)


def dot_nt(a, b):
    return lax.dot_general(a, b, (((1,), (1,)), ((), ())), preferred_element_type=F32)


def params(collective_id=None):
    return pltpu.CompilerParams(
        collective_id=collective_id,
        has_side_effects=collective_id is not None,
        vmem_limit_bytes=VMEM_LIMIT,
    )


def remote(src, dst, send, recv, where):
    return pltpu.make_async_remote_copy(
        src_ref=src, dst_ref=dst, send_sem=send, recv_sem=recv, device_id=where, device_id_type=MESH
    )


def place(seq_count, line):
    s = lax.axis_index("seq")
    g = lax.axis_index("grp")
    return s, lax.div(g, CORES), lax.rem(g, CORES), g


def greet(seq_count, line, s, z, c, g, chain=False, twin=False, side=False, whole_line=False):
    barrier = pltpu.get_barrier_semaphore()

    def call(where):
        pl.semaphore_signal(barrier, inc=1, device_id=where, device_id_type=MESH)

    expected = (1 if twin else 0) + (seq_count - 1 if side else 0) + (line - 1 if whole_line else 0)
    if twin:
        call({"grp": g + 1 - 2 * c})
    if side:
        for i in range(1, seq_count):
            call({"seq": lax.rem(s + i, seq_count)})
    if whole_line:
        for j in range(1, line):
            call({"grp": lax.rem(g + CORES * j, CORES * line)})
    if chain:
        expected = expected + (z > 0).astype(jnp.int32) + (z < line - 1).astype(jnp.int32)

        @pl.when(z > 0)
        def _():
            call({"grp": g - CORES})

        @pl.when(z < line - 1)
        def _():
            call({"grp": g + CORES})

    pl.semaphore_wait(barrier, expected)


def line_conditions(line, z, way, t):
    if way == 0:
        return (z < line - 1) & (z >= t), z >= t + 1, z - t, z - 1 - t
    return (z > 0) & (z + t <= line - 1), z + t + 1 <= line - 1, z + t, z + 1 + t


def gather_kernel(seq_count, line, n_deep, n_wide, *refs):
    n_in = 1 + n_deep + n_wide
    ins, outs = refs[:n_in], refs[n_in : 2 * n_in]
    rest = refs[2 * n_in :]
    stage = rest[:n_in]
    (local_sem, tok_send, tok_recv, zs, zr, ws, wr, ps, pr, dps, dpr) = rest[n_in:]
    s, z, c, g = place(seq_count, line)
    twin = {"grp": g + 1 - 2 * c}
    tok, tok_out = ins[0], outs[0]
    rows = tok.shape[1]
    items = list(range(n_deep + n_wide))

    def own(i, l):
        out = outs[1 + i]
        return out.at[l, c] if i < n_deep else out.at[s, l, c]

    loads = [pltpu.make_async_copy(ins[i], stage[i], local_sem.at[0, i]) for i in range(n_in)]
    for x in loads:
        x.start()
    greet(seq_count, line, s, z, c, g, chain=True, twin=True, side=True)

    toks = []
    for i in range(1, seq_count):
        toks.append(
            remote(
                tok,
                tok_out.at[:, pl.ds(pl.multiple_of(s * rows, rows), rows), :],
                tok_send.at[i - 1],
                tok_recv.at[i - 1],
                {"seq": lax.rem(s + i, seq_count)},
            )
        )
        toks[-1].start()

    def hop(i, way, t, origin):
        src = ins[1 + i] if t == 0 else own(i, origin)
        to = g + CORES if way == 0 else g - CORES
        return remote(src, own(i, origin), zs.at[i, way, t], zr.at[i, way, t], {"grp": to})

    def hops(which, t):
        for way in (0, 1):
            sends, _, origin, _ = line_conditions(line, z, way, t)

            @pl.when(sends)
            def _():
                for i in which:
                    hop(i, way, t, origin).start()

    def arrive(which, t, after=None):
        for way in (0, 1):
            _, receives, _, origin = line_conditions(line, z, way, t)

            @pl.when(receives)
            def _():
                for i in which:
                    hop(i, way, t, origin).wait_recv()
                if after is not None:
                    after(origin)

    deep, wide = items[:n_deep], items[n_deep:]
    for t in range(line - 1):
        hops(wide, t)
        if t == 0:
            stores = []
            for i in range(n_in):
                loads[i].wait()
                dst = (
                    tok_out.at[:, pl.ds(pl.multiple_of(s * rows, rows), rows), :]
                    if i == 0
                    else own(i - 1, z)
                )
                stores.append(pltpu.make_async_copy(stage[i], dst, local_sem.at[1, i]))
                stores[-1].start()
        arrive(wide, t)
    hops(deep, 0)
    for x in stores:
        x.wait()
    sides = []
    for i in wide:
        for j in range(1, seq_count):
            part = outs[1 + i].at[s, :, c]
            sides.append(
                remote(
                    part,
                    part,
                    ws.at[i - n_deep, j - 1],
                    wr.at[i - n_deep, j - 1],
                    {"seq": lax.rem(s + j, seq_count)},
                )
            )
            sides[-1].start()

    def twin_wide(i, k):
        part = outs[1 + i].at[k, :, c]
        return remote(part, part, ps.at[i - n_deep, k], pr.at[i - n_deep, k], twin)

    def twin_deep(i, l):
        part = outs[1 + i].at[l, c]
        return remote(part, part, dps.at[i, l], dpr.at[i, l], twin)

    for i in wide:
        twin_wide(i, s).start()
    for i in deep:
        twin_deep(i, z).start()

    def pass_on(origin):
        for i in deep:
            twin_deep(i, origin).start()

    for t in range(line - 1):
        if t > 0:
            hops(deep, t)
        arrive(deep, t, pass_on)
    for x in sides:
        x.wait_recv()
    for i in wide:
        for j in range(1, seq_count):
            twin_wide(i, lax.rem(s + seq_count - j, seq_count)).start()
    for x in toks:
        x.wait_recv()
    for i in deep:
        for l in range(line):
            twin_deep(i, l).wait()
    for i in wide:
        for k in range(seq_count):
            twin_wide(i, k).wait()
    for x in toks + sides:
        x.wait_send()
    for t in range(line - 1):
        for way in (0, 1):
            sends, _, origin, _ = line_conditions(line, z, way, t)

            @pl.when(sends)
            def _():
                for i in items:
                    hop(i, way, t, origin).wait_send()


def gather_all(seq_count, line, tok, deep, wide):
    n_deep, n_wide = len(deep), len(wide)
    shapes = [
        jax.ShapeDtypeStruct((tok.shape[0], tok.shape[1] * seq_count, tok.shape[2]), tok.dtype)
    ]
    shapes += [jax.ShapeDtypeStruct((line, CORES) + x.shape, x.dtype) for x in deep]
    shapes += [jax.ShapeDtypeStruct((seq_count, line, CORES) + x.shape, x.dtype) for x in wide]
    arrays = [tok] + list(deep) + list(wide)
    n = len(arrays)
    scratch = [pltpu.VMEM(x.shape, x.dtype) for x in arrays]
    scratch += [
        DMA((2, n)),
        DMA((seq_count - 1,)),
        DMA((seq_count - 1,)),
        DMA((n_deep + n_wide, 2, line - 1)),
        DMA((n_deep + n_wide, 2, line - 1)),
        DMA((n_wide, seq_count - 1)),
        DMA((n_wide, seq_count - 1)),
        DMA((n_wide, seq_count)),
        DMA((n_wide, seq_count)),
        DMA((n_deep, line)),
        DMA((n_deep, line)),
    ]
    return pl.pallas_call(
        functools.partial(gather_kernel, seq_count, line, n_deep, n_wide),
        out_shape=shapes,
        in_specs=[ANY] * n,
        out_specs=[ANY] * n,
        scratch_shapes=scratch,
        compiler_params=params(1),
        name="gather_all",
    )(*arrays)


def side_gather_kernel(seq_count, line, x_ref, out_ref, local_sem, send, recv):
    s, z, c, g = place(seq_count, line)
    rows = x_ref.shape[1]
    mine = out_ref.at[:, pl.ds(pl.multiple_of(s * rows, rows), rows), :]
    local = pltpu.make_async_copy(x_ref, mine, local_sem)
    local.start()
    greet(seq_count, line, s, z, c, g, side=True)
    copies = []
    for i in range(1, seq_count):
        copies.append(
            remote(
                x_ref, mine, send.at[i - 1], recv.at[i - 1], {"seq": lax.rem(s + i, seq_count)}
            )
        )
        copies[-1].start()
    local.wait()
    for x in copies:
        x.wait()


def side_gather(seq_count, line, x):
    return pl.pallas_call(
        functools.partial(side_gather_kernel, seq_count, line),
        out_shape=jax.ShapeDtypeStruct((x.shape[0], x.shape[1] * seq_count, x.shape[2]), x.dtype),
        in_specs=[WHOLE],
        out_specs=WHOLE,
        scratch_shapes=[DMA, DMA((seq_count - 1,)), DMA((seq_count - 1,))],
        compiler_params=params(2),
        name="side_gather",
    )(x)


def side_sum_kernel(seq_count, line, x_ref, out_ref, slots, send, recv):
    s, z, c, g = place(seq_count, line)
    rows = out_ref.shape[1]
    greet(seq_count, line, s, z, c, g, side=True)
    copies = []
    for i in range(1, seq_count):
        to = lax.rem(s + i, seq_count)
        copies.append(
            remote(
                x_ref.at[:, pl.ds(pl.multiple_of(to * rows, rows), rows), :],
                slots.at[i - 1],
                send.at[i - 1],
                recv.at[i - 1],
                {"seq": to},
            )
        )
        copies[-1].start()
    total = x_ref[:, pl.ds(pl.multiple_of(s * rows, rows), rows), :].astype(F32)
    for i, x in enumerate(copies):
        x.wait_recv()
        total = total + slots[i].astype(F32)
    out_ref[...] = total
    for x in copies:
        x.wait_send()


def side_sum(seq_count, line, x, collective_id):
    rows = x.shape[1] // seq_count
    return pl.pallas_call(
        functools.partial(side_sum_kernel, seq_count, line),
        out_shape=jax.ShapeDtypeStruct((x.shape[0], rows, x.shape[2]), F32),
        in_specs=[WHOLE],
        out_specs=WHOLE,
        scratch_shapes=[
            pltpu.VMEM((seq_count - 1, x.shape[0], rows, x.shape[2]), x.dtype),
            DMA((seq_count - 1,)),
            DMA((seq_count - 1,)),
        ],
        compiler_params=params(collective_id),
        name=f"side_sum_{collective_id}",
    )(x)


def sum_kernel(seq_count, line, n_deep, n_wide, *refs):
    n = n_deep + n_wide
    ins, outs = refs[: n + 1], refs[n + 1 : 2 * n + 2]
    rest = refs[2 * n + 2 :]
    pair, side, chain = rest[:n], rest[n : n + n_wide], rest[n + n_wide : 2 * n + n_wide]
    rest = rest[2 * n + n_wide :]
    g_pair, g_side, g_line, g_a, g_b = rest[:5]
    (ps, pr, ws, wr, zs, zr, gs, gr) = rest[5:]
    s, z, c, g = place(seq_count, line)
    twin = {"grp": g + 1 - 2 * c}
    deep, wide = list(range(n_deep)), list(range(n_deep, n))
    small = ins[n]
    greet(seq_count, line, s, z, c, g, twin=True, side=True, whole_line=True)

    def theirs(i):
        return ins[i].at[:, 1 - c] if i < n_deep else ins[i].at[:, :, 1 - c]

    pairs = [remote(theirs(i), pair[i], ps.at[i], pr.at[i], twin) for i in range(n)]
    small_pair = remote(small, g_pair, gs.at[0], gr.at[0], twin)
    small_pair.start()
    for x in pairs[n_deep:] + pairs[:n_deep]:
        x.start()

    small_pair.wait()
    g_a[...] = small[...] + g_pair[...]
    small_sides = []
    for j in range(1, seq_count):
        small_sides.append(
            remote(
                g_a,
                g_side.at[j - 1],
                gs.at[j],
                gr.at[j],
                {"seq": lax.rem(s + j, seq_count)},
            )
        )
        small_sides[-1].start()

    for i in wide:
        pairs[i].wait_recv()
        for k in range(seq_count):

            @pl.loop(0, line)
            def _(l):
                mixed = ins[i][k, l, c].astype(F32) + pair[i][k, l].astype(F32)
                pair[i][k, l] = mixed.astype(BF16)

    sides = {}
    for i in wide:
        for j in range(1, seq_count):
            to = lax.rem(s + j, seq_count)
            sides[i, j] = remote(
                pair[i].at[to],
                side[i - n_deep].at[j - 1],
                ws.at[i - n_deep, j - 1],
                wr.at[i - n_deep, j - 1],
                {"seq": to},
            )
            sides[i, j].start()
    for i in deep:
        pairs[i].wait_recv()
        for l in range(line):
            pair[i][l] = (ins[i][l, c].astype(F32) + pair[i][l].astype(F32)).astype(BF16)

    for x in small_sides:
        x.wait()
    total = g_a[...]
    for j in range(seq_count - 1):
        total = total + g_side[j]
    g_b[...] = total
    small_lines = []
    for j in range(1, line):
        small_lines.append(
            remote(
                g_b,
                g_line.at[j - 1],
                gs.at[seq_count - 1 + j],
                gr.at[seq_count - 1 + j],
                {"grp": lax.rem(g + CORES * j, CORES * line)},
            )
        )
        small_lines[-1].start()

    def piece(i, l):
        return pair[i].at[l] if i < n_deep else pair[i].at[s, l]

    def run_line(which):
        def hop(i, way, t, dest, first):
            src = piece(i, dest) if first else chain[i].at[way, t]
            to = g + CORES if way == 0 else g - CORES
            return remote(src, chain[i].at[way, t], zs.at[i, way, t], zr.at[i, way, t], {"grp": to})

        for t in range(line - 1):
            for way in (0, 1):
                dest = line - 1 - t if way == 0 else t
                starts = z == 0 if way == 0 else z == line - 1
                relays = (z > 0) & (z < dest) if way == 0 else (z < line - 1) & (z > dest)

                @pl.when(starts)
                def _():
                    for i in which:
                        hop(i, way, t, dest, True).start()

                @pl.when(relays)
                def _():
                    for i in which:
                        hop(i, way, t, dest, False).wait_recv()
                        mixed = chain[i][way, t].astype(F32) + piece(i, dest)[...].astype(F32)
                        chain[i][way, t] = mixed.astype(BF16)
                        hop(i, way, t, dest, False).start()

        for i in which:
            outs[i][...] = piece(i, z)[...].astype(F32)
        for t in range(line - 1):
            for way in (0, 1):
                dest = line - 1 - t if way == 0 else t

                @pl.when((z == dest))
                def _():
                    for i in which:
                        hop(i, way, t, dest, False).wait_recv()
                        outs[i][...] += chain[i][way, t].astype(F32)

                @pl.when(z == 0 if way == 0 else z == line - 1)
                def _():
                    for i in which:
                        hop(i, way, t, dest, True).wait_send()

                @pl.when((z > 0) & (z < dest) if way == 0 else (z < line - 1) & (z > dest))
                def _():
                    for i in which:
                        hop(i, way, t, dest, False).wait_send()

    run_line(deep)
    for i in wide:
        for j in range(1, seq_count):
            sides[i, j].wait()

        @pl.loop(0, line)
        def _(l):
            mixed = pair[i][s, l].astype(F32)
            for j in range(1, seq_count):
                mixed = mixed + side[i - n_deep][j - 1, l].astype(F32)
            pair[i][s, l] = mixed.astype(BF16)

    run_line(wide)
    for x in pairs:
        x.wait_send()
    for x in small_lines:
        x.wait()
    total = g_b[...]
    for j in range(line - 1):
        total = total + g_line[j]
    outs[n][...] = total


def sum_all(seq_count, line, deep, wide, small):
    n_deep, n_wide = len(deep), len(wide)
    n = n_deep + n_wide
    shapes = [jax.ShapeDtypeStruct(x.shape[2:], F32) for x in deep]
    shapes += [jax.ShapeDtypeStruct(x.shape[3:], F32) for x in wide]
    shapes += [jax.ShapeDtypeStruct(small.shape, F32)]
    scratch = [pltpu.VMEM((line,) + x.shape[2:], BF16) for x in deep]
    scratch += [pltpu.VMEM((seq_count, line) + x.shape[3:], BF16) for x in wide]
    scratch += [pltpu.VMEM((seq_count - 1, line) + x.shape[3:], BF16) for x in wide]
    scratch += [pltpu.VMEM((2, line - 1) + x.shape[2:], BF16) for x in deep]
    scratch += [pltpu.VMEM((2, line - 1) + x.shape[3:], BF16) for x in wide]
    scratch += [
        pltpu.VMEM(small.shape, F32),
        pltpu.VMEM((seq_count - 1,) + small.shape, F32),
        pltpu.VMEM((line - 1,) + small.shape, F32),
        pltpu.VMEM(small.shape, F32),
        pltpu.VMEM(small.shape, F32),
        DMA((n,)),
        DMA((n,)),
        DMA((n_wide, seq_count - 1)),
        DMA((n_wide, seq_count - 1)),
        DMA((n, 2, line - 1)),
        DMA((n, 2, line - 1)),
        DMA((seq_count + line,)),
        DMA((seq_count + line,)),
    ]
    return pl.pallas_call(
        functools.partial(sum_kernel, seq_count, line, n_deep, n_wide),
        out_shape=shapes,
        in_specs=[WHOLE] * (n + 1),
        out_specs=[WHOLE] * (n + 1),
        scratch_shapes=scratch,
        compiler_params=params(5),
        name="sum_all",
    )(*deep, *wide, small)


def signs_of(rows):
    pos = lax.broadcasted_iota(jnp.int32, (rows, 1), 0)
    return 1.0 - 2.0 * lax.rem(pos, 2).astype(F32)


def lagged(values, lag, span):
    pos = lax.broadcasted_iota(jnp.int32, (values.shape[0], 1), 0)
    return jnp.where(lax.rem(pos, span) >= lag, pltpu.roll(values, lag, 0), 0.0)


def led(values, lag, span):
    rows = values.shape[0]
    pos = lax.broadcasted_iota(jnp.int32, (rows, 1), 0)
    return jnp.where(lax.rem(pos, span) < span - lag, pltpu.roll(values, rows - lag, 0), 0.0)


def spread(row, rows):
    wide = jnp.broadcast_to(row, (rows, row.shape[1]))
    return pltpu.roll(wide, 0, 1, stride=1, stride_axis=0)[:, :rows].astype(BF16)


def forward_kernel(spans, x_ref, gain_ref, row_ref, w_ref, ar_ref, ul_ref, u_ref, y_ref, both, acc):
    k = pl.program_id(0)
    rows, width = x_ref.shape[1], x_ref.shape[2]
    signs = signs_of(rows)

    @pl.when(k == 0)
    def _():
        for m in range(2):
            x = x_ref[m].astype(F32)
            inv = lax.rsqrt(jnp.mean(x * x, axis=-1, keepdims=True) + EPSILON)
            u = (x * inv * gain_ref[...]).astype(BF16)
            wide = u.astype(F32)
            u_ref[m] = u
            both[m, :, :width] = u
            both[m, :, width:] = (wide * signs).astype(BF16)
            acc[m] = dot_nn(u, ar_ref[:width])
            for lag in (1, 2):
                acc[m] += dot_nn(
                    lagged(wide, lag, spans[m]).astype(BF16),
                    ar_ref[lag * width : (lag + 1) * width],
                )

    table = spread(row_ref[0], rows)
    for m in range(2):
        span = spans[m]
        for j in range(rows // span):
            part = slice(j * span, (j + 1) * span)
            conv = dot_nn(table[:span, :span], both[m, part, :])
            plus = conv[:, :width].astype(BF16)
            minus = (conv[:, width:] * signs[part]).astype(BF16)
            ul_ref[0, 0, m, part, :] = plus
            ul_ref[0, 1, m, part, :] = minus
        acc[m] += dot_nn(ul_ref[0, 0, m], w_ref[0, 0]) + dot_nn(ul_ref[0, 1, m], w_ref[0, 1])

    @pl.when(k == pl.num_programs(0) - 1)
    def _():
        y_ref[...] = acc[...].astype(BF16)


def forward_mix(spans, x, gain, table, w, ar):
    count = table.shape[0]
    _, rows, width = x.shape
    full = lambda *shape: pl.BlockSpec(shape, lambda k: (0,) * len(shape))
    return pl.pallas_call(
        functools.partial(forward_kernel, spans),
        grid=(count,),
        out_shape=[
            jax.ShapeDtypeStruct((count, 2, 2, rows, width), BF16),
            jax.ShapeDtypeStruct((2, rows, width), BF16),
            jax.ShapeDtypeStruct((2, rows, width), BF16),
        ],
        in_specs=[
            full(2, rows, width),
            full(1, width),
            pl.BlockSpec((1, 1, 2 * rows), lambda k: (k, 0, 0)),
            pl.BlockSpec((1, 2, width, width), lambda k: (k, 0, 0, 0)),
            full(3 * width, width),
        ],
        out_specs=[
            pl.BlockSpec((1, 2, 2, rows, width), lambda k: (k, 0, 0, 0, 0)),
            full(2, rows, width),
            full(2, rows, width),
        ],
        scratch_shapes=[pltpu.VMEM((2, rows, 2 * width), BF16), pltpu.VMEM((2, rows, width), F32)],
        compiler_params=params(),
        name="forward_mix",
    )(x, gain, table, w, ar)


def backward_kernel(
    spans, dy_ref, u_ref, row_ref, w_ref, ul_ref, ar_ref, dw_ref, dar_ref, du_ref, both, acc
):
    k = pl.program_id(0)
    rows, width = dy_ref.shape[1], dy_ref.shape[2]
    signs = signs_of(rows)

    @pl.when(k == 0)
    def _():
        for m in range(2):
            dy = dy_ref[m]
            both[m, :, :width] = dy
            both[m, :, width:] = (dy.astype(F32) * signs).astype(BF16)
            acc[m] = dot_nt(dy, ar_ref[:width])
            for lag in (1, 2):
                acc[m] += led(
                    dot_nt(dy, ar_ref[lag * width : (lag + 1) * width]), lag, spans[m]
                )
        for lag in (0, 1, 2):
            total = 0.0
            for m in range(2):
                u = u_ref[m]
                if lag:
                    u = lagged(u.astype(F32), lag, spans[m]).astype(BF16)
                total = total + dot_tn(u, dy_ref[m])
            dar_ref[lag * width : (lag + 1) * width, :] = total.astype(BF16)

    table = spread(row_ref[0], rows)
    for m in range(2):
        span = spans[m]
        for j in range(rows // span):
            part = slice(j * span, (j + 1) * span)
            conv = dot_nn(table[:span, :span], both[m, part, :])
            plus = conv[:, :width].astype(BF16)
            minus = (conv[:, width:] * signs[part]).astype(BF16)
            acc[m, part, :] += dot_nt(plus, w_ref[0, 0]) + dot_nt(minus, w_ref[0, 1])
    for p in range(2):
        total = dot_tn(ul_ref[0, p, 0], dy_ref[0]) + dot_tn(ul_ref[0, p, 1], dy_ref[1])
        dw_ref[0, p] = total.astype(BF16)

    @pl.when(k == pl.num_programs(0) - 1)
    def _():
        du_ref[...] = acc[...].astype(BF16)


def backward_mix(spans, dy, u, table, w, ul, ar):
    count = table.shape[0]
    _, rows, width = dy.shape
    full = lambda *shape: pl.BlockSpec(shape, lambda k: (0,) * len(shape))
    return pl.pallas_call(
        functools.partial(backward_kernel, spans),
        grid=(count,),
        out_shape=[
            jax.ShapeDtypeStruct((count, 2, width, width), BF16),
            jax.ShapeDtypeStruct((3 * width, width), BF16),
            jax.ShapeDtypeStruct((2, rows, width), BF16),
        ],
        in_specs=[
            full(2, rows, width),
            full(2, rows, width),
            pl.BlockSpec((1, 1, 2 * rows), lambda k: (k, 0, 0)),
            pl.BlockSpec((1, 2, width, width), lambda k: (k, 0, 0, 0)),
            pl.BlockSpec((1, 2, 2, rows, width), lambda k: (k, 0, 0, 0, 0)),
            full(3 * width, width),
        ],
        out_specs=[
            pl.BlockSpec((1, 2, width, width), lambda k: (k, 0, 0, 0)),
            full(3 * width, width),
            full(2, rows, width),
        ],
        scratch_shapes=[pltpu.VMEM((2, rows, 2 * width), BF16), pltpu.VMEM((2, rows, width), F32)],
        compiler_params=params(),
        name="backward_mix",
    )(dy, u, table, w, ul, ar)


def mix_back_kernel(seq_count, line, *refs):
    (layout_ref, row_ref, ar_ref, x_ref, scale_ref, cot_ref, mlp_ref, w_hbm, ul_hbm) = refs[:9]
    large = refs[9:16]
    (tg_hbm, dw_hbm, dar_ref, gg_ref, ug_ref, dg_ref, small_ref) = refs[16:23]
    (keep, dsig, acc, conv, du_in, ul_buf, w_buf, dar) = refs[23:31]
    (deep, deep_in, deep_run, wide, wide_in, wide_side, wide_run) = refs[31:38]
    (g_own, g_pair, g_side, g_sum, g_line) = refs[38:43]
    (dy, u_ref, z_ref, gb_ref, ub_ref, mixed_ref, hg_ref) = held = refs[43:50]
    (tg_ref, dw_ref, end_sem) = refs[50:53]
    (load_sem, dus, dur, ps, pr, zs, zr, wps, wpr, ws, wr, wzs, wzr, gs, gr) = refs[53:]
    tg_store = pltpu.make_async_copy(tg_ref, tg_hbm, end_sem.at[0])
    dw_store = pltpu.make_async_copy(dw_ref, dw_hbm, end_sem.at[1])
    s, z, c, g = place(seq_count, line)
    twin = {"grp": g + 1 - 2 * c}
    rows, width = dy.shape[1], dy.shape[2]
    block = x_ref.shape[1]
    short = [layout_ref[0, m].astype(F32) for m in range(2)]
    count = w_hbm.shape[0]
    per_chip = 2 * count // line
    n = per_chip * width // CORES
    ar_rows = ar_ref.shape[0]
    ar_share = ar_rows // (line * CORES)
    lanes = 128
    ar_chunks = ar_rows // lanes
    share = gg_ref.shape[0]
    mine = pl.ds(pl.multiple_of(s * block, block), block)
    low = (z < line // 2).astype(jnp.int32)

    def dest(i):
        return low * (line - 1 - 2 * i) + i

    def load(i):
        return pltpu.make_async_copy(
            ul_hbm.at[pl.ds(dest(i) * per_chip, per_chip)], ul_buf.at[i % 2], load_sem.at[i % 2]
        )

    load_w = pltpu.make_async_copy(w_hbm, w_buf, load_sem.at[2])
    fetch = [pltpu.make_async_copy(large[i], held[i], load_sem.at[3 + i]) for i in range(7)]
    for x in fetch[:2] + [load(0), load(1)] + fetch[2:] + [load_w]:
        x.start()
    greet(seq_count, line, s, z, c, g, twin=True, side=True, whole_line=True)

    def ar_place(i):
        at = s * ar_chunks + i
        lag = lax.div(at, width // lanes)
        col = lax.rem(at, width // lanes)
        return lag, pl.ds(pl.multiple_of(col * lanes, lanes), lanes)

    for x in fetch[:2]:
        x.wait()
    for i in range(ar_chunks):
        lag, cols = ar_place(i)
        total = 0.0
        for m in range(2):
            v = lagged_by(u_ref[m, :, cols].astype(F32), lag, short[m]).astype(BF16)
            total = total + dot_tn(v, dy[m])
        dar[i * lanes : (i + 1) * lanes, :] = total.astype(BF16)
    for l in range(line):
        for cc in range(CORES):
            r = (l * CORES + cc) * ar_share
            deep[cc, l, n:, :] = dar[r : r + ar_share, :]

    def twin_deep(i):
        l = dest(i)
        return remote(deep.at[1 - c, l], deep_in.at[l], ps.at[i], pr.at[i], twin)

    def hop(run, own, send, recv, way, t, first):
        target = line - 1 - t if way == 0 else t
        src = own(target) if first else run.at[way, t]
        to = g + CORES if way == 0 else g - CORES
        return remote(src, run.at[way, t], send.at[way, t], recv.at[way, t], {"grp": to})

    def deep_own(l):
        return deep_in.at[l]

    def wide_own(l):
        return wide_in.at[s, l]

    deep_line = (deep_run, deep_own, zs, zr)
    wide_line = (wide_run, wide_own, wzs, wzr)

    def begin(kind, t):
        for way in (0, 1):

            @pl.when(z == 0 if way == 0 else z == line - 1)
            def _():
                hop(*kind, way, t, True).start()

    def relay(kind, phase):
        run, own = kind[0], kind[1]
        for way in (0, 1):
            for t in range(phase):
                at = phase - t if way == 0 else line - 1 - (phase - t)
                target = line - 1 - t if way == 0 else t

                @pl.when(z == at)
                def _():
                    hop(*kind, way, t, False).wait_recv()
                    mixed = run[way, t].astype(F32) + own(target)[...].astype(F32)
                    run[way, t] = mixed.astype(BF16)
                    hop(*kind, way, t, False).start()

    def compute(i):
        l = dest(i)
        load(i).wait()
        for j in range(per_chip):
            val = dot_tn(ul_buf[i % 2, j, 0], dy[0]) + dot_tn(ul_buf[i % 2, j, 1], dy[1])
            val = val.astype(BF16)
            for cc in range(CORES):
                lo, hi = max(j * width, cc * n), min((j + 1) * width, (cc + 1) * n)
                if lo < hi:
                    deep[cc, l, lo - cc * n : hi - cc * n, :] = val[lo - j * width : hi - j * width]
        twin_deep(i).start()
        if i + 2 < line:
            load(i + 2).start()

    def combine(i):
        l = dest(i)
        twin_deep(i).wait_recv()
        deep_in[l] = (deep[c, l].astype(F32) + deep_in[l].astype(F32)).astype(BF16)
        if i < line - 1:
            begin(deep_line, i)

    compute(0)
    compute(1)
    combine(0)

    span_f = gb_ref.shape[1] // seq_count
    down_share = dg_ref.shape[0]
    for x in fetch[2:]:
        x.wait()

    @pl.loop(0, seq_count)
    def _(j):
        part = pl.ds(pl.multiple_of(j * span_f, span_f), span_f)
        for which, back in ((0, gb_ref), (1, ub_ref)):
            val = dot_tn(z_ref[...], back[:, part]).astype(BF16)
            for k in range(seq_count):
                for l in range(line):
                    for cc in range(CORES):
                        r = ((k * line + l) * CORES + cc) * share
                        wide[cc, k, l, which * share : (which + 1) * share, part] = val[
                            r : r + share
                        ]
        val = dot_tn(mixed_ref[:, part], cot_ref[...]).astype(BF16)
        for l in range(line):
            for cc in range(CORES):
                r = (l * CORES + cc) * down_share
                for q in range(down_share // share):
                    wide[cc, j, l, 2 * share :, q * width : (q + 1) * width] = val[
                        r + q * share : r + (q + 1) * share
                    ]
    wide_twin = remote(wide.at[1 - c], wide_in, wps, wpr, twin)
    wide_twin.start()

    for i in range(2, line):
        compute(i)
        combine(i - 1)
    combine(line - 1)

    wide_twin.wait_recv()
    for k in range(seq_count):

        @pl.loop(0, line)
        def _(l):
            mixed = wide[c, k, l].astype(F32) + wide_in[k, l].astype(F32)
            wide_in[k, l] = mixed.astype(BF16)

    sides = []
    for j in range(1, seq_count):
        to = lax.rem(s + j, seq_count)
        sides.append(
            remote(wide_in.at[to], wide_side.at[j - 1], ws.at[j - 1], wr.at[j - 1], {"seq": to})
        )
        sides[-1].start()

    signs = signs_of(rows)
    for m in range(2):
        dsig[m] = (dy[m].astype(F32) * signs).astype(BF16)
        keep[m] = reach(rows, short[m])
    acc[...] = jnp.zeros_like(acc)
    for i in range(ar_chunks):
        lag, cols = ar_place(i)
        for m in range(2):
            val = dot_nt(dy[m], ar_ref[i * lanes : (i + 1) * lanes, :])
            acc[m, :, cols] += led_by(val, lag, short[m])
    load_w.wait()

    def filter_step(k):
        table = shifted(row_ref[pl.ds(s * count + k, 1), :], rows)
        for m in range(2):
            kept_table = table * keep[m]
            conv[0] = dot_nn(kept_table, dy[m]).astype(BF16)
            conv[1] = (dot_nn(kept_table, dsig[m]) * signs).astype(BF16)
            acc[m] += dot_nt(conv[0], w_buf[k, 0]) + dot_nt(conv[1], w_buf[k, 1])

    half = count // 2
    pl.loop(0, half)(filter_step)
    for phase in range(1, line - 2):
        relay(deep_line, phase)
    pl.loop(half, count)(filter_step)
    conv[...] = acc[...].astype(BF16)
    du_copies = []
    for i in range(1, seq_count):
        to = lax.rem(s + i, seq_count)
        du_copies.append(
            remote(
                conv.at[:, pl.ds(pl.multiple_of(to * block, block), block), :],
                du_in.at[i - 1],
                dus.at[i - 1],
                dur.at[i - 1],
                {"seq": to},
            )
        )
        du_copies[-1].start()
    if line > 2:
        relay(deep_line, line - 2)

    for x in du_copies:
        x.wait_recv()
    gain = jnp.zeros((1, width), F32)
    for m in range(2):
        grad = conv[m, mine, :].astype(F32)
        for i in range(seq_count - 1):
            grad = grad + du_in[i, m].astype(F32)
        x = x_ref[m].astype(F32)
        inv = lax.rsqrt(jnp.mean(x * x, axis=-1, keepdims=True) + EPSILON)
        scaled = grad * scale_ref[0:1, :]
        gain = gain + jnp.sum(grad * x * inv, axis=0, keepdims=True)
        centre = jnp.mean(scaled * x, axis=-1, keepdims=True)
        tg_ref[m] = hg_ref[m] + inv * scaled - x * (inv * inv * inv) * centre
    tg_store.start()
    g_own[...] = jnp.zeros_like(g_own)
    g_own[0:1, :] = gain
    g_own[1:2, :] = mlp_ref[0:1, :]
    small_pair = remote(g_own, g_pair, gs.at[0], gr.at[0], twin)
    small_pair.start()

    for x in sides:
        x.wait_recv()

    @pl.loop(0, line)
    def _(l):
        mixed = wide_in[s, l].astype(F32)
        for j in range(seq_count - 1):
            mixed = mixed + wide_side[j, l].astype(F32)
        wide_in[s, l] = mixed.astype(BF16)

    for t in range(line - 1):
        begin(wide_line, t)

    small_pair.wait()
    g_own[...] = g_own[...] + g_pair[...]
    small_sides = []
    for j in range(1, seq_count):
        small_sides.append(
            remote(
                g_own, g_side.at[j - 1], gs.at[j], gr.at[j], {"seq": lax.rem(s + j, seq_count)}
            )
        )
        small_sides[-1].start()

    dw_ref[...] = deep_in[z, :n, :].astype(F32)
    dar_ref[...] = deep_in[z, n:, :].astype(F32)
    for x in small_sides:
        x.wait()
    total = g_own[...]
    for j in range(seq_count - 1):
        total = total + g_side[j]
    g_sum[...] = total
    small_lines = []
    for j in range(1, line):
        small_lines.append(
            remote(
                g_sum,
                g_line.at[j - 1],
                gs.at[seq_count - 1 + j],
                gr.at[seq_count - 1 + j],
                {"grp": lax.rem(g + CORES * j, CORES * line)},
            )
        )
        small_lines[-1].start()

    def last(kind, add):
        for t in range(line - 1):
            for way in (0, 1):
                target = line - 1 - t if way == 0 else t

                @pl.when(z == target)
                def _():
                    hop(*kind, way, t, False).wait_recv()
                    add(kind[0][way, t].astype(F32))

    def add_deep(val):
        dw_ref[...] += val[:n]
        dar_ref[...] += val[n:]

    def add_wide(val):
        gg_ref[...] += val[:share]
        ug_ref[...] += val[share : 2 * share]
        for q in range(down_share // share):
            dg_ref[q * share : (q + 1) * share, :] += val[2 * share :, q * width : (q + 1) * width]

    last(deep_line, add_deep)
    dw_store.start()
    for phase in range(1, line - 1):
        relay(wide_line, phase)
    own = wide_in[s, z].astype(F32)
    gg_ref[...] = own[:share]
    ug_ref[...] = own[share : 2 * share]
    for q in range(down_share // share):
        dg_ref[q * share : (q + 1) * share, :] = own[2 * share :, q * width : (q + 1) * width]
    last(wide_line, add_wide)

    for x in small_lines:
        x.wait()
    total = g_sum[...]
    for j in range(line - 1):
        total = total + g_line[j]
    at = (s * (CORES * line) + g) * (width // (seq_count * CORES * line))
    small_ref[...] = pltpu.roll(total, lax.rem(width - at, width), 1)

    for x in sides + du_copies:
        x.wait_send()
    tg_store.wait()
    dw_store.wait()
    wide_twin.wait_send()
    for i in range(line):
        twin_deep(i).wait_send()
    for kind in (deep_line, wide_line):
        for t in range(line - 1):
            for way in (0, 1):
                target = line - 1 - t if way == 0 else t

                @pl.when(z < target if way == 0 else z > target)
                def _():
                    hop(*kind, way, t, False).wait_send()


def mix_back(
    seq_count, line, layout, dy, u, filters, w, ul, ar, x, hg, scale, mlp, mlp_grad, shares
):
    z, gate_back, up_back, mixed, cot = mlp
    share, down_share, deep_share, ar_share = shares
    _, block, width = x.shape
    rows = block * seq_count
    count = w.shape[0]
    per_chip = 2 * count // line
    small = (8, width)
    hidden_units = gate_back.shape[1]
    part = (2 * share + down_share * width // hidden_units, hidden_units)
    out_shape = [
        jax.ShapeDtypeStruct((2, block, width), F32),
        jax.ShapeDtypeStruct((deep_share, width), F32),
        jax.ShapeDtypeStruct((ar_share, width), F32),
        jax.ShapeDtypeStruct((share, hidden_units), F32),
        jax.ShapeDtypeStruct((share, hidden_units), F32),
        jax.ShapeDtypeStruct((down_share, width), F32),
        jax.ShapeDtypeStruct(small, F32),
    ]
    deep = (deep_share + ar_share, width)
    scratch = [
        pltpu.VMEM((2, rows, rows), BF16),
        pltpu.VMEM((2, rows, width), BF16),
        pltpu.VMEM((2, rows, width), F32),
        pltpu.VMEM((2, rows, width), BF16),
        pltpu.VMEM((seq_count - 1, 2, block, width), BF16),
        pltpu.VMEM((2, per_chip, 2, rows, width), BF16),
        pltpu.VMEM(w.shape, BF16),
        pltpu.VMEM(ar.shape, BF16),
        pltpu.VMEM((CORES, line) + deep, BF16),
        pltpu.VMEM((line,) + deep, BF16),
        pltpu.VMEM((2, line - 1) + deep, BF16),
        pltpu.VMEM((CORES, seq_count, line) + part, BF16),
        pltpu.VMEM((seq_count, line) + part, BF16),
        pltpu.VMEM((seq_count - 1, line) + part, BF16),
        pltpu.VMEM((2, line - 1) + part, BF16),
        pltpu.VMEM(small, F32),
        pltpu.VMEM(small, F32),
        pltpu.VMEM((seq_count - 1,) + small, F32),
        pltpu.VMEM(small, F32),
        pltpu.VMEM((line - 1,) + small, F32),
    ]
    large = [dy, u, z, gate_back, up_back, mixed, hg]
    scratch += [pltpu.VMEM(v.shape, v.dtype) for v in large]
    scratch += [pltpu.VMEM(v.shape, F32) for v in out_shape[:2]]
    scratch += [
        DMA((2,)),
        DMA((10,)),
        DMA((seq_count - 1,)),
        DMA((seq_count - 1,)),
        DMA((line,)),
        DMA((line,)),
        DMA((2, line - 1)),
        DMA((2, line - 1)),
        DMA,
        DMA,
        DMA((seq_count - 1,)),
        DMA((seq_count - 1,)),
        DMA((2, line - 1)),
        DMA((2, line - 1)),
        DMA((seq_count + line,)),
        DMA((seq_count + line,)),
    ]
    return pl.pallas_call(
        functools.partial(mix_back_kernel, seq_count, line),
        out_shape=out_shape,
        in_specs=[pl.BlockSpec(memory_space=pltpu.SMEM)] + [WHOLE] * 6 + [ANY] * 9,
        out_specs=[ANY] * 2 + [WHOLE] * 5,
        scratch_shapes=scratch,
        compiler_params=params(6),
        name="mix_back",
    )(layout, filters, ar, x, scale, cot, mlp_grad, w, ul, *large)


def kept(rows, short, lag):
    pos = lax.broadcasted_iota(jnp.int32, (rows, 1), 0)
    whole = (pos >= lag).astype(F32)
    return whole * (1.0 - short * (1.0 - (lax.rem(pos, rows // 4) >= lag).astype(F32)))


def lagged_by(values, lag, short):
    rows = values.shape[0]
    one = pltpu.roll(values, 1, 0) * kept(rows, short, 1)
    two = pltpu.roll(values, 2, 0) * kept(rows, short, 2)
    return jnp.where(lag == 0, values, jnp.where(lag == 1, one, two))


def led_by(values, lag, short):
    rows = values.shape[0]
    one = pltpu.roll(values * kept(rows, short, 1), rows - 1, 0)
    two = pltpu.roll(values * kept(rows, short, 2), rows - 2, 0)
    return jnp.where(lag == 0, values, jnp.where(lag == 1, one, two))


def reach(rows, short):
    down = lax.broadcasted_iota(jnp.int32, (rows, rows), 0)
    over = lax.broadcasted_iota(jnp.int32, (rows, rows), 1)
    same = (lax.div(down, rows // 4) == lax.div(over, rows // 4)).astype(F32)
    return ((over >= down).astype(F32) * (1.0 - short * (1.0 - same))).astype(BF16)


def shifted(row, rows):
    wide = jnp.broadcast_to(row, (rows, rows))
    return pltpu.roll(wide, 0, 1, stride=1, stride_axis=0).astype(BF16)


def mix_front_kernel(seq_count, line, *refs):
    (layout_ref, tok_ref, row_ref, mix_gain, mlp_gain, cot_ref, spec_hbm, ar_hbm) = refs[:8]
    wide_in = refs[8:11]
    (w_hbm, ul_hbm, u_hbm) = refs[11:14]
    results = refs[14:20]
    dy_hbm = refs[20]
    (ar_ref, gain_out, mlp_ref) = refs[21:24]
    (x_all, both, acc, y_bf, y_in, w_buf, ul_buf, keep, hid, dz, dy_own) = refs[24:35]
    (z_ref, gb_ref, ub_ref, mixed_ref, hg_ref, out_ref) = local = refs[35:41]
    wide_buf = refs[41:44]
    (g_pad, g_own, g_side, g_sum, g_line, g_all, g_twin) = refs[44:51]
    (load_sem, ul_sem, w_sem, ts, tr, ys, yr, zs, zr, hs, hr) = refs[51:62]
    (ps, pr, ws, wr, wps, wpr, gs, gr, ds_, dr_, end_sem) = refs[62:]
    s, z, c, g = place(seq_count, line)
    twin = {"grp": g + 1 - 2 * c}
    rows, width = x_all.shape[1], x_all.shape[2]
    block = tok_ref.shape[1]
    n = spec_hbm.shape[0]
    hn = n // 2
    blocks = ul_buf.shape[0]
    count = blocks // 2
    per_chip = blocks // line
    lanes = 128
    wide = range(3)
    mine = pl.ds(pl.multiple_of(s * block, block), block)
    short = [layout_ref[0, m].astype(F32) for m in range(2)]

    def piece(l, h):
        return w_buf.at[l, pl.ds(pl.multiple_of(c * n + h * hn, hn), hn), :]

    def wide_own(i, l):
        return wide_buf[i].at[s, l, c]

    load_w = [
        pltpu.make_async_copy(spec_hbm.at[pl.ds(h * hn, hn)], piece(z, h), load_sem.at[h])
        for h in range(2)
    ]
    load_ar = pltpu.make_async_copy(ar_hbm, ar_ref.at[z, c], load_sem.at[2])
    loads = [pltpu.make_async_copy(wide_in[i], wide_own(i, z), load_sem.at[3 + i]) for i in wide]
    for x in load_w + [load_ar] + loads:
        x.start()
    at = (s * (CORES * line) + g) * (width // (seq_count * CORES * line))
    g_pad[...] = jnp.zeros_like(g_pad)
    g_pad[0:1, : mix_gain.shape[1]] = mix_gain[...].astype(F32)
    g_pad[1:2, : mlp_gain.shape[1]] = mlp_gain[...].astype(F32)
    g_own[...] = pltpu.roll(g_pad[...], at, 1).astype(BF16)
    greet(seq_count, line, s, z, c, g, twin=True, side=True, whole_line=True)

    gain_sides = []
    toks = []
    for i in range(1, seq_count):
        to = {"seq": lax.rem(s + i, seq_count)}
        gain_sides.append(remote(g_own, g_side.at[i - 1], gs.at[i - 1], gr.at[i - 1], to))
        gain_sides[-1].start()
    for i in range(1, seq_count):
        to = {"seq": lax.rem(s + i, seq_count)}
        toks.append(remote(tok_ref, x_all.at[:, mine, :], ts.at[i - 1], tr.at[i - 1], to))
        toks[-1].start()

    def onward(way):
        return {"grp": g + CORES if way == 0 else g - CORES}

    def early_own(i, l):
        return ar_ref.at[l, c] if i == 3 else wide_own(i, l)

    def early_hops(way, t, origin):
        hops = []
        for i in range(4):
            if t > 0:
                src = early_own(i, origin)
            else:
                src = ar_hbm if i == 3 else wide_in[i]
            hops.append(
                remote(src, early_own(i, origin), hs.at[i, way, t], hr.at[i, way, t], onward(way))
            )
        return hops

    def deep_hops(h):
        def build(way, t, origin):
            src = spec_hbm.at[pl.ds(h * hn, hn)] if t == 0 else piece(origin, h)
            dst = piece(origin, h)
            return [remote(src, dst, zs.at[h, way, t], zr.at[h, way, t], onward(way))]

        return build

    def first(build):
        for way in (0, 1):
            sends, _, origin, _ = line_conditions(line, z, way, 0)

            @pl.when(sends)
            def _():
                for x in build(way, 0, origin):
                    x.start()

    def arrive(build, t, after):
        for way in (0, 1):
            _, receives, _, origin = line_conditions(line, z, way, t)

            @pl.when(receives)
            def _():
                for x in build(way, t, origin):
                    x.wait_recv()
                if t + 1 < line - 1:
                    sends = line_conditions(line, z, way, t + 1)[0]

                    @pl.when(sends)
                    def _():
                        for x in build(way, t + 1, origin):
                            x.start()

                after(origin)

    def sent(build):
        for t in range(line - 1):
            for way in (0, 1):
                sends, _, origin, _ = line_conditions(line, z, way, t)

                @pl.when(sends)
                def _():
                    for x in build(way, t, origin):
                        x.wait_send()

    def sides(l, own=False):
        copies = []
        for i in wide:
            for j in range(1, seq_count):
                src = wide_in[i] if own else wide_own(i, l)
                to = {"seq": lax.rem(s + j, seq_count)}
                copies.append(
                    remote(src, wide_own(i, l), ws.at[i, l, j - 1], wr.at[i, l, j - 1], to)
                )
        return copies

    def begin_sides(l):
        for x in sides(l):
            x.start()

    def twin_deep(l, h):
        return remote(piece(l, h), piece(l, h), ps.at[h, l], pr.at[h, l], twin)

    first(early_hops)
    total = g_own[...]
    for i, x in enumerate(gain_sides):
        x.wait_recv()
        total = total + g_side[i]
    g_sum[...] = total
    gain_lines = []
    for j in range(1, line):
        k = seq_count - 2 + j
        to = {"grp": lax.rem(g + CORES * j, CORES * line)}
        gain_lines.append(remote(g_sum, g_line.at[j - 1], gs.at[k], gr.at[k], to))
        gain_lines[-1].start()
    first(deep_hops(0))
    for x in sides(z, True):
        x.start()
    x_all[:, mine, :] = tok_ref[...]
    for h in range(2):
        load_w[h].wait()
        twin_deep(z, h).start()
    for x in loads + [load_ar]:
        x.wait()
    for m in range(2):
        keep[m] = reach(rows, short[m])
    arrive(early_hops, 0, begin_sides)
    first(deep_hops(1))
    total = g_sum[...]
    for j, x in enumerate(gain_lines):
        x.wait_recv()
        total = total + g_line[j]
    g_all[...] = total
    k = seq_count + line - 2
    gain_twin = remote(g_all, g_twin, gs.at[k], gr.at[k], twin)
    gain_twin.start()
    for x in toks:
        x.wait_recv()
    gain_twin.wait_recv()
    gain = g_all[...].astype(F32) + g_twin[...].astype(F32)
    gain_out[...] = gain[:8]

    signs = signs_of(rows)
    for m in range(2):
        x = x_all[m].astype(F32)
        inv = lax.rsqrt(jnp.mean(x * x, axis=-1, keepdims=True) + EPSILON)
        u = (x * inv * gain[0:1, :]).astype(BF16)
        both[m, :, :width] = u
        both[m, :, width:] = (u.astype(F32) * signs).astype(BF16)
    u_store = pltpu.make_async_copy(both.at[:, :, pl.ds(0, width)], u_hbm, end_sem.at[0])
    u_store.start()

    def ul_store(k):
        part = pl.ds(2 * k, 2)
        return pltpu.make_async_copy(ul_buf.at[part], ul_hbm.at[part], ul_sem.at[k])

    def filter_step(k):
        table = shifted(row_ref[pl.ds(s * count + k, 1), :], rows)
        for m in range(2):
            val = dot_tn(table * keep[m], both[m])
            ul_buf[2 * k, m] = val[:, :width].astype(BF16)
            ul_buf[2 * k + 1, m] = (val[:, width:] * signs).astype(BF16)
        ul_store(k).start()

    def add_one(l, h, m):
        total = 0.0
        for cc in range(CORES):
            lo, end = cc * n + h * hn, cc * n + (h + 1) * hn
            while lo < end:
                j = lo // width
                hi = min(end, (j + 1) * width)
                left = ul_buf[l * per_chip + j, m, :, lo - j * width : hi - j * width]
                total = total + dot_nn(left, w_buf[l, lo:hi, :])
                lo = hi
        acc[m] += total

    def add_part(l, h):
        pl.loop(0, 2)(lambda m: add_one(l, h, m))

    def w_store(l):
        return pltpu.make_async_copy(w_buf.at[l], w_hbm.at[l], w_sem.at[l])

    def nothing(origin):
        pass

    def deep_arrive(t, h):
        arrive(deep_hops(h), t, lambda origin: twin_deep(origin, h).start())

    def deep_add(t, h):
        for way in (0, 1):
            _, receives, _, origin = line_conditions(line, z, way, t)

            @pl.when(receives)
            def _():
                twin_deep(origin, h).wait_recv()
                if h == 1:
                    w_store(origin).start()
                add_part(origin, h)

    half = count // 2
    acc[...] = jnp.zeros_like(acc)
    pl.loop(0, half)(filter_step)
    if line > 2:
        arrive(early_hops, 1, begin_sides)
    deep_arrive(0, 0)
    pl.loop(half, count)(filter_step)
    for h in range(2):
        twin_deep(z, h).wait_recv()
        add_part(z, h)
    w_store(z).start()
    deep_arrive(0, 1)
    for t in range(2, line - 1):
        arrive(early_hops, t, begin_sides)
    ar_twin = remote(ar_ref.at[:, c], ar_ref.at[:, c], wps.at[3, 0], wpr.at[3, 0], twin)
    ar_twin.start()
    for h in range(2):
        deep_add(0, h)

    ar_twin.wait_recv()
    ar_rows = ar_ref.shape[0] * ar_ref.shape[1] * ar_ref.shape[2]
    ar_all = ar_ref[...].reshape(ar_rows, width)
    chunks = ar_rows // lanes
    for i in range(chunks):
        place_at = s * chunks + i
        lag = lax.div(place_at, width // lanes)
        col = lax.rem(place_at, width // lanes)
        cols = pl.ds(pl.multiple_of(col * lanes, lanes), lanes)
        for m in range(2):
            v = lagged_by(both[m, :, cols].astype(F32), lag, short[m]).astype(BF16)
            acc[m] += dot_nn(v, ar_all[i * lanes : (i + 1) * lanes])

    def twin_wide(i, k):
        part = wide_buf[i].at[k, :, c]
        return remote(part, part, wps.at[i, k], wpr.at[i, k], twin)

    for t in range(1, line - 1):
        deep_arrive(t, 0)
        if t == line - 2:
            for l in range(line):
                for x in sides(l):
                    x.wait_recv()
            for i in wide:
                for k in range(seq_count):
                    twin_wide(i, k).start()
        deep_add(t, 0)
        deep_arrive(t, 1)
        if t < line - 2:
            deep_add(t, 1)

    y_copies = []
    for m in range(2):
        for way in (0, 1):
            _, receives, _, origin = line_conditions(line, z, way, line - 2)

            @pl.when(receives)
            def _():
                if m == 0:
                    twin_deep(origin, 1).wait_recv()
                    w_store(origin).start()
                add_one(origin, 1, m)

        y_bf[m] = acc[m].astype(BF16)
        y_copies.append([])
        for i in range(1, seq_count):
            to = lax.rem(s + i, seq_count)
            y_copies[m].append(
                remote(
                    y_bf.at[m, pl.ds(pl.multiple_of(to * block, block), block), :],
                    y_in.at[i - 1, m],
                    ys.at[m, i - 1],
                    yr.at[m, i - 1],
                    {"seq": to},
                )
            )
            y_copies[m][-1].start()

    for i in wide:
        for k in range(seq_count):
            twin_wide(i, k).wait()
    sent(early_hops)
    for h in range(2):
        sent(deep_hops(h))
        for l in range(line):
            twin_deep(l, h).wait_send()
    for l in range(line):
        w_store(l).wait()
        for x in sides(l):
            x.wait_send()
    for x in toks + gain_sides + gain_lines + [ar_twin, gain_twin]:
        x.wait_send()
    for k in range(count):
        ul_store(k).wait()

    mlp_scale = gain[1:2, :]
    hidden_units = gb_ref.shape[1]
    step = hidden_units // seq_count
    root = 0.7978845608028654
    mlp_ref[...] = jnp.zeros_like(mlp_ref)
    dy_copies = []
    ends = []
    for m in range(2):
        own = slice(m * block, (m + 1) * block)
        h = tok_ref[m].astype(F32) + acc[m, mine, :]
        for i, x in enumerate(y_copies[m]):
            x.wait_recv()
            h = h + y_in[i, m].astype(F32)
        hid[own, :] = h
        inv_two = lax.rsqrt(jnp.mean(h * h, axis=-1, keepdims=True) + EPSILON)
        z_ref[own, :] = (h * inv_two * mlp_scale).astype(BF16)
        dz[...] = jnp.zeros_like(dz)

        @pl.loop(0, seq_count)
        def _(j):
            part = pl.ds(pl.multiple_of(j * step, step), step)
            gate_w = wide_buf[0][:, :, :, :, part].reshape(width, step)
            up_w = wide_buf[1][:, :, :, :, part].reshape(width, step)
            down_w = wide_buf[2][j].reshape(step, width)
            gate = dot_nn(z_ref[own, :], gate_w)
            up = dot_nn(z_ref[own, :], up_w)
            back = dot_nt(cot_ref[own, :], down_w)
            square = gate * gate
            tan = jnp.tanh(root * (gate + 0.044715 * (square * gate)))
            share = 0.5 * (1.0 + tan)
            gelu = gate * share
            slope = share + 0.5 * gate * (1.0 - tan * tan) * (
                root * (1.0 + (3.0 * 0.044715) * square)
            )
            mixed_ref[own, part] = (gelu * up).astype(BF16)
            gate_back = (back * up * slope).astype(BF16)
            up_back = (back * gelu).astype(BF16)
            gb_ref[own, part] = gate_back
            ub_ref[own, part] = up_back
            dz[...] += dot_nt(gate_back, gate_w) + dot_nt(up_back, up_w)

        grad = dz[...]
        h = hid[own, :]
        scaled = grad * mlp_scale
        centre = jnp.mean(scaled * h, axis=-1, keepdims=True)
        cube = inv_two * inv_two * inv_two
        dh = cot_ref[own, :].astype(F32) + inv_two * scaled - h * cube * centre
        dy_own[m] = dh.astype(BF16)
        for i in range(1, seq_count):
            to = {"seq": lax.rem(s + i, seq_count)}
            dst = dy_hbm.at[m, mine, :]
            dy_copies.append(remote(dy_own.at[m], dst, ds_.at[m, i - 1], dr_.at[m, i - 1], to))
            dy_copies[-1].start()
        ends.append(pltpu.make_async_copy(dy_own.at[m], dy_hbm.at[m, mine, :], end_sem.at[7 + m]))
        ends[-1].start()
        hg_ref[m] = dh
        mlp_ref[0:1, :] += jnp.sum(grad * h * inv_two, axis=0, keepdims=True)
    for i in range(5):
        ends.append(pltpu.make_async_copy(local[i], results[i], end_sem.at[1 + i]))
        ends[-1].start()
    last = pltpu.make_async_copy(local[5], results[5], end_sem.at[6])
    total = hid[...]
    for j in range(seq_count):
        down_w = wide_buf[2][j].reshape(step, width)
        total = total + dot_nn(mixed_ref[:, j * step : (j + 1) * step], down_w)
    for m in range(2):
        out_ref[m] = total[m * block : (m + 1) * block]
    last.start()
    for x in y_copies[0] + y_copies[1]:
        x.wait_send()
    for x in ends + [last, u_store]:
        x.wait()
    for x in dy_copies:
        x.wait()


def mix_front(seq_count, line, layout, tok, filters, gains, cot, spec, ar, wide):
    _, block, width = tok.shape
    rows = block * seq_count
    count = filters.shape[0] // seq_count
    hidden_units = wide[0].shape[1]
    small = (16, width)
    vmem = pltpu.VMEM
    out_shape = [
        jax.ShapeDtypeStruct((line, CORES * spec.shape[0], width), BF16),
        jax.ShapeDtypeStruct((2 * count, 2, rows, width), BF16),
        jax.ShapeDtypeStruct((2, rows, width), BF16),
    ]
    local = [
        ((2 * block, width), BF16),
        ((2 * block, hidden_units), BF16),
        ((2 * block, hidden_units), BF16),
        ((2 * block, hidden_units), BF16),
        ((2, block, width), F32),
        ((2, block, width), F32),
    ]
    out_shape += [jax.ShapeDtypeStruct(*x) for x in local]
    out_shape += [
        jax.ShapeDtypeStruct((2, rows, width), BF16),
        jax.ShapeDtypeStruct((line, CORES) + ar.shape, BF16),
        jax.ShapeDtypeStruct((8, width), F32),
        jax.ShapeDtypeStruct((8, width), F32),
    ]
    scratch = [
        vmem((2, rows, width), BF16),
        vmem((2, rows, 2 * width), BF16),
        vmem((2, rows, width), F32),
        vmem((2, rows, width), BF16),
        vmem((seq_count - 1, 2, block, width), BF16),
        vmem((line, CORES * spec.shape[0], width), BF16),
        vmem((2 * count, 2, rows, width), BF16),
        vmem((2, rows, rows), BF16),
        vmem((2 * block, width), F32),
        vmem((block, width), F32),
        vmem((2, block, width), BF16),
    ]
    scratch += [vmem(*x) for x in local]
    scratch += [vmem((seq_count, line, CORES) + x.shape, BF16) for x in wide]
    scratch += [
        vmem(small, F32),
        vmem(small, BF16),
        vmem((seq_count - 1,) + small, BF16),
        vmem(small, BF16),
        vmem((line - 1,) + small, BF16),
        vmem(small, BF16),
        vmem(small, BF16),
        DMA((6,)),
        DMA((count,)),
        DMA((line,)),
        DMA((seq_count - 1,)),
        DMA((seq_count - 1,)),
        DMA((2, seq_count - 1)),
        DMA((2, seq_count - 1)),
        DMA((2, 2, line - 1)),
        DMA((2, 2, line - 1)),
        DMA((4, 2, line - 1)),
        DMA((4, 2, line - 1)),
        DMA((2, line)),
        DMA((2, line)),
        DMA((3, line, seq_count - 1)),
        DMA((3, line, seq_count - 1)),
        DMA((4, seq_count)),
        DMA((4, seq_count)),
        DMA((seq_count + line,)),
        DMA((seq_count + line,)),
        DMA((2, seq_count - 1)),
        DMA((2, seq_count - 1)),
        DMA((9,)),
    ]
    return pl.pallas_call(
        functools.partial(mix_front_kernel, seq_count, line),
        out_shape=out_shape,
        in_specs=[pl.BlockSpec(memory_space=pltpu.SMEM)] + [WHOLE] * 5 + [ANY] * 5,
        out_specs=[ANY] * 10 + [WHOLE] * 3,
        scratch_shapes=scratch,
        compiler_params=params(7),
        name="mix_front",
    )(layout, tok, filters, *gains, cot, spec, ar, *wide)


def finish_kernel(count, share, *refs):
    ins, small = refs[:count], refs[count]
    outs, first, second = refs[count + 1 : 2 * count + 1], refs[2 * count + 1], refs[2 * count + 2]
    held, sem = refs[2 * count + 3 : 3 * count + 3], refs[3 * count + 3]
    loads = [pltpu.make_async_copy(ins[i], held[i], sem.at[0, i]) for i in range(count)]
    stores = [pltpu.make_async_copy(held[i], outs[i], sem.at[1, i]) for i in range(count)]
    for x in loads:
        x.start()
    first[...] = small[0:1, :share]
    second[...] = small[1:2, :share]
    for x, y in zip(loads, stores):
        x.wait()
        y.start()
    for x in stores:
        x.wait()


def finish(share, arrays, small):
    count = len(arrays)
    row = jax.ShapeDtypeStruct((1, share), F32)
    return pl.pallas_call(
        functools.partial(finish_kernel, count, share),
        out_shape=[jax.ShapeDtypeStruct(x.shape, x.dtype) for x in arrays] + [row, row],
        in_specs=[ANY] * count + [WHOLE],
        out_specs=[ANY] * count + [WHOLE] * 2,
        scratch_shapes=[pltpu.VMEM(x.shape, x.dtype) for x in arrays] + [DMA((2, count))],
        compiler_params=params(),
        name="finish",
    )(*arrays, small)


def body(
    tokens,
    layout,
    filters,
    gain_mix,
    spectral_proj,
    ar_proj,
    gain_mlp,
    w_gate,
    w_up,
    w_down,
    out_grad,
):
    seq_count = lax.axis_size("seq")
    line = lax.axis_size("grp") // CORES
    s = lax.axis_index("seq")
    g = lax.axis_index("grp")
    block, width = tokens.shape[2], tokens.shape[3]
    rows = block * seq_count
    count = filters.shape[1] // seq_count
    hidden_units = w_gate.shape[1]
    spans = (rows, rows // 4)

    share = gain_mix.shape[0]
    ar_rows = ar_proj.shape[0] * CORES * line
    mine = lax.dynamic_slice(filters.T, (s * count, 0), (count, rows))[:, None, :]
    nothing = jnp.zeros((count, 1, rows), F32)
    back_table = jnp.concatenate([mine, nothing], axis=2)
    aligned = share % 16 == 0 and ar_proj.shape[0] % 16 == 0 and 2 * count % line == 0
    aligned = aligned and ar_rows % 128 == 0 and line > 2

    if aligned:
        own = tokens[:, 0]
        cot = out_grad.reshape(2 * block, width)
        flags = layout.reshape(1, 2)
        spec, ul, u, mlp_in, gate_back, up_back, mixed, dh, out, dy, ar, gains, mlp_grad = mix_front(
            seq_count,
            line,
            flags,
            own,
            filters.T,
            (gain_mix.reshape(1, share), gain_mlp.reshape(1, share)),
            cot,
            spectral_proj,
            ar_proj,
            (w_gate, w_up, w_down),
        )
        input_grad, dw, dar, gate_grad, up_grad, down_grad, small = mix_back(
            seq_count,
            line,
            flags,
            dy,
            u,
            filters.T,
            spec.reshape(count, 2, width, width),
            ul,
            ar.reshape(ar_rows, width),
            own,
            dh,
            gains,
            (mlp_in, gate_back, up_back, mixed, cot),
            mlp_grad,
            (share, w_down.shape[0], spectral_proj.shape[0], ar_proj.shape[0]),
        )
        dw, out, input_grad, down_grad, gate_grad, up_grad, dar, mix_grad, mlp_grad = finish(
            share, (dw, out, input_grad, down_grad, gate_grad, up_grad, dar), small
        )
        return (
            out.reshape(tokens.shape),
            input_grad.reshape(tokens.shape),
            mix_grad.reshape(share),
            dw,
            dar,
            mlp_grad.reshape(share),
            gate_grad,
            up_grad,
            down_grad,
        )

    swap = layout[0, 0] == 1
    own = jnp.where(swap, tokens[::-1, 0], tokens[:, 0])
    cotangent = jnp.where(swap, out_grad[::-1, 0], out_grad[:, 0])
    gains = jnp.zeros((16, 128), BF16)
    gains = gains.at[0, :share].set(gain_mix).at[1, :share].set(gain_mlp)
    x_all, spec, ar, gate_w, up_w, down_w, gains = gather_all(
        seq_count, line, own, (spectral_proj, ar_proj), (w_gate, w_up, w_down, gains)
    )
    ar_full = lax.dynamic_update_slice(
        jnp.zeros((3 * width, width), BF16), ar.reshape(ar_rows, width), (s * ar_rows, 0)
    )
    gains = gains.reshape(-1, 16, 128).astype(F32)
    mix_scale = gains[:, 0, :share].reshape(1, width)
    mlp_scale = gains[:, 1, :share].reshape(1, width)
    fore_table = jnp.concatenate([mine[:, :, :1], nothing, mine[:, :, :0:-1]], axis=2)
    split = spec.reshape(count, 2, width, width)
    ul, u, y = forward_mix(spans, x_all, mix_scale, fore_table, split, ar_full)
    mixer = side_sum(seq_count, line, y, 3).reshape(2 * block, width)
    spec = spec.reshape(count, 2, width, width)
    gate_w = gate_w.reshape(width, hidden_units)
    up_w = up_w.reshape(width, hidden_units)
    down_w = down_w.reshape(hidden_units, width)

    inputs = own.reshape(2 * block, width).astype(F32)
    cot = cotangent.reshape(2 * block, width)
    hidden = inputs + mixer
    inv_two = lax.rsqrt(jnp.mean(hidden * hidden, axis=-1, keepdims=True) + EPSILON)
    mlp_in = (hidden * inv_two * mlp_scale).astype(BF16)
    gate = dot_nn(mlp_in, gate_w)
    upval = dot_nn(mlp_in, up_w)
    product_val, gelu_pull = jax.vjp(lambda a, b: jax.nn.gelu(a) * b, gate, upval)
    mixed = product_val.astype(BF16)
    out = hidden + dot_nn(mixed, down_w)
    mixed_grad = dot_nt(cot, down_w)
    gate_back, up_back = gelu_pull(mixed_grad)
    gate_back = gate_back.astype(BF16)
    up_back = up_back.astype(BF16)
    mlp_in_grad = dot_nt(gate_back, gate_w) + dot_nt(up_back, up_w)
    scaled_two = mlp_in_grad * mlp_scale
    mlp_grad = jnp.sum(mlp_in_grad * hidden * inv_two, axis=0, keepdims=True)
    hidden_grad = (
        cot.astype(F32)
        + inv_two * scaled_two
        - hidden * inv_two**3 * jnp.mean(scaled_two * hidden, axis=-1, keepdims=True)
    )
    mixer_grad = hidden_grad.astype(BF16)

    down_grad = dot_tn(mixed, cot)
    gate_grad = dot_tn(mlp_in, gate_back)
    up_grad = dot_tn(mlp_in, up_back)
    dy = side_gather(seq_count, line, mixer_grad.reshape(2, block, width))
    dw, dar, du = backward_mix(spans, dy, u, back_table, spec, ul, ar_full)
    normed_grad = side_sum(seq_count, line, du, 4).reshape(2 * block, width)

    inv_one = lax.rsqrt(jnp.mean(inputs * inputs, axis=-1, keepdims=True) + EPSILON)
    scaled_one = normed_grad * mix_scale
    mix_grad = jnp.sum(normed_grad * inputs * inv_one, axis=0, keepdims=True)
    input_grad = (
        hidden_grad
        + inv_one * scaled_one
        - inputs * inv_one**3 * jnp.mean(scaled_one * inputs, axis=-1, keepdims=True)
    )

    dar = lax.dynamic_slice(dar, (s * ar_rows, 0), (ar_rows, width))
    deep = (dw.reshape(line, CORES, -1, width), dar.reshape(line, CORES, -1, width))
    wide = tuple(
        x.astype(BF16).reshape(seq_count, line, CORES, -1, x.shape[1])
        for x in (gate_grad, up_grad, down_grad)
    )
    small = jnp.concatenate([mix_grad, mlp_grad, jnp.zeros((6, width), F32)], axis=0)
    dw, dar, gate_grad, up_grad, down_grad, small = sum_all(seq_count, line, deep, wide, small)
    small = lax.dynamic_slice(small, (0, (s * CORES * line + g) * share), (2, share))

    def settle(x):
        x = x.reshape(2, 1, block, width)
        return jnp.where(swap, x[::-1], x)

    return (
        settle(out),
        settle(input_grad),
        small[0],
        dw,
        dar,
        small[1],
        gate_grad,
        up_grad,
        down_grad,
    )


def solution(mesh):
    placed = (
        P(None, "grp", "seq", None),
        P(None, "grp"),
        P(),
        P(("seq", "grp")),
        P(("seq", "grp"), None),
        P(("seq", "grp"), None),
        P(("seq", "grp")),
        P(("seq", "grp"), None),
        P(("seq", "grp"), None),
        P(("seq", "grp"), None),
        P(None, "grp", "seq", None),
    )
    return jax.shard_map(
        body,
        mesh=mesh,
        in_specs=placed,
        out_specs=(
            P(None, "grp", "seq", None),
            P(None, "grp", "seq", None),
            P(("seq", "grp")),
            P(("seq", "grp"), None),
            P(("seq", "grp"), None),
            P(("seq", "grp")),
            P(("seq", "grp"), None),
            P(("seq", "grp"), None),
            P(("seq", "grp"), None),
        ),
        check_vma=False,
    )
```

```python
import functools

import jax
import jax.numpy as jnp
from jax import lax
from jax.experimental import pallas as pl
from jax.experimental.pallas import tpu as pltpu
from jax.sharding import PartitionSpec as P

EPSILON = 1e-05
BF16 = jnp.bfloat16
F32 = jnp.float32
MESH = pl.DeviceIdType.MESH
DMA = pltpu.SemaphoreType.DMA
ANY = pl.BlockSpec(memory_space=pl.ANY)
WHOLE = pl.BlockSpec(memory_space=pltpu.VMEM)
VMEM_LIMIT = 60 * 1024 * 1024
CORES = 2


def dot_nn(a, b):
    return lax.dot_general(a, b, (((1,), (0,)), ((), ())), preferred_element_type=F32)


def dot_tn(a, b):
    return lax.dot_general(a, b, (((0,), (0,)), ((), ())), preferred_element_type=F32)


def dot_nt(a, b):
    return lax.dot_general(a, b, (((1,), (1,)), ((), ())), preferred_element_type=F32)


def params(collective_id=None):
    return pltpu.CompilerParams(
        collective_id=collective_id,
        has_side_effects=collective_id is not None,
        vmem_limit_bytes=VMEM_LIMIT,
    )


def remote(src, dst, send, recv, where):
    return pltpu.make_async_remote_copy(
        src_ref=src, dst_ref=dst, send_sem=send, recv_sem=recv, device_id=where, device_id_type=MESH
    )


def place(seq_count, line):
    s = lax.axis_index("seq")
    g = lax.axis_index("grp")
    return s, lax.div(g, CORES), lax.rem(g, CORES), g


def greet(seq_count, line, s, z, c, g, chain=False, twin=False, side=False, whole_line=False):
    barrier = pltpu.get_barrier_semaphore()

    def call(where):
        pl.semaphore_signal(barrier, inc=1, device_id=where, device_id_type=MESH)

    expected = (1 if twin else 0) + (seq_count - 1 if side else 0) + (line - 1 if whole_line else 0)
    if twin:
        call({"grp": g + 1 - 2 * c})
    if side:
        for i in range(1, seq_count):
            call({"seq": lax.rem(s + i, seq_count)})
    if whole_line:
        for j in range(1, line):
            call({"grp": lax.rem(g + CORES * j, CORES * line)})
    if chain:
        expected = expected + (z > 0).astype(jnp.int32) + (z < line - 1).astype(jnp.int32)

        @pl.when(z > 0)
        def _():
            call({"grp": g - CORES})

        @pl.when(z < line - 1)
        def _():
            call({"grp": g + CORES})

    pl.semaphore_wait(barrier, expected)


def line_conditions(line, z, way, t):
    if way == 0:
        return (z < line - 1) & (z >= t), z >= t + 1, z - t, z - 1 - t
    return (z > 0) & (z + t <= line - 1), z + t + 1 <= line - 1, z + t, z + 1 + t


def gather_kernel(seq_count, line, n_deep, n_wide, *refs):
    n_in = 1 + n_deep + n_wide
    ins, outs = refs[:n_in], refs[n_in : 2 * n_in]
    rest = refs[2 * n_in :]
    stage = rest[:n_in]
    (local_sem, tok_send, tok_recv, zs, zr, ws, wr, ps, pr, dps, dpr) = rest[n_in:]
    s, z, c, g = place(seq_count, line)
    twin = {"grp": g + 1 - 2 * c}
    tok, tok_out = ins[0], outs[0]
    rows = tok.shape[1]
    items = list(range(n_deep + n_wide))

    def own(i, l):
        out = outs[1 + i]
        return out.at[l, c] if i < n_deep else out.at[s, l, c]

    loads = [pltpu.make_async_copy(ins[i], stage[i], local_sem.at[0, i]) for i in range(n_in)]
    for x in loads:
        x.start()
    greet(seq_count, line, s, z, c, g, chain=True, twin=True, side=True)

    toks = []
    for i in range(1, seq_count):
        toks.append(
            remote(
                tok,
                tok_out.at[:, pl.ds(pl.multiple_of(s * rows, rows), rows), :],
                tok_send.at[i - 1],
                tok_recv.at[i - 1],
                {"seq": lax.rem(s + i, seq_count)},
            )
        )
        toks[-1].start()

    def hop(i, way, t, origin):
        src = ins[1 + i] if t == 0 else own(i, origin)
        to = g + CORES if way == 0 else g - CORES
        return remote(src, own(i, origin), zs.at[i, way, t], zr.at[i, way, t], {"grp": to})

    def hops(which, t):
        for way in (0, 1):
            sends, _, origin, _ = line_conditions(line, z, way, t)

            @pl.when(sends)
            def _():
                for i in which:
                    hop(i, way, t, origin).start()

    def arrive(which, t, after=None):
        for way in (0, 1):
            _, receives, _, origin = line_conditions(line, z, way, t)

            @pl.when(receives)
            def _():
                for i in which:
                    hop(i, way, t, origin).wait_recv()
                if after is not None:
                    after(origin)

    deep, wide = items[:n_deep], items[n_deep:]
    for t in range(line - 1):
        hops(wide, t)
        if t == 0:
            stores = []
            for i in range(n_in):
                loads[i].wait()
                dst = (
                    tok_out.at[:, pl.ds(pl.multiple_of(s * rows, rows), rows), :]
                    if i == 0
                    else own(i - 1, z)
                )
                stores.append(pltpu.make_async_copy(stage[i], dst, local_sem.at[1, i]))
                stores[-1].start()
        arrive(wide, t)
    hops(deep, 0)
    for x in stores:
        x.wait()
    sides = []
    for i in wide:
        for j in range(1, seq_count):
            part = outs[1 + i].at[s, :, c]
            sides.append(
                remote(
                    part,
                    part,
                    ws.at[i - n_deep, j - 1],
                    wr.at[i - n_deep, j - 1],
                    {"seq": lax.rem(s + j, seq_count)},
                )
            )
            sides[-1].start()

    def twin_wide(i, k):
        part = outs[1 + i].at[k, :, c]
        return remote(part, part, ps.at[i - n_deep, k], pr.at[i - n_deep, k], twin)

    def twin_deep(i, l):
        part = outs[1 + i].at[l, c]
        return remote(part, part, dps.at[i, l], dpr.at[i, l], twin)

    for i in wide:
        twin_wide(i, s).start()
    for i in deep:
        twin_deep(i, z).start()

    def pass_on(origin):
        for i in deep:
            twin_deep(i, origin).start()

    for t in range(line - 1):
        if t > 0:
            hops(deep, t)
        arrive(deep, t, pass_on)
    for x in sides:
        x.wait_recv()
    for i in wide:
        for j in range(1, seq_count):
            twin_wide(i, lax.rem(s + seq_count - j, seq_count)).start()
    for x in toks:
        x.wait_recv()
    for i in deep:
        for l in range(line):
            twin_deep(i, l).wait()
    for i in wide:
        for k in range(seq_count):
            twin_wide(i, k).wait()
    for x in toks + sides:
        x.wait_send()
    for t in range(line - 1):
        for way in (0, 1):
            sends, _, origin, _ = line_conditions(line, z, way, t)

            @pl.when(sends)
            def _():
                for i in items:
                    hop(i, way, t, origin).wait_send()


def gather_all(seq_count, line, tok, deep, wide):
    n_deep, n_wide = len(deep), len(wide)
    shapes = [
        jax.ShapeDtypeStruct((tok.shape[0], tok.shape[1] * seq_count, tok.shape[2]), tok.dtype)
    ]
    shapes += [jax.ShapeDtypeStruct((line, CORES) + x.shape, x.dtype) for x in deep]
    shapes += [jax.ShapeDtypeStruct((seq_count, line, CORES) + x.shape, x.dtype) for x in wide]
    arrays = [tok] + list(deep) + list(wide)
    n = len(arrays)
    scratch = [pltpu.VMEM(x.shape, x.dtype) for x in arrays]
    scratch += [
        DMA((2, n)),
        DMA((seq_count - 1,)),
        DMA((seq_count - 1,)),
        DMA((n_deep + n_wide, 2, line - 1)),
        DMA((n_deep + n_wide, 2, line - 1)),
        DMA((n_wide, seq_count - 1)),
        DMA((n_wide, seq_count - 1)),
        DMA((n_wide, seq_count)),
        DMA((n_wide, seq_count)),
        DMA((n_deep, line)),
        DMA((n_deep, line)),
    ]
    return pl.pallas_call(
        functools.partial(gather_kernel, seq_count, line, n_deep, n_wide),
        out_shape=shapes,
        in_specs=[ANY] * n,
        out_specs=[ANY] * n,
        scratch_shapes=scratch,
        compiler_params=params(1),
        name="gather_all",
    )(*arrays)


def side_gather_kernel(seq_count, line, x_ref, out_ref, local_sem, send, recv):
    s, z, c, g = place(seq_count, line)
    rows = x_ref.shape[1]
    mine = out_ref.at[:, pl.ds(pl.multiple_of(s * rows, rows), rows), :]
    local = pltpu.make_async_copy(x_ref, mine, local_sem)
    local.start()
    greet(seq_count, line, s, z, c, g, side=True)
    copies = []
    for i in range(1, seq_count):
        copies.append(
            remote(
                x_ref, mine, send.at[i - 1], recv.at[i - 1], {"seq": lax.rem(s + i, seq_count)}
            )
        )
        copies[-1].start()
    local.wait()
    for x in copies:
        x.wait()


def side_gather(seq_count, line, x):
    return pl.pallas_call(
        functools.partial(side_gather_kernel, seq_count, line),
        out_shape=jax.ShapeDtypeStruct((x.shape[0], x.shape[1] * seq_count, x.shape[2]), x.dtype),
        in_specs=[WHOLE],
        out_specs=WHOLE,
        scratch_shapes=[DMA, DMA((seq_count - 1,)), DMA((seq_count - 1,))],
        compiler_params=params(2),
        name="side_gather",
    )(x)


def side_sum_kernel(seq_count, line, x_ref, out_ref, slots, send, recv):
    s, z, c, g = place(seq_count, line)
    rows = out_ref.shape[1]
    greet(seq_count, line, s, z, c, g, side=True)
    copies = []
    for i in range(1, seq_count):
        to = lax.rem(s + i, seq_count)
        copies.append(
            remote(
                x_ref.at[:, pl.ds(pl.multiple_of(to * rows, rows), rows), :],
                slots.at[i - 1],
                send.at[i - 1],
                recv.at[i - 1],
                {"seq": to},
            )
        )
        copies[-1].start()
    total = x_ref[:, pl.ds(pl.multiple_of(s * rows, rows), rows), :].astype(F32)
    for i, x in enumerate(copies):
        x.wait_recv()
        total = total + slots[i].astype(F32)
    out_ref[...] = total
    for x in copies:
        x.wait_send()


def side_sum(seq_count, line, x, collective_id):
    rows = x.shape[1] // seq_count
    return pl.pallas_call(
        functools.partial(side_sum_kernel, seq_count, line),
        out_shape=jax.ShapeDtypeStruct((x.shape[0], rows, x.shape[2]), F32),
        in_specs=[WHOLE],
        out_specs=WHOLE,
        scratch_shapes=[
            pltpu.VMEM((seq_count - 1, x.shape[0], rows, x.shape[2]), x.dtype),
            DMA((seq_count - 1,)),
            DMA((seq_count - 1,)),
        ],
        compiler_params=params(collective_id),
        name=f"side_sum_{collective_id}",
    )(x)


def sum_kernel(seq_count, line, n_deep, n_wide, *refs):
    n = n_deep + n_wide
    ins, outs = refs[: n + 1], refs[n + 1 : 2 * n + 2]
    rest = refs[2 * n + 2 :]
    pair, side, chain = rest[:n], rest[n : n + n_wide], rest[n + n_wide : 2 * n + n_wide]
    rest = rest[2 * n + n_wide :]
    g_pair, g_side, g_line, g_a, g_b = rest[:5]
    (ps, pr, ws, wr, zs, zr, gs, gr) = rest[5:]
    s, z, c, g = place(seq_count, line)
    twin = {"grp": g + 1 - 2 * c}
    deep, wide = list(range(n_deep)), list(range(n_deep, n))
    small = ins[n]
    greet(seq_count, line, s, z, c, g, twin=True, side=True, whole_line=True)

    def theirs(i):
        return ins[i].at[:, 1 - c] if i < n_deep else ins[i].at[:, :, 1 - c]

    pairs = [remote(theirs(i), pair[i], ps.at[i], pr.at[i], twin) for i in range(n)]
    small_pair = remote(small, g_pair, gs.at[0], gr.at[0], twin)
    small_pair.start()
    for x in pairs[n_deep:] + pairs[:n_deep]:
        x.start()

    small_pair.wait()
    g_a[...] = small[...] + g_pair[...]
    small_sides = []
    for j in range(1, seq_count):
        small_sides.append(
            remote(
                g_a,
                g_side.at[j - 1],
                gs.at[j],
                gr.at[j],
                {"seq": lax.rem(s + j, seq_count)},
            )
        )
        small_sides[-1].start()

    for i in wide:
        pairs[i].wait_recv()
        for k in range(seq_count):

            @pl.loop(0, line)
            def _(l):
                mixed = ins[i][k, l, c].astype(F32) + pair[i][k, l].astype(F32)
                pair[i][k, l] = mixed.astype(BF16)

    sides = {}
    for i in wide:
        for j in range(1, seq_count):
            to = lax.rem(s + j, seq_count)
            sides[i, j] = remote(
                pair[i].at[to],
                side[i - n_deep].at[j - 1],
                ws.at[i - n_deep, j - 1],
                wr.at[i - n_deep, j - 1],
                {"seq": to},
            )
            sides[i, j].start()
    for i in deep:
        pairs[i].wait_recv()
        for l in range(line):
            pair[i][l] = (ins[i][l, c].astype(F32) + pair[i][l].astype(F32)).astype(BF16)

    for x in small_sides:
        x.wait()
    total = g_a[...]
    for j in range(seq_count - 1):
        total = total + g_side[j]
    g_b[...] = total
    small_lines = []
    for j in range(1, line):
        small_lines.append(
            remote(
                g_b,
                g_line.at[j - 1],
                gs.at[seq_count - 1 + j],
                gr.at[seq_count - 1 + j],
                {"grp": lax.rem(g + CORES * j, CORES * line)},
            )
        )
        small_lines[-1].start()

    def piece(i, l):
        return pair[i].at[l] if i < n_deep else pair[i].at[s, l]

    def run_line(which):
        def hop(i, way, t, dest, first):
            src = piece(i, dest) if first else chain[i].at[way, t]
            to = g + CORES if way == 0 else g - CORES
            return remote(src, chain[i].at[way, t], zs.at[i, way, t], zr.at[i, way, t], {"grp": to})

        for t in range(line - 1):
            for way in (0, 1):
                dest = line - 1 - t if way == 0 else t
                starts = z == 0 if way == 0 else z == line - 1
                relays = (z > 0) & (z < dest) if way == 0 else (z < line - 1) & (z > dest)

                @pl.when(starts)
                def _():
                    for i in which:
                        hop(i, way, t, dest, True).start()

                @pl.when(relays)
                def _():
                    for i in which:
                        hop(i, way, t, dest, False).wait_recv()
                        mixed = chain[i][way, t].astype(F32) + piece(i, dest)[...].astype(F32)
                        chain[i][way, t] = mixed.astype(BF16)
                        hop(i, way, t, dest, False).start()

        for i in which:
            outs[i][...] = piece(i, z)[...].astype(F32)
        for t in range(line - 1):
            for way in (0, 1):
                dest = line - 1 - t if way == 0 else t

                @pl.when((z == dest))
                def _():
                    for i in which:
                        hop(i, way, t, dest, False).wait_recv()
                        outs[i][...] += chain[i][way, t].astype(F32)

                @pl.when(z == 0 if way == 0 else z == line - 1)
                def _():
                    for i in which:
                        hop(i, way, t, dest, True).wait_send()

                @pl.when((z > 0) & (z < dest) if way == 0 else (z < line - 1) & (z > dest))
                def _():
                    for i in which:
                        hop(i, way, t, dest, False).wait_send()

    run_line(deep)
    for i in wide:
        for j in range(1, seq_count):
            sides[i, j].wait()

        @pl.loop(0, line)
        def _(l):
            mixed = pair[i][s, l].astype(F32)
            for j in range(1, seq_count):
                mixed = mixed + side[i - n_deep][j - 1, l].astype(F32)
            pair[i][s, l] = mixed.astype(BF16)

    run_line(wide)
    for x in pairs:
        x.wait_send()
    for x in small_lines:
        x.wait()
    total = g_b[...]
    for j in range(line - 1):
        total = total + g_line[j]
    outs[n][...] = total


def sum_all(seq_count, line, deep, wide, small):
    n_deep, n_wide = len(deep), len(wide)
    n = n_deep + n_wide
    shapes = [jax.ShapeDtypeStruct(x.shape[2:], F32) for x in deep]
    shapes += [jax.ShapeDtypeStruct(x.shape[3:], F32) for x in wide]
    shapes += [jax.ShapeDtypeStruct(small.shape, F32)]
    scratch = [pltpu.VMEM((line,) + x.shape[2:], BF16) for x in deep]
    scratch += [pltpu.VMEM((seq_count, line) + x.shape[3:], BF16) for x in wide]
    scratch += [pltpu.VMEM((seq_count - 1, line) + x.shape[3:], BF16) for x in wide]
    scratch += [pltpu.VMEM((2, line - 1) + x.shape[2:], BF16) for x in deep]
    scratch += [pltpu.VMEM((2, line - 1) + x.shape[3:], BF16) for x in wide]
    scratch += [
        pltpu.VMEM(small.shape, F32),
        pltpu.VMEM((seq_count - 1,) + small.shape, F32),
        pltpu.VMEM((line - 1,) + small.shape, F32),
        pltpu.VMEM(small.shape, F32),
        pltpu.VMEM(small.shape, F32),
        DMA((n,)),
        DMA((n,)),
        DMA((n_wide, seq_count - 1)),
        DMA((n_wide, seq_count - 1)),
        DMA((n, 2, line - 1)),
        DMA((n, 2, line - 1)),
        DMA((seq_count + line,)),
        DMA((seq_count + line,)),
    ]
    return pl.pallas_call(
        functools.partial(sum_kernel, seq_count, line, n_deep, n_wide),
        out_shape=shapes,
        in_specs=[WHOLE] * (n + 1),
        out_specs=[WHOLE] * (n + 1),
        scratch_shapes=scratch,
        compiler_params=params(5),
        name="sum_all",
    )(*deep, *wide, small)


def signs_of(rows):
    pos = lax.broadcasted_iota(jnp.int32, (rows, 1), 0)
    return 1.0 - 2.0 * lax.rem(pos, 2).astype(F32)


def lagged(values, lag, span):
    pos = lax.broadcasted_iota(jnp.int32, (values.shape[0], 1), 0)
    return jnp.where(lax.rem(pos, span) >= lag, pltpu.roll(values, lag, 0), 0.0)


def led(values, lag, span):
    rows = values.shape[0]
    pos = lax.broadcasted_iota(jnp.int32, (rows, 1), 0)
    return jnp.where(lax.rem(pos, span) < span - lag, pltpu.roll(values, rows - lag, 0), 0.0)


def spread(row, rows):
    wide = jnp.broadcast_to(row, (rows, row.shape[1]))
    return pltpu.roll(wide, 0, 1, stride=1, stride_axis=0)[:, :rows].astype(BF16)


def forward_kernel(spans, x_ref, gain_ref, row_ref, w_ref, ar_ref, ul_ref, u_ref, y_ref, both, acc):
    k = pl.program_id(0)
    rows, width = x_ref.shape[1], x_ref.shape[2]
    signs = signs_of(rows)

    @pl.when(k == 0)
    def _():
        for m in range(2):
            x = x_ref[m].astype(F32)
            inv = lax.rsqrt(jnp.mean(x * x, axis=-1, keepdims=True) + EPSILON)
            u = (x * inv * gain_ref[...]).astype(BF16)
            wide = u.astype(F32)
            u_ref[m] = u
            both[m, :, :width] = u
            both[m, :, width:] = (wide * signs).astype(BF16)
            acc[m] = dot_nn(u, ar_ref[:width])
            for lag in (1, 2):
                acc[m] += dot_nn(
                    lagged(wide, lag, spans[m]).astype(BF16),
                    ar_ref[lag * width : (lag + 1) * width],
                )

    table = spread(row_ref[0], rows)
    for m in range(2):
        span = spans[m]
        for j in range(rows // span):
            part = slice(j * span, (j + 1) * span)
            conv = dot_nn(table[:span, :span], both[m, part, :])
            plus = conv[:, :width].astype(BF16)
            minus = (conv[:, width:] * signs[part]).astype(BF16)
            ul_ref[0, 0, m, part, :] = plus
            ul_ref[0, 1, m, part, :] = minus
        acc[m] += dot_nn(ul_ref[0, 0, m], w_ref[0, 0]) + dot_nn(ul_ref[0, 1, m], w_ref[0, 1])

    @pl.when(k == pl.num_programs(0) - 1)
    def _():
        y_ref[...] = acc[...].astype(BF16)


def forward_mix(spans, x, gain, table, w, ar):
    count = table.shape[0]
    _, rows, width = x.shape
    full = lambda *shape: pl.BlockSpec(shape, lambda k: (0,) * len(shape))
    return pl.pallas_call(
        functools.partial(forward_kernel, spans),
        grid=(count,),
        out_shape=[
            jax.ShapeDtypeStruct((count, 2, 2, rows, width), BF16),
            jax.ShapeDtypeStruct((2, rows, width), BF16),
            jax.ShapeDtypeStruct((2, rows, width), BF16),
        ],
        in_specs=[
            full(2, rows, width),
            full(1, width),
            pl.BlockSpec((1, 1, 2 * rows), lambda k: (k, 0, 0)),
            pl.BlockSpec((1, 2, width, width), lambda k: (k, 0, 0, 0)),
            full(3 * width, width),
        ],
        out_specs=[
            pl.BlockSpec((1, 2, 2, rows, width), lambda k: (k, 0, 0, 0, 0)),
            full(2, rows, width),
            full(2, rows, width),
        ],
        scratch_shapes=[pltpu.VMEM((2, rows, 2 * width), BF16), pltpu.VMEM((2, rows, width), F32)],
        compiler_params=params(),
        name="forward_mix",
    )(x, gain, table, w, ar)


def backward_kernel(
    spans, dy_ref, u_ref, row_ref, w_ref, ul_ref, ar_ref, dw_ref, dar_ref, du_ref, both, acc
):
    k = pl.program_id(0)
    rows, width = dy_ref.shape[1], dy_ref.shape[2]
    signs = signs_of(rows)

    @pl.when(k == 0)
    def _():
        for m in range(2):
            dy = dy_ref[m]
            both[m, :, :width] = dy
            both[m, :, width:] = (dy.astype(F32) * signs).astype(BF16)
            acc[m] = dot_nt(dy, ar_ref[:width])
            for lag in (1, 2):
                acc[m] += led(
                    dot_nt(dy, ar_ref[lag * width : (lag + 1) * width]), lag, spans[m]
                )
        for lag in (0, 1, 2):
            total = 0.0
            for m in range(2):
                u = u_ref[m]
                if lag:
                    u = lagged(u.astype(F32), lag, spans[m]).astype(BF16)
                total = total + dot_tn(u, dy_ref[m])
            dar_ref[lag * width : (lag + 1) * width, :] = total.astype(BF16)

    table = spread(row_ref[0], rows)
    for m in range(2):
        span = spans[m]
        for j in range(rows // span):
            part = slice(j * span, (j + 1) * span)
            conv = dot_nn(table[:span, :span], both[m, part, :])
            plus = conv[:, :width].astype(BF16)
            minus = (conv[:, width:] * signs[part]).astype(BF16)
            acc[m, part, :] += dot_nt(plus, w_ref[0, 0]) + dot_nt(minus, w_ref[0, 1])
    for p in range(2):
        total = dot_tn(ul_ref[0, p, 0], dy_ref[0]) + dot_tn(ul_ref[0, p, 1], dy_ref[1])
        dw_ref[0, p] = total.astype(BF16)

    @pl.when(k == pl.num_programs(0) - 1)
    def _():
        du_ref[...] = acc[...].astype(BF16)


def backward_mix(spans, dy, u, table, w, ul, ar):
    count = table.shape[0]
    _, rows, width = dy.shape
    full = lambda *shape: pl.BlockSpec(shape, lambda k: (0,) * len(shape))
    return pl.pallas_call(
        functools.partial(backward_kernel, spans),
        grid=(count,),
        out_shape=[
            jax.ShapeDtypeStruct((count, 2, width, width), BF16),
            jax.ShapeDtypeStruct((3 * width, width), BF16),
            jax.ShapeDtypeStruct((2, rows, width), BF16),
        ],
        in_specs=[
            full(2, rows, width),
            full(2, rows, width),
            pl.BlockSpec((1, 1, 2 * rows), lambda k: (k, 0, 0)),
            pl.BlockSpec((1, 2, width, width), lambda k: (k, 0, 0, 0)),
            pl.BlockSpec((1, 2, 2, rows, width), lambda k: (k, 0, 0, 0, 0)),
            full(3 * width, width),
        ],
        out_specs=[
            pl.BlockSpec((1, 2, width, width), lambda k: (k, 0, 0, 0)),
            full(3 * width, width),
            full(2, rows, width),
        ],
        scratch_shapes=[pltpu.VMEM((2, rows, 2 * width), BF16), pltpu.VMEM((2, rows, width), F32)],
        compiler_params=params(),
        name="backward_mix",
    )(dy, u, table, w, ul, ar)


def mix_back_kernel(seq_count, line, *refs):
    (layout_ref, row_ref, ar_ref, x_ref, scale_ref, mlp_ref, w_hbm, ul_hbm, wide_hbm) = refs[:9]
    large = refs[9:12]
    (tg_hbm, dw_hbm, dar_ref, gg_ref, ug_ref, dg_ref, small_ref) = refs[12:19]
    (keep, dsig, acc, conv, du_in, ul_buf, w_buf, dar) = refs[19:27]
    (deep, deep_in, deep_run, wide, wide_in, wide_side, wide_run) = refs[27:34]
    (g_own, g_pair, g_side, g_sum, g_line) = refs[34:39]
    (dy, u_ref, hg_ref) = held = refs[39:42]
    (tg_ref, dw_ref, end_sem) = refs[42:45]
    (load_sem, dus, dur, ps, pr, zs, zr, wps, wpr, ws, wr, wzs, wzr, gs, gr) = refs[45:]
    tg_store = pltpu.make_async_copy(tg_ref, tg_hbm, end_sem.at[0])
    dw_store = pltpu.make_async_copy(dw_ref, dw_hbm, end_sem.at[1])
    s, z, c, g = place(seq_count, line)
    twin = {"grp": g + 1 - 2 * c}
    rows, width = dy.shape[1], dy.shape[2]
    block = x_ref.shape[1]
    short = [layout_ref[0, m].astype(F32) for m in range(2)]
    count = w_hbm.shape[0]
    per_chip = 2 * count // line
    n = per_chip * width // CORES
    ar_rows = ar_ref.shape[0]
    ar_share = ar_rows // (line * CORES)
    lanes = 128
    ar_chunks = ar_rows // lanes
    share = gg_ref.shape[0]
    hn = n // 2
    down_share = dg_ref.shape[0]
    mine = pl.ds(pl.multiple_of(s * block, block), block)
    low = (z < line // 2).astype(jnp.int32)

    def dest(i):
        return low * (line - 1 - 2 * i) + i

    def load(i):
        return pltpu.make_async_copy(
            ul_hbm.at[pl.ds(dest(i) * per_chip, per_chip)], ul_buf.at[i % 2], load_sem.at[i % 2]
        )

    load_w = pltpu.make_async_copy(w_hbm, w_buf, load_sem.at[2])
    fetch = [pltpu.make_async_copy(large[i], held[i], load_sem.at[3 + i]) for i in range(3)]
    load_wide = pltpu.make_async_copy(wide_hbm.at[c], wide, load_sem.at[6])
    for x in fetch[:1] + [load(0)] + fetch[1:2] + [load(1), load_wide, fetch[2], load_w]:
        x.start()
    greet(seq_count, line, s, z, c, g, twin=True, side=True, whole_line=True)

    def ar_place(i):
        at = s * ar_chunks + i
        lag = lax.div(at, width // lanes)
        col = lax.rem(at, width // lanes)
        return lag, pl.ds(pl.multiple_of(col * lanes, lanes), lanes)

    halves = (pl.ds(0, hn), pl.ds(hn, deep_in.shape[1] - hn))

    def twin_deep(i, h):
        l = dest(i)
        src, dst = deep.at[1 - c, l, halves[h]], deep_in.at[l, halves[h]]
        return remote(src, dst, ps.at[h, i], pr.at[h, i], twin)

    def hop(kind, way, t, h, first):
        run, own, send, recv, parts = kind
        target = line - 1 - t if way == 0 else t
        dst = run.at[way, t, parts[h]]
        src = own(target, parts[h]) if first else dst
        to = g + CORES if way == 0 else g - CORES
        return remote(src, dst, send.at[h, way, t], recv.at[h, way, t], {"grp": to})

    def deep_own(l, part):
        return deep_in.at[l, part]

    def wide_own(l, part):
        return wide_in.at[s, l, part]

    deep_line = (deep_run, deep_own, zs, zr, halves)
    wide_line = (wide_run, wide_own, wzs, wzr, (pl.ds(0, wide_run.shape[2]),))

    def begin(kind, t, h):
        for way in (0, 1):

            @pl.when(z == 0 if way == 0 else z == line - 1)
            def _():
                hop(kind, way, t, h, True).start()

    def relay(kind, phase, h):
        run, own, part = kind[0], kind[1], kind[4][h]
        for way in (0, 1):
            for t in range(phase):
                at = phase - t if way == 0 else line - 1 - (phase - t)
                target = line - 1 - t if way == 0 else t

                @pl.when(z == at)
                def _():
                    hop(kind, way, t, h, False).wait_recv()
                    mixed = run[way, t, part].astype(F32) + own(target, part)[...].astype(F32)
                    run[way, t, part] = mixed.astype(BF16)
                    hop(kind, way, t, h, False).start()

    def segment(i, cc, lo, hi):
        j = lo // width
        cols = slice(lo - j * width, hi - j * width)
        val = dot_tn(ul_buf[i % 2, j, 0, :, cols], dy[0])
        val = (val + dot_tn(ul_buf[i % 2, j, 1, :, cols], dy[1])).astype(BF16)
        deep[cc, dest(i), lo - cc * n : hi - cc * n, :] = val

    def compute_half(i, h):
        for cc in range(CORES):
            lo, end = cc * n + h * hn, cc * n + (h + 1) * hn
            while lo < end:
                hi = min(end, (lo // width + 1) * width)
                segment(i, cc, lo, hi)
                lo = hi
        twin_deep(i, h).start()

    def compute(i):
        l = dest(i)
        load(i).wait()
        for j in range(per_chip):
            val = dot_tn(ul_buf[i % 2, j, 0], dy[0]) + dot_tn(ul_buf[i % 2, j, 1], dy[1])
            val = val.astype(BF16)
            for cc in range(CORES):
                lo, hi = max(j * width, cc * n), min((j + 1) * width, (cc + 1) * n)
                if lo < hi:
                    deep[cc, l, lo - cc * n : hi - cc * n, :] = val[lo - j * width : hi - j * width]
        for h in range(2):
            twin_deep(i, h).start()
        if i + 2 < line:
            load(i + 2).start()

    def combine(i, h):
        l, part = dest(i), halves[h]
        twin_deep(i, h).wait_recv()
        mixed = deep[c, l, part].astype(F32) + deep_in[l, part].astype(F32)
        deep_in[l, part] = mixed.astype(BF16)
        if i < line - 1:
            begin(deep_line, i, h)

    fetch[0].wait()
    load(0).wait()
    compute_half(0, 0)
    fetch[1].wait()
    for i in range(ar_chunks):
        lag, cols = ar_place(i)
        total = 0.0
        for m in range(2):
            v = lagged_by(u_ref[m, :, cols].astype(F32), lag, short[m]).astype(BF16)
            total = total + dot_tn(v, dy[m])
        dar[i * lanes : (i + 1) * lanes, :] = total.astype(BF16)
    for l in range(line):
        for cc in range(CORES):
            r = (l * CORES + cc) * ar_share
            deep[cc, l, n:, :] = dar[r : r + ar_share, :]
    compute_half(0, 1)
    load(2).start()
    wide_twin = remote(wide_hbm.at[1 - c], wide_in, wps, wpr, twin)
    wide_twin.start()
    combine(0, 0)
    combine(0, 1)
    compute(1)

    load_wide.wait()
    wide_twin.wait_recv()
    for k in range(seq_count):

        @pl.loop(0, line)
        def _(l):
            mixed = wide[k, l].astype(F32) + wide_in[k, l].astype(F32)
            wide_in[k, l] = mixed.astype(BF16)

    sides = []
    for j in range(1, seq_count):
        to = lax.rem(s + j, seq_count)
        sides.append(
            remote(wide_in.at[to], wide_side.at[j - 1], ws.at[j - 1], wr.at[j - 1], {"seq": to})
        )
        sides[-1].start()

    for h in range(2):
        combine(1, h)
    for i in range(2, line):
        compute(i)
        for h in range(2):
            combine(i, h)
    for phase in range(1, line - 2):
        for h in range(2):
            relay(deep_line, phase, h)

    signs = signs_of(rows)
    for m in range(2):
        dsig[m] = (dy[m].astype(F32) * signs).astype(BF16)
        keep[m] = reach(rows, short[m])
    acc[...] = jnp.zeros_like(acc)
    for i in range(ar_chunks):
        lag, cols = ar_place(i)
        for m in range(2):
            val = dot_nt(dy[m], ar_ref[i * lanes : (i + 1) * lanes, :])
            acc[m, :, cols] += led_by(val, lag, short[m])
    load_w.wait()

    def filter_step(k):
        table = shifted(row_ref[pl.ds(s * count + k, 1), :], rows)
        for m in range(2):
            kept_table = table * keep[m]
            conv[0] = dot_nn(kept_table, dy[m]).astype(BF16)
            conv[1] = (dot_nn(kept_table, dsig[m]) * signs).astype(BF16)
            acc[m] += dot_nt(conv[0], w_buf[k, 0]) + dot_nt(conv[1], w_buf[k, 1])

    third = count // 3
    pl.loop(0, third)(filter_step)
    relay(deep_line, line - 2, 0)
    pl.loop(third, 2 * third)(filter_step)
    relay(deep_line, line - 2, 1)
    pl.loop(2 * third, count)(filter_step)
    conv[...] = acc[...].astype(BF16)
    du_copies = []
    for i in range(1, seq_count):
        to = lax.rem(s + i, seq_count)
        du_copies.append(
            remote(
                conv.at[:, pl.ds(pl.multiple_of(to * block, block), block), :],
                du_in.at[i - 1],
                dus.at[i - 1],
                dur.at[i - 1],
                {"seq": to},
            )
        )
        du_copies[-1].start()

    fetch[2].wait()
    for x in du_copies:
        x.wait_recv()
    gain = jnp.zeros((1, width), F32)
    for m in range(2):
        grad = conv[m, mine, :].astype(F32)
        for i in range(seq_count - 1):
            grad = grad + du_in[i, m].astype(F32)
        x = x_ref[m].astype(F32)
        inv = lax.rsqrt(jnp.mean(x * x, axis=-1, keepdims=True) + EPSILON)
        scaled = grad * scale_ref[0:1, :]
        gain = gain + jnp.sum(grad * x * inv, axis=0, keepdims=True)
        centre = jnp.mean(scaled * x, axis=-1, keepdims=True)
        tg_ref[m] = hg_ref[m] + inv * scaled - x * (inv * inv * inv) * centre
    tg_store.start()
    g_own[...] = jnp.zeros_like(g_own)
    g_own[0:1, :] = gain
    g_own[1:2, :] = mlp_ref[0:1, :]
    small_pair = remote(g_own, g_pair, gs.at[0], gr.at[0], twin)
    small_pair.start()

    for x in sides:
        x.wait_recv()

    @pl.loop(0, line)
    def _(l):
        mixed = wide_in[s, l].astype(F32)
        for j in range(seq_count - 1):
            mixed = mixed + wide_side[j, l].astype(F32)
        wide_in[s, l] = mixed.astype(BF16)

    for t in range(line - 1):
        begin(wide_line, t, 0)

    small_pair.wait()
    g_own[...] = g_own[...] + g_pair[...]
    small_sides = []
    for j in range(1, seq_count):
        small_sides.append(
            remote(
                g_own, g_side.at[j - 1], gs.at[j], gr.at[j], {"seq": lax.rem(s + j, seq_count)}
            )
        )
        small_sides[-1].start()

    dw_ref[...] = deep_in[z, :n, :].astype(F32)
    dar_ref[...] = deep_in[z, n:, :].astype(F32)
    for x in small_sides:
        x.wait()
    total = g_own[...]
    for j in range(seq_count - 1):
        total = total + g_side[j]
    g_sum[...] = total
    small_lines = []
    for j in range(1, line):
        small_lines.append(
            remote(
                g_sum,
                g_line.at[j - 1],
                gs.at[seq_count - 1 + j],
                gr.at[seq_count - 1 + j],
                {"grp": lax.rem(g + CORES * j, CORES * line)},
            )
        )
        small_lines[-1].start()

    def last(kind, add):
        for t in range(line - 1):
            for way in (0, 1):
                target = line - 1 - t if way == 0 else t

                @pl.when(z == target)
                def _():
                    for h in range(len(kind[4])):
                        hop(kind, way, t, h, False).wait_recv()
                    add(kind[0][way, t].astype(F32))

    def add_deep(val):
        dw_ref[...] += val[:n]
        dar_ref[...] += val[n:]

    def add_wide(val):
        gg_ref[...] += val[:share]
        ug_ref[...] += val[share : 2 * share]
        for q in range(down_share // share):
            dg_ref[q * share : (q + 1) * share, :] += val[2 * share :, q * width : (q + 1) * width]

    last(deep_line, add_deep)
    dw_store.start()
    for phase in range(1, line - 1):
        relay(wide_line, phase, 0)
    own = wide_in[s, z].astype(F32)
    gg_ref[...] = own[:share]
    ug_ref[...] = own[share : 2 * share]
    for q in range(down_share // share):
        dg_ref[q * share : (q + 1) * share, :] = own[2 * share :, q * width : (q + 1) * width]
    last(wide_line, add_wide)

    for x in small_lines:
        x.wait()
    total = g_sum[...]
    for j in range(line - 1):
        total = total + g_line[j]
    at = (s * (CORES * line) + g) * (width // (seq_count * CORES * line))
    small_ref[...] = pltpu.roll(total, lax.rem(width - at, width), 1)

    for x in sides + du_copies:
        x.wait_send()
    tg_store.wait()
    dw_store.wait()
    wide_twin.wait_send()
    for i in range(line):
        for h in range(2):
            twin_deep(i, h).wait_send()
    for kind in (deep_line, wide_line):
        for t in range(line - 1):
            for way in (0, 1):
                target = line - 1 - t if way == 0 else t

                @pl.when(z < target if way == 0 else z > target)
                def _():
                    for h in range(len(kind[4])):
                        hop(kind, way, t, h, False).wait_send()


def mix_back(
    seq_count, line, layout, dy, u, filters, w, ul, ar, x, hg, scale, grads, mlp_grad, shares
):
    share, down_share, deep_share, ar_share = shares
    _, block, width = x.shape
    rows = block * seq_count
    count = w.shape[0]
    per_chip = 2 * count // line
    small = (8, width)
    part = grads.shape[3:]
    hidden_units = part[1]
    out_shape = [
        jax.ShapeDtypeStruct((2, block, width), F32),
        jax.ShapeDtypeStruct((deep_share, width), F32),
        jax.ShapeDtypeStruct((ar_share, width), F32),
        jax.ShapeDtypeStruct((share, hidden_units), F32),
        jax.ShapeDtypeStruct((share, hidden_units), F32),
        jax.ShapeDtypeStruct((down_share, width), F32),
        jax.ShapeDtypeStruct(small, F32),
    ]
    deep = (deep_share + ar_share, width)
    scratch = [
        pltpu.VMEM((2, rows, rows), BF16),
        pltpu.VMEM((2, rows, width), BF16),
        pltpu.VMEM((2, rows, width), F32),
        pltpu.VMEM((2, rows, width), BF16),
        pltpu.VMEM((seq_count - 1, 2, block, width), BF16),
        pltpu.VMEM((2, per_chip, 2, rows, width), BF16),
        pltpu.VMEM(w.shape, BF16),
        pltpu.VMEM(ar.shape, BF16),
        pltpu.VMEM((CORES, line) + deep, BF16),
        pltpu.VMEM((line,) + deep, BF16),
        pltpu.VMEM((2, line - 1) + deep, BF16),
        pltpu.VMEM((seq_count, line) + part, BF16),
        pltpu.VMEM((seq_count, line) + part, BF16),
        pltpu.VMEM((seq_count - 1, line) + part, BF16),
        pltpu.VMEM((2, line - 1) + part, BF16),
        pltpu.VMEM(small, F32),
        pltpu.VMEM(small, F32),
        pltpu.VMEM((seq_count - 1,) + small, F32),
        pltpu.VMEM(small, F32),
        pltpu.VMEM((line - 1,) + small, F32),
    ]
    large = [dy, u, hg]
    scratch += [pltpu.VMEM(v.shape, v.dtype) for v in large]
    scratch += [pltpu.VMEM(v.shape, F32) for v in out_shape[:2]]
    scratch += [
        DMA((2,)),
        DMA((7,)),
        DMA((seq_count - 1,)),
        DMA((seq_count - 1,)),
        DMA((2, line)),
        DMA((2, line)),
        DMA((2, 2, line - 1)),
        DMA((2, 2, line - 1)),
        DMA,
        DMA,
        DMA((seq_count - 1,)),
        DMA((seq_count - 1,)),
        DMA((1, 2, line - 1)),
        DMA((1, 2, line - 1)),
        DMA((seq_count + line,)),
        DMA((seq_count + line,)),
    ]
    return pl.pallas_call(
        functools.partial(mix_back_kernel, seq_count, line),
        out_shape=out_shape,
        in_specs=[pl.BlockSpec(memory_space=pltpu.SMEM)] + [WHOLE] * 5 + [ANY] * 6,
        out_specs=[ANY] * 2 + [WHOLE] * 5,
        scratch_shapes=scratch,
        compiler_params=params(6),
        name="mix_back",
    )(layout, filters, ar, x, scale, mlp_grad, w, ul, grads, *large)


def kept(rows, short, lag):
    pos = lax.broadcasted_iota(jnp.int32, (rows, 1), 0)
    whole = (pos >= lag).astype(F32)
    return whole * (1.0 - short * (1.0 - (lax.rem(pos, rows // 4) >= lag).astype(F32)))


def lagged_by(values, lag, short):
    rows = values.shape[0]
    one = pltpu.roll(values, 1, 0) * kept(rows, short, 1)
    two = pltpu.roll(values, 2, 0) * kept(rows, short, 2)
    return jnp.where(lag == 0, values, jnp.where(lag == 1, one, two))


def led_by(values, lag, short):
    rows = values.shape[0]
    one = pltpu.roll(values * kept(rows, short, 1), rows - 1, 0)
    two = pltpu.roll(values * kept(rows, short, 2), rows - 2, 0)
    return jnp.where(lag == 0, values, jnp.where(lag == 1, one, two))


def reach(rows, short):
    down = lax.broadcasted_iota(jnp.int32, (rows, rows), 0)
    over = lax.broadcasted_iota(jnp.int32, (rows, rows), 1)
    same = (lax.div(down, rows // 4) == lax.div(over, rows // 4)).astype(F32)
    return ((over >= down).astype(F32) * (1.0 - short * (1.0 - same))).astype(BF16)


def shifted(row, rows):
    wide = jnp.broadcast_to(row, (rows, rows))
    return pltpu.roll(wide, 0, 1, stride=1, stride_axis=0).astype(BF16)


def mix_front_kernel(seq_count, line, *refs):
    (layout_ref, tok_ref, row_ref, mix_gain, mlp_gain, cot_ref, spec_hbm, ar_hbm) = refs[:8]
    wide_in = refs[8:11]
    (w_hbm, ul_hbm, u_hbm) = refs[11:14]
    results = refs[14:16]
    (dy_hbm, grads_hbm) = refs[16:18]
    (ar_ref, gain_out, mlp_ref) = refs[18:21]
    (grads, x_all, both, acc, y_bf, y_in, w_buf, ul_buf, keep, hid, dz, dy_own) = refs[21:33]
    (z_ref, gb_ref, ub_ref, mixed_ref, hg_ref, out_ref) = refs[33:39]
    wide_buf = refs[39:42]
    (g_pad, g_own, g_side, g_sum, g_line, g_all, g_twin) = refs[42:49]
    (load_sem, ul_sem, w_sem, ts, tr, ys, yr, zs, zr, hs, hr) = refs[49:60]
    (ps, pr, ws, wr, wps, wpr, gs, gr, ds_, dr_, end_sem) = refs[60:]
    s, z, c, g = place(seq_count, line)
    twin = {"grp": g + 1 - 2 * c}
    rows, width = x_all.shape[1], x_all.shape[2]
    block = tok_ref.shape[1]
    n = spec_hbm.shape[0]
    hn = n // 2
    blocks = ul_buf.shape[0]
    count = blocks // 2
    per_chip = blocks // line
    lanes = 128
    wide = range(3)
    mine = pl.ds(pl.multiple_of(s * block, block), block)
    short = [layout_ref[0, m].astype(F32) for m in range(2)]

    def piece(l, h):
        return w_buf.at[l, pl.ds(pl.multiple_of(c * n + h * hn, hn), hn), :]

    def wide_own(i, l):
        return wide_buf[i].at[s, l, c]

    load_w = [
        pltpu.make_async_copy(spec_hbm.at[pl.ds(h * hn, hn)], piece(z, h), load_sem.at[h])
        for h in range(2)
    ]
    load_ar = pltpu.make_async_copy(ar_hbm, ar_ref.at[z, c], load_sem.at[2])
    loads = [pltpu.make_async_copy(wide_in[i], wide_own(i, z), load_sem.at[3 + i]) for i in wide]
    for x in load_w + [load_ar] + loads:
        x.start()
    at = (s * (CORES * line) + g) * (width // (seq_count * CORES * line))
    g_pad[...] = jnp.zeros_like(g_pad)
    g_pad[0:1, : mix_gain.shape[1]] = mix_gain[...].astype(F32)
    g_pad[1:2, : mlp_gain.shape[1]] = mlp_gain[...].astype(F32)
    g_own[...] = pltpu.roll(g_pad[...], at, 1).astype(BF16)
    greet(seq_count, line, s, z, c, g, twin=True, side=True, whole_line=True)

    gain_sides = []
    toks = []
    for i in range(1, seq_count):
        to = {"seq": lax.rem(s + i, seq_count)}
        gain_sides.append(remote(g_own, g_side.at[i - 1], gs.at[i - 1], gr.at[i - 1], to))
        gain_sides[-1].start()
    for i in range(1, seq_count):
        to = {"seq": lax.rem(s + i, seq_count)}
        toks.append(remote(tok_ref, x_all.at[:, mine, :], ts.at[i - 1], tr.at[i - 1], to))
        toks[-1].start()

    def onward(way):
        return {"grp": g + CORES if way == 0 else g - CORES}

    def early_own(i, l):
        return ar_ref.at[l, c] if i == 3 else wide_own(i, l)

    def early_hops(way, t, origin):
        hops = []
        for i in range(4):
            if t > 0:
                src = early_own(i, origin)
            else:
                src = ar_hbm if i == 3 else wide_in[i]
            hops.append(
                remote(src, early_own(i, origin), hs.at[i, way, t], hr.at[i, way, t], onward(way))
            )
        return hops

    def deep_hops(h):
        def build(way, t, origin):
            src = spec_hbm.at[pl.ds(h * hn, hn)] if t == 0 else piece(origin, h)
            dst = piece(origin, h)
            return [remote(src, dst, zs.at[h, way, t], zr.at[h, way, t], onward(way))]

        return build

    def first(build):
        for way in (0, 1):
            sends, _, origin, _ = line_conditions(line, z, way, 0)

            @pl.when(sends)
            def _():
                for x in build(way, 0, origin):
                    x.start()

    def arrive(build, t, after):
        for way in (0, 1):
            _, receives, _, origin = line_conditions(line, z, way, t)

            @pl.when(receives)
            def _():
                for x in build(way, t, origin):
                    x.wait_recv()
                if t + 1 < line - 1:
                    sends = line_conditions(line, z, way, t + 1)[0]

                    @pl.when(sends)
                    def _():
                        for x in build(way, t + 1, origin):
                            x.start()

                after(origin)

    def sent(build):
        for t in range(line - 1):
            for way in (0, 1):
                sends, _, origin, _ = line_conditions(line, z, way, t)

                @pl.when(sends)
                def _():
                    for x in build(way, t, origin):
                        x.wait_send()

    def sides(l, own=False):
        copies = []
        for i in wide:
            for j in range(1, seq_count):
                src = wide_in[i] if own else wide_own(i, l)
                to = {"seq": lax.rem(s + j, seq_count)}
                copies.append(
                    remote(src, wide_own(i, l), ws.at[i, l, j - 1], wr.at[i, l, j - 1], to)
                )
        return copies

    def begin_sides(l):
        for x in sides(l):
            x.start()

    def twin_deep(l, h):
        return remote(piece(l, h), piece(l, h), ps.at[h, l], pr.at[h, l], twin)

    first(early_hops)
    total = g_own[...]
    for i, x in enumerate(gain_sides):
        x.wait_recv()
        total = total + g_side[i]
    g_sum[...] = total
    gain_lines = []
    for j in range(1, line):
        k = seq_count - 2 + j
        to = {"grp": lax.rem(g + CORES * j, CORES * line)}
        gain_lines.append(remote(g_sum, g_line.at[j - 1], gs.at[k], gr.at[k], to))
        gain_lines[-1].start()
    first(deep_hops(0))
    for x in sides(z, True):
        x.start()
    x_all[:, mine, :] = tok_ref[...]
    for h in range(2):
        load_w[h].wait()
        twin_deep(z, h).start()
    for x in loads + [load_ar]:
        x.wait()
    for m in range(2):
        keep[m] = reach(rows, short[m])
    arrive(early_hops, 0, begin_sides)
    first(deep_hops(1))
    total = g_sum[...]
    for j, x in enumerate(gain_lines):
        x.wait_recv()
        total = total + g_line[j]
    g_all[...] = total
    k = seq_count + line - 2
    gain_twin = remote(g_all, g_twin, gs.at[k], gr.at[k], twin)
    gain_twin.start()
    for x in toks:
        x.wait_recv()
    gain_twin.wait_recv()
    gain = g_all[...].astype(F32) + g_twin[...].astype(F32)
    gain_out[...] = gain[:8]

    signs = signs_of(rows)
    for m in range(2):
        x = x_all[m].astype(F32)
        inv = lax.rsqrt(jnp.mean(x * x, axis=-1, keepdims=True) + EPSILON)
        u = (x * inv * gain[0:1, :]).astype(BF16)
        both[m, :, :width] = u
        both[m, :, width:] = (u.astype(F32) * signs).astype(BF16)
    u_store = pltpu.make_async_copy(both.at[:, :, pl.ds(0, width)], u_hbm, end_sem.at[0])
    u_store.start()

    def ul_store(k):
        part = pl.ds(2 * k, 2)
        return pltpu.make_async_copy(ul_buf.at[part], ul_hbm.at[part], ul_sem.at[k])

    def filter_step(k):
        table = shifted(row_ref[pl.ds(s * count + k, 1), :], rows)
        for m in range(2):
            val = dot_tn(table * keep[m], both[m])
            ul_buf[2 * k, m] = val[:, :width].astype(BF16)
            ul_buf[2 * k + 1, m] = (val[:, width:] * signs).astype(BF16)
        ul_store(k).start()

    def add_one(l, h, m):
        total = 0.0
        for cc in range(CORES):
            lo, end = cc * n + h * hn, cc * n + (h + 1) * hn
            while lo < end:
                j = lo // width
                hi = min(end, (j + 1) * width)
                left = ul_buf[l * per_chip + j, m, :, lo - j * width : hi - j * width]
                total = total + dot_nn(left, w_buf[l, lo:hi, :])
                lo = hi
        acc[m] += total

    def add_part(l, h):
        pl.loop(0, 2)(lambda m: add_one(l, h, m))

    def w_store(l):
        return pltpu.make_async_copy(w_buf.at[l], w_hbm.at[l], w_sem.at[l])

    def nothing(origin):
        pass

    def deep_arrive(t, h):
        arrive(deep_hops(h), t, lambda origin: twin_deep(origin, h).start())

    def deep_add(t, h):
        for way in (0, 1):
            _, receives, _, origin = line_conditions(line, z, way, t)

            @pl.when(receives)
            def _():
                twin_deep(origin, h).wait_recv()
                if h == 1:
                    w_store(origin).start()
                add_part(origin, h)

    half = count // 2
    acc[...] = jnp.zeros_like(acc)
    pl.loop(0, half)(filter_step)
    if line > 2:
        arrive(early_hops, 1, begin_sides)
    deep_arrive(0, 0)
    pl.loop(half, count)(filter_step)
    for h in range(2):
        twin_deep(z, h).wait_recv()
        add_part(z, h)
    w_store(z).start()
    deep_arrive(0, 1)
    for t in range(2, line - 1):
        arrive(early_hops, t, begin_sides)
    ar_twin = remote(ar_ref.at[:, c], ar_ref.at[:, c], wps.at[3, 0], wpr.at[3, 0], twin)
    ar_twin.start()
    for h in range(2):
        deep_add(0, h)

    ar_twin.wait_recv()
    ar_rows = ar_ref.shape[0] * ar_ref.shape[1] * ar_ref.shape[2]
    ar_all = ar_ref[...].reshape(ar_rows, width)
    chunks = ar_rows // lanes
    for i in range(chunks):
        place_at = s * chunks + i
        lag = lax.div(place_at, width // lanes)
        col = lax.rem(place_at, width // lanes)
        cols = pl.ds(pl.multiple_of(col * lanes, lanes), lanes)
        for m in range(2):
            v = lagged_by(both[m, :, cols].astype(F32), lag, short[m]).astype(BF16)
            acc[m] += dot_nn(v, ar_all[i * lanes : (i + 1) * lanes])

    def twin_wide(i, k):
        part = wide_buf[i].at[k, :, c]
        return remote(part, part, wps.at[i, k], wpr.at[i, k], twin)

    for t in range(1, line - 1):
        deep_arrive(t, 0)
        if t == line - 2:
            for l in range(line):
                for x in sides(l):
                    x.wait_recv()
            for i in wide:
                for k in range(seq_count):
                    twin_wide(i, k).start()
        deep_add(t, 0)
        deep_arrive(t, 1)
        if t < line - 2:
            deep_add(t, 1)

    y_copies = []
    for m in range(2):
        for way in (0, 1):
            _, receives, _, origin = line_conditions(line, z, way, line - 2)

            @pl.when(receives)
            def _():
                if m == 0:
                    twin_deep(origin, 1).wait_recv()
                    w_store(origin).start()
                add_one(origin, 1, m)

        y_bf[m] = acc[m].astype(BF16)
        y_copies.append([])
        for i in range(1, seq_count):
            to = lax.rem(s + i, seq_count)
            y_copies[m].append(
                remote(
                    y_bf.at[m, pl.ds(pl.multiple_of(to * block, block), block), :],
                    y_in.at[i - 1, m],
                    ys.at[m, i - 1],
                    yr.at[m, i - 1],
                    {"seq": to},
                )
            )
            y_copies[m][-1].start()

    for i in wide:
        for k in range(seq_count):
            twin_wide(i, k).wait()
    sent(early_hops)
    for h in range(2):
        sent(deep_hops(h))
        for l in range(line):
            twin_deep(l, h).wait_send()
    for l in range(line):
        w_store(l).wait()
        for x in sides(l):
            x.wait_send()
    for x in toks + gain_sides + gain_lines + [ar_twin, gain_twin]:
        x.wait_send()
    for k in range(count):
        ul_store(k).wait()

    mlp_scale = gain[1:2, :]
    hidden_units = gb_ref.shape[1]
    step = hidden_units // seq_count
    root = 0.7978845608028654
    mlp_ref[...] = jnp.zeros_like(mlp_ref)
    dy_copies = []
    ends = []
    for m in range(2):
        own = slice(m * block, (m + 1) * block)
        h = tok_ref[m].astype(F32) + acc[m, mine, :]
        for i, x in enumerate(y_copies[m]):
            x.wait_recv()
            h = h + y_in[i, m].astype(F32)
        hid[own, :] = h
        inv_two = lax.rsqrt(jnp.mean(h * h, axis=-1, keepdims=True) + EPSILON)
        z_ref[own, :] = (h * inv_two * mlp_scale).astype(BF16)
        dz[...] = jnp.zeros_like(dz)

        @pl.loop(0, seq_count)
        def _(j):
            part = pl.ds(pl.multiple_of(j * step, step), step)
            gate_w = wide_buf[0][:, :, :, :, part].reshape(width, step)
            up_w = wide_buf[1][:, :, :, :, part].reshape(width, step)
            down_w = wide_buf[2][j].reshape(step, width)
            gate = dot_nn(z_ref[own, :], gate_w)
            up = dot_nn(z_ref[own, :], up_w)
            back = dot_nt(cot_ref[own, :], down_w)
            square = gate * gate
            tan = jnp.tanh(root * (gate + 0.044715 * (square * gate)))
            share = 0.5 * (1.0 + tan)
            gelu = gate * share
            slope = share + 0.5 * gate * (1.0 - tan * tan) * (
                root * (1.0 + (3.0 * 0.044715) * square)
            )
            mixed_ref[own, part] = (gelu * up).astype(BF16)
            gate_back = (back * up * slope).astype(BF16)
            up_back = (back * gelu).astype(BF16)
            gb_ref[own, part] = gate_back
            ub_ref[own, part] = up_back
            dz[...] += dot_nt(gate_back, gate_w) + dot_nt(up_back, up_w)

        grad = dz[...]
        h = hid[own, :]
        scaled = grad * mlp_scale
        centre = jnp.mean(scaled * h, axis=-1, keepdims=True)
        cube = inv_two * inv_two * inv_two
        dh = cot_ref[own, :].astype(F32) + inv_two * scaled - h * cube * centre
        dy_own[m] = dh.astype(BF16)
        for i in range(1, seq_count):
            to = {"seq": lax.rem(s + i, seq_count)}
            dst = dy_hbm.at[m, mine, :]
            dy_copies.append(remote(dy_own.at[m], dst, ds_.at[m, i - 1], dr_.at[m, i - 1], to))
            dy_copies[-1].start()
        ends.append(pltpu.make_async_copy(dy_own.at[m], dy_hbm.at[m, mine, :], end_sem.at[7 + m]))
        ends[-1].start()
        hg_ref[m] = dh
        mlp_ref[0:1, :] += jnp.sum(grad * h * inv_two, axis=0, keepdims=True)
    ends.append(pltpu.make_async_copy(hg_ref, results[0], end_sem.at[5]))
    ends[-1].start()
    share = wide_in[0].shape[0]
    down_share = wide_in[2].shape[0]

    @pl.loop(0, seq_count)
    def _(j):
        part = pl.ds(pl.multiple_of(j * step, step), step)
        for which, back in ((0, gb_ref), (1, ub_ref)):
            val = dot_tn(z_ref[...], back[:, part]).astype(BF16)
            for k in range(seq_count):
                for l in range(line):
                    for cc in range(CORES):
                        r = ((k * line + l) * CORES + cc) * share
                        grads[cc, k, l, which * share : (which + 1) * share, part] = val[
                            r : r + share
                        ]
        val = dot_tn(mixed_ref[:, part], cot_ref[...]).astype(BF16)
        for l in range(line):
            for cc in range(CORES):
                r = (l * CORES + cc) * down_share
                for q in range(down_share // share):
                    grads[cc, j, l, 2 * share :, q * width : (q + 1) * width] = val[
                        r + q * share : r + (q + 1) * share
                    ]

    ends.append(pltpu.make_async_copy(grads, grads_hbm, end_sem.at[9]))
    ends[-1].start()
    last = pltpu.make_async_copy(out_ref, results[1], end_sem.at[6])
    total = hid[...]
    for j in range(seq_count):
        down_w = wide_buf[2][j].reshape(step, width)
        total = total + dot_nn(mixed_ref[:, j * step : (j + 1) * step], down_w)
    for m in range(2):
        out_ref[m] = total[m * block : (m + 1) * block]
    last.start()
    for x in y_copies[0] + y_copies[1]:
        x.wait_send()
    for x in ends + [last, u_store]:
        x.wait()
    for x in dy_copies:
        x.wait()


def mix_front(seq_count, line, layout, tok, filters, gains, cot, spec, ar, wide):
    _, block, width = tok.shape
    rows = block * seq_count
    count = filters.shape[0] // seq_count
    hidden_units = wide[0].shape[1]
    small = (16, width)
    vmem = pltpu.VMEM
    share = wide[0].shape[0]
    part = 2 * share + wide[2].shape[0] * width // hidden_units
    grads = (CORES, seq_count, line, part, hidden_units)
    out_shape = [
        jax.ShapeDtypeStruct((line, CORES * spec.shape[0], width), BF16),
        jax.ShapeDtypeStruct((2 * count, 2, rows, width), BF16),
        jax.ShapeDtypeStruct((2, rows, width), BF16),
    ]
    local = [
        ((2 * block, width), BF16),
        ((2 * block, hidden_units), BF16),
        ((2 * block, hidden_units), BF16),
        ((2 * block, hidden_units), BF16),
        ((2, block, width), F32),
        ((2, block, width), F32),
    ]
    out_shape += [jax.ShapeDtypeStruct(*x) for x in local[4:]]
    out_shape += [
        jax.ShapeDtypeStruct((2, rows, width), BF16),
        jax.ShapeDtypeStruct(grads, BF16),
        jax.ShapeDtypeStruct((line, CORES) + ar.shape, BF16),
        jax.ShapeDtypeStruct((8, width), F32),
        jax.ShapeDtypeStruct((8, width), F32),
    ]
    scratch = [
        vmem(grads, BF16),
        vmem((2, rows, width), BF16),
        vmem((2, rows, 2 * width), BF16),
        vmem((2, rows, width), F32),
        vmem((2, rows, width), BF16),
        vmem((seq_count - 1, 2, block, width), BF16),
        vmem((line, CORES * spec.shape[0], width), BF16),
        vmem((2 * count, 2, rows, width), BF16),
        vmem((2, rows, rows), BF16),
        vmem((2 * block, width), F32),
        vmem((block, width), F32),
        vmem((2, block, width), BF16),
    ]
    scratch += [vmem(*x) for x in local]
    scratch += [vmem((seq_count, line, CORES) + x.shape, BF16) for x in wide]
    scratch += [
        vmem(small, F32),
        vmem(small, BF16),
        vmem((seq_count - 1,) + small, BF16),
        vmem(small, BF16),
        vmem((line - 1,) + small, BF16),
        vmem(small, BF16),
        vmem(small, BF16),
        DMA((6,)),
        DMA((count,)),
        DMA((line,)),
        DMA((seq_count - 1,)),
        DMA((seq_count - 1,)),
        DMA((2, seq_count - 1)),
        DMA((2, seq_count - 1)),
        DMA((2, 2, line - 1)),
        DMA((2, 2, line - 1)),
        DMA((4, 2, line - 1)),
        DMA((4, 2, line - 1)),
        DMA((2, line)),
        DMA((2, line)),
        DMA((3, line, seq_count - 1)),
        DMA((3, line, seq_count - 1)),
        DMA((4, seq_count)),
        DMA((4, seq_count)),
        DMA((seq_count + line,)),
        DMA((seq_count + line,)),
        DMA((2, seq_count - 1)),
        DMA((2, seq_count - 1)),
        DMA((10,)),
    ]
    return pl.pallas_call(
        functools.partial(mix_front_kernel, seq_count, line),
        out_shape=out_shape,
        in_specs=[pl.BlockSpec(memory_space=pltpu.SMEM)] + [WHOLE] * 5 + [ANY] * 5,
        out_specs=[ANY] * 7 + [WHOLE] * 3,
        scratch_shapes=scratch,
        compiler_params=params(7),
        name="mix_front",
    )(layout, tok, filters, *gains, cot, spec, ar, *wide)


def finish_kernel(count, share, *refs):
    ins, small = refs[:count], refs[count]
    outs, first, second = refs[count + 1 : 2 * count + 1], refs[2 * count + 1], refs[2 * count + 2]
    held, sem = refs[2 * count + 3 : 3 * count + 3], refs[3 * count + 3]
    loads = [pltpu.make_async_copy(ins[i], held[i], sem.at[0, i]) for i in range(count)]
    stores = [pltpu.make_async_copy(held[i], outs[i], sem.at[1, i]) for i in range(count)]
    for x in loads:
        x.start()
    first[...] = small[0:1, :share]
    second[...] = small[1:2, :share]
    for x, y in zip(loads, stores):
        x.wait()
        y.start()
    for x in stores:
        x.wait()


def finish(share, arrays, small):
    count = len(arrays)
    row = jax.ShapeDtypeStruct((1, share), F32)
    return pl.pallas_call(
        functools.partial(finish_kernel, count, share),
        out_shape=[jax.ShapeDtypeStruct(x.shape, x.dtype) for x in arrays] + [row, row],
        in_specs=[ANY] * count + [WHOLE],
        out_specs=[ANY] * count + [WHOLE] * 2,
        scratch_shapes=[pltpu.VMEM(x.shape, x.dtype) for x in arrays] + [DMA((2, count))],
        compiler_params=params(),
        name="finish",
    )(*arrays, small)


def body(
    tokens,
    layout,
    filters,
    gain_mix,
    spectral_proj,
    ar_proj,
    gain_mlp,
    w_gate,
    w_up,
    w_down,
    out_grad,
):
    seq_count = lax.axis_size("seq")
    line = lax.axis_size("grp") // CORES
    s = lax.axis_index("seq")
    g = lax.axis_index("grp")
    block, width = tokens.shape[2], tokens.shape[3]
    rows = block * seq_count
    count = filters.shape[1] // seq_count
    hidden_units = w_gate.shape[1]
    spans = (rows, rows // 4)

    share = gain_mix.shape[0]
    ar_rows = ar_proj.shape[0] * CORES * line
    mine = lax.dynamic_slice(filters.T, (s * count, 0), (count, rows))[:, None, :]
    nothing = jnp.zeros((count, 1, rows), F32)
    back_table = jnp.concatenate([mine, nothing], axis=2)
    aligned = share % 16 == 0 and ar_proj.shape[0] % 16 == 0 and 2 * count % line == 0
    aligned = aligned and ar_rows % 128 == 0 and line > 2

    if aligned:
        own = tokens[:, 0]
        cot = out_grad.reshape(2 * block, width)
        flags = layout.reshape(1, 2)
        spec, ul, u, dh, out, dy, grads, ar, gains, mlp_grad = mix_front(
            seq_count,
            line,
            flags,
            own,
            filters.T,
            (gain_mix.reshape(1, share), gain_mlp.reshape(1, share)),
            cot,
            spectral_proj,
            ar_proj,
            (w_gate, w_up, w_down),
        )
        input_grad, dw, dar, gate_grad, up_grad, down_grad, small = mix_back(
            seq_count,
            line,
            flags,
            dy,
            u,
            filters.T,
            spec.reshape(count, 2, width, width),
            ul,
            ar.reshape(ar_rows, width),
            own,
            dh,
            gains,
            grads,
            mlp_grad,
            (share, w_down.shape[0], spectral_proj.shape[0], ar_proj.shape[0]),
        )
        dw, out, input_grad, down_grad, gate_grad, up_grad, dar, mix_grad, mlp_grad = finish(
            share, (dw, out, input_grad, down_grad, gate_grad, up_grad, dar), small
        )
        return (
            out.reshape(tokens.shape),
            input_grad.reshape(tokens.shape),
            mix_grad.reshape(share),
            dw,
            dar,
            mlp_grad.reshape(share),
            gate_grad,
            up_grad,
            down_grad,
        )

    swap = layout[0, 0] == 1
    own = jnp.where(swap, tokens[::-1, 0], tokens[:, 0])
    cotangent = jnp.where(swap, out_grad[::-1, 0], out_grad[:, 0])
    gains = jnp.zeros((16, 128), BF16)
    gains = gains.at[0, :share].set(gain_mix).at[1, :share].set(gain_mlp)
    x_all, spec, ar, gate_w, up_w, down_w, gains = gather_all(
        seq_count, line, own, (spectral_proj, ar_proj), (w_gate, w_up, w_down, gains)
    )
    ar_full = lax.dynamic_update_slice(
        jnp.zeros((3 * width, width), BF16), ar.reshape(ar_rows, width), (s * ar_rows, 0)
    )
    gains = gains.reshape(-1, 16, 128).astype(F32)
    mix_scale = gains[:, 0, :share].reshape(1, width)
    mlp_scale = gains[:, 1, :share].reshape(1, width)
    fore_table = jnp.concatenate([mine[:, :, :1], nothing, mine[:, :, :0:-1]], axis=2)
    split = spec.reshape(count, 2, width, width)
    ul, u, y = forward_mix(spans, x_all, mix_scale, fore_table, split, ar_full)
    mixer = side_sum(seq_count, line, y, 3).reshape(2 * block, width)
    spec = spec.reshape(count, 2, width, width)
    gate_w = gate_w.reshape(width, hidden_units)
    up_w = up_w.reshape(width, hidden_units)
    down_w = down_w.reshape(hidden_units, width)

    inputs = own.reshape(2 * block, width).astype(F32)
    cot = cotangent.reshape(2 * block, width)
    hidden = inputs + mixer
    inv_two = lax.rsqrt(jnp.mean(hidden * hidden, axis=-1, keepdims=True) + EPSILON)
    mlp_in = (hidden * inv_two * mlp_scale).astype(BF16)
    gate = dot_nn(mlp_in, gate_w)
    upval = dot_nn(mlp_in, up_w)
    product_val, gelu_pull = jax.vjp(lambda a, b: jax.nn.gelu(a) * b, gate, upval)
    mixed = product_val.astype(BF16)
    out = hidden + dot_nn(mixed, down_w)
    mixed_grad = dot_nt(cot, down_w)
    gate_back, up_back = gelu_pull(mixed_grad)
    gate_back = gate_back.astype(BF16)
    up_back = up_back.astype(BF16)
    mlp_in_grad = dot_nt(gate_back, gate_w) + dot_nt(up_back, up_w)
    scaled_two = mlp_in_grad * mlp_scale
    mlp_grad = jnp.sum(mlp_in_grad * hidden * inv_two, axis=0, keepdims=True)
    hidden_grad = (
        cot.astype(F32)
        + inv_two * scaled_two
        - hidden * inv_two**3 * jnp.mean(scaled_two * hidden, axis=-1, keepdims=True)
    )
    mixer_grad = hidden_grad.astype(BF16)

    down_grad = dot_tn(mixed, cot)
    gate_grad = dot_tn(mlp_in, gate_back)
    up_grad = dot_tn(mlp_in, up_back)
    dy = side_gather(seq_count, line, mixer_grad.reshape(2, block, width))
    dw, dar, du = backward_mix(spans, dy, u, back_table, spec, ul, ar_full)
    normed_grad = side_sum(seq_count, line, du, 4).reshape(2 * block, width)

    inv_one = lax.rsqrt(jnp.mean(inputs * inputs, axis=-1, keepdims=True) + EPSILON)
    scaled_one = normed_grad * mix_scale
    mix_grad = jnp.sum(normed_grad * inputs * inv_one, axis=0, keepdims=True)
    input_grad = (
        hidden_grad
        + inv_one * scaled_one
        - inputs * inv_one**3 * jnp.mean(scaled_one * inputs, axis=-1, keepdims=True)
    )

    dar = lax.dynamic_slice(dar, (s * ar_rows, 0), (ar_rows, width))
    deep = (dw.reshape(line, CORES, -1, width), dar.reshape(line, CORES, -1, width))
    wide = tuple(
        x.astype(BF16).reshape(seq_count, line, CORES, -1, x.shape[1])
        for x in (gate_grad, up_grad, down_grad)
    )
    small = jnp.concatenate([mix_grad, mlp_grad, jnp.zeros((6, width), F32)], axis=0)
    dw, dar, gate_grad, up_grad, down_grad, small = sum_all(seq_count, line, deep, wide, small)
    small = lax.dynamic_slice(small, (0, (s * CORES * line + g) * share), (2, share))

    def settle(x):
        x = x.reshape(2, 1, block, width)
        return jnp.where(swap, x[::-1], x)

    return (
        settle(out),
        settle(input_grad),
        small[0],
        dw,
        dar,
        small[1],
        gate_grad,
        up_grad,
        down_grad,
    )


def solution(mesh):
    placed = (
        P(None, "grp", "seq", None),
        P(None, "grp"),
        P(),
        P(("seq", "grp")),
        P(("seq", "grp"), None),
        P(("seq", "grp"), None),
        P(("seq", "grp")),
        P(("seq", "grp"), None),
        P(("seq", "grp"), None),
        P(("seq", "grp"), None),
        P(None, "grp", "seq", None),
    )
    return jax.shard_map(
        body,
        mesh=mesh,
        in_specs=placed,
        out_specs=(
            P(None, "grp", "seq", None),
            P(None, "grp", "seq", None),
            P(("seq", "grp")),
            P(("seq", "grp"), None),
            P(("seq", "grp"), None),
            P(("seq", "grp")),
            P(("seq", "grp"), None),
            P(("seq", "grp"), None),
            P(("seq", "grp"), None),
        ),
        check_vma=False,
    )
```
